32 devices in a mesh: dp: 8 (over z, core), expert: 4 (over y, x).
Axes of the slice: x: 2, y: 2, z: 4, core: 2. Of those that a mesh axis runs over, the one named last changes fastest.
Arguments:
- tokens: bfloat16 [2, 8, 1024, 768], P(None, 'dp', 'expert'), may hold values from -6 to 6
- cotangent: bfloat16 [2, 8, 1024, 768], P(None, 'dp', 'expert'), may hold values from -6 to 6
- expert_ids: int32 [2, 8, 1024, 1], P(None, 'dp', 'expert'), may hold values from 0 to 3; in each aligned block of 256 rows (0 to 255, 256 to 511, ..., all dimensions but the last counted through in order) at most 128 rows name the same one
- w_qkv: bfloat16 [768, 2304], P(None, ('dp', 'expert')), may hold values from -0.21875 to 0.21875
- w_out: bfloat16 [768, 768], P(None, ('dp', 'expert')), may hold values from -2.5 to 2.5
- ln_gains: bfloat16 [2, 768], P(None, ('dp', 'expert')), may hold values from 0.5 to 1.5
- ln_biases: bfloat16 [2, 768], P(None, ('dp', 'expert')), may hold values from -1.1953125 to 1.1953125
- router: bfloat16 [768, 4], P(('dp', 'expert')), may hold values from -0.21875 to 0.21875
- w_up: bfloat16 [4, 768, 3072], P('expert', 'dp'), may hold values from -0.21875 to 0.21875
- w_down: bfloat16 [4, 3072, 768], P('expert', 'dp'), may hold values from -0.21875 to 0.21875
Outputs:
- output: bfloat16 [2, 8, 1024, 768], P(None, 'dp', 'expert')
- grad_tokens: float32 [2, 8, 1024, 768], P(None, 'dp', 'expert')
- grad_qkv: float32 [768, 2304], P(None, ('dp', 'expert'))
- grad_out: float32 [768, 768], P(None, ('dp', 'expert'))
- grad_gains: float32 [2, 768], P(None, ('dp', 'expert'))
- grad_biases: float32 [2, 768], P(None, ('dp', 'expert'))
- grad_router: float32 [768, 4], P(('dp', 'expert'))
- grad_up: float32 [4, 768, 3072], P('expert', 'dp')
- grad_down: float32 [4, 3072, 768], P('expert', 'dp')
The draws below stay inside these ranges and needn't reach their ends.
Inputs may be any that keep to these rules, and one draw needn't show every extreme that they name: `expert_ids`: in every aligned block of 256 positions of a sequence no expert is named more than 128 times, and in some blocks one expert is named exactly 128 times.
All inputs are finite; a program needn't handle non-finite values.
Results may differ from the reference program's by a relative error of at most 0.019.
Values may be sent and summed in bfloat16 or wider, within the bound.
A program may use at most 256 MiB of HBM per device.

```python
import math
import jax
import jax.numpy as jnp
import numpy as np
from jax import lax

D = 768
HEADS = 12
FF = 3072
LOCAL_LEN = 256
BLK = 256
MICRO = 2
SEQ_LEN = 1024
SEQS = 8
EXPERTS = 4
CAP = 128
N_EXPERT = 4


def block_levels(stream_key, dims, split, least, high):
    factor_of = 1.0
    for dim, shards_of in split:
        draws = jax.random.uniform(jax.random.fold_in(jax.random.fold_in(stream_key, 6), dim), (shards_of,), jnp.float32, least / len(split), high / len(split))
        factor_of = factor_of * jnp.repeat(jnp.exp(draws), dims[dim] // shards_of).reshape((-1,) + (1,) * (len(dims) - 1 - dim))
    return factor_of


def routed_block(key, own, number, rows, count, top, reach, skew):
    order = jax.random.permutation(key, count)
    crowded, common = shares(count, rows * top, reach, skew, True), shares(count, rows * top, reach, skew, False)
    places = jnp.arange(count)

    def named(tallies, offset_by):
        used = int((tallies > 0).sum())
        fixed = max(1, used // 4)
        moved = fixed + (places - fixed + offset_by * (used - fixed)) % max(1, count - fixed)
        return jnp.zeros((count,), jnp.int32).at[order[jnp.where(places < fixed, places, moved)]].set(jnp.asarray(tallies, jnp.int32))

    tallies = jnp.where(number % 4 == 0, named(crowded, number // 4), named(common, number - number // 4 - 1))
    mixed = jax.random.permutation(jax.random.fold_in(own, 3), count)
    source_of, sink = mixed[0:count // 2 * 2:2], mixed[1:count // 2 * 2:2]
    room = jnp.minimum(tallies[source_of] - 1, reach - tallies[sink]) // 2
    room = jnp.where((source_of == order[0]) | (sink == order[0]) | (tallies[sink] == 0), 0, jnp.maximum(room, 0))
    moved = jax.random.randint(jax.random.fold_in(own, 4), (count // 2,), 0, 1 << 20) % (room + 1)
    tallies = tallies.at[source_of].add(-moved).at[sink].add(moved)
    labels = jnp.searchsorted(jnp.cumsum(tallies), jnp.arange(rows * top), side="right").astype(jnp.int32)
    table = labels.reshape(top, rows).T
    table = table[jax.random.permutation(jax.random.fold_in(own, 1), rows)]
    offset_by = jax.random.randint(jax.random.fold_in(own, 2), (rows, 1), 0, top)
    return jnp.take_along_axis(table, (jnp.arange(top)[None, :] + offset_by) % top, axis=1)


def shares(count, total, most, slope, full):
    weights = [(1 << 20) // math.isqrt(rank ** slope) + 1 for rank in range(1, count + 1)]
    largest = most if full else min(most, max(-(-total // count), total * weights[0] // sum(weights)))
    least = 1 if total - largest >= count - 1 else 0
    holding, rest = [largest] + [least] * (count - 1), total - largest - least * (count - 1)
    while rest > 0:
        movable = [i for i in range(1, count) if holding[i] < largest] or [i for i in range(1, count) if holding[i] < most]
        pool, left = sum([weights[i] for i in movable]), rest
        for i in movable:
            addition = min(most - holding[i], max(1, left * weights[i] // pool), rest)
            holding[i] = holding[i] + addition
            rest = rest - addition
    return np.array(holding)


def scatter_about(own_key, dims, width, limit, shards=(), kind=jnp.bfloat16):
    drawn = jax.random.normal(own_key, dims, jnp.float32) * width
    if len(shards) > 0:
        drawn = block_levels(own_key, dims, shards, -0.22, 0.18) * drawn
    return jnp.clip(drawn, min=-limit, max=limit).astype(kind)


def setup_inputs(seed: int = 0) -> dict:
    arg_keys = jax.random.split(jax.random.key(seed), 11)
    tokens = scatter_about(arg_keys[0], (MICRO, SEQS, SEQ_LEN, D), 1.0, 6.0, ((1, 8), (2, 4)))
    cotangent = scatter_about(arg_keys[1], (MICRO, SEQS, SEQ_LEN, D), 1.0, 6.0, ((1, 8), (2, 4)))
    expert_ids_keys = jax.random.split(jax.random.fold_in(arg_keys[2], 1), MICRO * SEQS * SEQ_LEN // LOCAL_LEN)
    expert_ids_turns = jax.random.permutation(jax.random.fold_in(arg_keys[2], 3), MICRO * SEQS * SEQ_LEN // LOCAL_LEN)
    expert_ids = jax.vmap(lambda own, number: routed_block(jax.random.fold_in(arg_keys[2], 2), own, number, LOCAL_LEN, EXPERTS, 1, CAP, 1))(expert_ids_keys, expert_ids_turns).reshape((MICRO, SEQS, SEQ_LEN, 1))
    w_qkv = scatter_about(arg_keys[3], (D, 3 * D), D ** -0.5, 0.21875, ((1, 32),))
    w_out = scatter_about(arg_keys[4], (D, D), (D // 128) ** -0.5, 2.5, ((1, 32),))
    ln_gains = jnp.clip(1.0 + 0.1 * jax.random.normal(arg_keys[5], (2, D), jnp.float32), 0.5, 1.5).astype(jnp.bfloat16)
    ln_biases = scatter_about(arg_keys[6], (2, D), 0.2, 1.1953125, ((1, 32),))
    router = scatter_about(arg_keys[7], (D, EXPERTS), D ** -0.5, 0.21875, ((0, 32),))
    w_up = scatter_about(arg_keys[8], (EXPERTS, D, FF), D ** -0.5, 0.21875, ((0, 4), (1, 8)))
    w_down = scatter_about(arg_keys[9], (EXPERTS, FF, D), (FF // 4) ** -0.5, 0.21875, ((0, 4), (1, 8)))
    return {"tokens": tokens, "cotangent": cotangent, "expert_ids": expert_ids, "w_qkv": w_qkv, "w_out": w_out, "ln_gains": ln_gains, "ln_biases": ln_biases, "router": router, "w_up": w_up, "w_down": w_down}


epsilon = 1e-05
balance_coef = 8.0
neg_big = -1e+30
highest = lax.Precision.HIGHEST

@jax.custom_vjp
def low(v):
    return lax.optimization_barrier(v.astype(jnp.bfloat16)).astype(jnp.float32)

@jax.custom_vjp
def low_back(v):
    return v

def low_keep(v):
    return (low(v), None)

def low_pass(kept, grad):
    return (grad,)

def back_keep(v):
    return (v, None)

def back_low(kept, grad):
    return (low(grad),)
low.defvjp(low_keep, low_pass)
low_back.defvjp(back_keep, back_low)

def layer_norm(features, gain_vec, shift_vec):
    centre = features - lax.optimization_barrier(jnp.mean(features, axis=-1, keepdims=True))
    spread = lax.optimization_barrier(jnp.mean(centre * centre, axis=-1, keepdims=True))
    return centre * lax.rsqrt(spread + epsilon) * gain_vec + shift_vec

def gelu_exact(preact):
    return jax.nn.gelu(preact, approximate=False)

def attention(queries, key_rows, value_rows):
    seq_len = queries.shape[0]
    head_dim = D // HEADS
    block_rows = math.gcd(seq_len, 512)
    key_heads = key_rows.reshape(seq_len, HEADS, head_dim)
    value_heads = value_rows.reshape(seq_len, HEADS, head_dim)
    key_block = lax.iota(jnp.int32, seq_len) // BLK

    def one_block(block_index):
        first = block_index * block_rows
        query_rows = lax.dynamic_slice_in_dim(queries, first, block_rows, 0).reshape(block_rows, HEADS, head_dim)
        query_block = (first + lax.iota(jnp.int32, block_rows)) // BLK
        raw = low_back(jnp.einsum('qhd,khd->hqk', query_rows, key_heads, precision=highest))
        scores = raw * (1.0 / math.sqrt(head_dim))
        allowed = key_block[None, :] <= query_block[:, None]
        scores = jnp.where(allowed[None, :, :], scores, neg_big)
        weights = jax.nn.softmax(scores, axis=-1)
        mixed_out = jnp.einsum('hqk,khd->qhd', low(weights), value_heads, precision=highest)
        return mixed_out.reshape(block_rows, D)
    blocks = lax.map(jax.checkpoint(one_block), jnp.arange(seq_len // block_rows, dtype=jnp.int32))
    return blocks.reshape(seq_len, D)

def forward(inputs, expert_of, params, load_ratio):
    qkv_w, out_w, gains, shifts, router_w, up_w, down_w = params
    seq_len = inputs.shape[0]
    normed = layer_norm(inputs, gains[0], shifts[0])
    projected = low(low_back(jnp.dot(low(normed), qkv_w, precision=highest, preferred_element_type=jnp.float32)))
    queries = projected[:, :D]
    key_rows = projected[:, D:2 * D]
    value_rows = projected[:, 2 * D:]
    attended = low(low_back(attention(queries, key_rows, value_rows)))
    middle = inputs + low_back(jnp.dot(attended, out_w, precision=highest, preferred_element_type=jnp.float32))
    mixed_rows = low(layer_norm(middle, gains[1], shifts[1]))
    matches = expert_of[:, None] == jnp.arange(EXPERTS, dtype=jnp.int32)[None, :]
    onehot = matches.astype(jnp.float32)
    logits = jnp.dot(mixed_rows, router_w, precision=highest, preferred_element_type=jnp.float32)
    gates = jax.nn.sigmoid(lax.optimization_barrier(jnp.sum(logits * onehot, axis=1)))
    expert_in = low_back(mixed_rows)
    counted = matches.astype(jnp.int32)
    order_in = lax.optimization_barrier(jnp.sum((jnp.cumsum(counted, axis=0) - counted) * counted, axis=1))
    slot_count = N_EXPERT * CAP
    target = expert_of * slot_count + order_in
    slot_table = jnp.full((EXPERTS * slot_count,), seq_len, jnp.int32).at[target].set(jnp.arange(seq_len, dtype=jnp.int32))
    padded = jnp.concatenate([expert_in, jnp.zeros((1, D), jnp.float32)], axis=0)
    slot_rows = padded[slot_table].reshape(EXPERTS, slot_count, D)
    preact = low_back(jnp.einsum('esd,edf->esf', slot_rows, up_w, precision=highest))
    hidden = low(gelu_exact(preact))
    result = low_back(low(jnp.einsum('esf,efd->esd', hidden, down_w, precision=highest)))
    returned = result.reshape(EXPERTS * slot_count, D)[target]
    final = middle + gates[:, None] * returned
    balance = balance_coef * jnp.sum(lax.optimization_barrier(jnp.sum(onehot * load_ratio[None, :], axis=1)) * gates)
    return (final, balance)

def reference(tokens, cotangent, expert_ids, w_qkv, w_out, ln_gains, ln_biases, router, w_up, w_down):
    seq_total = MICRO * SEQS
    expert_of = expert_ids.reshape(seq_total, SEQ_LEN)
    flat_ids = expert_of.reshape(-1)
    counts = lax.optimization_barrier(jnp.sum((flat_ids[:, None] == jnp.arange(EXPERTS, dtype=jnp.int32)[None, :]).astype(jnp.float32), axis=0))
    mean_load = jnp.sum(counts) / EXPERTS
    load_ratio = (counts - mean_load) / mean_load
    params = tuple((weight.astype(jnp.float32) for weight in (w_qkv, w_out, ln_gains, ln_biases, router, w_up, w_down)))
    inputs_all = tokens.reshape(seq_total, SEQ_LEN, D).astype(jnp.float32)
    cot_all = cotangent.reshape(seq_total, SEQ_LEN, D).astype(jnp.float32)

    def one_sequence(totals, item):
        inputs, cot_rows, seq_ids = item
        outcome, pullback = jax.vjp(lambda x_in, weights: forward(x_in, seq_ids, weights, load_ratio), inputs, params)
        grad_in, grad_weights = pullback((cot_rows, jnp.ones_like(outcome[1])))
        totals = jax.tree.map(lambda running, addend: running + addend, totals, grad_weights)
        return (totals, (outcome[0].astype(jnp.bfloat16), grad_in))
    start_totals = jax.tree.map(jnp.zeros_like, params)
    totals, (finals, grads_in) = lax.scan(one_sequence, start_totals, (inputs_all, cot_all, expert_of))
    output = finals.reshape(MICRO, SEQS, SEQ_LEN, D)
    grad_tokens = grads_in.reshape(MICRO, SEQS, SEQ_LEN, D)
    return (output, grad_tokens, totals[0], totals[1], totals[2], totals[3], totals[4], totals[5], totals[6])
```

```python
import math

import jax
import jax.numpy as jnp
from jax import lax
from jax.sharding import PartitionSpec as P

HEADS = 12
FF = 3072
BLK = 256
MICRO = 2


epsilon = 1e-05
balance_coef = 8.0
neg_big = -1e30


def layer_norm(features, gain_vec, shift_vec):
    centre = features - jnp.mean(features, axis=-1, keepdims=True)
    spread = jnp.mean(centre * centre, axis=-1, keepdims=True)
    return centre * lax.rsqrt(spread + epsilon) * gain_vec + shift_vec


def gelu_exact(preact):
    return jax.nn.gelu(preact, approximate=False)


def fetch_all(w_qkv, w_out, ln_gains, ln_biases, router, w_up, w_down):
    dense_set = (
        lax.all_gather(w_qkv, ("dp", "expert"), axis=1, tiled=True),
        lax.all_gather(w_out, ("dp", "expert"), axis=1, tiled=True),
        lax.all_gather(ln_gains, ("dp", "expert"), axis=1, tiled=True),
        lax.all_gather(ln_biases, ("dp", "expert"), axis=1, tiled=True),
        lax.all_gather(router, ("dp", "expert"), axis=0, tiled=True),
    )
    expert_set = (
        lax.all_gather(w_up, "dp", axis=1, tiled=True),
        lax.all_gather(w_down, "dp", axis=1, tiled=True),
    )
    return tuple(dense_set) + tuple(expert_set)


def route_slots(expert_of, experts, capacity):
    seq_here, local_len = expert_of.shape
    matches = (expert_of[..., None] == lax.iota(jnp.int32, experts)).astype(jnp.int32)
    order_in = jnp.sum((jnp.cumsum(matches, axis=1) - matches) * matches, axis=-1)
    seq_index = lax.broadcasted_iota(jnp.int32, (seq_here, local_len), 0)
    target = (expert_of * (seq_here * capacity) + seq_index * capacity + order_in).reshape(-1)
    slot_table = jnp.full((experts * seq_here * capacity,), seq_here * local_len, jnp.int32)
    slot_table = slot_table.at[target].set(lax.iota(jnp.int32, seq_here * local_len))
    return (target, slot_table)


def to_slots(features, slot_table):
    flat_rows = features.reshape(-1, features.shape[-1])
    padded = jnp.concatenate(
        [flat_rows, jnp.zeros((1, flat_rows.shape[1]), flat_rows.dtype)], axis=0
    )
    return padded[slot_table]


def score_terms(
    queries, grad_rows, key_block, value_block, log_total, row_delta, allowed, score_scale
):
    scores = (
        jnp.einsum("sqhd,skhd->shqk", queries, key_block, preferred_element_type=jnp.float32)
        * score_scale
    )
    weights = jnp.where(allowed, jnp.exp(scores - log_total[..., None]), 0.0)
    grad_weights = jnp.einsum(
        "sqhd,skhd->shqk", grad_rows, value_block, preferred_element_type=jnp.float32
    )
    grad_scores = (weights * (grad_weights - row_delta[..., None]) * score_scale).astype(
        jnp.bfloat16
    )
    return (weights.astype(jnp.bfloat16), grad_scores)


def attention_forward(queries, key_rows, value_rows, query_pos, score_scale):
    seq_here, local_len, head_count, head_dim = queries.shape
    last_block = query_pos[local_len - 1] // BLK
    start_state = (
        jnp.full((seq_here, head_count, local_len), neg_big, jnp.float32),
        jnp.zeros((seq_here, head_count, local_len), jnp.float32),
        jnp.zeros((seq_here, local_len, head_count, head_dim), jnp.float32),
    )
    key_part = lax.all_gather(key_rows, "expert", axis=1, tiled=True)
    value_part = lax.all_gather(value_rows, "expert", axis=1, tiled=True)
    piece_len = key_part.shape[1]
    block_len = math.gcd(piece_len, 512)

    def attention_one_block(block_index, carried):
        within = block_index * block_len
        key_block = lax.dynamic_slice_in_dim(key_part, within, block_len, 1).reshape(
            seq_here, block_len, head_count, head_dim
        )
        value_block = lax.dynamic_slice_in_dim(value_part, within, block_len, 1).reshape(
            seq_here, block_len, head_count, head_dim
        )
        key_pos = within + lax.iota(jnp.int32, block_len)
        allowed = key_pos[None, :] // BLK <= query_pos[:, None] // BLK

        def attention_compute(current):
            run_max, run_sum, weighted = current
            scores = (
                jnp.einsum(
                    "sqhd,skhd->shqk", queries, key_block, preferred_element_type=jnp.float32
                )
                * score_scale
            )
            new_max = jnp.maximum(run_max, jnp.max(jnp.where(allowed, scores, neg_big), axis=-1))
            weights = jnp.where(allowed, jnp.exp(scores - new_max[..., None]), 0.0)
            factor = jnp.exp(run_max - new_max)
            run_sum = run_sum * factor + jnp.sum(weights, axis=-1)
            addition = jnp.einsum(
                "shqk,skhd->sqhd",
                weights.astype(jnp.bfloat16),
                value_block,
                preferred_element_type=jnp.float32,
            )
            weighted = weighted * jnp.swapaxes(factor, 1, 2)[..., None] + addition
            return (new_max, run_sum, weighted)

        return lax.cond(
            within // BLK <= last_block, attention_compute, lambda current: current, carried
        )

    run_max, run_sum, weighted = lax.fori_loop(
        0, piece_len // block_len, attention_one_block, start_state
    )
    log_total = run_max + jnp.log(run_sum)
    attended = weighted / jnp.swapaxes(run_sum, 1, 2)[..., None]
    return (log_total, attended)


def query_grads(
    queries, grad_rows, key_rows, value_rows, log_total, row_delta, query_pos, score_scale, seq_len
):
    seq_here, local_len, head_count, head_dim = queries.shape
    model_dim = head_count * head_dim
    last_block = query_pos[local_len - 1] // BLK
    start_query = jnp.zeros((seq_here, local_len, head_count, head_dim), jnp.float32)
    start_state = (start_query, jnp.zeros((seq_here, seq_len, 2 * model_dim), jnp.float32))
    key_part = lax.all_gather(key_rows, "expert", axis=1, tiled=True)
    value_part = lax.all_gather(value_rows, "expert", axis=1, tiled=True)
    piece_len = key_part.shape[1]
    block_len = math.gcd(piece_len, 512)

    def query_one_block(block_index, carried):
        within = block_index * block_len
        key_block = lax.dynamic_slice_in_dim(key_part, within, block_len, 1).reshape(
            seq_here, block_len, head_count, head_dim
        )
        value_block = lax.dynamic_slice_in_dim(value_part, within, block_len, 1).reshape(
            seq_here, block_len, head_count, head_dim
        )
        key_pos = within + lax.iota(jnp.int32, block_len)
        allowed = key_pos[None, :] // BLK <= query_pos[:, None] // BLK

        def query_compute(current):
            weights, grad_scores = score_terms(
                queries,
                grad_rows,
                key_block,
                value_block,
                log_total,
                row_delta,
                allowed,
                score_scale,
            )
            grad_query = current[0] + jnp.einsum(
                "shqk,skhd->sqhd", grad_scores, key_block, preferred_element_type=jnp.float32
            )
            grad_key = jnp.einsum(
                "shqk,sqhd->skhd", grad_scores, queries, preferred_element_type=jnp.float32
            ).reshape(seq_here, block_len, model_dim)
            grad_value = jnp.einsum(
                "shqk,sqhd->skhd", weights, grad_rows, preferred_element_type=jnp.float32
            ).reshape(seq_here, block_len, model_dim)
            old_rows = lax.dynamic_slice_in_dim(current[1], within, block_len, 1)
            summed = old_rows + jnp.concatenate([grad_key, grad_value], axis=-1)
            return (grad_query, lax.dynamic_update_slice_in_dim(current[1], summed, within, 1))

        return lax.cond(
            within // BLK <= last_block, query_compute, lambda current: current, carried
        )

    return lax.fori_loop(0, piece_len // block_len, query_one_block, start_state)


def body(tokens, cotangent, expert_ids, w_qkv, w_out, ln_gains, ln_biases, router, w_up, w_down):
    n_expert = lax.axis_size("expert")
    seq_part = lax.axis_index("expert")
    seq_here, local_len, model_dim = (tokens.shape[1], tokens.shape[2], tokens.shape[3])
    head_count = HEADS
    head_dim = model_dim // head_count
    score_scale = head_dim ** (-0.5)
    exp_dev = w_up.shape[0]
    experts = exp_dev * n_expert
    capacity = 2 * local_len // experts
    seq_len = local_len * n_expert
    query_pos = seq_part * local_len + lax.iota(jnp.int32, local_len)
    expert_range = lax.iota(jnp.int32, experts)
    all_ids = expert_ids[..., 0]
    local_counts = jnp.sum((all_ids[..., None] == expert_range).astype(jnp.float32), axis=(0, 1, 2))
    counts = lax.psum(local_counts, ("dp", "expert"))
    mean_load = jnp.sum(counts) / experts
    load_ratio = (counts - mean_load) / mean_load
    grad_qkv_w = jnp.zeros((model_dim, 3 * model_dim), jnp.float32)
    grad_out_w = jnp.zeros((model_dim, model_dim), jnp.float32)
    grad_gains = jnp.zeros((2, model_dim), jnp.float32)
    grad_shifts = jnp.zeros((2, model_dim), jnp.float32)
    grad_router = jnp.zeros((model_dim, experts), jnp.float32)
    grad_up = jnp.zeros((exp_dev, model_dim, FF), jnp.float32)
    grad_down = jnp.zeros((exp_dev, FF, model_dim), jnp.float32)
    outputs = []
    input_grads = []
    for micro_index in range(MICRO):
        fetched = fetch_all(w_qkv, w_out, ln_gains, ln_biases, router, w_up, w_down)
        qkv_full, out_full, gains_full, shifts_full, router_full, up_full, down_full = fetched
        gain_rows = gains_full.astype(jnp.float32)
        shift_rows = shifts_full.astype(jnp.float32)
        inputs = tokens[micro_index].astype(jnp.float32)
        expert_of = all_ids[micro_index]
        normed = layer_norm(inputs, gain_rows[0], shift_rows[0])
        normed_low = normed.astype(jnp.bfloat16)
        projected = jnp.einsum(
            "scd,de->sce", normed_low, qkv_full, preferred_element_type=jnp.float32
        ).astype(jnp.bfloat16)
        query_rows = projected[..., :model_dim]
        queries = query_rows.reshape(seq_here, local_len, head_count, head_dim)
        key_rows = projected[..., model_dim : 2 * model_dim]
        value_rows = projected[..., 2 * model_dim :]
        log_total, attended = attention_forward(
            queries, key_rows, value_rows, query_pos, score_scale
        )
        attended_low = attended.reshape(seq_here, local_len, model_dim).astype(jnp.bfloat16)
        middle = inputs + jnp.einsum(
            "scd,de->sce", attended_low, out_full, preferred_element_type=jnp.float32
        )
        mixed_low = layer_norm(middle, gain_rows[1], shift_rows[1]).astype(jnp.bfloat16)
        onehot = (expert_of[..., None] == expert_range).astype(jnp.float32)
        logits = jnp.einsum(
            "scd,de->sce", mixed_low, router_full, preferred_element_type=jnp.float32
        )
        gates = jax.nn.sigmoid(jnp.sum(logits * onehot, axis=-1))
        target, slot_table = route_slots(expert_of, experts, capacity)
        outgoing = to_slots(mixed_low, slot_table).reshape(
            n_expert, exp_dev, seq_here * capacity, model_dim
        )
        arrived = lax.all_to_all(outgoing, "expert", split_axis=0, concat_axis=0, tiled=True)
        preact = jnp.einsum("pesd,edf->pesf", arrived, up_full, preferred_element_type=jnp.float32)
        hidden = gelu_exact(preact).astype(jnp.bfloat16)
        result = jnp.einsum(
            "pesf,efd->pesd", hidden, down_full, preferred_element_type=jnp.float32
        ).astype(jnp.bfloat16)
        returned = lax.all_to_all(result, "expert", split_axis=0, concat_axis=0, tiled=True)
        expert_out = (
            returned.reshape(-1, model_dim)[target]
            .reshape(seq_here, local_len, model_dim)
            .astype(jnp.float32)
        )
        final = middle + gates[..., None] * expert_out
        outputs.append(final.astype(jnp.bfloat16))
        fetched = fetch_all(w_qkv, w_out, ln_gains, ln_biases, router, w_up, w_down)
        qkv_full, out_full, gains_full, shifts_full, router_full, up_full, down_full = fetched
        gain_rows = gains_full.astype(jnp.float32)
        shift_rows = shifts_full.astype(jnp.float32)
        grad_final = cotangent[micro_index].astype(jnp.float32)
        grad_gate = jnp.sum(grad_final * expert_out, axis=-1) + balance_coef * jnp.sum(
            onehot * load_ratio, axis=-1
        )
        grad_logit = grad_gate * gates * (1.0 - gates)
        grad_expert = (gates[..., None] * grad_final).astype(jnp.bfloat16)
        sent_grads = to_slots(grad_expert, slot_table).reshape(
            n_expert, exp_dev, seq_here * capacity, model_dim
        )
        grads_here = lax.all_to_all(sent_grads, "expert", split_axis=0, concat_axis=0, tiled=True)
        hidden_low = gelu_exact(preact).astype(jnp.bfloat16)
        grad_down = grad_down + jnp.einsum(
            "pesf,pesd->efd", hidden_low, grads_here, preferred_element_type=jnp.float32
        )
        grad_hidden = jnp.einsum(
            "pesd,efd->pesf", grads_here, down_full, preferred_element_type=jnp.float32
        )
        grad_pre = jax.vjp(gelu_exact, preact)[1](grad_hidden)[0].astype(jnp.bfloat16)
        grad_up = grad_up + jnp.einsum(
            "pesd,pesf->edf", arrived, grad_pre, preferred_element_type=jnp.float32
        )
        grad_arrived = jnp.einsum(
            "pesf,edf->pesd", grad_pre, up_full, preferred_element_type=jnp.float32
        ).astype(jnp.bfloat16)
        grads_back = lax.all_to_all(grad_arrived, "expert", split_axis=0, concat_axis=0, tiled=True)
        grad_mixed = (
            grads_back.reshape(-1, model_dim)[target]
            .reshape(seq_here, local_len, model_dim)
            .astype(jnp.float32)
        )
        router_cols = jnp.einsum("sce,de->scd", onehot, router_full.astype(jnp.float32))
        grad_mixed = grad_mixed + grad_logit[..., None] * router_cols
        grad_router = grad_router + jnp.einsum(
            "scd,sce->de", mixed_low.astype(jnp.float32), grad_logit[..., None] * onehot
        )
        second_back = jax.vjp(layer_norm, middle, gain_rows[1], shift_rows[1])[1]
        grad_middle, grad_gain_two, grad_shift_two = second_back(grad_mixed)
        grad_middle = grad_middle + grad_final
        grad_branch = grad_middle.astype(jnp.bfloat16)
        grad_out_w = grad_out_w + jnp.einsum(
            "scd,sce->de", attended_low, grad_branch, preferred_element_type=jnp.float32
        )
        grad_attended = jnp.einsum(
            "sce,de->scd", grad_branch, out_full, preferred_element_type=jnp.float32
        ).astype(jnp.bfloat16)
        grad_heads = grad_attended.reshape(seq_here, local_len, head_count, head_dim)
        row_delta = jnp.swapaxes(jnp.sum(grad_heads.astype(jnp.float32) * attended, axis=-1), 1, 2)
        folded = query_grads(
            queries,
            grad_heads,
            key_rows,
            value_rows,
            log_total,
            row_delta,
            query_pos,
            score_scale,
            seq_len,
        )
        grad_query = folded[0].reshape(seq_here, local_len, model_dim)
        key_value = lax.psum_scatter(
            folded[1].astype(jnp.bfloat16), "expert", scatter_dimension=1, tiled=True
        ).astype(jnp.float32)
        grad_key = key_value[..., :model_dim]
        grad_value = key_value[..., model_dim:]
        grad_projected = jnp.concatenate([grad_query, grad_key, grad_value], axis=-1).astype(
            jnp.bfloat16
        )
        grad_qkv_w = grad_qkv_w + jnp.einsum(
            "scd,sce->de", normed_low, grad_projected, preferred_element_type=jnp.float32
        )
        grad_normed = jnp.einsum(
            "sce,de->scd", grad_projected, qkv_full, preferred_element_type=jnp.float32
        )
        first_back = jax.vjp(layer_norm, inputs, gain_rows[0], shift_rows[0])[1]
        grad_inputs, grad_gain_one, grad_shift_one = first_back(grad_normed)
        grad_gains = grad_gains + jnp.stack([grad_gain_one, grad_gain_two])
        grad_shifts = grad_shifts + jnp.stack([grad_shift_one, grad_shift_two])
        input_grads.append(grad_middle + grad_inputs)
    dense_grads = (
        lax.psum_scatter(grad_qkv_w, ("dp", "expert"), scatter_dimension=1, tiled=True),
        lax.psum_scatter(grad_out_w, ("dp", "expert"), scatter_dimension=1, tiled=True),
        lax.psum_scatter(grad_gains, ("dp", "expert"), scatter_dimension=1, tiled=True),
        lax.psum_scatter(grad_shifts, ("dp", "expert"), scatter_dimension=1, tiled=True),
        lax.psum_scatter(grad_router, ("dp", "expert"), scatter_dimension=0, tiled=True),
    )
    expert_grads = (
        lax.psum_scatter(
            grad_up.astype(jnp.bfloat16), "dp", scatter_dimension=1, tiled=True
        ).astype(jnp.float32),
        lax.psum_scatter(
            grad_down.astype(jnp.bfloat16), "dp", scatter_dimension=1, tiled=True
        ).astype(jnp.float32),
    )
    return (jnp.stack(outputs), jnp.stack(input_grads)) + tuple(dense_grads) + tuple(expert_grads)


def fast_body(tokens, cotangent, expert_ids, w_qkv, w_out, ln_gains, ln_biases, router, w_up, w_down):
    bf, f32 = jnp.bfloat16, jnp.float32
    n_expert, n_dp = lax.axis_size("expert"), lax.axis_size("dp")
    ex, dp = lax.axis_index("expert"), lax.axis_index("dp")
    both = ("dp", "expert")
    n_dev = n_dp * n_expert
    seqs, local_len, dim = tokens.shape[0] * tokens.shape[1], tokens.shape[2], tokens.shape[3]
    head_dim = dim // HEADS
    heads = HEADS // n_expert
    width = heads * head_dim
    total_len = local_len * n_expert
    experts = n_expert
    cap = 2 * local_len // experts
    scale = head_dim ** -0.5
    qc, oc = w_qkv.shape[1], w_out.shape[1]
    ids = expert_ids.reshape(seqs, local_len)
    onehot = (ids[..., None] == lax.iota(jnp.int32, experts)).astype(f32)
    counts = jnp.sum(onehot, axis=(0, 1))
    high = jnp.floor(counts / 16)
    tally = jnp.concatenate([high, counts - 16 * high]).astype(bf)
    small = jnp.concatenate([ln_gains, ln_biases, router.T], axis=0)
    rows = [w_qkv.T, w_out.T, jnp.pad(small, ((0, 0), (0, dim - oc))), jnp.pad(tally[None], ((0, 7), (0, dim - 2 * experts)))]
    g = lax.all_gather(jnp.concatenate(rows, axis=0), both, axis=0, tiled=False)
    n_small = small.shape[0]
    wq_t = g[:, :qc].reshape(3, n_expert, width, dim)
    w_own = lax.dynamic_index_in_dim(wq_t, ex, 1, keepdims=False).reshape(3 * width, dim)
    wo_t = g[:, qc : qc + oc].reshape(dim, dim)
    smalls = g[:, qc + oc : qc + oc + n_small, :oc].transpose(1, 0, 2).reshape(n_small, dim).astype(f32)
    gains, shifts, router_t = smalls[0:2], smalls[2:4], smalls[4:]
    t = g[:, qc + oc + n_small, : 2 * experts].astype(f32)
    all_counts = jnp.sum(16 * t[:, :experts] + t[:, experts:], axis=0)
    mean_load = jnp.sum(all_counts) / experts
    load_ratio = (all_counts - mean_load) / mean_load
    x = tokens.reshape(seqs, local_len, dim)
    cot = cotangent.reshape(seqs, local_len, dim).astype(f32)
    x_all = lax.all_gather(x, "expert", axis=1, tiled=True)
    up_full = lax.all_gather(w_up[0], "dp", axis=0, tiled=True)
    down_full = lax.all_gather(w_down[0], "dp", axis=0, tiled=True)
    xn = layer_norm(x_all.astype(f32), gains[0], shifts[0]).astype(bf)
    qkv = jnp.einsum("std,kd->stk", xn, w_own, preferred_element_type=f32).astype(bf)
    qkv = qkv.reshape(seqs, total_len, 3, heads, head_dim)
    q, k, v = qkv[:, :, 0], qkv[:, :, 1], qkv[:, :, 2]
    pos = lax.iota(jnp.int32, total_len) // BLK
    allowed = pos[None, :] <= pos[:, None]
    s = jnp.einsum("sqhd,skhd->shqk", q, k, preferred_element_type=f32) * scale
    s = jnp.where(allowed, s, neg_big)
    lse = jax.nn.logsumexp(s, axis=-1)
    p = jnp.exp(s - lse[..., None])
    p_low = p.astype(bf)
    att = jnp.einsum("shqk,skhd->sqhd", p_low, v, preferred_element_type=f32)
    a = att.astype(bf).reshape(seqs, n_expert, local_len, width)
    a = lax.all_to_all(a, "expert", split_axis=1, concat_axis=1, tiled=True)
    att_own = a.transpose(0, 2, 1, 3).reshape(seqs, local_len, dim)
    middle = x.astype(f32) + jnp.einsum("sld,ed->sle", att_own, wo_t, preferred_element_type=f32)
    mixed = layer_norm(middle, gains[1], shifts[1]).astype(bf)
    logits = jnp.einsum("sld,ed->sle", mixed, router_t.astype(bf), preferred_element_type=f32)
    gates = jax.nn.sigmoid(jnp.sum(logits * onehot, axis=-1))
    counted = onehot.astype(jnp.int32)
    order_in = jnp.sum((jnp.cumsum(counted, axis=1) - counted) * counted, axis=-1)
    target = ids * cap + order_in
    place = (target[:, None, :] == lax.iota(jnp.int32, experts * cap)[None, :, None]).astype(bf)
    grad_expert = (gates[..., None] * cot).astype(bf)
    sent = jnp.stack([
        jnp.einsum("spl,sld->spd", place, mixed, preferred_element_type=f32).astype(bf),
        jnp.einsum("spl,sld->spd", place, grad_expert, preferred_element_type=f32).astype(bf),
    ]).reshape(2, seqs, n_expert, cap, dim)
    arrived = lax.all_to_all(sent, "expert", split_axis=2, concat_axis=2, tiled=True).reshape(2, seqs * n_expert * cap, dim)
    rows_in, grads_in = arrived[0], arrived[1]
    preact = jnp.dot(rows_in, up_full, preferred_element_type=f32)
    cdf = 0.5 * (1.0 + lax.erf(preact * (2.0 ** -0.5)))
    hidden = (preact * cdf).astype(bf)
    slope = cdf + preact * jnp.exp(-0.5 * preact * preact) * ((2.0 * math.pi) ** -0.5)
    result = jnp.dot(hidden, down_full, preferred_element_type=f32).astype(bf)
    grad_hidden = lax.dot_general(grads_in, down_full, (((1,), (1,)), ((), ())), preferred_element_type=f32)
    grad_pre = (grad_hidden * slope).astype(bf)
    grad_down = lax.dot_general(hidden, grads_in, (((0,), (0,)), ((), ())), preferred_element_type=f32)
    grad_up = lax.dot_general(rows_in, grad_pre, (((0,), (0,)), ((), ())), preferred_element_type=f32)
    grad_arrived = lax.dot_general(grad_pre, up_full, (((1,), (1,)), ((), ())), preferred_element_type=f32).astype(bf)
    back = jnp.stack([result, grad_arrived]).reshape(2, seqs, n_expert, cap, dim)
    back = lax.all_to_all(back, "expert", split_axis=2, concat_axis=2, tiled=True).reshape(2, seqs, experts * cap, dim)
    both_rows = jnp.einsum("spl,cspd->csld", place, back, preferred_element_type=f32)
    expert_out, grad_mixed = both_rows[0], both_rows[1]
    output = (middle + gates[..., None] * expert_out).astype(bf)
    grad_gate = jnp.sum(cot * expert_out, axis=-1) + balance_coef * jnp.sum(onehot * load_ratio, axis=-1)
    grad_logit = grad_gate * gates * (1.0 - gates)
    routed = onehot * grad_logit[..., None]
    grad_mixed = grad_mixed + jnp.einsum("sle,ed->sld", routed, router_t, precision="highest")
    grad_router = jnp.einsum("sle,sld->ed", routed, mixed.astype(f32), precision="highest")
    grad_middle, gg2, gb2 = jax.vjp(layer_norm, middle, gains[1], shifts[1])[1](grad_mixed)
    grad_middle = grad_middle + cot
    grad_branch = grad_middle.astype(bf)
    grad_out_t = jnp.einsum("sle,sld->ed", grad_branch, att_own, preferred_element_type=f32)
    grad_att = jnp.einsum("sle,ed->sld", grad_branch, wo_t, preferred_element_type=f32).astype(bf)
    ga = grad_att.reshape(seqs, local_len, n_expert, width).transpose(0, 2, 1, 3)
    ga = lax.all_to_all(ga, "expert", split_axis=1, concat_axis=1, tiled=True).reshape(seqs, total_len, heads, head_dim)
    delta = jnp.sum(ga.astype(f32) * att, axis=-1).transpose(0, 2, 1)
    gp = jnp.einsum("sqhd,skhd->shqk", ga, v, preferred_element_type=f32)
    ds = (p * (gp - delta[..., None]) * scale).astype(bf)
    dq = jnp.einsum("shqk,skhd->sqhd", ds, k, preferred_element_type=f32)
    dk = jnp.einsum("shqk,sqhd->skhd", ds, q, preferred_element_type=f32)
    dv = jnp.einsum("shqk,sqhd->skhd", p_low, ga, preferred_element_type=f32)
    gproj = jnp.stack([dq, dk, dv], axis=2).astype(bf).reshape(seqs, total_len, 3 * width)
    grad_w = jnp.einsum("stk,std->kd", gproj, xn, preferred_element_type=f32)
    part = jnp.einsum("stk,kd->std", gproj, w_own, preferred_element_type=f32).astype(bf)
    grad_normed = lax.psum_scatter(part, "expert", scatter_dimension=1, tiled=True).astype(f32)
    grad_x, gg1, gb1 = jax.vjp(layer_norm, x.astype(f32), gains[0], shifts[0])[1](grad_normed)
    grad_tokens = grad_middle + grad_x
    piece = width // n_dp
    gw = lax.psum_scatter(grad_w.reshape(3, n_dp, piece, dim).astype(bf), "dp", scatter_dimension=1, tiled=False).astype(f32)
    j = ex * n_dp + dp
    pieces = []
    for r in range(3):
        sec = lax.rem((r - j) * pow(n_dev, -1, 3) % 3 + 3, 3)
        mine = lax.dynamic_index_in_dim(gw, sec, 0, keepdims=False)
        perm = []
        for src in range(n_dev):
            d_, e_ = divmod(src, n_expert)
            jj = e_ * n_dp + d_
            c = [q_ * n_dev + jj for q_ in range(3) if (q_ * n_dev + jj) % 3 == r][0]
            perm.append((src, c // 3))
        pieces.append(lax.ppermute(mine, both, perm))
    grad_qkv = jnp.concatenate(pieces, axis=0).T
    gs = jnp.concatenate([jnp.stack([gg1, gg2, gb1, gb2]), grad_router], axis=0)
    gs = jnp.pad(gs.reshape(n_small, n_dev, oc).transpose(1, 0, 2), ((0, 0), (0, 0), (0, dim - oc)))
    dense = jnp.concatenate([grad_out_t.reshape(n_dev, oc, dim), gs], axis=1)
    dense = lax.psum_scatter(dense, both, scatter_dimension=0, tiled=False)
    grad_out = dense[:oc].T
    gs = dense[oc:, :oc]
    gu = lax.psum_scatter(grad_up.astype(bf), "dp", scatter_dimension=0, tiled=True).astype(f32)
    gd = lax.psum_scatter(grad_down.astype(bf), "dp", scatter_dimension=0, tiled=True).astype(f32)
    shape = tokens.shape
    return (output.reshape(shape), grad_tokens.reshape(shape), grad_qkv, grad_out, gs[0:2], gs[2:4], gs[4:].T, gu[None], gd[None])


def solution(mesh):
    in_specs = (
        P(None, "dp", "expert", None),
        P(None, "dp", "expert", None),
        P(None, "dp", "expert", None),
        P(None, ("dp", "expert")),
        P(None, ("dp", "expert")),
        P(None, ("dp", "expert")),
        P(None, ("dp", "expert")),
        P(("dp", "expert"), None),
        P("expert", "dp", None),
        P("expert", "dp", None),
    )
    out_specs = (
        P(None, "dp", "expert", None),
        P(None, "dp", "expert", None),
        P(None, ("dp", "expert")),
        P(None, ("dp", "expert")),
        P(None, ("dp", "expert")),
        P(None, ("dp", "expert")),
        P(("dp", "expert"), None),
        P("expert", "dp", None),
        P("expert", "dp", None),
    )
    n_expert, n_dp = mesh.shape["expert"], mesh.shape["dp"]
    split_heads = HEADS % n_expert == 0 and (HEADS // n_expert) * 64 % n_dp == 0
    chosen = fast_body if split_heads else body
    return jax.shard_map(chosen, mesh=mesh, in_specs=in_specs, out_specs=out_specs, check_vma=False)
```

```python
import functools
import math

import jax
import jax.numpy as jnp
from jax import lax
from jax.experimental import pallas as pl
from jax.experimental.pallas import tpu as pltpu
from jax.sharding import PartitionSpec as P

HEADS = 12
FF = 3072
BLK = 256
MICRO = 2


epsilon = 1e-05
balance_coef = 8.0
neg_big = -1e30


def layer_norm(features, gain_vec, shift_vec):
    centre = features - jnp.mean(features, axis=-1, keepdims=True)
    spread = jnp.mean(centre * centre, axis=-1, keepdims=True)
    return centre * lax.rsqrt(spread + epsilon) * gain_vec + shift_vec


def gelu_exact(preact):
    return jax.nn.gelu(preact, approximate=False)


def fetch_all(w_qkv, w_out, ln_gains, ln_biases, router, w_up, w_down):
    dense_set = (
        lax.all_gather(w_qkv, ("dp", "expert"), axis=1, tiled=True),
        lax.all_gather(w_out, ("dp", "expert"), axis=1, tiled=True),
        lax.all_gather(ln_gains, ("dp", "expert"), axis=1, tiled=True),
        lax.all_gather(ln_biases, ("dp", "expert"), axis=1, tiled=True),
        lax.all_gather(router, ("dp", "expert"), axis=0, tiled=True),
    )
    expert_set = (
        lax.all_gather(w_up, "dp", axis=1, tiled=True),
        lax.all_gather(w_down, "dp", axis=1, tiled=True),
    )
    return tuple(dense_set) + tuple(expert_set)


def route_slots(expert_of, experts, capacity):
    seq_here, local_len = expert_of.shape
    matches = (expert_of[..., None] == lax.iota(jnp.int32, experts)).astype(jnp.int32)
    order_in = jnp.sum((jnp.cumsum(matches, axis=1) - matches) * matches, axis=-1)
    seq_index = lax.broadcasted_iota(jnp.int32, (seq_here, local_len), 0)
    target = (expert_of * (seq_here * capacity) + seq_index * capacity + order_in).reshape(-1)
    slot_table = jnp.full((experts * seq_here * capacity,), seq_here * local_len, jnp.int32)
    slot_table = slot_table.at[target].set(lax.iota(jnp.int32, seq_here * local_len))
    return (target, slot_table)


def to_slots(features, slot_table):
    flat_rows = features.reshape(-1, features.shape[-1])
    padded = jnp.concatenate(
        [flat_rows, jnp.zeros((1, flat_rows.shape[1]), flat_rows.dtype)], axis=0
    )
    return padded[slot_table]


def score_terms(
    queries, grad_rows, key_block, value_block, log_total, row_delta, allowed, score_scale
):
    scores = (
        jnp.einsum("sqhd,skhd->shqk", queries, key_block, preferred_element_type=jnp.float32)
        * score_scale
    )
    weights = jnp.where(allowed, jnp.exp(scores - log_total[..., None]), 0.0)
    grad_weights = jnp.einsum(
        "sqhd,skhd->shqk", grad_rows, value_block, preferred_element_type=jnp.float32
    )
    grad_scores = (weights * (grad_weights - row_delta[..., None]) * score_scale).astype(
        jnp.bfloat16
    )
    return (weights.astype(jnp.bfloat16), grad_scores)


def attention_forward(queries, key_rows, value_rows, query_pos, score_scale):
    seq_here, local_len, head_count, head_dim = queries.shape
    last_block = query_pos[local_len - 1] // BLK
    start_state = (
        jnp.full((seq_here, head_count, local_len), neg_big, jnp.float32),
        jnp.zeros((seq_here, head_count, local_len), jnp.float32),
        jnp.zeros((seq_here, local_len, head_count, head_dim), jnp.float32),
    )
    key_part = lax.all_gather(key_rows, "expert", axis=1, tiled=True)
    value_part = lax.all_gather(value_rows, "expert", axis=1, tiled=True)
    piece_len = key_part.shape[1]
    block_len = math.gcd(piece_len, 512)

    def attention_one_block(block_index, carried):
        within = block_index * block_len
        key_block = lax.dynamic_slice_in_dim(key_part, within, block_len, 1).reshape(
            seq_here, block_len, head_count, head_dim
        )
        value_block = lax.dynamic_slice_in_dim(value_part, within, block_len, 1).reshape(
            seq_here, block_len, head_count, head_dim
        )
        key_pos = within + lax.iota(jnp.int32, block_len)
        allowed = key_pos[None, :] // BLK <= query_pos[:, None] // BLK

        def attention_compute(current):
            run_max, run_sum, weighted = current
            scores = (
                jnp.einsum(
                    "sqhd,skhd->shqk", queries, key_block, preferred_element_type=jnp.float32
                )
                * score_scale
            )
            new_max = jnp.maximum(run_max, jnp.max(jnp.where(allowed, scores, neg_big), axis=-1))
            weights = jnp.where(allowed, jnp.exp(scores - new_max[..., None]), 0.0)
            factor = jnp.exp(run_max - new_max)
            run_sum = run_sum * factor + jnp.sum(weights, axis=-1)
            addition = jnp.einsum(
                "shqk,skhd->sqhd",
                weights.astype(jnp.bfloat16),
                value_block,
                preferred_element_type=jnp.float32,
            )
            weighted = weighted * jnp.swapaxes(factor, 1, 2)[..., None] + addition
            return (new_max, run_sum, weighted)

        return lax.cond(
            within // BLK <= last_block, attention_compute, lambda current: current, carried
        )

    run_max, run_sum, weighted = lax.fori_loop(
        0, piece_len // block_len, attention_one_block, start_state
    )
    log_total = run_max + jnp.log(run_sum)
    attended = weighted / jnp.swapaxes(run_sum, 1, 2)[..., None]
    return (log_total, attended)


def query_grads(
    queries, grad_rows, key_rows, value_rows, log_total, row_delta, query_pos, score_scale, seq_len
):
    seq_here, local_len, head_count, head_dim = queries.shape
    model_dim = head_count * head_dim
    last_block = query_pos[local_len - 1] // BLK
    start_query = jnp.zeros((seq_here, local_len, head_count, head_dim), jnp.float32)
    start_state = (start_query, jnp.zeros((seq_here, seq_len, 2 * model_dim), jnp.float32))
    key_part = lax.all_gather(key_rows, "expert", axis=1, tiled=True)
    value_part = lax.all_gather(value_rows, "expert", axis=1, tiled=True)
    piece_len = key_part.shape[1]
    block_len = math.gcd(piece_len, 512)

    def query_one_block(block_index, carried):
        within = block_index * block_len
        key_block = lax.dynamic_slice_in_dim(key_part, within, block_len, 1).reshape(
            seq_here, block_len, head_count, head_dim
        )
        value_block = lax.dynamic_slice_in_dim(value_part, within, block_len, 1).reshape(
            seq_here, block_len, head_count, head_dim
        )
        key_pos = within + lax.iota(jnp.int32, block_len)
        allowed = key_pos[None, :] // BLK <= query_pos[:, None] // BLK

        def query_compute(current):
            weights, grad_scores = score_terms(
                queries,
                grad_rows,
                key_block,
                value_block,
                log_total,
                row_delta,
                allowed,
                score_scale,
            )
            grad_query = current[0] + jnp.einsum(
                "shqk,skhd->sqhd", grad_scores, key_block, preferred_element_type=jnp.float32
            )
            grad_key = jnp.einsum(
                "shqk,sqhd->skhd", grad_scores, queries, preferred_element_type=jnp.float32
            ).reshape(seq_here, block_len, model_dim)
            grad_value = jnp.einsum(
                "shqk,sqhd->skhd", weights, grad_rows, preferred_element_type=jnp.float32
            ).reshape(seq_here, block_len, model_dim)
            old_rows = lax.dynamic_slice_in_dim(current[1], within, block_len, 1)
            summed = old_rows + jnp.concatenate([grad_key, grad_value], axis=-1)
            return (grad_query, lax.dynamic_update_slice_in_dim(current[1], summed, within, 1))

        return lax.cond(
            within // BLK <= last_block, query_compute, lambda current: current, carried
        )

    return lax.fori_loop(0, piece_len // block_len, query_one_block, start_state)


def body(tokens, cotangent, expert_ids, w_qkv, w_out, ln_gains, ln_biases, router, w_up, w_down):
    n_expert = lax.axis_size("expert")
    seq_part = lax.axis_index("expert")
    seq_here, local_len, model_dim = (tokens.shape[1], tokens.shape[2], tokens.shape[3])
    head_count = HEADS
    head_dim = model_dim // head_count
    score_scale = head_dim ** (-0.5)
    exp_dev = w_up.shape[0]
    experts = exp_dev * n_expert
    capacity = 2 * local_len // experts
    seq_len = local_len * n_expert
    query_pos = seq_part * local_len + lax.iota(jnp.int32, local_len)
    expert_range = lax.iota(jnp.int32, experts)
    all_ids = expert_ids[..., 0]
    local_counts = jnp.sum((all_ids[..., None] == expert_range).astype(jnp.float32), axis=(0, 1, 2))
    counts = lax.psum(local_counts, ("dp", "expert"))
    mean_load = jnp.sum(counts) / experts
    load_ratio = (counts - mean_load) / mean_load
    grad_qkv_w = jnp.zeros((model_dim, 3 * model_dim), jnp.float32)
    grad_out_w = jnp.zeros((model_dim, model_dim), jnp.float32)
    grad_gains = jnp.zeros((2, model_dim), jnp.float32)
    grad_shifts = jnp.zeros((2, model_dim), jnp.float32)
    grad_router = jnp.zeros((model_dim, experts), jnp.float32)
    grad_up = jnp.zeros((exp_dev, model_dim, FF), jnp.float32)
    grad_down = jnp.zeros((exp_dev, FF, model_dim), jnp.float32)
    outputs = []
    input_grads = []
    for micro_index in range(MICRO):
        fetched = fetch_all(w_qkv, w_out, ln_gains, ln_biases, router, w_up, w_down)
        qkv_full, out_full, gains_full, shifts_full, router_full, up_full, down_full = fetched
        gain_rows = gains_full.astype(jnp.float32)
        shift_rows = shifts_full.astype(jnp.float32)
        inputs = tokens[micro_index].astype(jnp.float32)
        expert_of = all_ids[micro_index]
        normed = layer_norm(inputs, gain_rows[0], shift_rows[0])
        normed_low = normed.astype(jnp.bfloat16)
        projected = jnp.einsum(
            "scd,de->sce", normed_low, qkv_full, preferred_element_type=jnp.float32
        ).astype(jnp.bfloat16)
        query_rows = projected[..., :model_dim]
        queries = query_rows.reshape(seq_here, local_len, head_count, head_dim)
        key_rows = projected[..., model_dim : 2 * model_dim]
        value_rows = projected[..., 2 * model_dim :]
        log_total, attended = attention_forward(
            queries, key_rows, value_rows, query_pos, score_scale
        )
        attended_low = attended.reshape(seq_here, local_len, model_dim).astype(jnp.bfloat16)
        middle = inputs + jnp.einsum(
            "scd,de->sce", attended_low, out_full, preferred_element_type=jnp.float32
        )
        mixed_low = layer_norm(middle, gain_rows[1], shift_rows[1]).astype(jnp.bfloat16)
        onehot = (expert_of[..., None] == expert_range).astype(jnp.float32)
        logits = jnp.einsum(
            "scd,de->sce", mixed_low, router_full, preferred_element_type=jnp.float32
        )
        gates = jax.nn.sigmoid(jnp.sum(logits * onehot, axis=-1))
        target, slot_table = route_slots(expert_of, experts, capacity)
        outgoing = to_slots(mixed_low, slot_table).reshape(
            n_expert, exp_dev, seq_here * capacity, model_dim
        )
        arrived = lax.all_to_all(outgoing, "expert", split_axis=0, concat_axis=0, tiled=True)
        preact = jnp.einsum("pesd,edf->pesf", arrived, up_full, preferred_element_type=jnp.float32)
        hidden = gelu_exact(preact).astype(jnp.bfloat16)
        result = jnp.einsum(
            "pesf,efd->pesd", hidden, down_full, preferred_element_type=jnp.float32
        ).astype(jnp.bfloat16)
        returned = lax.all_to_all(result, "expert", split_axis=0, concat_axis=0, tiled=True)
        expert_out = (
            returned.reshape(-1, model_dim)[target]
            .reshape(seq_here, local_len, model_dim)
            .astype(jnp.float32)
        )
        final = middle + gates[..., None] * expert_out
        outputs.append(final.astype(jnp.bfloat16))
        fetched = fetch_all(w_qkv, w_out, ln_gains, ln_biases, router, w_up, w_down)
        qkv_full, out_full, gains_full, shifts_full, router_full, up_full, down_full = fetched
        gain_rows = gains_full.astype(jnp.float32)
        shift_rows = shifts_full.astype(jnp.float32)
        grad_final = cotangent[micro_index].astype(jnp.float32)
        grad_gate = jnp.sum(grad_final * expert_out, axis=-1) + balance_coef * jnp.sum(
            onehot * load_ratio, axis=-1
        )
        grad_logit = grad_gate * gates * (1.0 - gates)
        grad_expert = (gates[..., None] * grad_final).astype(jnp.bfloat16)
        sent_grads = to_slots(grad_expert, slot_table).reshape(
            n_expert, exp_dev, seq_here * capacity, model_dim
        )
        grads_here = lax.all_to_all(sent_grads, "expert", split_axis=0, concat_axis=0, tiled=True)
        hidden_low = gelu_exact(preact).astype(jnp.bfloat16)
        grad_down = grad_down + jnp.einsum(
            "pesf,pesd->efd", hidden_low, grads_here, preferred_element_type=jnp.float32
        )
        grad_hidden = jnp.einsum(
            "pesd,efd->pesf", grads_here, down_full, preferred_element_type=jnp.float32
        )
        grad_pre = jax.vjp(gelu_exact, preact)[1](grad_hidden)[0].astype(jnp.bfloat16)
        grad_up = grad_up + jnp.einsum(
            "pesd,pesf->edf", arrived, grad_pre, preferred_element_type=jnp.float32
        )
        grad_arrived = jnp.einsum(
            "pesf,edf->pesd", grad_pre, up_full, preferred_element_type=jnp.float32
        ).astype(jnp.bfloat16)
        grads_back = lax.all_to_all(grad_arrived, "expert", split_axis=0, concat_axis=0, tiled=True)
        grad_mixed = (
            grads_back.reshape(-1, model_dim)[target]
            .reshape(seq_here, local_len, model_dim)
            .astype(jnp.float32)
        )
        router_cols = jnp.einsum("sce,de->scd", onehot, router_full.astype(jnp.float32))
        grad_mixed = grad_mixed + grad_logit[..., None] * router_cols
        grad_router = grad_router + jnp.einsum(
            "scd,sce->de", mixed_low.astype(jnp.float32), grad_logit[..., None] * onehot
        )
        second_back = jax.vjp(layer_norm, middle, gain_rows[1], shift_rows[1])[1]
        grad_middle, grad_gain_two, grad_shift_two = second_back(grad_mixed)
        grad_middle = grad_middle + grad_final
        grad_branch = grad_middle.astype(jnp.bfloat16)
        grad_out_w = grad_out_w + jnp.einsum(
            "scd,sce->de", attended_low, grad_branch, preferred_element_type=jnp.float32
        )
        grad_attended = jnp.einsum(
            "sce,de->scd", grad_branch, out_full, preferred_element_type=jnp.float32
        ).astype(jnp.bfloat16)
        grad_heads = grad_attended.reshape(seq_here, local_len, head_count, head_dim)
        row_delta = jnp.swapaxes(jnp.sum(grad_heads.astype(jnp.float32) * attended, axis=-1), 1, 2)
        folded = query_grads(
            queries,
            grad_heads,
            key_rows,
            value_rows,
            log_total,
            row_delta,
            query_pos,
            score_scale,
            seq_len,
        )
        grad_query = folded[0].reshape(seq_here, local_len, model_dim)
        key_value = lax.psum_scatter(
            folded[1].astype(jnp.bfloat16), "expert", scatter_dimension=1, tiled=True
        ).astype(jnp.float32)
        grad_key = key_value[..., :model_dim]
        grad_value = key_value[..., model_dim:]
        grad_projected = jnp.concatenate([grad_query, grad_key, grad_value], axis=-1).astype(
            jnp.bfloat16
        )
        grad_qkv_w = grad_qkv_w + jnp.einsum(
            "scd,sce->de", normed_low, grad_projected, preferred_element_type=jnp.float32
        )
        grad_normed = jnp.einsum(
            "sce,de->scd", grad_projected, qkv_full, preferred_element_type=jnp.float32
        )
        first_back = jax.vjp(layer_norm, inputs, gain_rows[0], shift_rows[0])[1]
        grad_inputs, grad_gain_one, grad_shift_one = first_back(grad_normed)
        grad_gains = grad_gains + jnp.stack([grad_gain_one, grad_gain_two])
        grad_shifts = grad_shifts + jnp.stack([grad_shift_one, grad_shift_two])
        input_grads.append(grad_middle + grad_inputs)
    dense_grads = (
        lax.psum_scatter(grad_qkv_w, ("dp", "expert"), scatter_dimension=1, tiled=True),
        lax.psum_scatter(grad_out_w, ("dp", "expert"), scatter_dimension=1, tiled=True),
        lax.psum_scatter(grad_gains, ("dp", "expert"), scatter_dimension=1, tiled=True),
        lax.psum_scatter(grad_shifts, ("dp", "expert"), scatter_dimension=1, tiled=True),
        lax.psum_scatter(grad_router, ("dp", "expert"), scatter_dimension=0, tiled=True),
    )
    expert_grads = (
        lax.psum_scatter(
            grad_up.astype(jnp.bfloat16), "dp", scatter_dimension=1, tiled=True
        ).astype(jnp.float32),
        lax.psum_scatter(
            grad_down.astype(jnp.bfloat16), "dp", scatter_dimension=1, tiled=True
        ).astype(jnp.float32),
    )
    return (jnp.stack(outputs), jnp.stack(input_grads)) + tuple(dense_grads) + tuple(expert_grads)


MESH_ID = pl.DeviceIdType.MESH
NT = (((1,), (1,)), ((), ()))
NN = (((1,), (0,)), ((), ()))
TN = (((0,), (0,)), ((), ()))
VMEM = pl.BlockSpec(memory_space=pltpu.VMEM)


def mm(a, b, dims=NN):
    return lax.dot_general(a, b, dims, preferred_element_type=jnp.float32)


def normalised(v):
    centre = v - jnp.mean(v, axis=-1, keepdims=True)
    spread = jnp.mean(centre * centre, axis=-1, keepdims=True)
    inv = lax.rsqrt(spread + epsilon)
    return centre * inv, inv


class Place:
    def __init__(self, n_dp, n_ex):
        self.n_dp, self.n_ex, self.n_dev, self.n_z = n_dp, n_ex, n_dp * n_ex, n_dp // 2
        self.dp, self.ex = lax.axis_index("dp"), lax.axis_index("expert")
        self.z, self.core = self.dp // 2, self.dp % 2
        self.flat = self.dp * n_ex + self.ex

    def z_peer(self, d):
        return (self.z + d) % self.n_z

    def ex_peer(self, d):
        return (self.ex + d) % self.n_ex

    def on_z(self, z):
        return (z * 2 + self.core, self.ex)

    def on_ex(self, e):
        return (self.dp, e)

    def partner(self):
        return (self.z * 2 + 1 - self.core, self.ex)

    def numbered(self, t):
        return (t // self.n_ex, t % self.n_ex)


def entry_barrier(at):
    sem = pltpu.get_barrier_semaphore()

    def tell(i, carry):
        pl.semaphore_signal(sem, inc=1, device_id=at.numbered((at.flat + i) % at.n_dev), device_id_type=MESH_ID)
        return carry

    lax.fori_loop(1, at.n_dev, tell, 0)
    pl.semaphore_wait(sem, at.n_dev - 1)


class Wires:
    def __init__(self, send_sems, recv_sems):
        self.send_sems, self.recv_sems, self.used = send_sems, recv_sems, 0

    def take(self, n):
        base = self.used
        self.used = base + n
        return base

    def copy(self, i, src, dst, device):
        return pltpu.make_async_remote_copy(
            src_ref=src, dst_ref=dst, send_sem=self.send_sems.at[i], recv_sem=self.recv_sems.at[i],
            device_id=device, device_id_type=MESH_ID,
        )


def first_kernel(
    n_dp, n_ex, x_ref, cot_ref, slot_ref, eid_ref, wq_ref, wo_ref, small_ref,
    rows_ref, grads_ref, q_ref, k_ref, v_ref, xn_ref, lse_ref, att_ref, attr_ref, mid_ref, mix_ref, gate_ref, w_ref, wo_all_ref, smalls_ref,
    xg, small_all, wt_a, wt_b, wo_b, wide, attb, disp, send_sems, recv_sems,
):
    bf, f32 = jnp.bfloat16, jnp.float32
    at = Place(n_dp, n_ex)
    wires = Wires(send_sems, recv_sems)
    n_dev, n_z, ex = at.n_dev, at.n_z, at.ex
    seqs, local_len, dim = x_ref.shape
    width = q_ref.shape[2]
    head_dim = dim // HEADS
    heads = width // head_dim
    piece, oc = wq_ref.shape[1], wo_ref.shape[1]
    cap = rows_ref.shape[2]
    scale = head_dim ** -0.5
    entry_barrier(at)

    i_small = wires.take(n_dev)

    def small_copy(i):
        return wires.copy(i_small + i, small_ref, small_all.at[at.flat], at.numbered((at.flat + i) % n_dev))

    def small_start(i, carry):
        small_copy(i).start()
        return carry

    lax.fori_loop(1, n_dev, small_start, 0)
    me_j = ex * n_dp + at.dp
    i_piece = wires.take(3)
    pieces = []
    for r in range(3):
        c = 3 * at.flat + r
        sec, j = c // n_dev, c % n_dev
        copy = wires.copy(i_piece + r, wq_ref.at[r], wt_a.at[sec], (j % n_dp, j // n_dp))
        away = j != me_j
        pl.when(away)(copy.start)
        pieces.append((copy, away, sec))
    i_wo = wires.take(n_z)
    wo_line = [wires.copy(i_wo + d, wo_ref, wo_b.at[at.core, ex, at.z], at.on_z(at.z_peer(d))) for d in range(1, n_z)]
    for c in wo_line:
        c.start()
    i_tok = wires.take(seqs * n_ex)

    def token_copy(m, d):
        return wires.copy(i_tok + m * n_ex + d, x_ref.at[m], xg.at[m, ex], at.on_ex(at.ex_peer(d)))

    for d in range(1, n_ex):
        token_copy(0, d).start()
    small_all[at.flat] = small_ref[...]
    wo_b[at.core, ex, at.z] = wo_ref[...]
    for m in range(seqs):
        xg[m, ex] = x_ref[m]
    for r, (copy, away, sec) in enumerate(pieces):
        pl.when(away)(copy.wait_recv)

        @pl.when(jnp.logical_not(away))
        def _():
            wt_a[sec] = wq_ref[r]

    i_line = wires.take(n_z)
    w_line = [wires.copy(i_line + d, wt_a, wt_b.at[at.core, at.z], at.on_z(at.z_peer(d))) for d in range(1, n_z)]
    for c in w_line:
        c.start()
    wt_b[at.core, at.z] = wt_a[...]
    for c in w_line:
        c.wait_recv()
    w_pair = wires.copy(wires.take(1), wt_b.at[at.core], wt_b.at[at.core], at.partner())
    w_pair.start()
    for c in wo_line:
        c.wait_recv()
    i_wo2 = wires.take(n_ex)
    wo_plane = [wires.copy(i_wo2 + d, wo_b.at[at.core, ex], wo_b.at[at.core, ex], at.on_ex(at.ex_peer(d))) for d in range(1, n_ex)]
    for c in wo_plane:
        c.start()
    for m in range(1, seqs):
        for d in range(1, n_ex):
            token_copy(m, d).start()

    def small_wait(i, carry):
        small_copy(i).wait_recv()
        return carry

    lax.fori_loop(1, n_dev, small_wait, 0)
    smalls_ref[...] = jnp.zeros(smalls_ref.shape, f32)
    for s in range(n_dev):
        lo = s * oc // 128 * 128
        hi = min(lo + 256, dim)
        smalls_ref[:, lo:hi] += small_all[s][:, 0 : hi - lo].astype(f32)
    gain_one, shift_one = smalls_ref[0:1, :], smalls_ref[2:3, :]
    gain_two, shift_two = smalls_ref[1:2, :], smalls_ref[3:4, :]
    w_pair.wait_recv()
    for sec in range(3):
        for z in range(n_z):
            for core in range(2):
                row = (z * 2 + core) * piece
                wide[row : row + piece, :] = wt_b[core, z, sec].astype(f32)
        w_ref[sec] = wide[0:width, :].astype(bf)

    i_back = wires.take(seqs * n_ex)

    def back_copy(m, d):
        peer = at.ex_peer(d)
        return wires.copy(i_back + m * n_ex + d, attb.at[m, peer], attr_ref.at[m, ex], at.on_ex(peer))

    lane_head = lax.broadcasted_iota(jnp.int32, (1, width), 1) // head_dim
    lane = lax.broadcasted_iota(jnp.int32, (1, 128), 1)

    def attend(m, carry):
        def project(d, c_):
            src = (ex - d + n_ex) % n_ex
            pl.when(d > 0)(lambda: token_copy(m, d).wait_recv())
            rows = pl.ds(pl.multiple_of(src * local_len, local_len), local_len)
            hat, _ = normalised(xg[m, src].astype(f32))
            low = (hat * gain_one + shift_one).astype(bf)
            xn_ref[m, rows, :] = low
            q_ref[m, rows, :] = mm(low, w_ref[0], NT).astype(bf)
            k_ref[m, rows, :] = mm(low, w_ref[1], NT).astype(bf)
            v_ref[m, rows, :] = mm(low, w_ref[2], NT).astype(bf)
            return c_

        lax.fori_loop(0, n_ex, project, 0)
        for i in range(n_ex):
            reach = (i + 1) * local_len
            here = slice(i * local_len, reach)
            att_ref[m, here, :] = jnp.zeros((local_len, width), f32)
            lse_ref[m, here, :] = jnp.zeros((local_len, 128), f32)

            def one_head(h, c_):
                mine = lane_head == h
                qb = q_ref[m, here, :]
                s = mm(jnp.where(mine, qb, jnp.zeros_like(qb)), k_ref[m, 0:reach, :], NT) * scale
                top = jnp.max(s, axis=-1, keepdims=True)
                e = jnp.exp(s - top)
                total = jnp.sum(e, axis=-1, keepdims=True)
                p = (e / total).astype(bf)
                att_ref[m, here, :] = jnp.where(mine, mm(p, v_ref[m, 0:reach, :]), att_ref[m, here, :])
                lse_ref[m, here, :] = jnp.where(lane == h, top + jnp.log(total), lse_ref[m, here, :])
                return c_

            lax.fori_loop(0, heads, one_head, 0)
            attb[m, i] = att_ref[m, here, :].astype(bf)
        for d in range(1, n_ex):
            back_copy(m, d).start()
        attr_ref[m, ex] = attb[m, ex]
        return carry

    lax.fori_loop(0, seqs, attend, 0)
    for c in wo_plane:
        c.wait_recv()
    wo_pair = wires.copy(wires.take(1), wo_b.at[at.core], wo_b.at[at.core], at.partner())
    wo_pair.start()
    wo_pair.wait_recv()
    for b in range(n_ex):
        for s in range(n_dev):
            wide[s * oc : (s + 1) * oc, 0:width] = wo_b[s // n_ex % 2, s % n_ex, s // n_ex // 2, b].astype(f32)
        wo_all_ref[b] = wide[0:dim, 0:width].astype(bf)

    arrive = (rows_ref, grads_ref)
    i_out = wires.take(2 * seqs * n_ex)

    def out_copy(m, a, d):
        peer = at.ex_peer(d)
        return wires.copy(i_out + (m * 2 + a) * n_ex + d, disp.at[m, a, peer], arrive[a].at[m, ex], at.on_ex(peer))

    def route(m, carry):
        for d in range(1, n_ex):
            back_copy(m, d).wait_recv()
        mid_ref[m] = x_ref[m].astype(f32)
        for b in range(n_ex):
            mid_ref[m] += mm(attr_ref[m, b], wo_all_ref[b], NT)
        hat, _ = normalised(mid_ref[m])
        mixed = (hat * gain_two + shift_two).astype(bf)
        mix_ref[m] = mixed
        logits = mm(mixed, smalls_ref[...].astype(bf), NT)
        mine = lax.broadcasted_iota(jnp.int32, logits.shape, 1) == eid_ref[m] + 4
        gate = jax.nn.sigmoid(jnp.sum(jnp.where(mine, logits, 0.0), axis=1, keepdims=True))
        gate_ref[m] = jnp.broadcast_to(gate, (local_len, 128))
        scaled = (gate * cot_ref[m].astype(f32)).astype(bf)
        place = jnp.where(slot_ref[m] == lax.broadcasted_iota(jnp.int32, (n_ex * cap, local_len), 0), 1.0, 0.0).astype(bf)
        for a, value in ((0, mixed), (1, scaled)):
            disp[m, a] = mm(place, value).astype(bf).reshape(n_ex, cap, dim)
            for d in range(1, n_ex):
                out_copy(m, a, d).start()
            arrive[a][m, ex] = disp[m, a, ex]
        return carry

    lax.fori_loop(0, seqs, route, 0)
    for m in range(seqs):
        for a in range(2):
            for d in range(1, n_ex):
                out_copy(m, a, d).wait()
        for d in range(1, n_ex):
            back_copy(m, d).wait_send()
            token_copy(m, d).wait_send()

    def small_done(i, carry):
        small_copy(i).wait_send()
        return carry

    lax.fori_loop(1, n_dev, small_done, 0)
    for copy, away, _ in pieces:
        pl.when(away)(copy.wait_send)
    for c in [*wo_line, *w_line, w_pair, *wo_plane, wo_pair]:
        c.wait_send()


def first_stage(n_dp, n_ex, x, cot, slots, eid, wq, wo, small):
    bf, f32 = jnp.bfloat16, jnp.float32
    seqs, local_len, dim = x.shape
    width, total_len, n_z = dim // n_ex, local_len * n_ex, n_dp // 2
    cap = 2 * local_len // n_ex
    piece, oc, n_dev = wq.shape[1], wo.shape[1], n_dp * n_ex
    shapes = [
        ((seqs, n_ex, cap, dim), bf), ((seqs, n_ex, cap, dim), bf),
        ((seqs, total_len, width), bf), ((seqs, total_len, width), bf), ((seqs, total_len, width), bf),
        ((seqs, total_len, dim), bf), ((seqs, total_len, 128), f32), ((seqs, total_len, width), f32),
        ((seqs, n_ex, local_len, width), bf), ((seqs, local_len, dim), f32), ((seqs, local_len, dim), bf), ((seqs, local_len, 128), f32),
        ((3, width, dim), bf), ((n_ex, dim, width), bf), ((16, dim), f32),
    ]
    n_sems = n_dev + 3 + n_z + seqs * n_ex + n_z + 1 + n_ex + seqs * n_ex + 1 + 2 * seqs * n_ex
    return pl.pallas_call(
        functools.partial(first_kernel, n_dp, n_ex),
        out_shape=[jax.ShapeDtypeStruct(s, d) for s, d in shapes],
        in_specs=[VMEM] * 7,
        out_specs=[VMEM] * len(shapes),
        scratch_shapes=[
            pltpu.VMEM((seqs, n_ex, local_len, dim), bf),
            pltpu.VMEM((n_dev, 16, 256), bf),
            pltpu.VMEM((3, piece, dim), bf),
            pltpu.VMEM((2, n_z, 3, piece, dim), bf),
            pltpu.VMEM((2, n_ex, n_z, n_ex, oc, width), bf),
            pltpu.VMEM((dim, dim), f32),
            pltpu.VMEM((seqs, n_ex, local_len, width), bf),
            pltpu.VMEM((seqs, 2, n_ex, cap, dim), bf),
            pltpu.SemaphoreType.DMA((n_sems,)),
            pltpu.SemaphoreType.DMA((n_sems,)),
        ],
        compiler_params=pltpu.CompilerParams(collective_id=0, has_side_effects=True, vmem_limit_bytes=64000 * 1024),
        name="attend_and_send",
    )(x, cot, slots, eid, wq, wo, small)


def fast_body(tokens, cotangent, expert_ids, w_qkv, w_out, ln_gains, ln_biases, router, w_up, w_down):
    bf, f32 = jnp.bfloat16, jnp.float32
    n_expert, n_dp = lax.axis_size("expert"), lax.axis_size("dp")
    ex, dp = lax.axis_index("expert"), lax.axis_index("dp")
    both = ("dp", "expert")
    n_dev = n_dp * n_expert
    seqs, local_len, dim = tokens.shape[0] * tokens.shape[1], tokens.shape[2], tokens.shape[3]
    head_dim = dim // HEADS
    heads = HEADS // n_expert
    width = heads * head_dim
    total_len = local_len * n_expert
    experts = n_expert
    cap = 2 * local_len // experts
    scale = head_dim ** -0.5
    qc, oc = w_qkv.shape[1], w_out.shape[1]
    ids = expert_ids.reshape(seqs, local_len)
    onehot = (ids[..., None] == lax.iota(jnp.int32, experts)).astype(f32)
    counts = jnp.sum(onehot, axis=(0, 1))
    high = jnp.floor(counts / 16)
    small = jnp.concatenate([ln_gains, ln_biases, router.T], axis=0)
    n_small = small.shape[0]
    flat = dp * n_expert + ex
    tally = jnp.stack([high, counts - 16 * high]).astype(bf)
    block = jnp.zeros((16, 256), bf)
    block = lax.dynamic_update_slice(block, small, (0, lax.rem(flat * oc, 128)))
    block = lax.dynamic_update_slice(block, tally, (n_small, 0))
    x = tokens.reshape(seqs, local_len, dim)
    cot16 = cotangent.reshape(seqs, local_len, dim)
    cot = cot16.astype(f32)
    counted = onehot.astype(jnp.int32)
    order_in = jnp.sum((jnp.cumsum(counted, axis=1) - counted) * counted, axis=-1)
    target = ids * cap + order_in
    place = (target[:, None, :] == lax.iota(jnp.int32, experts * cap)[None, :, None]).astype(bf)
    wq = w_qkv.T.reshape(3, qc // 3, dim)
    wo = w_out.reshape(n_expert, width, oc).transpose(0, 2, 1)
    up_full = lax.all_gather(w_up[0], "dp", axis=0, tiled=True)
    down_full = lax.all_gather(w_down[0], "dp", axis=0, tiled=True)
    (rows_in, grads_in, q, k, v, xn, lse, att, att_r, middle, mixed, gates, w_own, wo_b, smalls) = first_stage(
        n_dp, n_expert, x, cot16, target[:, None, :], ids[..., None], wq, wo, block)
    rows_in, grads_in = rows_in.reshape(-1, dim), grads_in.reshape(-1, dim)
    gates = gates[..., 0]
    gains, shifts, router_t = smalls[0:2], smalls[2:4], smalls[4 : 4 + experts]
    t = smalls[n_small : n_small + 2].reshape(2, dim // 128, 128)[:, :, :experts].sum(1)
    all_counts = 16 * t[0] + t[1]
    mean_load = jnp.sum(all_counts) / experts
    load_ratio = (all_counts - mean_load) / mean_load
    wo_t = wo_b.transpose(1, 0, 2).reshape(dim, dim)
    w_own = w_own.reshape(3 * width, dim)
    att_own = att_r.transpose(0, 2, 1, 3).reshape(seqs, local_len, dim)
    q, k, v, att = (u.reshape(seqs, total_len, heads, head_dim) for u in (q, k, v, att))
    pos = lax.iota(jnp.int32, total_len) // BLK
    allowed = pos[None, :] <= pos[:, None]
    s = jnp.einsum("sqhd,skhd->shqk", q, k, preferred_element_type=f32) * scale
    s = jnp.where(allowed, s, neg_big)
    p = jnp.exp(s - lse[:, :, :heads].transpose(0, 2, 1)[..., None])
    p_low = p.astype(bf)
    preact = jnp.dot(rows_in, up_full, preferred_element_type=f32)
    cdf = 0.5 * (1.0 + lax.erf(preact * (2.0 ** -0.5)))
    hidden = (preact * cdf).astype(bf)
    slope = cdf + preact * jnp.exp(-0.5 * preact * preact) * ((2.0 * math.pi) ** -0.5)
    result = jnp.dot(hidden, down_full, preferred_element_type=f32).astype(bf)
    grad_hidden = lax.dot_general(grads_in, down_full, (((1,), (1,)), ((), ())), preferred_element_type=f32)
    grad_pre = (grad_hidden * slope).astype(bf)
    grad_down = lax.dot_general(hidden, grads_in, (((0,), (0,)), ((), ())), preferred_element_type=f32)
    grad_up = lax.dot_general(rows_in, grad_pre, (((0,), (0,)), ((), ())), preferred_element_type=f32)
    grad_arrived = lax.dot_general(grad_pre, up_full, (((1,), (1,)), ((), ())), preferred_element_type=f32).astype(bf)
    back = jnp.stack([result, grad_arrived]).reshape(2, seqs, n_expert, cap, dim)
    back = lax.all_to_all(back, "expert", split_axis=2, concat_axis=2, tiled=True).reshape(2, seqs, experts * cap, dim)
    both_rows = jnp.einsum("spl,cspd->csld", place, back, preferred_element_type=f32)
    expert_out, grad_mixed = both_rows[0], both_rows[1]
    output = (middle + gates[..., None] * expert_out).astype(bf)
    grad_gate = jnp.sum(cot * expert_out, axis=-1) + balance_coef * jnp.sum(onehot * load_ratio, axis=-1)
    grad_logit = grad_gate * gates * (1.0 - gates)
    routed = onehot * grad_logit[..., None]
    grad_mixed = grad_mixed + jnp.einsum("sle,ed->sld", routed, router_t, precision="highest")
    grad_router = jnp.einsum("sle,sld->ed", routed, mixed.astype(f32), precision="highest")
    grad_middle, gg2, gb2 = jax.vjp(layer_norm, middle, gains[1], shifts[1])[1](grad_mixed)
    grad_middle = grad_middle + cot
    grad_branch = grad_middle.astype(bf)
    grad_out_t = jnp.einsum("sle,sld->ed", grad_branch, att_own, preferred_element_type=f32)
    grad_att = jnp.einsum("sle,ed->sld", grad_branch, wo_t, preferred_element_type=f32).astype(bf)
    ga = grad_att.reshape(seqs, local_len, n_expert, width).transpose(0, 2, 1, 3)
    ga = lax.all_to_all(ga, "expert", split_axis=1, concat_axis=1, tiled=True).reshape(seqs, total_len, heads, head_dim)
    delta = jnp.sum(ga.astype(f32) * att, axis=-1).transpose(0, 2, 1)
    gp = jnp.einsum("sqhd,skhd->shqk", ga, v, preferred_element_type=f32)
    ds = (p * (gp - delta[..., None]) * scale).astype(bf)
    dq = jnp.einsum("shqk,skhd->sqhd", ds, k, preferred_element_type=f32)
    dk = jnp.einsum("shqk,sqhd->skhd", ds, q, preferred_element_type=f32)
    dv = jnp.einsum("shqk,sqhd->skhd", p_low, ga, preferred_element_type=f32)
    gproj = jnp.stack([dq, dk, dv], axis=2).astype(bf).reshape(seqs, total_len, 3 * width)
    grad_w = jnp.einsum("stk,std->kd", gproj, xn, preferred_element_type=f32)
    part = jnp.einsum("stk,kd->std", gproj, w_own, preferred_element_type=f32).astype(bf)
    grad_normed = lax.psum_scatter(part, "expert", scatter_dimension=1, tiled=True).astype(f32)
    grad_x, gg1, gb1 = jax.vjp(layer_norm, x.astype(f32), gains[0], shifts[0])[1](grad_normed)
    grad_tokens = grad_middle + grad_x
    piece = width // n_dp
    gw = lax.psum_scatter(grad_w.reshape(3, n_dp, piece, dim).astype(bf), "dp", scatter_dimension=1, tiled=False).astype(f32)
    j = ex * n_dp + dp
    pieces = []
    for r in range(3):
        sec = lax.rem((r - j) * pow(n_dev, -1, 3) % 3 + 3, 3)
        mine = lax.dynamic_index_in_dim(gw, sec, 0, keepdims=False)
        perm = []
        for src in range(n_dev):
            d_, e_ = divmod(src, n_expert)
            jj = e_ * n_dp + d_
            c = [q_ * n_dev + jj for q_ in range(3) if (q_ * n_dev + jj) % 3 == r][0]
            perm.append((src, c // 3))
        pieces.append(lax.ppermute(mine, both, perm))
    grad_qkv = jnp.concatenate(pieces, axis=0).T
    gs = jnp.concatenate([jnp.stack([gg1, gg2, gb1, gb2]), grad_router], axis=0)
    gs = jnp.pad(gs.reshape(n_small, n_dev, oc).transpose(1, 0, 2), ((0, 0), (0, 0), (0, dim - oc)))
    dense = jnp.concatenate([grad_out_t.reshape(n_dev, oc, dim), gs], axis=1)
    dense = lax.psum_scatter(dense, both, scatter_dimension=0, tiled=False)
    grad_out = dense[:oc].T
    gs = dense[oc:, :oc]
    gu = lax.psum_scatter(grad_up.astype(bf), "dp", scatter_dimension=0, tiled=True).astype(f32)
    gd = lax.psum_scatter(grad_down.astype(bf), "dp", scatter_dimension=0, tiled=True).astype(f32)
    shape = tokens.shape
    return (output.reshape(shape), grad_tokens.reshape(shape), grad_qkv, grad_out, gs[0:2], gs[2:4], gs[4:].T, gu[None], gd[None])


def solution(mesh):
    in_specs = (
        P(None, "dp", "expert", None),
        P(None, "dp", "expert", None),
        P(None, "dp", "expert", None),
        P(None, ("dp", "expert")),
        P(None, ("dp", "expert")),
        P(None, ("dp", "expert")),
        P(None, ("dp", "expert")),
        P(("dp", "expert"), None),
        P("expert", "dp", None),
        P("expert", "dp", None),
    )
    out_specs = (
        P(None, "dp", "expert", None),
        P(None, "dp", "expert", None),
        P(None, ("dp", "expert")),
        P(None, ("dp", "expert")),
        P(None, ("dp", "expert")),
        P(None, ("dp", "expert")),
        P(("dp", "expert"), None),
        P("expert", "dp", None),
        P("expert", "dp", None),
    )
    n_expert, n_dp = mesh.shape["expert"], mesh.shape["dp"]
    split_heads = HEADS % n_expert == 0 and (HEADS // n_expert) * 64 % n_dp == 0
    chosen = fast_body if split_heads else body
    return jax.shard_map(chosen, mesh=mesh, in_specs=in_specs, out_specs=out_specs, check_vma=False)
```

```python
import functools
import math

import jax
import jax.numpy as jnp
from jax import lax
from jax.experimental import pallas as pl
from jax.experimental.pallas import tpu as pltpu
from jax.sharding import PartitionSpec as P

HEADS = 12
FF = 3072
BLK = 256
MICRO = 2


epsilon = 1e-05
balance_coef = 8.0
neg_big = -1e30


def layer_norm(features, gain_vec, shift_vec):
    centre = features - jnp.mean(features, axis=-1, keepdims=True)
    spread = jnp.mean(centre * centre, axis=-1, keepdims=True)
    return centre * lax.rsqrt(spread + epsilon) * gain_vec + shift_vec


def gelu_exact(preact):
    return jax.nn.gelu(preact, approximate=False)


def fetch_all(w_qkv, w_out, ln_gains, ln_biases, router, w_up, w_down):
    dense_set = (
        lax.all_gather(w_qkv, ("dp", "expert"), axis=1, tiled=True),
        lax.all_gather(w_out, ("dp", "expert"), axis=1, tiled=True),
        lax.all_gather(ln_gains, ("dp", "expert"), axis=1, tiled=True),
        lax.all_gather(ln_biases, ("dp", "expert"), axis=1, tiled=True),
        lax.all_gather(router, ("dp", "expert"), axis=0, tiled=True),
    )
    expert_set = (
        lax.all_gather(w_up, "dp", axis=1, tiled=True),
        lax.all_gather(w_down, "dp", axis=1, tiled=True),
    )
    return tuple(dense_set) + tuple(expert_set)


def route_slots(expert_of, experts, capacity):
    seq_here, local_len = expert_of.shape
    matches = (expert_of[..., None] == lax.iota(jnp.int32, experts)).astype(jnp.int32)
    order_in = jnp.sum((jnp.cumsum(matches, axis=1) - matches) * matches, axis=-1)
    seq_index = lax.broadcasted_iota(jnp.int32, (seq_here, local_len), 0)
    target = (expert_of * (seq_here * capacity) + seq_index * capacity + order_in).reshape(-1)
    slot_table = jnp.full((experts * seq_here * capacity,), seq_here * local_len, jnp.int32)
    slot_table = slot_table.at[target].set(lax.iota(jnp.int32, seq_here * local_len))
    return (target, slot_table)


def to_slots(features, slot_table):
    flat_rows = features.reshape(-1, features.shape[-1])
    padded = jnp.concatenate(
        [flat_rows, jnp.zeros((1, flat_rows.shape[1]), flat_rows.dtype)], axis=0
    )
    return padded[slot_table]


def score_terms(
    queries, grad_rows, key_block, value_block, log_total, row_delta, allowed, score_scale
):
    scores = (
        jnp.einsum("sqhd,skhd->shqk", queries, key_block, preferred_element_type=jnp.float32)
        * score_scale
    )
    weights = jnp.where(allowed, jnp.exp(scores - log_total[..., None]), 0.0)
    grad_weights = jnp.einsum(
        "sqhd,skhd->shqk", grad_rows, value_block, preferred_element_type=jnp.float32
    )
    grad_scores = (weights * (grad_weights - row_delta[..., None]) * score_scale).astype(
        jnp.bfloat16
    )
    return (weights.astype(jnp.bfloat16), grad_scores)


def attention_forward(queries, key_rows, value_rows, query_pos, score_scale):
    seq_here, local_len, head_count, head_dim = queries.shape
    last_block = query_pos[local_len - 1] // BLK
    start_state = (
        jnp.full((seq_here, head_count, local_len), neg_big, jnp.float32),
        jnp.zeros((seq_here, head_count, local_len), jnp.float32),
        jnp.zeros((seq_here, local_len, head_count, head_dim), jnp.float32),
    )
    key_part = lax.all_gather(key_rows, "expert", axis=1, tiled=True)
    value_part = lax.all_gather(value_rows, "expert", axis=1, tiled=True)
    piece_len = key_part.shape[1]
    block_len = math.gcd(piece_len, 512)

    def attention_one_block(block_index, carried):
        within = block_index * block_len
        key_block = lax.dynamic_slice_in_dim(key_part, within, block_len, 1).reshape(
            seq_here, block_len, head_count, head_dim
        )
        value_block = lax.dynamic_slice_in_dim(value_part, within, block_len, 1).reshape(
            seq_here, block_len, head_count, head_dim
        )
        key_pos = within + lax.iota(jnp.int32, block_len)
        allowed = key_pos[None, :] // BLK <= query_pos[:, None] // BLK

        def attention_compute(current):
            run_max, run_sum, weighted = current
            scores = (
                jnp.einsum(
                    "sqhd,skhd->shqk", queries, key_block, preferred_element_type=jnp.float32
                )
                * score_scale
            )
            new_max = jnp.maximum(run_max, jnp.max(jnp.where(allowed, scores, neg_big), axis=-1))
            weights = jnp.where(allowed, jnp.exp(scores - new_max[..., None]), 0.0)
            factor = jnp.exp(run_max - new_max)
            run_sum = run_sum * factor + jnp.sum(weights, axis=-1)
            addition = jnp.einsum(
                "shqk,skhd->sqhd",
                weights.astype(jnp.bfloat16),
                value_block,
                preferred_element_type=jnp.float32,
            )
            weighted = weighted * jnp.swapaxes(factor, 1, 2)[..., None] + addition
            return (new_max, run_sum, weighted)

        return lax.cond(
            within // BLK <= last_block, attention_compute, lambda current: current, carried
        )

    run_max, run_sum, weighted = lax.fori_loop(
        0, piece_len // block_len, attention_one_block, start_state
    )
    log_total = run_max + jnp.log(run_sum)
    attended = weighted / jnp.swapaxes(run_sum, 1, 2)[..., None]
    return (log_total, attended)


def query_grads(
    queries, grad_rows, key_rows, value_rows, log_total, row_delta, query_pos, score_scale, seq_len
):
    seq_here, local_len, head_count, head_dim = queries.shape
    model_dim = head_count * head_dim
    last_block = query_pos[local_len - 1] // BLK
    start_query = jnp.zeros((seq_here, local_len, head_count, head_dim), jnp.float32)
    start_state = (start_query, jnp.zeros((seq_here, seq_len, 2 * model_dim), jnp.float32))
    key_part = lax.all_gather(key_rows, "expert", axis=1, tiled=True)
    value_part = lax.all_gather(value_rows, "expert", axis=1, tiled=True)
    piece_len = key_part.shape[1]
    block_len = math.gcd(piece_len, 512)

    def query_one_block(block_index, carried):
        within = block_index * block_len
        key_block = lax.dynamic_slice_in_dim(key_part, within, block_len, 1).reshape(
            seq_here, block_len, head_count, head_dim
        )
        value_block = lax.dynamic_slice_in_dim(value_part, within, block_len, 1).reshape(
            seq_here, block_len, head_count, head_dim
        )
        key_pos = within + lax.iota(jnp.int32, block_len)
        allowed = key_pos[None, :] // BLK <= query_pos[:, None] // BLK

        def query_compute(current):
            weights, grad_scores = score_terms(
                queries,
                grad_rows,
                key_block,
                value_block,
                log_total,
                row_delta,
                allowed,
                score_scale,
            )
            grad_query = current[0] + jnp.einsum(
                "shqk,skhd->sqhd", grad_scores, key_block, preferred_element_type=jnp.float32
            )
            grad_key = jnp.einsum(
                "shqk,sqhd->skhd", grad_scores, queries, preferred_element_type=jnp.float32
            ).reshape(seq_here, block_len, model_dim)
            grad_value = jnp.einsum(
                "shqk,sqhd->skhd", weights, grad_rows, preferred_element_type=jnp.float32
            ).reshape(seq_here, block_len, model_dim)
            old_rows = lax.dynamic_slice_in_dim(current[1], within, block_len, 1)
            summed = old_rows + jnp.concatenate([grad_key, grad_value], axis=-1)
            return (grad_query, lax.dynamic_update_slice_in_dim(current[1], summed, within, 1))

        return lax.cond(
            within // BLK <= last_block, query_compute, lambda current: current, carried
        )

    return lax.fori_loop(0, piece_len // block_len, query_one_block, start_state)


def body(tokens, cotangent, expert_ids, w_qkv, w_out, ln_gains, ln_biases, router, w_up, w_down):
    n_expert = lax.axis_size("expert")
    seq_part = lax.axis_index("expert")
    seq_here, local_len, model_dim = (tokens.shape[1], tokens.shape[2], tokens.shape[3])
    head_count = HEADS
    head_dim = model_dim // head_count
    score_scale = head_dim ** (-0.5)
    exp_dev = w_up.shape[0]
    experts = exp_dev * n_expert
    capacity = 2 * local_len // experts
    seq_len = local_len * n_expert
    query_pos = seq_part * local_len + lax.iota(jnp.int32, local_len)
    expert_range = lax.iota(jnp.int32, experts)
    all_ids = expert_ids[..., 0]
    local_counts = jnp.sum((all_ids[..., None] == expert_range).astype(jnp.float32), axis=(0, 1, 2))
    counts = lax.psum(local_counts, ("dp", "expert"))
    mean_load = jnp.sum(counts) / experts
    load_ratio = (counts - mean_load) / mean_load
    grad_qkv_w = jnp.zeros((model_dim, 3 * model_dim), jnp.float32)
    grad_out_w = jnp.zeros((model_dim, model_dim), jnp.float32)
    grad_gains = jnp.zeros((2, model_dim), jnp.float32)
    grad_shifts = jnp.zeros((2, model_dim), jnp.float32)
    grad_router = jnp.zeros((model_dim, experts), jnp.float32)
    grad_up = jnp.zeros((exp_dev, model_dim, FF), jnp.float32)
    grad_down = jnp.zeros((exp_dev, FF, model_dim), jnp.float32)
    outputs = []
    input_grads = []
    for micro_index in range(MICRO):
        fetched = fetch_all(w_qkv, w_out, ln_gains, ln_biases, router, w_up, w_down)
        qkv_full, out_full, gains_full, shifts_full, router_full, up_full, down_full = fetched
        gain_rows = gains_full.astype(jnp.float32)
        shift_rows = shifts_full.astype(jnp.float32)
        inputs = tokens[micro_index].astype(jnp.float32)
        expert_of = all_ids[micro_index]
        normed = layer_norm(inputs, gain_rows[0], shift_rows[0])
        normed_low = normed.astype(jnp.bfloat16)
        projected = jnp.einsum(
            "scd,de->sce", normed_low, qkv_full, preferred_element_type=jnp.float32
        ).astype(jnp.bfloat16)
        query_rows = projected[..., :model_dim]
        queries = query_rows.reshape(seq_here, local_len, head_count, head_dim)
        key_rows = projected[..., model_dim : 2 * model_dim]
        value_rows = projected[..., 2 * model_dim :]
        log_total, attended = attention_forward(
            queries, key_rows, value_rows, query_pos, score_scale
        )
        attended_low = attended.reshape(seq_here, local_len, model_dim).astype(jnp.bfloat16)
        middle = inputs + jnp.einsum(
            "scd,de->sce", attended_low, out_full, preferred_element_type=jnp.float32
        )
        mixed_low = layer_norm(middle, gain_rows[1], shift_rows[1]).astype(jnp.bfloat16)
        onehot = (expert_of[..., None] == expert_range).astype(jnp.float32)
        logits = jnp.einsum(
            "scd,de->sce", mixed_low, router_full, preferred_element_type=jnp.float32
        )
        gates = jax.nn.sigmoid(jnp.sum(logits * onehot, axis=-1))
        target, slot_table = route_slots(expert_of, experts, capacity)
        outgoing = to_slots(mixed_low, slot_table).reshape(
            n_expert, exp_dev, seq_here * capacity, model_dim
        )
        arrived = lax.all_to_all(outgoing, "expert", split_axis=0, concat_axis=0, tiled=True)
        preact = jnp.einsum("pesd,edf->pesf", arrived, up_full, preferred_element_type=jnp.float32)
        hidden = gelu_exact(preact).astype(jnp.bfloat16)
        result = jnp.einsum(
            "pesf,efd->pesd", hidden, down_full, preferred_element_type=jnp.float32
        ).astype(jnp.bfloat16)
        returned = lax.all_to_all(result, "expert", split_axis=0, concat_axis=0, tiled=True)
        expert_out = (
            returned.reshape(-1, model_dim)[target]
            .reshape(seq_here, local_len, model_dim)
            .astype(jnp.float32)
        )
        final = middle + gates[..., None] * expert_out
        outputs.append(final.astype(jnp.bfloat16))
        fetched = fetch_all(w_qkv, w_out, ln_gains, ln_biases, router, w_up, w_down)
        qkv_full, out_full, gains_full, shifts_full, router_full, up_full, down_full = fetched
        gain_rows = gains_full.astype(jnp.float32)
        shift_rows = shifts_full.astype(jnp.float32)
        grad_final = cotangent[micro_index].astype(jnp.float32)
        grad_gate = jnp.sum(grad_final * expert_out, axis=-1) + balance_coef * jnp.sum(
            onehot * load_ratio, axis=-1
        )
        grad_logit = grad_gate * gates * (1.0 - gates)
        grad_expert = (gates[..., None] * grad_final).astype(jnp.bfloat16)
        sent_grads = to_slots(grad_expert, slot_table).reshape(
            n_expert, exp_dev, seq_here * capacity, model_dim
        )
        grads_here = lax.all_to_all(sent_grads, "expert", split_axis=0, concat_axis=0, tiled=True)
        hidden_low = gelu_exact(preact).astype(jnp.bfloat16)
        grad_down = grad_down + jnp.einsum(
            "pesf,pesd->efd", hidden_low, grads_here, preferred_element_type=jnp.float32
        )
        grad_hidden = jnp.einsum(
            "pesd,efd->pesf", grads_here, down_full, preferred_element_type=jnp.float32
        )
        grad_pre = jax.vjp(gelu_exact, preact)[1](grad_hidden)[0].astype(jnp.bfloat16)
        grad_up = grad_up + jnp.einsum(
            "pesd,pesf->edf", arrived, grad_pre, preferred_element_type=jnp.float32
        )
        grad_arrived = jnp.einsum(
            "pesf,edf->pesd", grad_pre, up_full, preferred_element_type=jnp.float32
        ).astype(jnp.bfloat16)
        grads_back = lax.all_to_all(grad_arrived, "expert", split_axis=0, concat_axis=0, tiled=True)
        grad_mixed = (
            grads_back.reshape(-1, model_dim)[target]
            .reshape(seq_here, local_len, model_dim)
            .astype(jnp.float32)
        )
        router_cols = jnp.einsum("sce,de->scd", onehot, router_full.astype(jnp.float32))
        grad_mixed = grad_mixed + grad_logit[..., None] * router_cols
        grad_router = grad_router + jnp.einsum(
            "scd,sce->de", mixed_low.astype(jnp.float32), grad_logit[..., None] * onehot
        )
        second_back = jax.vjp(layer_norm, middle, gain_rows[1], shift_rows[1])[1]
        grad_middle, grad_gain_two, grad_shift_two = second_back(grad_mixed)
        grad_middle = grad_middle + grad_final
        grad_branch = grad_middle.astype(jnp.bfloat16)
        grad_out_w = grad_out_w + jnp.einsum(
            "scd,sce->de", attended_low, grad_branch, preferred_element_type=jnp.float32
        )
        grad_attended = jnp.einsum(
            "sce,de->scd", grad_branch, out_full, preferred_element_type=jnp.float32
        ).astype(jnp.bfloat16)
        grad_heads = grad_attended.reshape(seq_here, local_len, head_count, head_dim)
        row_delta = jnp.swapaxes(jnp.sum(grad_heads.astype(jnp.float32) * attended, axis=-1), 1, 2)
        folded = query_grads(
            queries,
            grad_heads,
            key_rows,
            value_rows,
            log_total,
            row_delta,
            query_pos,
            score_scale,
            seq_len,
        )
        grad_query = folded[0].reshape(seq_here, local_len, model_dim)
        key_value = lax.psum_scatter(
            folded[1].astype(jnp.bfloat16), "expert", scatter_dimension=1, tiled=True
        ).astype(jnp.float32)
        grad_key = key_value[..., :model_dim]
        grad_value = key_value[..., model_dim:]
        grad_projected = jnp.concatenate([grad_query, grad_key, grad_value], axis=-1).astype(
            jnp.bfloat16
        )
        grad_qkv_w = grad_qkv_w + jnp.einsum(
            "scd,sce->de", normed_low, grad_projected, preferred_element_type=jnp.float32
        )
        grad_normed = jnp.einsum(
            "sce,de->scd", grad_projected, qkv_full, preferred_element_type=jnp.float32
        )
        first_back = jax.vjp(layer_norm, inputs, gain_rows[0], shift_rows[0])[1]
        grad_inputs, grad_gain_one, grad_shift_one = first_back(grad_normed)
        grad_gains = grad_gains + jnp.stack([grad_gain_one, grad_gain_two])
        grad_shifts = grad_shifts + jnp.stack([grad_shift_one, grad_shift_two])
        input_grads.append(grad_middle + grad_inputs)
    dense_grads = (
        lax.psum_scatter(grad_qkv_w, ("dp", "expert"), scatter_dimension=1, tiled=True),
        lax.psum_scatter(grad_out_w, ("dp", "expert"), scatter_dimension=1, tiled=True),
        lax.psum_scatter(grad_gains, ("dp", "expert"), scatter_dimension=1, tiled=True),
        lax.psum_scatter(grad_shifts, ("dp", "expert"), scatter_dimension=1, tiled=True),
        lax.psum_scatter(grad_router, ("dp", "expert"), scatter_dimension=0, tiled=True),
    )
    expert_grads = (
        lax.psum_scatter(
            grad_up.astype(jnp.bfloat16), "dp", scatter_dimension=1, tiled=True
        ).astype(jnp.float32),
        lax.psum_scatter(
            grad_down.astype(jnp.bfloat16), "dp", scatter_dimension=1, tiled=True
        ).astype(jnp.float32),
    )
    return (jnp.stack(outputs), jnp.stack(input_grads)) + tuple(dense_grads) + tuple(expert_grads)


MESH_ID = pl.DeviceIdType.MESH
NT = (((1,), (1,)), ((), ()))
NN = (((1,), (0,)), ((), ()))
TN = (((0,), (0,)), ((), ()))
VMEM = pl.BlockSpec(memory_space=pltpu.VMEM)


def mm(a, b, dims=NN):
    return lax.dot_general(a, b, dims, preferred_element_type=jnp.float32)


def normalised(v):
    centre = v - jnp.mean(v, axis=-1, keepdims=True)
    spread = jnp.mean(centre * centre, axis=-1, keepdims=True)
    inv = lax.rsqrt(spread + epsilon)
    return centre * inv, inv


class Place:
    def __init__(self, n_dp, n_ex):
        self.n_dp, self.n_ex, self.n_dev, self.n_z = n_dp, n_ex, n_dp * n_ex, n_dp // 2
        self.dp, self.ex = lax.axis_index("dp"), lax.axis_index("expert")
        self.z, self.core = self.dp // 2, self.dp % 2
        self.flat = self.dp * n_ex + self.ex

    def z_peer(self, d):
        return (self.z + d) % self.n_z

    def ex_peer(self, d):
        return (self.ex + d) % self.n_ex

    def on_z(self, z):
        return (z * 2 + self.core, self.ex)

    def on_ex(self, e):
        return (self.dp, e)

    def partner(self):
        return (self.z * 2 + 1 - self.core, self.ex)

    def numbered(self, t):
        return (t // self.n_ex, t % self.n_ex)


def entry_barrier(at):
    sem = pltpu.get_barrier_semaphore()

    def tell(i, carry):
        pl.semaphore_signal(sem, inc=1, device_id=at.numbered((at.flat + i) % at.n_dev), device_id_type=MESH_ID)
        return carry

    lax.fori_loop(1, at.n_dev, tell, 0)
    pl.semaphore_wait(sem, at.n_dev - 1)


class Wires:
    def __init__(self, send_sems, recv_sems):
        self.send_sems, self.recv_sems, self.used = send_sems, recv_sems, 0

    def take(self, n):
        base = self.used
        self.used = base + n
        return base

    def copy(self, i, src, dst, device):
        return pltpu.make_async_remote_copy(
            src_ref=src, dst_ref=dst, send_sem=self.send_sems.at[i], recv_sem=self.recv_sems.at[i],
            device_id=device, device_id_type=MESH_ID,
        )


def first_kernel(
    n_dp, n_ex, x_ref, cot_ref, slot_ref, eid_ref, wq_ref, wo_ref, small_ref,
    rows_ref, grads_ref, q_ref, k_ref, v_ref, xn_ref, lse_ref, attr_ref, mid_ref, mix_ref, gate_ref, w_ref, wo_all_ref, smalls_ref,
    xg, small_all, wt_a, wt_b, wo_b, wide, att_acc, lse_acc, attb, disp, send_sems, recv_sems,
):
    bf, f32 = jnp.bfloat16, jnp.float32
    at = Place(n_dp, n_ex)
    wires = Wires(send_sems, recv_sems)
    n_dev, n_z, ex = at.n_dev, at.n_z, at.ex
    seqs, local_len, dim = x_ref.shape
    width = q_ref.shape[2]
    head_dim = dim // HEADS
    heads = width // head_dim
    piece, oc = wq_ref.shape[1], wo_ref.shape[1]
    cap = rows_ref.shape[2]
    scale = head_dim ** -0.5
    entry_barrier(at)

    i_small = wires.take(n_dev)

    def small_copy(i):
        return wires.copy(i_small + i, small_ref, small_all.at[at.flat], at.numbered((at.flat + i) % n_dev))

    def small_start(i, carry):
        small_copy(i).start()
        return carry

    lax.fori_loop(1, n_dev, small_start, 0)
    me_j = ex * n_dp + at.dp
    i_piece = wires.take(3)
    pieces = []
    for r in range(3):
        c = 3 * at.flat + r
        sec, j = c // n_dev, c % n_dev
        copy = wires.copy(i_piece + r, wq_ref.at[r], wt_a.at[sec], (j % n_dp, j // n_dp))
        away = j != me_j
        pl.when(away)(copy.start)
        pieces.append((copy, away, sec))
    i_wo = wires.take(n_z)
    wo_line = [wires.copy(i_wo + d, wo_ref, wo_b.at[at.core, ex, at.z], at.on_z(at.z_peer(d))) for d in range(1, n_z)]
    for c in wo_line:
        c.start()
    i_tok = wires.take(seqs * n_ex)

    def token_copy(m, d):
        return wires.copy(i_tok + m * n_ex + d, x_ref.at[m], xg.at[m, ex], at.on_ex(at.ex_peer(d)))

    for d in range(1, n_ex):
        token_copy(0, d).start()
    small_all[at.flat] = small_ref[...]
    wo_b[at.core, ex, at.z] = wo_ref[...]
    for m in range(seqs):
        xg[m, ex] = x_ref[m]
    for r, (copy, away, sec) in enumerate(pieces):
        pl.when(away)(copy.wait_recv)

        @pl.when(jnp.logical_not(away))
        def _():
            wt_a[sec] = wq_ref[r]

    i_line = wires.take(n_z)
    w_line = [wires.copy(i_line + d, wt_a, wt_b.at[at.core, at.z], at.on_z(at.z_peer(d))) for d in range(1, n_z)]
    for c in w_line:
        c.start()
    wt_b[at.core, at.z] = wt_a[...]
    for c in w_line:
        c.wait_recv()
    w_pair = wires.copy(wires.take(1), wt_b.at[at.core], wt_b.at[at.core], at.partner())
    w_pair.start()
    for c in wo_line:
        c.wait_recv()
    i_wo2 = wires.take(n_ex)
    wo_plane = [wires.copy(i_wo2 + d, wo_b.at[at.core, ex], wo_b.at[at.core, ex], at.on_ex(at.ex_peer(d))) for d in range(1, n_ex)]
    for c in wo_plane:
        c.start()
    for m in range(1, seqs):
        for d in range(1, n_ex):
            token_copy(m, d).start()

    def small_wait(i, carry):
        small_copy(i).wait_recv()
        return carry

    lax.fori_loop(1, n_dev, small_wait, 0)
    smalls_ref[...] = jnp.zeros(smalls_ref.shape, f32)
    for s in range(n_dev):
        lo = s * oc // 128 * 128
        hi = min(lo + 256, dim)
        smalls_ref[:, lo:hi] += small_all[s][:, 0 : hi - lo].astype(f32)
    gain_one, shift_one = smalls_ref[0:1, :], smalls_ref[2:3, :]
    gain_two, shift_two = smalls_ref[1:2, :], smalls_ref[3:4, :]
    w_pair.wait_recv()
    for sec in range(3):
        for z in range(n_z):
            for core in range(2):
                row = (z * 2 + core) * piece
                wide[row : row + piece, :] = wt_b[core, z, sec].astype(f32)
        w_ref[sec] = wide[0:width, :].astype(bf)

    i_back = wires.take(seqs * n_ex)

    def back_copy(m, d):
        peer = at.ex_peer(d)
        return wires.copy(i_back + m * n_ex + d, attb.at[m, peer], attr_ref.at[m, ex], at.on_ex(peer))

    lane_head = lax.broadcasted_iota(jnp.int32, (1, width), 1) // head_dim
    lane = lax.broadcasted_iota(jnp.int32, (1, 128), 1)

    def attend(m, carry):
        def project(d, c_):
            src = (ex - d + n_ex) % n_ex
            pl.when(d > 0)(lambda: token_copy(m, d).wait_recv())
            rows = pl.ds(pl.multiple_of(src * local_len, local_len), local_len)
            hat, _ = normalised(xg[m, src].astype(f32))
            low = (hat * gain_one + shift_one).astype(bf)
            xn_ref[m, rows, :] = low
            q_ref[m, rows, :] = mm(low, w_ref[0], NT).astype(bf)
            k_ref[m, rows, :] = mm(low, w_ref[1], NT).astype(bf)
            v_ref[m, rows, :] = mm(low, w_ref[2], NT).astype(bf)
            return c_

        lax.fori_loop(0, n_ex, project, 0)
        for i in range(n_ex):
            reach = (i + 1) * local_len
            here = slice(i * local_len, reach)
            att_acc[...] = jnp.zeros((local_len, width), f32)
            lse_acc[...] = jnp.zeros((local_len, 128), f32)

            def one_head(h, c_):
                mine = lane_head == h
                qb = q_ref[m, here, :]
                s = mm(jnp.where(mine, qb, jnp.zeros_like(qb)), k_ref[m, 0:reach, :], NT) * scale
                top = jnp.max(s, axis=-1, keepdims=True)
                e = jnp.exp(s - top)
                total = jnp.sum(e, axis=-1, keepdims=True)
                p = (e / total).astype(bf)
                att_acc[...] = jnp.where(mine, mm(p, v_ref[m, 0:reach, :]), att_acc[...])
                lse_acc[...] = jnp.where(lane == h, top + jnp.log(total), lse_acc[...])
                return c_

            lax.fori_loop(0, heads, one_head, 0)
            attb[m, i] = att_acc[...].astype(bf)
            lse_ref[m, :, here] = lse_acc[...].T[0:8, :]
        for d in range(1, n_ex):
            back_copy(m, d).start()
        attr_ref[m, ex] = attb[m, ex]
        return carry

    lax.fori_loop(0, seqs, attend, 0)
    for c in wo_plane:
        c.wait_recv()
    wo_pair = wires.copy(wires.take(1), wo_b.at[at.core], wo_b.at[at.core], at.partner())
    wo_pair.start()
    wo_pair.wait_recv()
    for b in range(n_ex):
        for s in range(n_dev):
            wide[s * oc : (s + 1) * oc, 0:width] = wo_b[s // n_ex % 2, s % n_ex, s // n_ex // 2, b].astype(f32)
        wo_all_ref[b] = wide[0:dim, 0:width].astype(bf)

    arrive = (rows_ref, grads_ref)
    i_out = wires.take(2 * seqs * n_ex)

    def out_copy(m, a, d):
        peer = at.ex_peer(d)
        return wires.copy(i_out + (m * 2 + a) * n_ex + d, disp.at[m, a, peer], arrive[a].at[m, ex], at.on_ex(peer))

    def route(m, carry):
        for d in range(1, n_ex):
            back_copy(m, d).wait_recv()
        mid_ref[m] = x_ref[m].astype(f32)
        for b in range(n_ex):
            mid_ref[m] += mm(attr_ref[m, b], wo_all_ref[b], NT)
        hat, _ = normalised(mid_ref[m])
        mixed = (hat * gain_two + shift_two).astype(bf)
        mix_ref[m] = mixed
        logits = mm(mixed, smalls_ref[...].astype(bf), NT)
        mine = lax.broadcasted_iota(jnp.int32, logits.shape, 1) == eid_ref[m] + 4
        gate = jax.nn.sigmoid(jnp.sum(jnp.where(mine, logits, 0.0), axis=1, keepdims=True))
        gate_ref[m] = jnp.broadcast_to(gate, (local_len, 128))
        scaled = (gate * cot_ref[m].astype(f32)).astype(bf)
        place = jnp.where(slot_ref[m] == lax.broadcasted_iota(jnp.int32, (n_ex * cap, local_len), 0), 1.0, 0.0).astype(bf)
        for a, value in ((0, mixed), (1, scaled)):
            disp[m, a] = mm(place, value).astype(bf).reshape(n_ex, cap, dim)
            for d in range(1, n_ex):
                out_copy(m, a, d).start()
            arrive[a][m, ex] = disp[m, a, ex]
        return carry

    lax.fori_loop(0, seqs, route, 0)
    for m in range(seqs):
        for a in range(2):
            for d in range(1, n_ex):
                out_copy(m, a, d).wait()
        for d in range(1, n_ex):
            back_copy(m, d).wait_send()
            token_copy(m, d).wait_send()

    def small_done(i, carry):
        small_copy(i).wait_send()
        return carry

    lax.fori_loop(1, n_dev, small_done, 0)
    for copy, away, _ in pieces:
        pl.when(away)(copy.wait_send)
    for c in [*wo_line, *w_line, w_pair, *wo_plane, wo_pair]:
        c.wait_send()


def first_stage(n_dp, n_ex, x, cot, slots, eid, wq, wo, small):
    bf, f32 = jnp.bfloat16, jnp.float32
    seqs, local_len, dim = x.shape
    width, total_len, n_z = dim // n_ex, local_len * n_ex, n_dp // 2
    cap = 2 * local_len // n_ex
    piece, oc, n_dev = wq.shape[1], wo.shape[1], n_dp * n_ex
    shapes = [
        ((seqs, n_ex, cap, dim), bf), ((seqs, n_ex, cap, dim), bf),
        ((seqs, total_len, width), bf), ((seqs, total_len, width), bf), ((seqs, total_len, width), bf),
        ((seqs, total_len, dim), bf), ((seqs, 8, total_len), f32),
        ((seqs, n_ex, local_len, width), bf), ((seqs, local_len, dim), f32), ((seqs, local_len, dim), bf), ((seqs, local_len, 128), f32),
        ((3, width, dim), bf), ((n_ex, dim, width), bf), ((16, dim), f32),
    ]
    n_sems = n_dev + 3 + n_z + seqs * n_ex + n_z + 1 + n_ex + seqs * n_ex + 1 + 2 * seqs * n_ex
    return pl.pallas_call(
        functools.partial(first_kernel, n_dp, n_ex),
        out_shape=[jax.ShapeDtypeStruct(s, d) for s, d in shapes],
        in_specs=[VMEM] * 7,
        out_specs=[VMEM] * len(shapes),
        scratch_shapes=[
            pltpu.VMEM((seqs, n_ex, local_len, dim), bf),
            pltpu.VMEM((n_dev, 16, 256), bf),
            pltpu.VMEM((3, piece, dim), bf),
            pltpu.VMEM((2, n_z, 3, piece, dim), bf),
            pltpu.VMEM((2, n_ex, n_z, n_ex, oc, width), bf),
            pltpu.VMEM((dim, dim), f32),
            pltpu.VMEM((local_len, width), f32),
            pltpu.VMEM((local_len, 128), f32),
            pltpu.VMEM((seqs, n_ex, local_len, width), bf),
            pltpu.VMEM((seqs, 2, n_ex, cap, dim), bf),
            pltpu.SemaphoreType.DMA((n_sems,)),
            pltpu.SemaphoreType.DMA((n_sems,)),
        ],
        compiler_params=pltpu.CompilerParams(collective_id=0, has_side_effects=True, vmem_limit_bytes=64000 * 1024),
        name="attend_and_send",
    )(x, cot, slots, eid, wq, wo, small)


def second_kernel(
    n_dp, n_ex, cot_ref, slot_ref, eid_ref, rows_ref, grads_ref, lse_ref, mid_ref, gate_ref, smalls_ref,
    up_hbm, down_hbm, q_hbm, k_hbm, v_hbm, xn_hbm, mix_hbm, attr_hbm, w_hbm, wo_hbm, x_hbm,
    out_ref, gtok_ref, gq_ref, gout_ref, gsmall_ref, gup_ref, gdown_ref,
    outbox, inbox, gdt, gup, pin_dn, pin_up, zin_dn, zin_up, gas, gar, gob, gob_pair, gob_plane, gob_line, gws, gws_pair, gws_line, gws_sum,
    small_in, small_out, send_sems, recv_sems, load_sems,
):
    bf, f32 = jnp.bfloat16, jnp.float32
    at = Place(n_dp, n_ex)
    wires = Wires(send_sems, recv_sems)
    n_dev, n_z, ex, z, core = at.n_dev, at.n_z, at.ex, at.z, at.core
    seqs, local_len, dim = cot_ref.shape
    width = attr_hbm.shape[3]
    head_dim = dim // HEADS
    heads = width // head_dim
    total_len = local_len * n_ex
    cap = rows_ref.shape[2]
    slots = n_ex * cap
    tile = up_hbm.shape[1] // n_z
    shard = dim // n_dp
    oc, piece = gob.shape[4], gws.shape[3]
    scale = head_dim ** -0.5
    entry_barrier(at)

    i_ret = wires.take(seqs * n_ex)

    def return_copy(m, d):
        peer = at.ex_peer(d)
        return wires.copy(i_ret + m * n_ex + d, outbox.at[m, peer], inbox.at[m, ex], at.on_ex(peer))

    i_pair = wires.take(2 * n_z)

    def pair_copies(t):
        return (
            wires.copy(i_pair + 2 * t, gdt.at[t, 1 - core], pin_dn.at[t], at.partner()),
            wires.copy(i_pair + 2 * t + 1, gup.at[1 - core, t], pin_up.at[t], at.partner()),
        )

    i_line_up = wires.take(n_z * n_z)
    i_line_dn = wires.take(n_z)

    def line_up(t, d):
        peer = at.z_peer(d)
        return wires.copy(i_line_up + t * n_z + d, gup.at[core, t, peer], zin_up.at[d - 1, t], at.on_z(peer))

    def line_dn(t):
        d = (t - z + n_z) % n_z
        return wires.copy(i_line_dn + d, gdt.at[t, core], zin_dn.at[d - 1], at.on_z(t))

    def order(step):
        return (n_z - 1) * step % n_z

    def fold_pair(t):
        for c in pair_copies(t):
            c.wait_recv()
        gdt[t, core] = (gdt[t, core].astype(f32) + pin_dn[t].astype(f32)).astype(bf)
        gup[core, t] = (gup[core, t].astype(f32) + pin_up[t].astype(f32)).astype(bf)
        pl.when(t != z)(lambda: line_dn(t).start())
        for d in range(1, n_z):
            line_up(t, d).start()

    def experts(up_t, down_t, res_acc, gar_acc, hid, gpre, x_t, g_t):
        def loads(step):
            cols = pl.ds(pl.multiple_of(order(step) * tile, tile), tile)
            return (
                pltpu.make_async_copy(up_hbm.at[:, cols], up_t, load_sems.at[0]),
                pltpu.make_async_copy(down_hbm.at[cols, :], down_t, load_sems.at[1]),
            )

        for c in loads(0):
            c.start()
        for m in range(seqs):
            lanes = slice(m * slots, (m + 1) * slots)
            x_t[:, lanes] = rows_ref[m].reshape(slots, dim).T
            g_t[:, lanes] = grads_ref[m].reshape(slots, dim).T
            res_acc[m] = jnp.zeros((slots, dim), f32)
            gar_acc[m] = jnp.zeros((slots, dim), f32)

        def one_tile(step, carry):
            t = order(step)
            for c in loads(step):
                c.wait()

            def one_seq(m, c_):
                rows = rows_ref[m].reshape(slots, dim)
                pre = mm(rows, up_t[...])
                cdf = 0.5 * (1.0 + lax.erf(pre * (2.0 ** -0.5)))
                hidden = (pre * cdf).astype(bf)
                slope = cdf + pre * jnp.exp(-0.5 * pre * pre) * ((2.0 * math.pi) ** -0.5)
                mine = pl.ds(pl.multiple_of(m * slots, slots), slots)
                hid[mine, :] = hidden
                res_acc[m] += mm(hidden, down_t[...])
                low = (mm(grads_ref[m].reshape(slots, dim), down_t[...], NT) * slope).astype(bf)
                gpre[mine, :] = low
                gar_acc[m] += mm(low, up_t[...], NT)

                @pl.when(step == n_z - 1)
                def _():
                    outbox[m, :, 0] = res_acc[m].astype(bf).reshape(n_ex, cap, dim)
                    outbox[m, :, 1] = gar_acc[m].astype(bf).reshape(n_ex, cap, dim)
                    for d in range(1, n_ex):
                        return_copy(m, d).start()
                    inbox[m, ex] = outbox[m, ex]

                return c_

            lax.fori_loop(0, seqs, one_seq, 0)

            @pl.when(step + 1 < n_z)
            def _():
                for c in loads(step + 1):
                    c.start()

            down_grad = mm(g_t[...], hid[...])
            half = tile // 2
            for c in range(2):
                gdt[t, c] = down_grad[:, c * half : (c + 1) * half].astype(bf)
            up_grad = mm(x_t[...], gpre[...]).astype(bf).reshape(n_z, 2, shard, tile)
            for c in range(2):
                gup[c, t] = up_grad[:, c]
            for c in pair_copies(t):
                c.start()
            pl.when(step > 0)(lambda: fold_pair(order(step - 1)))
            return carry

        lax.fori_loop(0, n_z, one_tile, 0)

    slots_all = seqs * slots
    pl.run_scoped(
        experts,
        pltpu.VMEM((dim, tile), bf), pltpu.VMEM((tile, dim), bf),
        pltpu.VMEM((seqs, slots, dim), f32), pltpu.VMEM((seqs, slots, dim), f32),
        pltpu.VMEM((slots_all, tile), bf), pltpu.VMEM((slots_all, tile), bf),
        pltpu.VMEM((dim, slots_all), bf), pltpu.VMEM((dim, slots_all), bf),
    )
    fold_pair(order(n_z - 1))

    gain_one, gain_two = smalls_ref[0:1, :], smalls_ref[1:2, :]
    tally = smalls_ref[4 + n_ex : 6 + n_ex, 0:128]
    for i in range(1, dim // 128):
        tally += smalls_ref[4 + n_ex : 6 + n_ex, i * 128 : (i + 1) * 128]
    lane = lax.broadcasted_iota(jnp.int32, (1, 128), 1)
    counts = jnp.where(lane < n_ex, 16.0 * tally[0:1] + tally[1:2], 0.0)
    mean_load = jnp.sum(counts, axis=1, keepdims=True) / n_ex
    load_ratio = (counts - mean_load) / mean_load
    small_out[...] = jnp.zeros(small_out.shape, f32)

    i_ga = wires.take(seqs * n_ex)

    def ga_copy(m, d):
        peer = at.ex_peer(d)
        return wires.copy(i_ga + m * n_ex + d, gas.at[m, peer], gar.at[m, ex], at.on_ex(peer))

    i_gob = wires.take(1 + n_ex + n_z)
    gob_pair_copy = wires.copy(i_gob, gob.at[1 - core], gob_pair, at.partner())

    def gob_plane_copy(d):
        peer = at.ex_peer(d)
        return wires.copy(i_gob + 1 + d, gob.at[core, peer], gob_plane.at[d], at.on_ex(peer))

    def gob_line_copy(d):
        peer = at.z_peer(d)
        return wires.copy(i_gob + 1 + n_ex + d, gob_plane.at[0, peer], gob_line.at[d], at.on_z(peer))

    i_gw = wires.take(1 + n_z + 3)
    gws_pair_copy = wires.copy(i_gw, gws.at[1 - core], gws_pair, at.partner())

    def gws_line_copy(d):
        peer = at.z_peer(d)
        return wires.copy(i_gw + 1 + d, gws.at[core, peer], gws_line.at[d], at.on_z(peer))

    i_part = wires.take(seqs * n_ex)

    def part_copy(m, d):
        peer = at.ex_peer(d)
        return wires.copy(i_part + m * n_ex + d, outbox.at[m, peer], inbox.at[m, ex], at.on_ex(peer))

    def backward(gb_t, q_v, k_v, v_v, xn_v, mix_ref, attr_ref, w_ref, wo_ref, dq, dk, dv, gw):
        brought = [
            pltpu.make_async_copy(src, dst, load_sems.at[i])
            for i, (src, dst) in enumerate(((wo_hbm, wo_ref), (mix_hbm, mix_ref), (attr_hbm, attr_ref), (w_hbm, w_ref), (q_hbm, q_v), (k_hbm, k_v), (v_hbm, v_v)))
        ]
        for c in brought:
            c.start()
        brought[0].wait()
        brought[1].wait()

        def head(m, carry):
            for d in range(1, n_ex):
                return_copy(m, d).wait()
            place = jnp.where(slot_ref[m] == lax.broadcasted_iota(jnp.int32, (local_len, slots), 1), 1.0, 0.0).astype(bf)
            expert_out = mm(place, inbox[m, :, 0].reshape(slots, dim))
            gate = gate_ref[m][:, 0:1]
            cot = cot_ref[m].astype(f32)
            out_ref[m] = (mid_ref[m] + gate * expert_out).astype(bf)
            mine = lane == eid_ref[m]
            grad_gate = jnp.sum(cot * expert_out, axis=1, keepdims=True) + balance_coef * jnp.sum(jnp.where(mine, load_ratio, 0.0), axis=1, keepdims=True)
            grad_logit = grad_gate * gate * (1.0 - gate)
            grad_mixed = mm(place, inbox[m, :, 1].reshape(slots, dim))
            mixed = mix_ref[m].astype(f32)
            for e in range(n_ex):
                routed = jnp.where(eid_ref[m] == e, grad_logit, 0.0)
                grad_mixed += routed * smalls_ref[4 + e : 5 + e, :]
                small_out[4 + e : 5 + e, 0:dim] += jnp.sum(routed * mixed, axis=0, keepdims=True)
            hat, inv = normalised(mid_ref[m])
            small_out[1:2, 0:dim] += jnp.sum(grad_mixed * hat, axis=0, keepdims=True)
            small_out[3:4, 0:dim] += jnp.sum(grad_mixed, axis=0, keepdims=True)
            dhat = grad_mixed * gain_two
            grad_middle = inv * (dhat - jnp.mean(dhat, axis=1, keepdims=True) - hat * jnp.mean(dhat * hat, axis=1, keepdims=True)) + cot
            gtok_ref[m] = grad_middle
            branch = grad_middle.astype(bf)
            for e in range(n_ex):
                gas[m, e] = mm(branch, wo_ref[e]).astype(bf)
            for d in range(1, n_ex):
                ga_copy(m, d).start()
            gar[m, ex] = gas[m, ex]
            gb_t[m] = branch.T
            return carry

        lax.fori_loop(0, seqs, head, 0)

        for c in brought[2:]:
            c.wait()
        for b in range(n_ex):
            total = mm(gb_t[0], attr_ref[0, b])
            for m in range(1, seqs):
                total += mm(gb_t[m], attr_ref[m, b])
            for s in range(n_dev):
                gob[s // n_ex % 2, s % n_ex, s // n_ex // 2, b] = total[s * oc : (s + 1) * oc].astype(bf)
        gob_pair_copy.start()
        gw[...] = jnp.zeros(gw.shape, f32)
        lane_head = lax.broadcasted_iota(jnp.int32, (1, width), 1) // head_dim

        def attention_back(m, carry):
            xn_copy = pltpu.make_async_copy(xn_hbm.at[m], xn_v, load_sems.at[7])
            xn_copy.start()
            for d in range(1, n_ex):
                ga_copy(m, d).wait()
            dk[...] = jnp.zeros(dk.shape, f32)
            dv[...] = jnp.zeros(dv.shape, f32)
            dq[...] = jnp.zeros(dq.shape, f32)
            for i in range(n_ex):
                reach = (i + 1) * local_len
                here = slice(i * local_len, reach)

                def one_head(h, c_):
                    mine = lane_head == h
                    qb, ga = q_v[m, here, :], gar[m, i]
                    q_h = jnp.where(mine, qb, jnp.zeros_like(qb))
                    ga_h = jnp.where(mine, ga, jnp.zeros_like(ga))
                    kk = k_v[m, 0:reach, :]
                    s = mm(kk, q_h, NT)
                    p = jnp.exp(s * scale - lse_ref[m, pl.ds(h, 1), here])
                    dp = mm(v_v[m, 0:reach, :], ga_h, NT)
                    delta = jnp.sum(p * dp, axis=0, keepdims=True)
                    ds = (p * (dp - delta) * scale).astype(bf)
                    dv[0:reach, :] += mm(p.astype(bf), ga_h)
                    dk[0:reach, :] += mm(ds, q_h)
                    dq[here, :] += jnp.where(mine, mm(ds, kk, TN), 0.0)
                    return c_

                lax.fori_loop(0, heads, one_head, 0)
            low = [g[...].astype(bf) for g in (dq, dk, dv)]
            xn_copy.wait()
            for sec in range(3):
                gw[sec] += mm(low[sec], xn_v[...], TN)
            part = mm(low[0], w_ref[0]) + mm(low[1], w_ref[1]) + mm(low[2], w_ref[2])
            outbox[m] = part.astype(bf).reshape(n_ex, 2, cap, dim)
            for d in range(1, n_ex):
                part_copy(m, d).start()
            inbox[m, ex] = outbox[m, ex]
            return carry

        lax.fori_loop(0, seqs, attention_back, 0)
        for sec in range(3):
            for j in range(n_dp):
                gws[j % 2, j // 2, sec] = gw[sec, j * piece : (j + 1) * piece, :].astype(bf)

    pl.run_scoped(
        backward,
        pltpu.VMEM((seqs, dim, local_len), bf),
        pltpu.VMEM((seqs, total_len, width), bf), pltpu.VMEM((seqs, total_len, width), bf), pltpu.VMEM((seqs, total_len, width), bf),
        pltpu.VMEM((total_len, dim), bf), pltpu.VMEM((seqs, local_len, dim), bf),
        pltpu.VMEM((seqs, n_ex, local_len, width), bf), pltpu.VMEM((3, width, dim), bf), pltpu.VMEM((n_ex, dim, width), bf),
        pltpu.VMEM((total_len, width), f32), pltpu.VMEM((total_len, width), f32), pltpu.VMEM((total_len, width), f32),
        pltpu.VMEM((3, width, dim), f32),
    )
    gws_pair_copy.start()
    gob_pair_copy.wait()
    gob[core] = (gob[core].astype(f32) + gob_pair[...].astype(f32)).astype(bf)
    for d in range(1, n_ex):
        gob_plane_copy(d).start()
    gws_pair_copy.wait()
    gws[core] = (gws[core].astype(f32) + gws_pair[...].astype(f32)).astype(bf)
    for d in range(1, n_z):
        gws_line_copy(d).start()

    def tail(x_v, m, carry):
        brought = pltpu.make_async_copy(x_hbm.at[m], x_v, load_sems.at[0])
        brought.start()
        brought.wait()
        for d in range(1, n_ex):
            part_copy(m, d).wait()
        grad_normed = jnp.zeros((local_len, dim), f32)
        for e in range(n_ex):
            grad_normed += inbox[m, e].reshape(local_len, dim).astype(f32)
        hat, inv = normalised(x_v[...].astype(f32))
        small_out[0:1, 0:dim] += jnp.sum(grad_normed * hat, axis=0, keepdims=True)
        small_out[2:3, 0:dim] += jnp.sum(grad_normed, axis=0, keepdims=True)
        dhat = grad_normed * gain_one
        gtok_ref[m] += inv * (dhat - jnp.mean(dhat, axis=1, keepdims=True) - hat * jnp.mean(dhat * hat, axis=1, keepdims=True))
        return carry

    def tails(x_v):
        lax.fori_loop(0, seqs, functools.partial(tail, x_v), 0)

    pl.run_scoped(tails, pltpu.VMEM((local_len, dim), bf))

    i_small = wires.take(n_dev)
    def window(t):
        return pl.ds(pl.multiple_of(t * oc // 128 * 128, 128), 256)

    def small_copy(i):
        t = (at.flat + i) % n_dev
        return wires.copy(i_small + i, small_out.at[:, window(t)], small_in.at[at.flat], at.numbered(t))

    def small_start(i, carry):
        small_copy(i).start()
        return carry

    lax.fori_loop(1, n_dev, small_start, 0)
    small_in[at.flat] = small_out[:, window(at.flat)]

    for d in range(1, n_ex):
        gob_plane_copy(d).wait()
    total = gob[core, ex].astype(f32)
    for d in range(1, n_ex):
        total += gob_plane[d].astype(f32)
    gob_plane[0] = total.astype(bf)
    for d in range(1, n_z):
        gob_line_copy(d).start()

    for d in range(1, n_z):
        gws_line_copy(d).wait()
    total = gws[core, z].astype(f32)
    for d in range(1, n_z):
        total += gws_line[d].astype(f32)
    gws_sum[...] = total.astype(bf)
    me_j = ex * n_dp + at.dp
    finals = []
    for sec in range(3):
        c = sec * n_dev + me_j
        owner, r = c // 3, c % 3
        copy = wires.copy(i_gw + 1 + n_z + r, gws_sum.at[sec], gq_ref.at[r], at.numbered(owner))
        away = owner != at.flat
        pl.when(away)(copy.start)
        finals.append((copy, away, sec, r))

    for t in range(n_z):
        for c in pair_copies(t):
            c.wait_send()
        for d in range(1, n_z):
            line_up(t, d).wait()
        pl.when(t != z)(lambda: line_dn(t).wait_send())
    total = gdt[z, core].astype(f32)
    for d in range(1, n_z):
        wires.copy(i_line_dn + d, gdt.at[0, core], zin_dn.at[d - 1], at.on_z(at.z_peer(d))).wait_recv()
        total += zin_dn[d - 1].astype(f32)
    gdown_ref[...] = total.T
    for t in range(n_z):
        total = gup[core, t, z].astype(f32)
        for d in range(1, n_z):
            total += zin_up[d - 1, t].astype(f32)
        gup_ref[:, t * tile : (t + 1) * tile] = total

    for copy, away, sec, r in finals:
        @pl.when(away)
        def _():
            copy.wait()

        @pl.when(jnp.logical_not(away))
        def _():
            gq_ref[r] = gws_sum[sec]

    for d in range(1, n_z):
        gob_line_copy(d).wait()
    total = gob_plane[0, z].astype(f32)
    for d in range(1, n_z):
        total += gob_line[d].astype(f32)
    gout_ref[...] = total

    def small_wait(i, carry):
        small_copy(i).wait()
        return carry

    lax.fori_loop(1, n_dev, small_wait, 0)
    total = jnp.zeros((8, 256), f32)
    for s in range(n_dev):
        total += small_in[s]
    gsmall_ref[...] = total


def second_stage(n_dp, n_ex, *args):
    bf, f32 = jnp.bfloat16, jnp.float32
    x, rows = args[0], args[3]
    seqs, local_len, dim = x.shape
    width, total_len, n_z, n_dev = dim // n_ex, local_len * n_ex, n_dp // 2, n_dp * n_ex
    cap = rows.shape[2]
    ff = args[9].shape[1]
    tile, shard = ff // n_z, dim // n_dp
    oc, piece = dim // n_dev, width // n_dp
    half = tile // 2
    shapes = [
        ((seqs, local_len, dim), bf), ((seqs, local_len, dim), f32), ((3, piece, dim), bf), ((n_ex, oc, width), f32), ((8, 256), f32),
        ((shard, ff), f32), ((half, dim), f32),
    ]
    n_sems = seqs * n_ex + 2 * n_z + n_z * n_z + n_z + seqs * n_ex + 1 + n_ex + n_z + 1 + n_z + 3 + seqs * n_ex + n_dev
    hbm = pl.BlockSpec(memory_space=pl.ANY)
    return pl.pallas_call(
        functools.partial(second_kernel, n_dp, n_ex),
        out_shape=[jax.ShapeDtypeStruct(s, d) for s, d in shapes],
        in_specs=[VMEM] * 9 + [hbm] * 11,
        out_specs=[VMEM] * len(shapes),
        scratch_shapes=[
            pltpu.VMEM((seqs, n_ex, 2, cap, dim), bf), pltpu.VMEM((seqs, n_ex, 2, cap, dim), bf),
            pltpu.VMEM((n_z, 2, dim, half), bf), pltpu.VMEM((2, n_z, n_z, shard, tile), bf),
            pltpu.VMEM((n_z, dim, half), bf), pltpu.VMEM((n_z, n_z, shard, tile), bf),
            pltpu.VMEM((n_z - 1, dim, half), bf), pltpu.VMEM((n_z - 1, n_z, shard, tile), bf),
            pltpu.VMEM((seqs, n_ex, local_len, width), bf), pltpu.VMEM((seqs, n_ex, local_len, width), bf),
            pltpu.VMEM((2, n_ex, n_z, n_ex, oc, width), bf), pltpu.VMEM((n_ex, n_z, n_ex, oc, width), bf),
            pltpu.VMEM((n_ex, n_z, n_ex, oc, width), bf), pltpu.VMEM((n_z, n_ex, oc, width), bf),
            pltpu.VMEM((2, n_z, 3, piece, dim), bf), pltpu.VMEM((n_z, 3, piece, dim), bf), pltpu.VMEM((n_z, 3, piece, dim), bf), pltpu.VMEM((3, piece, dim), bf),
            pltpu.VMEM((n_dev, 8, 256), f32), pltpu.VMEM((8, dim + 256), f32),
            pltpu.SemaphoreType.DMA((n_sems,)), pltpu.SemaphoreType.DMA((n_sems,)), pltpu.SemaphoreType.DMA((8,)),
        ],
        compiler_params=pltpu.CompilerParams(collective_id=1, has_side_effects=True, vmem_limit_bytes=67043328),
        name="experts_and_backward",
    )(*args)


def fast_body(tokens, cotangent, expert_ids, w_qkv, w_out, ln_gains, ln_biases, router, w_up, w_down):
    bf, f32 = jnp.bfloat16, jnp.float32
    n_expert, n_dp = lax.axis_size("expert"), lax.axis_size("dp")
    ex, dp = lax.axis_index("expert"), lax.axis_index("dp")
    both = ("dp", "expert")
    n_dev = n_dp * n_expert
    seqs, local_len, dim = tokens.shape[0] * tokens.shape[1], tokens.shape[2], tokens.shape[3]
    head_dim = dim // HEADS
    heads = HEADS // n_expert
    width = heads * head_dim
    total_len = local_len * n_expert
    experts = n_expert
    cap = 2 * local_len // experts
    scale = head_dim ** -0.5
    qc, oc = w_qkv.shape[1], w_out.shape[1]
    ids = expert_ids.reshape(seqs, local_len)
    onehot = (ids[..., None] == lax.iota(jnp.int32, experts)).astype(f32)
    counts = jnp.sum(onehot, axis=(0, 1))
    high = jnp.floor(counts / 16)
    small = jnp.concatenate([ln_gains, ln_biases, router.T], axis=0)
    n_small = small.shape[0]
    flat = dp * n_expert + ex
    tally = jnp.stack([high, counts - 16 * high]).astype(bf)
    block = jnp.zeros((16, 256), bf)
    block = lax.dynamic_update_slice(block, small, (0, lax.rem(flat * oc, 128)))
    block = lax.dynamic_update_slice(block, tally, (n_small, 0))
    x = tokens.reshape(seqs, local_len, dim)
    cot16 = cotangent.reshape(seqs, local_len, dim)
    cot = cot16.astype(f32)
    counted = onehot.astype(jnp.int32)
    order_in = jnp.sum((jnp.cumsum(counted, axis=1) - counted) * counted, axis=-1)
    target = ids * cap + order_in
    place = (target[:, None, :] == lax.iota(jnp.int32, experts * cap)[None, :, None]).astype(bf)
    wq = w_qkv.T.reshape(3, qc // 3, dim)
    wo = w_out.reshape(n_expert, width, oc).transpose(0, 2, 1)
    up_full = lax.all_gather(w_up[0], "dp", axis=0, tiled=True)
    down_full = lax.all_gather(w_down[0], "dp", axis=0, tiled=True)
    (rows_in, grads_in, q, k, v, xn, lse, att_r, middle, mixed, gates, w_own, wo_b, smalls) = first_stage(
        n_dp, n_expert, x, cot16, target[:, None, :], ids[..., None], wq, wo, block)
    (output, grad_tokens, gq, gout, gs, gu, gd) = second_stage(
        n_dp, n_expert, cot16, target[..., None], ids[..., None], rows_in, grads_in, lse, middle, gates, smalls,
        up_full, down_full, q, k, v, xn, mixed, att_r, w_own, wo_b, x)
    grad_qkv = gq.reshape(qc, dim).T.astype(f32)
    grad_out = gout.transpose(0, 2, 1).reshape(dim, oc)
    gs = lax.dynamic_slice(gs, (0, lax.rem(flat * oc, 128)), (n_small, oc))
    shape = tokens.shape
    return (output.reshape(shape), grad_tokens.reshape(shape), grad_qkv, grad_out, gs[0:2], gs[2:4], gs[4:].T, gu[None], gd[None])


def solution(mesh):
    in_specs = (
        P(None, "dp", "expert", None),
        P(None, "dp", "expert", None),
        P(None, "dp", "expert", None),
        P(None, ("dp", "expert")),
        P(None, ("dp", "expert")),
        P(None, ("dp", "expert")),
        P(None, ("dp", "expert")),
        P(("dp", "expert"), None),
        P("expert", "dp", None),
        P("expert", "dp", None),
    )
    out_specs = (
        P(None, "dp", "expert", None),
        P(None, "dp", "expert", None),
        P(None, ("dp", "expert")),
        P(None, ("dp", "expert")),
        P(None, ("dp", "expert")),
        P(None, ("dp", "expert")),
        P(("dp", "expert"), None),
        P("expert", "dp", None),
        P("expert", "dp", None),
    )
    n_expert, n_dp = mesh.shape["expert"], mesh.shape["dp"]
    split_heads = HEADS % n_expert == 0 and (HEADS // n_expert) * 64 % n_dp == 0
    chosen = fast_body if split_heads else body
    return jax.shard_map(chosen, mesh=mesh, in_specs=in_specs, out_specs=out_specs, check_vma=False)
```

```python
import functools
import math

import jax
import jax.numpy as jnp
from jax import lax
from jax.experimental import pallas as pl
from jax.experimental.pallas import tpu as pltpu
from jax.sharding import PartitionSpec as P

HEADS = 12
FF = 3072
BLK = 256
MICRO = 2


epsilon = 1e-05
balance_coef = 8.0
neg_big = -1e30


def layer_norm(features, gain_vec, shift_vec):
    centre = features - jnp.mean(features, axis=-1, keepdims=True)
    spread = jnp.mean(centre * centre, axis=-1, keepdims=True)
    return centre * lax.rsqrt(spread + epsilon) * gain_vec + shift_vec


def gelu_exact(preact):
    return jax.nn.gelu(preact, approximate=False)


def fetch_all(w_qkv, w_out, ln_gains, ln_biases, router, w_up, w_down):
    dense_set = (
        lax.all_gather(w_qkv, ("dp", "expert"), axis=1, tiled=True),
        lax.all_gather(w_out, ("dp", "expert"), axis=1, tiled=True),
        lax.all_gather(ln_gains, ("dp", "expert"), axis=1, tiled=True),
        lax.all_gather(ln_biases, ("dp", "expert"), axis=1, tiled=True),
        lax.all_gather(router, ("dp", "expert"), axis=0, tiled=True),
    )
    expert_set = (
        lax.all_gather(w_up, "dp", axis=1, tiled=True),
        lax.all_gather(w_down, "dp", axis=1, tiled=True),
    )
    return tuple(dense_set) + tuple(expert_set)


def route_slots(expert_of, experts, capacity):
    seq_here, local_len = expert_of.shape
    matches = (expert_of[..., None] == lax.iota(jnp.int32, experts)).astype(jnp.int32)
    order_in = jnp.sum((jnp.cumsum(matches, axis=1) - matches) * matches, axis=-1)
    seq_index = lax.broadcasted_iota(jnp.int32, (seq_here, local_len), 0)
    target = (expert_of * (seq_here * capacity) + seq_index * capacity + order_in).reshape(-1)
    slot_table = jnp.full((experts * seq_here * capacity,), seq_here * local_len, jnp.int32)
    slot_table = slot_table.at[target].set(lax.iota(jnp.int32, seq_here * local_len))
    return (target, slot_table)


def to_slots(features, slot_table):
    flat_rows = features.reshape(-1, features.shape[-1])
    padded = jnp.concatenate(
        [flat_rows, jnp.zeros((1, flat_rows.shape[1]), flat_rows.dtype)], axis=0
    )
    return padded[slot_table]


def score_terms(
    queries, grad_rows, key_block, value_block, log_total, row_delta, allowed, score_scale
):
    scores = (
        jnp.einsum("sqhd,skhd->shqk", queries, key_block, preferred_element_type=jnp.float32)
        * score_scale
    )
    weights = jnp.where(allowed, jnp.exp(scores - log_total[..., None]), 0.0)
    grad_weights = jnp.einsum(
        "sqhd,skhd->shqk", grad_rows, value_block, preferred_element_type=jnp.float32
    )
    grad_scores = (weights * (grad_weights - row_delta[..., None]) * score_scale).astype(
        jnp.bfloat16
    )
    return (weights.astype(jnp.bfloat16), grad_scores)


def attention_forward(queries, key_rows, value_rows, query_pos, score_scale):
    seq_here, local_len, head_count, head_dim = queries.shape
    last_block = query_pos[local_len - 1] // BLK
    start_state = (
        jnp.full((seq_here, head_count, local_len), neg_big, jnp.float32),
        jnp.zeros((seq_here, head_count, local_len), jnp.float32),
        jnp.zeros((seq_here, local_len, head_count, head_dim), jnp.float32),
    )
    key_part = lax.all_gather(key_rows, "expert", axis=1, tiled=True)
    value_part = lax.all_gather(value_rows, "expert", axis=1, tiled=True)
    piece_len = key_part.shape[1]
    block_len = math.gcd(piece_len, 512)

    def attention_one_block(block_index, carried):
        within = block_index * block_len
        key_block = lax.dynamic_slice_in_dim(key_part, within, block_len, 1).reshape(
            seq_here, block_len, head_count, head_dim
        )
        value_block = lax.dynamic_slice_in_dim(value_part, within, block_len, 1).reshape(
            seq_here, block_len, head_count, head_dim
        )
        key_pos = within + lax.iota(jnp.int32, block_len)
        allowed = key_pos[None, :] // BLK <= query_pos[:, None] // BLK

        def attention_compute(current):
            run_max, run_sum, weighted = current
            scores = (
                jnp.einsum(
                    "sqhd,skhd->shqk", queries, key_block, preferred_element_type=jnp.float32
                )
                * score_scale
            )
            new_max = jnp.maximum(run_max, jnp.max(jnp.where(allowed, scores, neg_big), axis=-1))
            weights = jnp.where(allowed, jnp.exp(scores - new_max[..., None]), 0.0)
            factor = jnp.exp(run_max - new_max)
            run_sum = run_sum * factor + jnp.sum(weights, axis=-1)
            addition = jnp.einsum(
                "shqk,skhd->sqhd",
                weights.astype(jnp.bfloat16),
                value_block,
                preferred_element_type=jnp.float32,
            )
            weighted = weighted * jnp.swapaxes(factor, 1, 2)[..., None] + addition
            return (new_max, run_sum, weighted)

        return lax.cond(
            within // BLK <= last_block, attention_compute, lambda current: current, carried
        )

    run_max, run_sum, weighted = lax.fori_loop(
        0, piece_len // block_len, attention_one_block, start_state
    )
    log_total = run_max + jnp.log(run_sum)
    attended = weighted / jnp.swapaxes(run_sum, 1, 2)[..., None]
    return (log_total, attended)


def query_grads(
    queries, grad_rows, key_rows, value_rows, log_total, row_delta, query_pos, score_scale, seq_len
):
    seq_here, local_len, head_count, head_dim = queries.shape
    model_dim = head_count * head_dim
    last_block = query_pos[local_len - 1] // BLK
    start_query = jnp.zeros((seq_here, local_len, head_count, head_dim), jnp.float32)
    start_state = (start_query, jnp.zeros((seq_here, seq_len, 2 * model_dim), jnp.float32))
    key_part = lax.all_gather(key_rows, "expert", axis=1, tiled=True)
    value_part = lax.all_gather(value_rows, "expert", axis=1, tiled=True)
    piece_len = key_part.shape[1]
    block_len = math.gcd(piece_len, 512)

    def query_one_block(block_index, carried):
        within = block_index * block_len
        key_block = lax.dynamic_slice_in_dim(key_part, within, block_len, 1).reshape(
            seq_here, block_len, head_count, head_dim
        )
        value_block = lax.dynamic_slice_in_dim(value_part, within, block_len, 1).reshape(
            seq_here, block_len, head_count, head_dim
        )
        key_pos = within + lax.iota(jnp.int32, block_len)
        allowed = key_pos[None, :] // BLK <= query_pos[:, None] // BLK

        def query_compute(current):
            weights, grad_scores = score_terms(
                queries,
                grad_rows,
                key_block,
                value_block,
                log_total,
                row_delta,
                allowed,
                score_scale,
            )
            grad_query = current[0] + jnp.einsum(
                "shqk,skhd->sqhd", grad_scores, key_block, preferred_element_type=jnp.float32
            )
            grad_key = jnp.einsum(
                "shqk,sqhd->skhd", grad_scores, queries, preferred_element_type=jnp.float32
            ).reshape(seq_here, block_len, model_dim)
            grad_value = jnp.einsum(
                "shqk,sqhd->skhd", weights, grad_rows, preferred_element_type=jnp.float32
            ).reshape(seq_here, block_len, model_dim)
            old_rows = lax.dynamic_slice_in_dim(current[1], within, block_len, 1)
            summed = old_rows + jnp.concatenate([grad_key, grad_value], axis=-1)
            return (grad_query, lax.dynamic_update_slice_in_dim(current[1], summed, within, 1))

        return lax.cond(
            within // BLK <= last_block, query_compute, lambda current: current, carried
        )

    return lax.fori_loop(0, piece_len // block_len, query_one_block, start_state)


def body(tokens, cotangent, expert_ids, w_qkv, w_out, ln_gains, ln_biases, router, w_up, w_down):
    n_expert = lax.axis_size("expert")
    seq_part = lax.axis_index("expert")
    seq_here, local_len, model_dim = (tokens.shape[1], tokens.shape[2], tokens.shape[3])
    head_count = HEADS
    head_dim = model_dim // head_count
    score_scale = head_dim ** (-0.5)
    exp_dev = w_up.shape[0]
    experts = exp_dev * n_expert
    capacity = 2 * local_len // experts
    seq_len = local_len * n_expert
    query_pos = seq_part * local_len + lax.iota(jnp.int32, local_len)
    expert_range = lax.iota(jnp.int32, experts)
    all_ids = expert_ids[..., 0]
    local_counts = jnp.sum((all_ids[..., None] == expert_range).astype(jnp.float32), axis=(0, 1, 2))
    counts = lax.psum(local_counts, ("dp", "expert"))
    mean_load = jnp.sum(counts) / experts
    load_ratio = (counts - mean_load) / mean_load
    grad_qkv_w = jnp.zeros((model_dim, 3 * model_dim), jnp.float32)
    grad_out_w = jnp.zeros((model_dim, model_dim), jnp.float32)
    grad_gains = jnp.zeros((2, model_dim), jnp.float32)
    grad_shifts = jnp.zeros((2, model_dim), jnp.float32)
    grad_router = jnp.zeros((model_dim, experts), jnp.float32)
    grad_up = jnp.zeros((exp_dev, model_dim, FF), jnp.float32)
    grad_down = jnp.zeros((exp_dev, FF, model_dim), jnp.float32)
    outputs = []
    input_grads = []
    for micro_index in range(MICRO):
        fetched = fetch_all(w_qkv, w_out, ln_gains, ln_biases, router, w_up, w_down)
        qkv_full, out_full, gains_full, shifts_full, router_full, up_full, down_full = fetched
        gain_rows = gains_full.astype(jnp.float32)
        shift_rows = shifts_full.astype(jnp.float32)
        inputs = tokens[micro_index].astype(jnp.float32)
        expert_of = all_ids[micro_index]
        normed = layer_norm(inputs, gain_rows[0], shift_rows[0])
        normed_low = normed.astype(jnp.bfloat16)
        projected = jnp.einsum(
            "scd,de->sce", normed_low, qkv_full, preferred_element_type=jnp.float32
        ).astype(jnp.bfloat16)
        query_rows = projected[..., :model_dim]
        queries = query_rows.reshape(seq_here, local_len, head_count, head_dim)
        key_rows = projected[..., model_dim : 2 * model_dim]
        value_rows = projected[..., 2 * model_dim :]
        log_total, attended = attention_forward(
            queries, key_rows, value_rows, query_pos, score_scale
        )
        attended_low = attended.reshape(seq_here, local_len, model_dim).astype(jnp.bfloat16)
        middle = inputs + jnp.einsum(
            "scd,de->sce", attended_low, out_full, preferred_element_type=jnp.float32
        )
        mixed_low = layer_norm(middle, gain_rows[1], shift_rows[1]).astype(jnp.bfloat16)
        onehot = (expert_of[..., None] == expert_range).astype(jnp.float32)
        logits = jnp.einsum(
            "scd,de->sce", mixed_low, router_full, preferred_element_type=jnp.float32
        )
        gates = jax.nn.sigmoid(jnp.sum(logits * onehot, axis=-1))
        target, slot_table = route_slots(expert_of, experts, capacity)
        outgoing = to_slots(mixed_low, slot_table).reshape(
            n_expert, exp_dev, seq_here * capacity, model_dim
        )
        arrived = lax.all_to_all(outgoing, "expert", split_axis=0, concat_axis=0, tiled=True)
        preact = jnp.einsum("pesd,edf->pesf", arrived, up_full, preferred_element_type=jnp.float32)
        hidden = gelu_exact(preact).astype(jnp.bfloat16)
        result = jnp.einsum(
            "pesf,efd->pesd", hidden, down_full, preferred_element_type=jnp.float32
        ).astype(jnp.bfloat16)
        returned = lax.all_to_all(result, "expert", split_axis=0, concat_axis=0, tiled=True)
        expert_out = (
            returned.reshape(-1, model_dim)[target]
            .reshape(seq_here, local_len, model_dim)
            .astype(jnp.float32)
        )
        final = middle + gates[..., None] * expert_out
        outputs.append(final.astype(jnp.bfloat16))
        fetched = fetch_all(w_qkv, w_out, ln_gains, ln_biases, router, w_up, w_down)
        qkv_full, out_full, gains_full, shifts_full, router_full, up_full, down_full = fetched
        gain_rows = gains_full.astype(jnp.float32)
        shift_rows = shifts_full.astype(jnp.float32)
        grad_final = cotangent[micro_index].astype(jnp.float32)
        grad_gate = jnp.sum(grad_final * expert_out, axis=-1) + balance_coef * jnp.sum(
            onehot * load_ratio, axis=-1
        )
        grad_logit = grad_gate * gates * (1.0 - gates)
        grad_expert = (gates[..., None] * grad_final).astype(jnp.bfloat16)
        sent_grads = to_slots(grad_expert, slot_table).reshape(
            n_expert, exp_dev, seq_here * capacity, model_dim
        )
        grads_here = lax.all_to_all(sent_grads, "expert", split_axis=0, concat_axis=0, tiled=True)
        hidden_low = gelu_exact(preact).astype(jnp.bfloat16)
        grad_down = grad_down + jnp.einsum(
            "pesf,pesd->efd", hidden_low, grads_here, preferred_element_type=jnp.float32
        )
        grad_hidden = jnp.einsum(
            "pesd,efd->pesf", grads_here, down_full, preferred_element_type=jnp.float32
        )
        grad_pre = jax.vjp(gelu_exact, preact)[1](grad_hidden)[0].astype(jnp.bfloat16)
        grad_up = grad_up + jnp.einsum(
            "pesd,pesf->edf", arrived, grad_pre, preferred_element_type=jnp.float32
        )
        grad_arrived = jnp.einsum(
            "pesf,edf->pesd", grad_pre, up_full, preferred_element_type=jnp.float32
        ).astype(jnp.bfloat16)
        grads_back = lax.all_to_all(grad_arrived, "expert", split_axis=0, concat_axis=0, tiled=True)
        grad_mixed = (
            grads_back.reshape(-1, model_dim)[target]
            .reshape(seq_here, local_len, model_dim)
            .astype(jnp.float32)
        )
        router_cols = jnp.einsum("sce,de->scd", onehot, router_full.astype(jnp.float32))
        grad_mixed = grad_mixed + grad_logit[..., None] * router_cols
        grad_router = grad_router + jnp.einsum(
            "scd,sce->de", mixed_low.astype(jnp.float32), grad_logit[..., None] * onehot
        )
        second_back = jax.vjp(layer_norm, middle, gain_rows[1], shift_rows[1])[1]
        grad_middle, grad_gain_two, grad_shift_two = second_back(grad_mixed)
        grad_middle = grad_middle + grad_final
        grad_branch = grad_middle.astype(jnp.bfloat16)
        grad_out_w = grad_out_w + jnp.einsum(
            "scd,sce->de", attended_low, grad_branch, preferred_element_type=jnp.float32
        )
        grad_attended = jnp.einsum(
            "sce,de->scd", grad_branch, out_full, preferred_element_type=jnp.float32
        ).astype(jnp.bfloat16)
        grad_heads = grad_attended.reshape(seq_here, local_len, head_count, head_dim)
        row_delta = jnp.swapaxes(jnp.sum(grad_heads.astype(jnp.float32) * attended, axis=-1), 1, 2)
        folded = query_grads(
            queries,
            grad_heads,
            key_rows,
            value_rows,
            log_total,
            row_delta,
            query_pos,
            score_scale,
            seq_len,
        )
        grad_query = folded[0].reshape(seq_here, local_len, model_dim)
        key_value = lax.psum_scatter(
            folded[1].astype(jnp.bfloat16), "expert", scatter_dimension=1, tiled=True
        ).astype(jnp.float32)
        grad_key = key_value[..., :model_dim]
        grad_value = key_value[..., model_dim:]
        grad_projected = jnp.concatenate([grad_query, grad_key, grad_value], axis=-1).astype(
            jnp.bfloat16
        )
        grad_qkv_w = grad_qkv_w + jnp.einsum(
            "scd,sce->de", normed_low, grad_projected, preferred_element_type=jnp.float32
        )
        grad_normed = jnp.einsum(
            "sce,de->scd", grad_projected, qkv_full, preferred_element_type=jnp.float32
        )
        first_back = jax.vjp(layer_norm, inputs, gain_rows[0], shift_rows[0])[1]
        grad_inputs, grad_gain_one, grad_shift_one = first_back(grad_normed)
        grad_gains = grad_gains + jnp.stack([grad_gain_one, grad_gain_two])
        grad_shifts = grad_shifts + jnp.stack([grad_shift_one, grad_shift_two])
        input_grads.append(grad_middle + grad_inputs)
    dense_grads = (
        lax.psum_scatter(grad_qkv_w, ("dp", "expert"), scatter_dimension=1, tiled=True),
        lax.psum_scatter(grad_out_w, ("dp", "expert"), scatter_dimension=1, tiled=True),
        lax.psum_scatter(grad_gains, ("dp", "expert"), scatter_dimension=1, tiled=True),
        lax.psum_scatter(grad_shifts, ("dp", "expert"), scatter_dimension=1, tiled=True),
        lax.psum_scatter(grad_router, ("dp", "expert"), scatter_dimension=0, tiled=True),
    )
    expert_grads = (
        lax.psum_scatter(
            grad_up.astype(jnp.bfloat16), "dp", scatter_dimension=1, tiled=True
        ).astype(jnp.float32),
        lax.psum_scatter(
            grad_down.astype(jnp.bfloat16), "dp", scatter_dimension=1, tiled=True
        ).astype(jnp.float32),
    )
    return (jnp.stack(outputs), jnp.stack(input_grads)) + tuple(dense_grads) + tuple(expert_grads)


MESH_ID = pl.DeviceIdType.MESH
NT = (((1,), (1,)), ((), ()))
NN = (((1,), (0,)), ((), ()))
TN = (((0,), (0,)), ((), ()))
VMEM = pl.BlockSpec(memory_space=pltpu.VMEM)
HBM = pl.BlockSpec(memory_space=pl.ANY)


def mm(a, b, dims=NN):
    return lax.dot_general(a, b, dims, preferred_element_type=jnp.float32)


def normalised(v):
    centre = v - jnp.mean(v, axis=-1, keepdims=True)
    spread = jnp.mean(centre * centre, axis=-1, keepdims=True)
    inv = lax.rsqrt(spread + epsilon)
    return centre * inv, inv


def norm_back(grad_hat, hat, inv):
    return inv * (grad_hat - jnp.mean(grad_hat, axis=1, keepdims=True) - hat * jnp.mean(grad_hat * hat, axis=1, keepdims=True))


def add_into(target, other, step):
    def some(u, carry):
        rows = pl.ds(pl.multiple_of(u * step, step), step)
        target[rows, :] = (target[rows, :].astype(jnp.float32) + other[rows, :].astype(jnp.float32)).astype(target.dtype)
        return carry

    lax.fori_loop(0, target.shape[0] // step, some, 0)


class Place:
    def __init__(self, n_dp, n_ex):
        self.n_dp, self.n_ex, self.n_dev, self.n_z = n_dp, n_ex, n_dp * n_ex, n_dp // 2
        self.dp, self.ex = lax.axis_index("dp"), lax.axis_index("expert")
        self.z, self.core = self.dp // 2, self.dp % 2
        self.flat = self.dp * n_ex + self.ex

    def z_peer(self, d):
        return (self.z + d) % self.n_z

    def ex_peer(self, d):
        return (self.ex + d) % self.n_ex

    def on_z(self, z):
        return (z * 2 + self.core, self.ex)

    def on_ex(self, e):
        return (self.dp, e)

    def partner(self):
        return (self.z * 2 + 1 - self.core, self.ex)

    def numbered(self, t):
        return (t // self.n_ex, t % self.n_ex)


def entry_barrier(at):
    sem = pltpu.get_barrier_semaphore()

    def tell(i, carry):
        pl.semaphore_signal(sem, inc=1, device_id=at.numbered((at.flat + i) % at.n_dev), device_id_type=MESH_ID)
        return carry

    lax.fori_loop(1, at.n_dev, tell, 0)
    pl.semaphore_wait(sem, at.n_dev - 1)


class Wires:
    def __init__(self, send_sems, recv_sems):
        self.send_sems, self.recv_sems, self.used = send_sems, recv_sems, 0

    def take(self, n):
        base = self.used
        self.used = base + n
        return base

    def copy(self, i, src, dst, device):
        return pltpu.make_async_remote_copy(
            src_ref=src, dst_ref=dst, send_sem=self.send_sems.at[i], recv_sem=self.recv_sems.at[i],
            device_id=device, device_id_type=MESH_ID,
        )


def layer_kernel(
    n_dp, n_ex, x_ref, cot_ref, eid_ref, wq_ref, wo_ref, small_ref, up_hbm, down_hbm,
    gq_ref, gout_ref, gsmall_ref, out_hbm, gtok_hbm, gup_hbm, gdown_hbm, up_full, down_full, q_hbm, k_hbm, v_hbm, xn_hbm, mix_hbm, mid_hbm, w_hbm, wo_hbm,
    outbox, inbox, work, gdt, gup, pin_dn, pin_up, zin_dn, zin_up, via_dn, via_up, rowbox, attr, gar,
    gob, gob_pair, gob_line, gob_mine, gob_plane, wt_a, gws, gws_pair, gws_line, gws_sum,
    small_all, small_in, small_out, smalls, tally, gate_s, slot_s, lse, send_sems, recv_sems, load_sems,
):
    bf, f32 = jnp.bfloat16, jnp.float32
    at = Place(n_dp, n_ex)
    wires = Wires(send_sems, recv_sems)
    n_dev, n_z, ex, z, core = at.n_dev, at.n_z, at.ex, at.z, at.core
    seqs, dim = x_ref.shape[0], x_ref.shape[3]
    cap = x_ref.shape[2]
    local_len = 2 * cap
    total_len, width, slots = local_len * n_ex, dim // n_ex, n_ex * cap
    head_dim = dim // HEADS
    heads = width // head_dim
    piece, oc = wq_ref.shape[1], wo_ref.shape[1]
    shard, ff = up_hbm.shape
    half = down_hbm.shape[0]
    tile, mid_dim = ff // n_z, dim // 2
    scale = head_dim ** -0.5
    wt_b, wo_b = gws, gob
    lane = lax.broadcasted_iota(jnp.int32, (1, 128), 1)
    lane_head = lax.broadcasted_iota(jnp.int32, (1, width), 1) // head_dim
    peers = range(1, n_ex)
    lines = range(1, n_z)
    entry_barrier(at)

    i_tok, i_back, i_out, i_ret, i_ga, i_part = (wires.take(seqs * n_ex) for _ in range(6))

    def token_copy(m, d):
        return wires.copy(i_tok + m * n_ex + d, x_ref.at[m], inbox.at[m, ex], at.on_ex(at.ex_peer(d)))

    def back_copy(m, d):
        peer = at.ex_peer(d)
        return wires.copy(i_back + m * n_ex + d, rowbox.at[m, peer], attr.at[m, ex], at.on_ex(peer))

    def out_copy(m, d):
        peer = at.ex_peer(d)
        return wires.copy(i_out + m * n_ex + d, outbox.at[m, peer], work.at[m, ex], at.on_ex(peer))

    def return_copy(m, d):
        peer = at.ex_peer(d)
        return wires.copy(i_ret + m * n_ex + d, outbox.at[m, peer], inbox.at[m, ex], at.on_ex(peer))

    def ga_copy(m, d):
        peer = at.ex_peer(d)
        return wires.copy(i_ga + m * n_ex + d, rowbox.at[m, peer], gar.at[m, ex], at.on_ex(peer))

    def part_copy(m, d):
        peer = at.ex_peer(d)
        return wires.copy(i_part + m * n_ex + d, outbox.at[m, peer], inbox.at[m, ex], at.on_ex(peer))

    reach = [d for d in (2, 1) if d < n_z]

    def order(step):
        return (n_z - 1) * step % n_z

    relay = n_z > 3
    kinds = n_z + 1
    i_ag, i_agp = wires.take(8 * kinds), wires.take(8 * kinds)

    def ag_columns(t):
        return pl.ds(pl.multiple_of(t * tile, tile), tile)

    def ag_block(t, zz, cc, down):
        if down:
            return down_full.at[pl.ds(pl.multiple_of((zz * 2 + cc) * half, half), half), :]
        return up_full.at[t, pl.ds(pl.multiple_of((zz * 2 + cc) * shard, shard), shard), :]

    def ag_own(t, down):
        return down_hbm if down else up_hbm.at[:, ag_columns(t)]

    def ag_code(right, d, t, down):
        return ((0 if right else 4) + d) * kinds + (n_z if down else t)

    def ag_copy(right, d, t, down):
        return wires.copy(i_ag + ag_code(right, d, t, down), ag_own(t, down), ag_block(t, z, core, down), at.on_z(z + d if right else z - d))

    def ag_relay(right, t, down):
        block = ag_block(t, z - 2 if right else z + 2, core, down)
        return wires.copy(i_ag + ag_code(right, 3, t, down), block, block, at.on_z(z + 1 if right else z - 1))

    def ag_pair(right, d, t, down):
        block = ag_block(t, z - d if right else z + d, core, down)
        return wires.copy(i_agp + ag_code(right, d, t, down), ag_own(t, down) if d == 0 else block, block, at.partner())

    def ag_sends(right, d):
        return z + d < n_z if right else z - d >= 0

    def ag_comes(right, d):
        return z - d >= 0 if right else z + d < n_z

    def ag_relays(right):
        return z == n_z - 2 if right else z == 1

    def ag_from(right, d, t, act):
        @pl.when(ag_comes(right, d))
        def _():
            act(False)
            pl.when((z - d if right else z + d) == t)(lambda: act(True))

    def ag_start(t, downs):
        def act(right, d, down):
            return ag_pair(True, 0, t, down).start if d == 0 else ag_copy(right, d, t, down).start

        for d in [*reach, 0]:
            for right in (True, False) if d else (True,):
                @pl.when(ag_sends(right, d))
                def _():
                    for down in downs:
                        if down:
                            pl.when(z == t)(act(right, d, True))
                        else:
                            act(right, d, False)()

    def ag_pass(t):
        for d in reach:
            for right in (True, False):
                def act(down, right=right, d=d):
                    ag_copy(right, d, t, down).wait_recv()
                    if d == 2 and relay:
                        pl.when(ag_relays(right))(ag_relay(right, t, down).start)
                    ag_pair(right, d, t, down).start()

                ag_from(right, d, t, act)

    def ag_far(t):
        if relay:
            for right in (True, False):
                def act(down, right=right):
                    ag_copy(right, 3, t, down).wait_recv()
                    ag_pair(right, 3, t, down).start()

                ag_from(right, 3, t, act)

    far = [0] + sorted(reach) + ([3] if relay else [])

    def ag_ready(t):
        for d in far:
            for right in (True, False) if d else (True,):
                ag_from(right, d, t, lambda down, right=right, d=d: ag_pair(right, d, t, down).wait_recv())

    def ag_finish():
        def one(t, carry):
            for d in far:
                for right in (True, False) if d else (True,):
                    ag_from(right, d, t, lambda down, right=right, d=d: ag_pair(right, d, t, down).wait_send())
            for d in reach:
                for right in (True, False):
                    @pl.when(ag_sends(right, d))
                    def _():
                        ag_copy(right, d, t, False).wait_send()
                        pl.when(z == t)(ag_copy(right, d, t, True).wait_send)
            if relay:
                for right in (True, False):
                    @pl.when(ag_relays(right))
                    def _():
                        ag_relay(right, t, False).wait_send()
                        pl.when((z - 2 if right else z + 2) == t)(ag_relay(right, t, True).wait_send)
            return carry

        lax.fori_loop(0, n_z, one, 0)

    i_gp, i_gl, i_gv = wires.take(2 * n_z), wires.take(8 * kinds), wires.take(kinds)

    def pair_copies(t):
        return (
            wires.copy(i_gp + 2 * t, gdt.at[1 - core, t], pin_dn.at[t], at.partner()),
            wires.copy(i_gp + 2 * t + 1, gup.at[1 - core, t], pin_up.at[t], at.partner()),
        )

    def line_copy(t, src, dest, down):
        right, d = dest > src, abs(dest - src)
        block = gdt.at[core, t] if down else gup.at[core, t, dest]
        kind = n_z if down else t
        if d == 3:
            return wires.copy(i_gv + kind, block, via_dn if down else via_up.at[t], at.on_z(src + 1 if right else src - 1))
        slot = 2 if d == 2 else 0 if right else 1
        return wires.copy(
            i_gl + ((0 if right else 4) + d) * kinds + kind, block, zin_dn.at[slot] if down else zin_up.at[slot, t], at.on_z(dest)
        )

    pairs_far_first = sorted(((s_, d_) for s_ in range(n_z) for d_ in range(n_z) if s_ != d_), key=lambda u: -abs(u[0] - u[1]))

    def held(src, dest):
        return relay and abs(dest - src) == 2 and src in (1, n_z - 2) and dest in (0, n_z - 1)

    def line_each(t, src, dest, act):
        act(False)
        pl.when(t == dest)(lambda: act(True))

    def fold(t):
        for c in pair_copies(t):
            c.wait_recv()
        add_into(gdt.at[core, t], pin_dn.at[t], 96)
        for zz in range(n_z):
            add_into(gup.at[core, t, zz], pin_up.at[t, zz], 48)
        for src, dest in pairs_far_first:
            if not held(src, dest):
                @pl.when(z == src)
                def _():
                    line_each(t, src, dest, lambda down: line_copy(t, src, dest, down).start())

    def add_far(t):
        for src, dest in pairs_far_first:
            if held(src, dest):
                @pl.when(z == src)
                def _():
                    def act(down):
                        line_copy(t, dest - 3 if dest > src else dest + 3, dest, down).wait_recv()
                        if down:
                            add_into(gdt.at[core, t], via_dn, 96)
                        else:
                            add_into(gup.at[core, t, dest], via_up.at[t], 48)
                        line_copy(t, src, dest, down).start()

                    line_each(t, src, dest, act)

    i_small = wires.take(n_dev)

    def small_copy(i):
        return wires.copy(i_small + i, small_ref, small_all.at[at.flat], at.numbered((at.flat + i) % n_dev))

    def each(n, act):
        def step(i, carry):
            act(i)
            return carry

        lax.fori_loop(1, n, step, 0)

    i_piece, i_line, i_pair, i_wo, i_wo2 = wires.take(3), wires.take(n_z), wires.take(2), wires.take(n_z), wires.take(n_ex)

    def forward(q_v, k_v, v_v, xn_v, wide, att_acc, lse_acc, mid_v, mix_v, w_v, wo_v, up_s, down_s):
        stage = (
            pltpu.make_async_copy(up_hbm, up_s, load_sems.at[0]),
            pltpu.make_async_copy(down_hbm, down_s, load_sems.at[1]),
        )
        for c in stage:
            c.start()
        each(n_dev, lambda i: small_copy(i).start())
        me_j = ex * n_dp + at.dp
        pieces = []
        for r in range(3):
            c = 3 * at.flat + r
            sec, j = c // n_dev, c % n_dev
            copy = wires.copy(i_piece + r, wq_ref.at[r], wt_a.at[sec], (j % n_dp, j // n_dp))
            away = j != me_j
            pl.when(away)(copy.start)
            pieces.append((copy, away, sec))
        for m in range(seqs):
            for d in peers:
                token_copy(m, d).start()
        ag_start(order(0), (False,))
        small_all[at.flat] = small_ref[...]
        wo_b[core, z, ex] = wo_ref[...]
        for m in range(seqs):
            inbox[m, ex] = x_ref[m]
        for r, (copy, away, sec) in enumerate(pieces):
            pl.when(away)(copy.wait_recv)

            @pl.when(jnp.logical_not(away))
            def _():
                wt_a[sec] = wq_ref[r]

        w_line = [wires.copy(i_line + d, wt_a, wt_b.at[core, z], at.on_z(at.z_peer(d))) for d in lines]
        for c in w_line:
            c.start()
        wo_line = [wires.copy(i_wo + d, wo_ref, wo_b.at[core, z, ex], at.on_z(at.z_peer(d))) for d in lines]
        for c in wo_line:
            c.start()
        wt_b[core, z] = wt_a[...]
        for c in stage:
            c.wait()
        own = [
            pltpu.make_async_copy(up_s.at[:, t * tile : (t + 1) * tile], ag_block(t, z, core, False), load_sems.at[t % 2])
            for t in range(n_z)
        ] + [pltpu.make_async_copy(down_s, ag_block(0, z, core, True), load_sems.at[3])]
        for c in own[:2]:
            c.start()

        before = jnp.where(
            lax.broadcasted_iota(jnp.int32, (local_len, local_len), 1) < lax.broadcasted_iota(jnp.int32, (local_len, local_len), 0), 1.0, 0.0
        ).astype(bf)
        for m in range(seqs):
            named = jnp.where(lane == eid_ref[m], 1.0, 0.0)
            earlier = jnp.sum(mm(before, named.astype(bf)) * named, axis=1, keepdims=True)
            slot_s[m] = jnp.broadcast_to(eid_ref[m].astype(f32) * cap + earlier, (local_len, 128))

        each(n_dev, lambda i: small_copy(i).wait_recv())
        smalls[...] = jnp.zeros(smalls.shape, f32)
        tally[...] = jnp.zeros(tally.shape, f32)
        for s in range(n_dev):
            block = small_all[s].astype(f32)
            tally[...] += block[8:16, :]
            lo = s * oc // 128 * 128
            spread = pltpu.roll(jnp.concatenate([block, jnp.zeros_like(block)], axis=1), s * oc - lo, 1)
            hi = min(lo + 256, dim)
            smalls[:, lo:hi] += spread[:, 0 : hi - lo]
        gain_one, shift_one = smalls[0:1, :], smalls[2:3, :]
        gain_two, shift_two = smalls[1:2, :], smalls[3:4, :]
        for c in w_line:
            c.wait_recv()
        w_pair = wires.copy(i_pair, wt_b.at[core], wt_b.at[core], at.partner())
        w_pair.start()
        for c in wo_line:
            c.wait_recv()
        ag_start(order(0), (True,))
        for step in range(1, n_z):
            ag_start(order(step), (False, True))
        wo_plane = [wires.copy(i_wo2 + d, wo_b.at[core, :, ex], wo_b.at[core, :, ex], at.on_ex(at.ex_peer(d))) for d in peers]
        for c in wo_plane:
            c.start()
        w_pair.wait_recv()
        for sec in range(3):
            for zz in range(n_z):
                for cc in range(2):
                    row = (zz * 2 + cc) * piece
                    wide[row : row + piece, :] = wt_b[cc, zz, sec].astype(f32)
            w_v[sec] = wide[0:width, :].astype(bf)

        def project(m):
            def one(d, carry):
                src = (ex - d + n_ex) % n_ex
                pl.when(d > 0)(lambda: token_copy(m, d).wait_recv())
                rows = pl.ds(pl.multiple_of(src * local_len, local_len), local_len)
                hat, _ = normalised(inbox[m, src].reshape(local_len, dim).astype(f32))
                low = (hat * gain_one + shift_one).astype(bf)
                xn_v[rows, :] = low
                q_v[m, rows, :] = mm(low, w_v[0], NT).astype(bf)
                k_v[m, rows, :] = mm(low, w_v[1], NT).astype(bf)
                v_v[m, rows, :] = mm(low, w_v[2], NT).astype(bf)
                return carry

            lax.fori_loop(0, n_ex, one, 0)

        def attend(m):
            for i in range(n_ex):
                end = (i + 1) * local_len
                here = slice(i * local_len, end)

                def one_head(h, carry):
                    mine = lane_head == h
                    qb = q_v[m, here, :]
                    s = mm(jnp.where(mine, qb, jnp.zeros_like(qb)), k_v[m, 0:end, :], NT) * scale
                    top = jnp.max(s, axis=-1, keepdims=True)
                    e = jnp.exp(s - top)
                    total = jnp.sum(e, axis=-1, keepdims=True)
                    p = (e / total).astype(bf)
                    att_acc[...] = jnp.where(mine, mm(p, v_v[m, 0:end, :]), att_acc[...])
                    lse_acc[...] = jnp.where(lane == h, top + jnp.log(total), lse_acc[...])
                    return carry

                lax.fori_loop(0, heads, one_head, 0)
                rowbox[m, i] = att_acc[...].astype(bf)
                lse[m, :, here] = lse_acc[...].T[0:8, :]
            for d in peers:
                back_copy(m, d).start()
            attr[m, ex] = rowbox[m, ex]

        def route(m):
            for d in peers:
                back_copy(m, d).wait_recv()
            mid = x_ref[m].reshape(local_len, dim).astype(f32)
            for b in range(n_ex):
                mid += mm(attr[m, b], wo_v[b], NT)
            mid_v[m] = mid
            hat, _ = normalised(mid)
            mixed = (hat * gain_two + shift_two).astype(bf)
            mix_v[m] = mixed
            logits = mm(mixed, smalls[...].astype(bf), NT)
            mine = lax.broadcasted_iota(jnp.int32, logits.shape, 1) == eid_ref[m] + 4
            gate = jax.nn.sigmoid(jnp.sum(jnp.where(mine, logits, 0.0), axis=1, keepdims=True))
            gate_s[m] = jnp.broadcast_to(gate, (local_len, 128))
            scaled = (gate * cot_ref[m].astype(f32)).astype(bf)
            place = jnp.where(
                slot_s[m].T[0:1, :] == lax.broadcasted_iota(jnp.int32, (slots, local_len), 0).astype(f32), 1.0, 0.0
            ).astype(bf)
            outbox[m, :, 0] = mm(place, mixed).astype(bf).reshape(n_ex, cap, dim)
            outbox[m, :, 1] = mm(place, scaled).astype(bf).reshape(n_ex, cap, dim)
            for d in peers:
                out_copy(m, d).start()
            work[m, ex] = outbox[m, ex]

        att_acc[...] = jnp.zeros(att_acc.shape, f32)
        lse_acc[...] = jnp.zeros(lse_acc.shape, f32)

        def xn_out(m):
            return pltpu.make_async_copy(xn_v, xn_hbm.at[m], load_sems.at[2])

        for m in range(seqs):
            project(m)
            xn_out(m).start()
            attend(m)
            if m == 0:
                for i, c in enumerate(own):
                    if i >= 2:
                        if i < n_z:
                            own[i - 2].wait()
                        c.start()
                for c in own[n_z - 2 :]:
                    c.wait()
            if m < seqs - 1:
                xn_out(m).wait()
        ag_pass(order(0))
        for c in wo_plane:
            c.wait_recv()
        wo_pair = wires.copy(i_pair + 1, wo_b.at[core], wo_b.at[core], at.partner())
        wo_pair.start()
        wo_pair.wait_recv()
        for b in range(n_ex):
            for s in range(n_dev):
                wide[s * oc : (s + 1) * oc, 0:width] = wo_b[s // n_ex % 2, s // n_ex // 2, s % n_ex, b].astype(f32)
            wo_v[b] = wide[0:dim, 0:width].astype(bf)
        for m in range(seqs):
            route(m)
        ag_pass(order(1))
        xn_out(seqs - 1).wait()
        keep = [
            pltpu.make_async_copy(src, dst, load_sems.at[i])
            for i, (src, dst) in enumerate(((q_v, q_hbm), (k_v, k_hbm), (v_v, v_hbm), (mid_v, mid_hbm), (mix_v, mix_hbm), (w_v, w_hbm), (wo_v, wo_hbm)))
        ]
        for c in keep:
            c.start()
        for m in range(seqs):
            for d in peers:
                back_copy(m, d).wait_send()
                token_copy(m, d).wait_send()
        for copy, away, _ in pieces:
            pl.when(away)(copy.wait_send)
        each(n_dev, lambda i: small_copy(i).wait_send())
        for c in [*w_line, w_pair, *wo_line, *wo_plane, wo_pair]:
            c.wait_send()
        for c in keep:
            c.wait()

    pl.run_scoped(
        forward,
        pltpu.VMEM((seqs, total_len, width), bf), pltpu.VMEM((seqs, total_len, width), bf), pltpu.VMEM((seqs, total_len, width), bf),
        pltpu.VMEM((total_len, dim), bf), pltpu.VMEM((dim, dim), f32),
        pltpu.VMEM((local_len, width), f32), pltpu.VMEM((local_len, 128), f32),
        pltpu.VMEM((seqs, local_len, dim), f32), pltpu.VMEM((seqs, local_len, dim), bf),
        pltpu.VMEM((3, width, dim), bf), pltpu.VMEM((n_ex, dim, width), bf),
        pltpu.VMEM((shard, ff), bf), pltpu.VMEM((half, dim), bf),
    )

    def experts(up_t, down_t, res_acc, gar_acc, hid, gpre, x_t, g_t):
        sub = 256 if tile % 256 == 0 else tile

        def one_tile(step, carry):
            t = order(step)
            ag_far(t)
            ag_ready(t)
            loads = (
                pltpu.make_async_copy(up_full.at[t], up_t, load_sems.at[0]),
                pltpu.make_async_copy(down_full.at[ag_columns(t), :], down_t, load_sems.at[1]),
            )
            for c in loads:
                c.start()
            for c in loads:
                c.wait()

            def one_seq(m, m_carry):
                mine = pl.ds(pl.multiple_of(m * slots, slots), slots)

                @pl.when(step == 0)
                def _():
                    for d in peers:
                        out_copy(m, d).wait()
                    res_acc[m] = jnp.zeros((slots, dim), f32)
                    gar_acc[m] = jnp.zeros((slots, dim), f32)

                def one_sub(u, c_):
                    cols = pl.ds(pl.multiple_of(u * sub, sub), sub)
                    rows = work[m, :, 0].reshape(slots, dim)
                    grads = work[m, :, 1].reshape(slots, dim)
                    pre = mm(rows, up_t[:, cols])
                    cdf = 0.5 * (1.0 + lax.erf(pre * (2.0 ** -0.5)))
                    hidden = (pre * cdf).astype(bf)
                    slope = cdf + pre * jnp.exp(-0.5 * pre * pre) * ((2.0 * math.pi) ** -0.5)
                    hid[mine, cols] = hidden
                    res_acc[m] += mm(hidden, down_t[cols, :])
                    low = (mm(grads, down_t[cols, :], NT) * slope).astype(bf)
                    gpre[mine, cols] = low
                    gar_acc[m] += mm(low, up_t[:, cols], NT)
                    return c_

                lax.fori_loop(0, tile // sub, one_sub, 0)

                @pl.when(step == n_z - 1)
                def _():
                    outbox[m, :, 0] = res_acc[m].astype(bf).reshape(n_ex, cap, dim)
                    outbox[m, :, 1] = gar_acc[m].astype(bf).reshape(n_ex, cap, dim)
                    for d in peers:
                        return_copy(m, d).start()
                    inbox[m, ex] = outbox[m, ex]

                @pl.when((m == 0) & (step + 2 < n_z))
                def _():
                    ag_pass(order(step + 2))

                return m_carry

            lax.fori_loop(0, seqs, one_seq, 0)

            @pl.when(step == 0)
            def _():
                for s in range(seqs):
                    lanes = slice(s * slots, (s + 1) * slots)
                    x_t[:, lanes] = work[s, :, 0].reshape(slots, dim).T
                    g_t[:, lanes] = work[s, :, 1].reshape(slots, dim).T

            def some(u, c_):
                at_rows = pl.ds(pl.multiple_of(u * mid_dim, mid_dim), mid_dim)
                up_grad = mm(x_t[at_rows, :], gpre[...]).astype(bf)
                for s in range(n_z):
                    gup[s % 2, t, u * (n_z // 2) + s // 2] = up_grad[s * shard : (s + 1) * shard, :]
                down_grad = mm(g_t[at_rows, :], hid[...]).astype(bf)
                for c in range(2):
                    gdt[c, t, at_rows, :] = down_grad[:, c * half : (c + 1) * half]
                return c_

            lax.fori_loop(0, 2, some, 0)
            for c in pair_copies(t):
                c.start()
            pl.when(step > 0)(lambda: fold(order(step - 1)))
            pl.when(step > 1)(lambda: add_far(order(step - 2)))
            return carry

        lax.fori_loop(0, n_z, one_tile, 0)

    every = seqs * slots
    pl.run_scoped(
        experts,
        pltpu.VMEM((dim, tile), bf), pltpu.VMEM((tile, dim), bf),
        pltpu.VMEM((seqs, slots, dim), f32), pltpu.VMEM((seqs, slots, dim), f32),
        pltpu.VMEM((every, tile), bf), pltpu.VMEM((every, tile), bf),
        pltpu.VMEM((dim, every), bf), pltpu.VMEM((dim, every), bf),
    )
    fold(order(n_z - 1))
    ag_finish()

    gain_one, gain_two = smalls[0:1, :], smalls[1:2, :]
    counts = jnp.where(lane < n_ex, 16.0 * tally[0:1, :] + tally[1:2, :], 0.0)
    mean_load = jnp.sum(counts, axis=1, keepdims=True) / n_ex
    load_ratio = (counts - mean_load) / mean_load
    small_out[...] = jnp.zeros(small_out.shape, f32)
    i_gob, i_gw = wires.take(1 + n_ex + n_z), wires.take(1 + n_z + 3)
    gob_pair_copy = wires.copy(i_gob, gob.at[1 - core], gob_pair, at.partner())

    def gob_line_copy(d):
        peer = at.z_peer(d)
        return wires.copy(i_gob + 1 + d, gob.at[core, peer], gob_line.at[d - 1], at.on_z(peer))

    def gob_plane_copy(d):
        peer = at.ex_peer(d)
        return wires.copy(i_gob + 1 + n_z + d, gob_mine.at[peer], gob_plane.at[d - 1], at.on_ex(peer))

    gws_pair_copy = wires.copy(i_gw, gws.at[1 - core], gws_pair, at.partner())

    def gws_line_copy(d):
        peer = at.z_peer(d)
        return wires.copy(i_gw + 1 + d, gws.at[core, peer], gws_line.at[d - 1], at.on_z(peer))

    me_j = ex * n_dp + at.dp
    finals = []
    for sec in range(3):
        c = sec * n_dev + me_j
        owner, r = c // 3, c % 3
        copy = wires.copy(i_gw + 1 + n_z + r, gws_sum.at[sec], gq_ref.at[r], at.numbered(owner))
        finals.append((copy, owner != at.flat, sec, r))

    def backward(gb_t, q_v, k_v, v_v, xn_v, mix_v, mid_v, w_v, wo_v, dq, dk, dv, gw, gtok, out_v):
        pairs = ((wo_hbm, wo_v), (mix_hbm, mix_v), (mid_hbm, mid_v), (w_hbm, w_v), (q_hbm, q_v), (k_hbm, k_v), (v_hbm, v_v))
        brought = [pltpu.make_async_copy(src, dst, load_sems.at[i]) for i, (src, dst) in enumerate(pairs)]
        for c in brought:
            c.start()
        for c in brought:
            c.wait()

        def head(m):
            for d in peers:
                return_copy(m, d).wait()
            def some_rows(u, carry):
                at_rows = pl.ds(pl.multiple_of(u * 128, 128), 128)
                place = jnp.where(
                    slot_s[m, at_rows, 0:1] == lax.broadcasted_iota(jnp.int32, (128, slots), 1).astype(f32), 1.0, 0.0
                ).astype(bf)
                expert_out = mm(place, inbox[m, :, 0].reshape(slots, dim))
                gate, named = gate_s[m, at_rows, 0:1], eid_ref[m, at_rows, :]
                cot = cot_ref[m, at_rows, :].astype(f32)
                out_v[m, at_rows, :] = (mid_v[m, at_rows, :] + gate * expert_out).astype(bf)
                grad_gate = jnp.sum(cot * expert_out, axis=1, keepdims=True) + balance_coef * jnp.sum(
                    jnp.where(lane == named, load_ratio, 0.0), axis=1, keepdims=True
                )
                grad_logit = grad_gate * gate * (1.0 - gate)
                grad_mixed = mm(place, inbox[m, :, 1].reshape(slots, dim))
                mixed = mix_v[m, at_rows, :].astype(f32)
                for e in range(n_ex):
                    routed = jnp.where(named == e, grad_logit, 0.0)
                    grad_mixed += routed * smalls[4 + e : 5 + e, :]
                    small_out[4 + e : 5 + e, 0:dim] += jnp.sum(routed * mixed, axis=0, keepdims=True)
                hat, inv = normalised(mid_v[m, at_rows, :])
                small_out[1:2, 0:dim] += jnp.sum(grad_mixed * hat, axis=0, keepdims=True)
                small_out[3:4, 0:dim] += jnp.sum(grad_mixed, axis=0, keepdims=True)
                grad_middle = norm_back(grad_mixed * gain_two, hat, inv) + cot
                gtok[m, at_rows, :] = grad_middle
                branch = grad_middle.astype(bf)
                for e in range(n_ex):
                    rowbox[m, e, at_rows, :] = mm(branch, wo_v[e]).astype(bf)
                gb_t[m, :, at_rows] = branch.T
                return carry

            lax.fori_loop(0, local_len // 128, some_rows, 0)
            for d in peers:
                ga_copy(m, d).start()
            gar[m, ex] = rowbox[m, ex]

        head(0)
        add_far(order(n_z - 2))
        for m in range(1, seqs):
            head(m)
        wrote = pltpu.make_async_copy(out_v, out_hbm, load_sems.at[0])
        wrote.start()

        for b in range(n_ex):
            total = mm(gb_t[0], attr[0, b])
            for m in range(1, seqs):
                total += mm(gb_t[m], attr[m, b])
            for s in range(n_dev):
                gob[s // n_ex % 2, s // n_ex // 2, s % n_ex, b] = total[s * oc : (s + 1) * oc].astype(bf)
        gob_pair_copy.start()
        gw[...] = jnp.zeros(gw.shape, f32)

        def attention_back(m):
            xn_copy = pltpu.make_async_copy(xn_hbm.at[m], xn_v, load_sems.at[7])
            xn_copy.start()
            for d in peers:
                ga_copy(m, d).wait()
            dk[...] = jnp.zeros(dk.shape, f32)
            dv[...] = jnp.zeros(dv.shape, f32)
            dq[...] = jnp.zeros(dq.shape, f32)
            for i in reversed(range(n_ex)):
                end = (i + 1) * local_len
                here = slice(i * local_len, end)

                def one_head(h, carry):
                    mine = lane_head == h
                    qb, ga = q_v[m, here, :], gar[m, i]
                    q_h = jnp.where(mine, qb, jnp.zeros_like(qb))
                    ga_h = jnp.where(mine, ga, jnp.zeros_like(ga))
                    kk = k_v[m, 0:end, :]
                    p = jnp.exp(mm(kk, q_h, NT) * scale - lse[m, pl.ds(h, 1), here])
                    dp = mm(v_v[m, 0:end, :], ga_h, NT)
                    delta = jnp.sum(p * dp, axis=0, keepdims=True)
                    ds = (p * (dp - delta) * scale).astype(bf)
                    dv[0:end, :] += mm(p.astype(bf), ga_h)
                    dk[0:end, :] += mm(ds, q_h)
                    dq[here, :] += jnp.where(mine, mm(ds, kk, TN), 0.0)
                    return carry

                lax.fori_loop(0, heads, one_head, 0)
                part = mm(dq[here, :].astype(bf), w_v[0]) + mm(dk[here, :].astype(bf), w_v[1]) + mm(dv[here, :].astype(bf), w_v[2])
                outbox[m, i] = part.astype(bf).reshape(2, cap, dim)
                for d in peers:
                    pl.when(at.ex_peer(d) == i)(part_copy(m, d).start)
            inbox[m, ex] = outbox[m, ex]
            xn_copy.wait()
            for sec, g in enumerate((dq, dk, dv)):
                gw[sec] += mm(g[...].astype(bf), xn_v[...], TN)

        attention_back(0)
        add_far(order(n_z - 1))
        gob_pair_copy.wait()
        gob[core] = (gob[core].astype(f32) + gob_pair[...].astype(f32)).astype(bf)
        for d in lines:
            gob_line_copy(d).start()
        for m in range(1, seqs):
            attention_back(m)
        for sec in range(3):
            for j in range(n_dp):
                gws[j % 2, j // 2, sec] = gw[sec, j * piece : (j + 1) * piece, :].astype(bf)
        gws_pair_copy.start()
        for d in lines:
            gob_line_copy(d).wait()
        for e in range(n_ex):
            total = gob[core, z, e].astype(f32)
            for d in lines:
                total += gob_line[d - 1, e].astype(f32)
            gob_mine[e] = total.astype(bf)
        for d in peers:
            gob_plane_copy(d).start()
        gws_pair_copy.wait()
        gws[core] = (gws[core].astype(f32) + gws_pair[...].astype(f32)).astype(bf)
        for d in lines:
            gws_line_copy(d).start()

        def tail(m):
            for d in peers:
                part_copy(m, d).wait()
            grad_normed = jnp.zeros((local_len, dim), f32)
            for e in range(n_ex):
                grad_normed += inbox[m, e].reshape(local_len, dim).astype(f32)
            hat, inv = normalised(x_ref[m].reshape(local_len, dim).astype(f32))
            small_out[0:1, 0:dim] += jnp.sum(grad_normed * hat, axis=0, keepdims=True)
            small_out[2:3, 0:dim] += jnp.sum(grad_normed, axis=0, keepdims=True)
            gtok[m] += norm_back(grad_normed * gain_one, hat, inv)

        for m in range(seqs - 1):
            tail(m)
        for d in lines:
            gws_line_copy(d).wait()
        total = gws[core, z].astype(f32)
        for d in lines:
            total += gws_line[d - 1].astype(f32)
        gws_sum[...] = total.astype(bf)
        for copy, away, sec, r in finals:
            pl.when(away)(copy.start)
        tail(seqs - 1)
        wrote.wait()
        wrote_tok = pltpu.make_async_copy(gtok, gtok_hbm, load_sems.at[0])
        wrote_tok.start()
        wrote_tok.wait()

    pl.run_scoped(
        backward,
        pltpu.VMEM((seqs, dim, local_len), bf),
        pltpu.VMEM((seqs, total_len, width), bf), pltpu.VMEM((seqs, total_len, width), bf), pltpu.VMEM((seqs, total_len, width), bf),
        pltpu.VMEM((total_len, dim), bf), pltpu.VMEM((seqs, local_len, dim), bf), pltpu.VMEM((seqs, local_len, dim), f32),
        pltpu.VMEM((3, width, dim), bf), pltpu.VMEM((n_ex, dim, width), bf),
        pltpu.VMEM((total_len, width), f32), pltpu.VMEM((total_len, width), f32), pltpu.VMEM((total_len, width), f32),
        pltpu.VMEM((3, width, dim), f32),
        pltpu.VMEM((seqs, local_len, dim), f32), pltpu.VMEM((seqs, local_len, dim), bf),
    )

    i_last = wires.take(n_dev)

    def window(t):
        return pl.ds(pl.multiple_of(t * oc // 128 * 128, 128), 256)

    def last_copy(i):
        t = (at.flat + i) % n_dev
        return wires.copy(i_last + i, small_out.at[:, window(t)], small_in.at[at.flat], at.numbered(t))

    each(n_dev, lambda i: last_copy(i).start())
    small_in[at.flat] = small_out[:, window(at.flat)]
    for d in peers:
        gob_plane_copy(d).wait()
    total = gob_mine[ex].astype(f32)
    for d in peers:
        total += gob_plane[d - 1].astype(f32)
    gout_ref[...] = total

    def settle(up_v, down_v):
        def done(t, carry):
            for c in pair_copies(t):
                c.wait_send()
            for src, dest in pairs_far_first:
                pl.when(z == src)(lambda: line_each(t, src, dest, lambda down: line_copy(t, src, dest, down).wait_send()))
                if abs(dest - src) < 3:
                    pl.when(z == dest)(lambda: line_each(t, src, dest, lambda down: line_copy(t, src, dest, down).wait_recv()))
            return carry

        lax.fori_loop(0, n_z, done, 0)
        for dest in range(n_z):
            came = [s for s in range(n_z) if s != dest and abs(s - dest) < 3]
            places = [2 if abs(s - dest) == 2 else 0 if dest > s else 1 for s in came]

            @pl.when(z == dest)
            def _():
                def some_up(t, carry):
                    total = gup[core, t, dest].astype(f32)
                    for s in places:
                        total += zin_up[s, t].astype(f32)
                    up_v[:, ag_columns(t)] = total
                    return carry

                def some_down(u, carry):
                    at_rows = pl.ds(pl.multiple_of(u * 128, 128), 128)
                    total = gdt[core, dest, at_rows, :].astype(f32)
                    for s in places:
                        total += zin_dn[s, at_rows, :].astype(f32)
                    down_v[:, at_rows] = total.T
                    return carry

                lax.fori_loop(0, n_z, some_up, 0)
                lax.fori_loop(0, dim // 128, some_down, 0)

        wrote = (pltpu.make_async_copy(up_v, gup_hbm, load_sems.at[0]), pltpu.make_async_copy(down_v, gdown_hbm, load_sems.at[1]))
        for c in wrote:
            c.start()
        for c in wrote:
            c.wait()

    pl.run_scoped(settle, pltpu.VMEM((shard, ff), f32), pltpu.VMEM((half, dim), f32))
    for copy, away, sec, r in finals:
        @pl.when(away)
        def _():
            copy.wait()

        @pl.when(jnp.logical_not(away))
        def _():
            gq_ref[r] = gws_sum[sec]

    each(n_dev, lambda i: last_copy(i).wait())
    total = jnp.zeros((8, 256), f32)
    for s in range(n_dev):
        total += small_in[s]
    gsmall_ref[...] = total


def whole_layer(n_dp, n_ex, x, cot, eid, wq, wo, small, w_up, w_down):
    bf, f32, i32 = jnp.bfloat16, jnp.float32, jnp.int32
    seqs, local_len, dim = cot.shape
    width, total_len, n_z, n_dev = dim // n_ex, local_len * n_ex, n_dp // 2, n_dp * n_ex
    cap = x.shape[2]
    shard, ff = w_up.shape
    half = w_down.shape[0]
    piece, oc, tile = wq.shape[1], wo.shape[1], ff // n_z
    vmem_outs = [((3, piece, dim), bf), ((n_ex, oc, width), f32), ((8, 256), f32)]
    hbm_outs = [
        ((seqs, local_len, dim), bf), ((seqs, local_len, dim), f32), ((shard, ff), f32), ((half, dim), f32),
        ((n_z, dim, ff // n_z), bf), ((ff, dim), bf),
        ((seqs, total_len, width), bf), ((seqs, total_len, width), bf), ((seqs, total_len, width), bf), ((seqs, total_len, dim), bf),
        ((seqs, local_len, dim), bf), ((seqs, local_len, dim), f32), ((3, width, dim), bf), ((n_ex, dim, width), bf),
    ]
    box = pltpu.VMEM((seqs, n_ex, 2, cap, dim), bf)
    rows = pltpu.VMEM((seqs, n_ex, local_len, width), bf)
    n_sems = 2 * n_dev + 6 * seqs * n_ex + 25 * (n_z + 1) + 2 * n_z + 3 + 2 + 2 * n_z + n_ex + 1 + n_ex + n_z + 1 + n_z + 3
    sems = pltpu.SemaphoreType.DMA((n_sems,))
    return pl.pallas_call(
        functools.partial(layer_kernel, n_dp, n_ex),
        out_shape=[jax.ShapeDtypeStruct(s, d) for s, d in vmem_outs + hbm_outs],
        in_specs=[VMEM] * 6 + [HBM] * 2,
        out_specs=[VMEM] * len(vmem_outs) + [HBM] * len(hbm_outs),
        scratch_shapes=[
            box, box, box,
            pltpu.VMEM((2, n_z, dim, half), bf), pltpu.VMEM((2, n_z, n_z, shard, tile), bf),
            pltpu.VMEM((n_z, dim, half), bf), pltpu.VMEM((n_z, n_z, shard, tile), bf),
            pltpu.VMEM((3, dim, half), bf), pltpu.VMEM((3, n_z, shard, tile), bf),
            pltpu.VMEM((dim, half), bf), pltpu.VMEM((n_z, shard, tile), bf),
            rows, rows, rows,
            pltpu.VMEM((2, n_z, n_ex, n_ex, oc, width), bf), pltpu.VMEM((n_z, n_ex, n_ex, oc, width), bf),
            pltpu.VMEM((n_z - 1, n_ex, n_ex, oc, width), bf), pltpu.VMEM((n_ex, n_ex, oc, width), bf), pltpu.VMEM((n_ex - 1, n_ex, oc, width), bf),
            pltpu.VMEM((3, piece, dim), bf), pltpu.VMEM((2, n_z, 3, piece, dim), bf), pltpu.VMEM((n_z, 3, piece, dim), bf),
            pltpu.VMEM((n_z - 1, 3, piece, dim), bf), pltpu.VMEM((3, piece, dim), bf),
            pltpu.VMEM((n_dev, 16, 128), bf), pltpu.VMEM((n_dev, 8, 256), f32), pltpu.VMEM((8, dim + 256), f32),
            pltpu.VMEM((16, dim), f32), pltpu.VMEM((8, 128), f32),
            pltpu.VMEM((seqs, local_len, 128), f32), pltpu.VMEM((seqs, local_len, 128), f32), pltpu.VMEM((seqs, 8, total_len), f32),
            sems, sems, pltpu.SemaphoreType.DMA((8,)),
        ],
        compiler_params=pltpu.CompilerParams(collective_id=0, has_side_effects=True, vmem_limit_bytes=67043328),
        name="whole_layer",
    )(x, cot, eid, wq, wo, small, w_up, w_down)


def fast_body(tokens, cotangent, expert_ids, w_qkv, w_out, ln_gains, ln_biases, router, w_up, w_down):
    bf, f32 = jnp.bfloat16, jnp.float32
    n_expert, n_dp = lax.axis_size("expert"), lax.axis_size("dp")
    seqs, local_len, dim = tokens.shape[0] * tokens.shape[1], tokens.shape[2], tokens.shape[3]
    experts, width = n_expert, dim // n_expert
    qc, oc = w_qkv.shape[1], w_out.shape[1]
    flat = lax.axis_index("dp") * n_expert + lax.axis_index("expert")
    ids = expert_ids.reshape(seqs, local_len)
    counts = jnp.sum((ids[..., None] == lax.iota(jnp.int32, experts)).astype(f32), axis=(0, 1))
    high = jnp.floor(counts / 16)
    tally = jnp.stack([high, counts - 16 * high]).astype(bf)
    n_small = 4 + experts
    small = jnp.concatenate([ln_gains, ln_biases, router.T], axis=0)
    small = jnp.pad(small, ((0, 0), (0, 128 - oc)))
    tally = jnp.pad(tally, ((0, 16 - n_small - 2), (0, 128 - experts)))
    wq = w_qkv.T.reshape(3, qc // 3, dim)
    wo = w_out.reshape(n_expert, width, oc).transpose(0, 2, 1)
    got = whole_layer(
        n_dp, n_expert, tokens.reshape(seqs, 2, local_len // 2, dim), cotangent.reshape(seqs, local_len, dim), ids[..., None], wq, wo,
        jnp.concatenate([small, tally], axis=0), w_up[0], w_down[0],
    )
    gq, gout, gs, output, grad_tokens, gu, gd = got[:7]
    grad_qkv = gq.reshape(qc, dim).T.astype(f32)
    grad_out = gout.transpose(0, 2, 1).reshape(dim, oc)
    gs = lax.dynamic_slice(gs, (0, lax.rem(flat * oc, 128)), (n_small, oc))
    shape = tokens.shape
    return (output.reshape(shape), grad_tokens.reshape(shape), grad_qkv, grad_out, gs[0:2], gs[2:4], gs[4:].T, gu[None], gd[None])


def solution(mesh):
    in_specs = (
        P(None, "dp", "expert", None),
        P(None, "dp", "expert", None),
        P(None, "dp", "expert", None),
        P(None, ("dp", "expert")),
        P(None, ("dp", "expert")),
        P(None, ("dp", "expert")),
        P(None, ("dp", "expert")),
        P(("dp", "expert"), None),
        P("expert", "dp", None),
        P("expert", "dp", None),
    )
    out_specs = (
        P(None, "dp", "expert", None),
        P(None, "dp", "expert", None),
        P(None, ("dp", "expert")),
        P(None, ("dp", "expert")),
        P(None, ("dp", "expert")),
        P(None, ("dp", "expert")),
        P(("dp", "expert"), None),
        P("expert", "dp", None),
        P("expert", "dp", None),
    )
    n_expert, n_dp = mesh.shape["expert"], mesh.shape["dp"]
    chosen = fast_body if n_expert == 4 and n_dp % 4 == 0 and n_dp <= 8 else body
    return jax.shard_map(chosen, mesh=mesh, in_specs=in_specs, out_specs=out_specs, check_vma=False)
```

```python
import functools
import math

import jax
import jax.numpy as jnp
from jax import lax
from jax.experimental import pallas as pl
from jax.experimental.pallas import tpu as pltpu
from jax.sharding import PartitionSpec as P

HEADS = 12
FF = 3072
BLK = 256
MICRO = 2


epsilon = 1e-05
balance_coef = 8.0
neg_big = -1e30


def layer_norm(features, gain_vec, shift_vec):
    centre = features - jnp.mean(features, axis=-1, keepdims=True)
    spread = jnp.mean(centre * centre, axis=-1, keepdims=True)
    return centre * lax.rsqrt(spread + epsilon) * gain_vec + shift_vec


def gelu_exact(preact):
    return jax.nn.gelu(preact, approximate=False)


def fetch_all(w_qkv, w_out, ln_gains, ln_biases, router, w_up, w_down):
    dense_set = (
        lax.all_gather(w_qkv, ("dp", "expert"), axis=1, tiled=True),
        lax.all_gather(w_out, ("dp", "expert"), axis=1, tiled=True),
        lax.all_gather(ln_gains, ("dp", "expert"), axis=1, tiled=True),
        lax.all_gather(ln_biases, ("dp", "expert"), axis=1, tiled=True),
        lax.all_gather(router, ("dp", "expert"), axis=0, tiled=True),
    )
    expert_set = (
        lax.all_gather(w_up, "dp", axis=1, tiled=True),
        lax.all_gather(w_down, "dp", axis=1, tiled=True),
    )
    return tuple(dense_set) + tuple(expert_set)


def route_slots(expert_of, experts, capacity):
    seq_here, local_len = expert_of.shape
    matches = (expert_of[..., None] == lax.iota(jnp.int32, experts)).astype(jnp.int32)
    order_in = jnp.sum((jnp.cumsum(matches, axis=1) - matches) * matches, axis=-1)
    seq_index = lax.broadcasted_iota(jnp.int32, (seq_here, local_len), 0)
    target = (expert_of * (seq_here * capacity) + seq_index * capacity + order_in).reshape(-1)
    slot_table = jnp.full((experts * seq_here * capacity,), seq_here * local_len, jnp.int32)
    slot_table = slot_table.at[target].set(lax.iota(jnp.int32, seq_here * local_len))
    return (target, slot_table)


def to_slots(features, slot_table):
    flat_rows = features.reshape(-1, features.shape[-1])
    padded = jnp.concatenate(
        [flat_rows, jnp.zeros((1, flat_rows.shape[1]), flat_rows.dtype)], axis=0
    )
    return padded[slot_table]


def score_terms(
    queries, grad_rows, key_block, value_block, log_total, row_delta, allowed, score_scale
):
    scores = (
        jnp.einsum("sqhd,skhd->shqk", queries, key_block, preferred_element_type=jnp.float32)
        * score_scale
    )
    weights = jnp.where(allowed, jnp.exp(scores - log_total[..., None]), 0.0)
    grad_weights = jnp.einsum(
        "sqhd,skhd->shqk", grad_rows, value_block, preferred_element_type=jnp.float32
    )
    grad_scores = (weights * (grad_weights - row_delta[..., None]) * score_scale).astype(
        jnp.bfloat16
    )
    return (weights.astype(jnp.bfloat16), grad_scores)


def attention_forward(queries, key_rows, value_rows, query_pos, score_scale):
    seq_here, local_len, head_count, head_dim = queries.shape
    last_block = query_pos[local_len - 1] // BLK
    start_state = (
        jnp.full((seq_here, head_count, local_len), neg_big, jnp.float32),
        jnp.zeros((seq_here, head_count, local_len), jnp.float32),
        jnp.zeros((seq_here, local_len, head_count, head_dim), jnp.float32),
    )
    key_part = lax.all_gather(key_rows, "expert", axis=1, tiled=True)
    value_part = lax.all_gather(value_rows, "expert", axis=1, tiled=True)
    piece_len = key_part.shape[1]
    block_len = math.gcd(piece_len, 512)

    def attention_one_block(block_index, carried):
        within = block_index * block_len
        key_block = lax.dynamic_slice_in_dim(key_part, within, block_len, 1).reshape(
            seq_here, block_len, head_count, head_dim
        )
        value_block = lax.dynamic_slice_in_dim(value_part, within, block_len, 1).reshape(
            seq_here, block_len, head_count, head_dim
        )
        key_pos = within + lax.iota(jnp.int32, block_len)
        allowed = key_pos[None, :] // BLK <= query_pos[:, None] // BLK

        def attention_compute(current):
            run_max, run_sum, weighted = current
            scores = (
                jnp.einsum(
                    "sqhd,skhd->shqk", queries, key_block, preferred_element_type=jnp.float32
                )
                * score_scale
            )
            new_max = jnp.maximum(run_max, jnp.max(jnp.where(allowed, scores, neg_big), axis=-1))
            weights = jnp.where(allowed, jnp.exp(scores - new_max[..., None]), 0.0)
            factor = jnp.exp(run_max - new_max)
            run_sum = run_sum * factor + jnp.sum(weights, axis=-1)
            addition = jnp.einsum(
                "shqk,skhd->sqhd",
                weights.astype(jnp.bfloat16),
                value_block,
                preferred_element_type=jnp.float32,
            )
            weighted = weighted * jnp.swapaxes(factor, 1, 2)[..., None] + addition
            return (new_max, run_sum, weighted)

        return lax.cond(
            within // BLK <= last_block, attention_compute, lambda current: current, carried
        )

    run_max, run_sum, weighted = lax.fori_loop(
        0, piece_len // block_len, attention_one_block, start_state
    )
    log_total = run_max + jnp.log(run_sum)
    attended = weighted / jnp.swapaxes(run_sum, 1, 2)[..., None]
    return (log_total, attended)


def query_grads(
    queries, grad_rows, key_rows, value_rows, log_total, row_delta, query_pos, score_scale, seq_len
):
    seq_here, local_len, head_count, head_dim = queries.shape
    model_dim = head_count * head_dim
    last_block = query_pos[local_len - 1] // BLK
    start_query = jnp.zeros((seq_here, local_len, head_count, head_dim), jnp.float32)
    start_state = (start_query, jnp.zeros((seq_here, seq_len, 2 * model_dim), jnp.float32))
    key_part = lax.all_gather(key_rows, "expert", axis=1, tiled=True)
    value_part = lax.all_gather(value_rows, "expert", axis=1, tiled=True)
    piece_len = key_part.shape[1]
    block_len = math.gcd(piece_len, 512)

    def query_one_block(block_index, carried):
        within = block_index * block_len
        key_block = lax.dynamic_slice_in_dim(key_part, within, block_len, 1).reshape(
            seq_here, block_len, head_count, head_dim
        )
        value_block = lax.dynamic_slice_in_dim(value_part, within, block_len, 1).reshape(
            seq_here, block_len, head_count, head_dim
        )
        key_pos = within + lax.iota(jnp.int32, block_len)
        allowed = key_pos[None, :] // BLK <= query_pos[:, None] // BLK

        def query_compute(current):
            weights, grad_scores = score_terms(
                queries,
                grad_rows,
                key_block,
                value_block,
                log_total,
                row_delta,
                allowed,
                score_scale,
            )
            grad_query = current[0] + jnp.einsum(
                "shqk,skhd->sqhd", grad_scores, key_block, preferred_element_type=jnp.float32
            )
            grad_key = jnp.einsum(
                "shqk,sqhd->skhd", grad_scores, queries, preferred_element_type=jnp.float32
            ).reshape(seq_here, block_len, model_dim)
            grad_value = jnp.einsum(
                "shqk,sqhd->skhd", weights, grad_rows, preferred_element_type=jnp.float32
            ).reshape(seq_here, block_len, model_dim)
            old_rows = lax.dynamic_slice_in_dim(current[1], within, block_len, 1)
            summed = old_rows + jnp.concatenate([grad_key, grad_value], axis=-1)
            return (grad_query, lax.dynamic_update_slice_in_dim(current[1], summed, within, 1))

        return lax.cond(
            within // BLK <= last_block, query_compute, lambda current: current, carried
        )

    return lax.fori_loop(0, piece_len // block_len, query_one_block, start_state)


def body(tokens, cotangent, expert_ids, w_qkv, w_out, ln_gains, ln_biases, router, w_up, w_down):
    n_expert = lax.axis_size("expert")
    seq_part = lax.axis_index("expert")
    seq_here, local_len, model_dim = (tokens.shape[1], tokens.shape[2], tokens.shape[3])
    head_count = HEADS
    head_dim = model_dim // head_count
    score_scale = head_dim ** (-0.5)
    exp_dev = w_up.shape[0]
    experts = exp_dev * n_expert
    capacity = 2 * local_len // experts
    seq_len = local_len * n_expert
    query_pos = seq_part * local_len + lax.iota(jnp.int32, local_len)
    expert_range = lax.iota(jnp.int32, experts)
    all_ids = expert_ids[..., 0]
    local_counts = jnp.sum((all_ids[..., None] == expert_range).astype(jnp.float32), axis=(0, 1, 2))
    counts = lax.psum(local_counts, ("dp", "expert"))
    mean_load = jnp.sum(counts) / experts
    load_ratio = (counts - mean_load) / mean_load
    grad_qkv_w = jnp.zeros((model_dim, 3 * model_dim), jnp.float32)
    grad_out_w = jnp.zeros((model_dim, model_dim), jnp.float32)
    grad_gains = jnp.zeros((2, model_dim), jnp.float32)
    grad_shifts = jnp.zeros((2, model_dim), jnp.float32)
    grad_router = jnp.zeros((model_dim, experts), jnp.float32)
    grad_up = jnp.zeros((exp_dev, model_dim, FF), jnp.float32)
    grad_down = jnp.zeros((exp_dev, FF, model_dim), jnp.float32)
    outputs = []
    input_grads = []
    for micro_index in range(MICRO):
        fetched = fetch_all(w_qkv, w_out, ln_gains, ln_biases, router, w_up, w_down)
        qkv_full, out_full, gains_full, shifts_full, router_full, up_full, down_full = fetched
        gain_rows = gains_full.astype(jnp.float32)
        shift_rows = shifts_full.astype(jnp.float32)
        inputs = tokens[micro_index].astype(jnp.float32)
        expert_of = all_ids[micro_index]
        normed = layer_norm(inputs, gain_rows[0], shift_rows[0])
        normed_low = normed.astype(jnp.bfloat16)
        projected = jnp.einsum(
            "scd,de->sce", normed_low, qkv_full, preferred_element_type=jnp.float32
        ).astype(jnp.bfloat16)
        query_rows = projected[..., :model_dim]
        queries = query_rows.reshape(seq_here, local_len, head_count, head_dim)
        key_rows = projected[..., model_dim : 2 * model_dim]
        value_rows = projected[..., 2 * model_dim :]
        log_total, attended = attention_forward(
            queries, key_rows, value_rows, query_pos, score_scale
        )
        attended_low = attended.reshape(seq_here, local_len, model_dim).astype(jnp.bfloat16)
        middle = inputs + jnp.einsum(
            "scd,de->sce", attended_low, out_full, preferred_element_type=jnp.float32
        )
        mixed_low = layer_norm(middle, gain_rows[1], shift_rows[1]).astype(jnp.bfloat16)
        onehot = (expert_of[..., None] == expert_range).astype(jnp.float32)
        logits = jnp.einsum(
            "scd,de->sce", mixed_low, router_full, preferred_element_type=jnp.float32
        )
        gates = jax.nn.sigmoid(jnp.sum(logits * onehot, axis=-1))
        target, slot_table = route_slots(expert_of, experts, capacity)
        outgoing = to_slots(mixed_low, slot_table).reshape(
            n_expert, exp_dev, seq_here * capacity, model_dim
        )
        arrived = lax.all_to_all(outgoing, "expert", split_axis=0, concat_axis=0, tiled=True)
        preact = jnp.einsum("pesd,edf->pesf", arrived, up_full, preferred_element_type=jnp.float32)
        hidden = gelu_exact(preact).astype(jnp.bfloat16)
        result = jnp.einsum(
            "pesf,efd->pesd", hidden, down_full, preferred_element_type=jnp.float32
        ).astype(jnp.bfloat16)
        returned = lax.all_to_all(result, "expert", split_axis=0, concat_axis=0, tiled=True)
        expert_out = (
            returned.reshape(-1, model_dim)[target]
            .reshape(seq_here, local_len, model_dim)
            .astype(jnp.float32)
        )
        final = middle + gates[..., None] * expert_out
        outputs.append(final.astype(jnp.bfloat16))
        fetched = fetch_all(w_qkv, w_out, ln_gains, ln_biases, router, w_up, w_down)
        qkv_full, out_full, gains_full, shifts_full, router_full, up_full, down_full = fetched
        gain_rows = gains_full.astype(jnp.float32)
        shift_rows = shifts_full.astype(jnp.float32)
        grad_final = cotangent[micro_index].astype(jnp.float32)
        grad_gate = jnp.sum(grad_final * expert_out, axis=-1) + balance_coef * jnp.sum(
            onehot * load_ratio, axis=-1
        )
        grad_logit = grad_gate * gates * (1.0 - gates)
        grad_expert = (gates[..., None] * grad_final).astype(jnp.bfloat16)
        sent_grads = to_slots(grad_expert, slot_table).reshape(
            n_expert, exp_dev, seq_here * capacity, model_dim
        )
        grads_here = lax.all_to_all(sent_grads, "expert", split_axis=0, concat_axis=0, tiled=True)
        hidden_low = gelu_exact(preact).astype(jnp.bfloat16)
        grad_down = grad_down + jnp.einsum(
            "pesf,pesd->efd", hidden_low, grads_here, preferred_element_type=jnp.float32
        )
        grad_hidden = jnp.einsum(
            "pesd,efd->pesf", grads_here, down_full, preferred_element_type=jnp.float32
        )
        grad_pre = jax.vjp(gelu_exact, preact)[1](grad_hidden)[0].astype(jnp.bfloat16)
        grad_up = grad_up + jnp.einsum(
            "pesd,pesf->edf", arrived, grad_pre, preferred_element_type=jnp.float32
        )
        grad_arrived = jnp.einsum(
            "pesf,edf->pesd", grad_pre, up_full, preferred_element_type=jnp.float32
        ).astype(jnp.bfloat16)
        grads_back = lax.all_to_all(grad_arrived, "expert", split_axis=0, concat_axis=0, tiled=True)
        grad_mixed = (
            grads_back.reshape(-1, model_dim)[target]
            .reshape(seq_here, local_len, model_dim)
            .astype(jnp.float32)
        )
        router_cols = jnp.einsum("sce,de->scd", onehot, router_full.astype(jnp.float32))
        grad_mixed = grad_mixed + grad_logit[..., None] * router_cols
        grad_router = grad_router + jnp.einsum(
            "scd,sce->de", mixed_low.astype(jnp.float32), grad_logit[..., None] * onehot
        )
        second_back = jax.vjp(layer_norm, middle, gain_rows[1], shift_rows[1])[1]
        grad_middle, grad_gain_two, grad_shift_two = second_back(grad_mixed)
        grad_middle = grad_middle + grad_final
        grad_branch = grad_middle.astype(jnp.bfloat16)
        grad_out_w = grad_out_w + jnp.einsum(
            "scd,sce->de", attended_low, grad_branch, preferred_element_type=jnp.float32
        )
        grad_attended = jnp.einsum(
            "sce,de->scd", grad_branch, out_full, preferred_element_type=jnp.float32
        ).astype(jnp.bfloat16)
        grad_heads = grad_attended.reshape(seq_here, local_len, head_count, head_dim)
        row_delta = jnp.swapaxes(jnp.sum(grad_heads.astype(jnp.float32) * attended, axis=-1), 1, 2)
        folded = query_grads(
            queries,
            grad_heads,
            key_rows,
            value_rows,
            log_total,
            row_delta,
            query_pos,
            score_scale,
            seq_len,
        )
        grad_query = folded[0].reshape(seq_here, local_len, model_dim)
        key_value = lax.psum_scatter(
            folded[1].astype(jnp.bfloat16), "expert", scatter_dimension=1, tiled=True
        ).astype(jnp.float32)
        grad_key = key_value[..., :model_dim]
        grad_value = key_value[..., model_dim:]
        grad_projected = jnp.concatenate([grad_query, grad_key, grad_value], axis=-1).astype(
            jnp.bfloat16
        )
        grad_qkv_w = grad_qkv_w + jnp.einsum(
            "scd,sce->de", normed_low, grad_projected, preferred_element_type=jnp.float32
        )
        grad_normed = jnp.einsum(
            "sce,de->scd", grad_projected, qkv_full, preferred_element_type=jnp.float32
        )
        first_back = jax.vjp(layer_norm, inputs, gain_rows[0], shift_rows[0])[1]
        grad_inputs, grad_gain_one, grad_shift_one = first_back(grad_normed)
        grad_gains = grad_gains + jnp.stack([grad_gain_one, grad_gain_two])
        grad_shifts = grad_shifts + jnp.stack([grad_shift_one, grad_shift_two])
        input_grads.append(grad_middle + grad_inputs)
    dense_grads = (
        lax.psum_scatter(grad_qkv_w, ("dp", "expert"), scatter_dimension=1, tiled=True),
        lax.psum_scatter(grad_out_w, ("dp", "expert"), scatter_dimension=1, tiled=True),
        lax.psum_scatter(grad_gains, ("dp", "expert"), scatter_dimension=1, tiled=True),
        lax.psum_scatter(grad_shifts, ("dp", "expert"), scatter_dimension=1, tiled=True),
        lax.psum_scatter(grad_router, ("dp", "expert"), scatter_dimension=0, tiled=True),
    )
    expert_grads = (
        lax.psum_scatter(
            grad_up.astype(jnp.bfloat16), "dp", scatter_dimension=1, tiled=True
        ).astype(jnp.float32),
        lax.psum_scatter(
            grad_down.astype(jnp.bfloat16), "dp", scatter_dimension=1, tiled=True
        ).astype(jnp.float32),
    )
    return (jnp.stack(outputs), jnp.stack(input_grads)) + tuple(dense_grads) + tuple(expert_grads)


MESH_ID = pl.DeviceIdType.MESH
NT = (((1,), (1,)), ((), ()))
NN = (((1,), (0,)), ((), ()))
TN = (((0,), (0,)), ((), ()))
VMEM = pl.BlockSpec(memory_space=pltpu.VMEM)
HBM = pl.BlockSpec(memory_space=pl.ANY)


def mm(a, b, dims=NN):
    return lax.dot_general(a, b, dims, preferred_element_type=jnp.float32)


def normalised(v):
    centre = v - jnp.mean(v, axis=-1, keepdims=True)
    spread = jnp.mean(centre * centre, axis=-1, keepdims=True)
    inv = lax.rsqrt(spread + epsilon)
    return centre * inv, inv


def norm_back(grad_hat, hat, inv):
    return inv * (grad_hat - jnp.mean(grad_hat, axis=1, keepdims=True) - hat * jnp.mean(grad_hat * hat, axis=1, keepdims=True))


def add_into(target, other, step):
    def some(u, carry):
        rows = pl.ds(pl.multiple_of(u * step, step), step)
        target[rows, :] = (target[rows, :].astype(jnp.float32) + other[rows, :].astype(jnp.float32)).astype(target.dtype)
        return carry

    lax.fori_loop(0, target.shape[0] // step, some, 0)


class Place:
    def __init__(self, n_dp, n_ex):
        self.n_dp, self.n_ex, self.n_dev, self.n_z = n_dp, n_ex, n_dp * n_ex, n_dp // 2
        self.dp, self.ex = lax.axis_index("dp"), lax.axis_index("expert")
        self.z, self.core = self.dp // 2, self.dp % 2
        self.flat = self.dp * n_ex + self.ex

    def z_peer(self, d):
        return (self.z + d) % self.n_z

    def ex_peer(self, d):
        return (self.ex + d) % self.n_ex

    def on_z(self, z):
        return (z * 2 + self.core, self.ex)

    def on_ex(self, e):
        return (self.dp, e)

    def partner(self):
        return (self.z * 2 + 1 - self.core, self.ex)

    def numbered(self, t):
        return (t // self.n_ex, t % self.n_ex)


def entry_barrier(at):
    sem = pltpu.get_barrier_semaphore()

    def tell(i, carry):
        pl.semaphore_signal(sem, inc=1, device_id=at.numbered((at.flat + i) % at.n_dev), device_id_type=MESH_ID)
        return carry

    lax.fori_loop(1, at.n_dev, tell, 0)
    pl.semaphore_wait(sem, at.n_dev - 1)


class Wires:
    def __init__(self, send_sems, recv_sems):
        self.send_sems, self.recv_sems, self.used = send_sems, recv_sems, 0

    def take(self, n):
        base = self.used
        self.used = base + n
        return base

    def copy(self, i, src, dst, device):
        return pltpu.make_async_remote_copy(
            src_ref=src, dst_ref=dst, send_sem=self.send_sems.at[i], recv_sem=self.recv_sems.at[i],
            device_id=device, device_id_type=MESH_ID,
        )


def layer_kernel(
    n_dp, n_ex, x_ref, cot_ref, eid_ref, wq_ref, wo_ref, small_ref, up_hbm, down_hbm,
    gq_ref, gout_ref, gsmall_ref, out_hbm, gtok_hbm, gup_hbm, gdown_hbm, up_full, down_full, q_hbm, k_hbm, v_hbm, xn_hbm, mix_hbm, mid_hbm, w_hbm, wo_hbm,
    outbox, inbox, work, gdt, gup, pin_dn, pin_up, zin_dn, zin_up, via_dn, via_up, rowbox, attr, gar,
    gob, gob_pair, gob_line, gob_mine, gob_plane, wt_a, gws, gws_pair, gws_line, gws_sum,
    small_all, small_in, small_out, smalls, tally, gate_s, slot_s, lse, send_sems, recv_sems, load_sems,
):
    bf, f32 = jnp.bfloat16, jnp.float32
    at = Place(n_dp, n_ex)
    wires = Wires(send_sems, recv_sems)
    n_dev, n_z, ex, z, core = at.n_dev, at.n_z, at.ex, at.z, at.core
    seqs, dim = x_ref.shape[0], x_ref.shape[3]
    cap = x_ref.shape[2]
    local_len = 2 * cap
    total_len, width, slots = local_len * n_ex, dim // n_ex, n_ex * cap
    head_dim = dim // HEADS
    heads = width // head_dim
    piece, oc = wq_ref.shape[1], wo_ref.shape[1]
    shard, ff = up_hbm.shape
    half = down_hbm.shape[0]
    tile, mid_dim = ff // n_z, dim // 2
    scale = head_dim ** -0.5
    wt_b, wo_b = gws, gob
    lane = lax.broadcasted_iota(jnp.int32, (1, 128), 1)
    lane_head = lax.broadcasted_iota(jnp.int32, (1, width), 1) // head_dim
    peers = range(1, n_ex)
    lines = range(1, n_z)
    entry_barrier(at)

    i_tok, i_back, i_out, i_ret, i_ga, i_part = (wires.take(seqs * n_ex) for _ in range(6))

    def token_copy(m, d):
        return wires.copy(i_tok + m * n_ex + d, x_ref.at[m], inbox.at[m, ex], at.on_ex(at.ex_peer(d)))

    def back_copy(m, d):
        peer = at.ex_peer(d)
        return wires.copy(i_back + m * n_ex + d, rowbox.at[m, peer], attr.at[m, ex], at.on_ex(peer))

    def out_copy(m, d):
        peer = at.ex_peer(d)
        return wires.copy(i_out + m * n_ex + d, outbox.at[m, peer], work.at[m, ex], at.on_ex(peer))

    def return_copy(m, d):
        peer = at.ex_peer(d)
        return wires.copy(i_ret + m * n_ex + d, outbox.at[m, peer], inbox.at[m, ex], at.on_ex(peer))

    def ga_copy(m, d):
        peer = at.ex_peer(d)
        return wires.copy(i_ga + m * n_ex + d, rowbox.at[m, peer], gar.at[m, ex], at.on_ex(peer))

    def part_copy(m, d):
        peer = at.ex_peer(d)
        return wires.copy(i_part + m * n_ex + d, outbox.at[m, peer], inbox.at[m, ex], at.on_ex(peer))

    reach = [d for d in (2, 1) if d < n_z]

    def order(step):
        return (n_z - 1) * step % n_z

    relay = n_z > 3
    kinds = n_z + 1
    i_ag, i_agp = wires.take(8 * kinds), wires.take(8 * kinds)

    def ag_columns(t):
        return pl.ds(pl.multiple_of(t * tile, tile), tile)

    def ag_block(t, zz, cc, down):
        if down:
            return down_full.at[pl.ds(pl.multiple_of((zz * 2 + cc) * half, half), half), :]
        return up_full.at[t, pl.ds(pl.multiple_of((zz * 2 + cc) * shard, shard), shard), :]

    def ag_own(t, down):
        return down_hbm if down else up_hbm.at[:, ag_columns(t)]

    def ag_code(right, d, t, down):
        return ((0 if right else 4) + d) * kinds + (n_z if down else t)

    def ag_copy(right, d, t, down):
        return wires.copy(i_ag + ag_code(right, d, t, down), ag_own(t, down), ag_block(t, z, core, down), at.on_z(z + d if right else z - d))

    def ag_relay(right, t, down):
        block = ag_block(t, z - 2 if right else z + 2, core, down)
        return wires.copy(i_ag + ag_code(right, 3, t, down), block, block, at.on_z(z + 1 if right else z - 1))

    def ag_pair(right, d, t, down):
        block = ag_block(t, z - d if right else z + d, core, down)
        return wires.copy(i_agp + ag_code(right, d, t, down), ag_own(t, down) if d == 0 else block, block, at.partner())

    def ag_sends(right, d):
        return z + d < n_z if right else z - d >= 0

    def ag_comes(right, d):
        return z - d >= 0 if right else z + d < n_z

    def ag_relays(right):
        return z == n_z - 2 if right else z == 1

    def ag_from(right, d, t, act):
        @pl.when(ag_comes(right, d))
        def _():
            act(False)
            pl.when((z - d if right else z + d) == t)(lambda: act(True))

    def ag_start(t):
        for d in reach:
            for right in (True, False):
                @pl.when(ag_sends(right, d))
                def _():
                    ag_copy(right, d, t, False).start()
                    pl.when(z == t)(ag_copy(right, d, t, True).start)
        ag_from(True, 0, t, lambda down: ag_pair(True, 0, t, down).start())

    def ag_pass(t):
        for d in reach:
            for right in (True, False):
                def act(down, right=right, d=d):
                    ag_copy(right, d, t, down).wait_recv()
                    if d == 2 and relay:
                        pl.when(ag_relays(right))(ag_relay(right, t, down).start)
                    ag_pair(right, d, t, down).start()

                ag_from(right, d, t, act)

    def ag_far(t):
        if relay:
            for right in (True, False):
                def act(down, right=right):
                    ag_copy(right, 3, t, down).wait_recv()
                    ag_pair(right, 3, t, down).start()

                ag_from(right, 3, t, act)

    far = [0] + sorted(reach) + ([3] if relay else [])

    def ag_ready(t):
        for d in far:
            for right in (True, False) if d else (True,):
                ag_from(right, d, t, lambda down, right=right, d=d: ag_pair(right, d, t, down).wait_recv())

    def ag_finish():
        def one(t, carry):
            for d in far:
                for right in (True, False) if d else (True,):
                    ag_from(right, d, t, lambda down, right=right, d=d: ag_pair(right, d, t, down).wait_send())
            for d in reach:
                for right in (True, False):
                    @pl.when(ag_sends(right, d))
                    def _():
                        ag_copy(right, d, t, False).wait_send()
                        pl.when(z == t)(ag_copy(right, d, t, True).wait_send)
            if relay:
                for right in (True, False):
                    @pl.when(ag_relays(right))
                    def _():
                        ag_relay(right, t, False).wait_send()
                        pl.when((z - 2 if right else z + 2) == t)(ag_relay(right, t, True).wait_send)
            return carry

        lax.fori_loop(0, n_z, one, 0)

    i_gp, i_gl, i_gv = wires.take(2 * n_z), wires.take(8 * kinds), wires.take(kinds)

    def pair_copies(t):
        return (
            wires.copy(i_gp + 2 * t, gdt.at[1 - core, t], pin_dn.at[t], at.partner()),
            wires.copy(i_gp + 2 * t + 1, gup.at[1 - core, t], pin_up.at[t], at.partner()),
        )

    def line_copy(t, src, dest, down):
        right, d = dest > src, abs(dest - src)
        block = gdt.at[core, t] if down else gup.at[core, t, dest]
        kind = n_z if down else t
        if d == 3:
            return wires.copy(i_gv + kind, block, via_dn if down else via_up.at[t], at.on_z(src + 1 if right else src - 1))
        slot = 2 if d == 2 else 0 if right else 1
        return wires.copy(
            i_gl + ((0 if right else 4) + d) * kinds + kind, block, zin_dn.at[slot] if down else zin_up.at[slot, t], at.on_z(dest)
        )

    pairs_far_first = sorted(((s_, d_) for s_ in range(n_z) for d_ in range(n_z) if s_ != d_), key=lambda u: -abs(u[0] - u[1]))

    def held(src, dest):
        return relay and abs(dest - src) == 2 and src in (1, n_z - 2) and dest in (0, n_z - 1)

    def line_each(t, src, dest, act):
        act(False)
        pl.when(t == dest)(lambda: act(True))

    def fold(t):
        for c in pair_copies(t):
            c.wait_recv()
        add_into(gdt.at[core, t], pin_dn.at[t], 96)
        for zz in range(n_z):
            add_into(gup.at[core, t, zz], pin_up.at[t, zz], 48)
        for src, dest in pairs_far_first:
            if not held(src, dest):
                @pl.when(z == src)
                def _():
                    line_each(t, src, dest, lambda down: line_copy(t, src, dest, down).start())

    def add_far(t):
        for src, dest in pairs_far_first:
            if held(src, dest):
                @pl.when(z == src)
                def _():
                    def act(down):
                        line_copy(t, dest - 3 if dest > src else dest + 3, dest, down).wait_recv()
                        if down:
                            add_into(gdt.at[core, t], via_dn, 96)
                        else:
                            add_into(gup.at[core, t, dest], via_up.at[t], 48)
                        line_copy(t, src, dest, down).start()

                    line_each(t, src, dest, act)

    i_small = wires.take(n_dev)

    def small_copy(i):
        return wires.copy(i_small + i, small_ref, small_all.at[at.flat], at.numbered((at.flat + i) % n_dev))

    def each(n, act):
        def step(i, carry):
            act(i)
            return carry

        lax.fori_loop(1, n, step, 0)

    i_piece, i_line, i_pair, i_wo, i_wo2 = wires.take(3), wires.take(n_z), wires.take(2), wires.take(n_z), wires.take(n_ex)

    def forward(q_v, k_v, v_v, xn_v, wide, att_acc, lse_acc, mid_v, mix_v, w_v, wo_v, up_s, down_s):
        stage = (
            pltpu.make_async_copy(up_hbm, up_s, load_sems.at[0]),
            pltpu.make_async_copy(down_hbm, down_s, load_sems.at[1]),
        )
        for c in stage:
            c.start()
        me_j = ex * n_dp + at.dp
        pieces = []
        for r in range(3):
            c = 3 * at.flat + r
            sec, j = c // n_dev, c % n_dev
            copy = wires.copy(i_piece + r, wq_ref.at[r], wt_a.at[sec], (j % n_dp, j // n_dp))
            away = j != me_j
            pl.when(away)(copy.start)
            pieces.append((copy, away, sec))
        each(n_dev, lambda i: small_copy(i).start())
        for m in range(seqs):
            for d in peers:
                token_copy(m, d).start()
        small_all[at.flat] = small_ref[...]
        wo_b[core, ex, z] = wo_ref[...]
        for m in range(seqs):
            inbox[m, ex] = x_ref[m]
        for r, (copy, away, sec) in enumerate(pieces):
            pl.when(away)(copy.wait_recv)

            @pl.when(jnp.logical_not(away))
            def _():
                wt_a[sec] = wq_ref[r]

        w_line = [wires.copy(i_line + d, wt_a, wt_b.at[core, z], at.on_z(at.z_peer(d))) for d in lines]
        for c in w_line:
            c.start()
        wo_line = [wires.copy(i_wo + d, wo_ref, wo_b.at[core, ex, z], at.on_z(at.z_peer(d))) for d in lines]
        for c in wo_line:
            c.start()
        wt_b[core, z] = wt_a[...]
        for c in stage:
            c.wait()
        own = [
            pltpu.make_async_copy(up_s.at[:, t * tile : (t + 1) * tile], ag_block(t, z, core, False), load_sems.at[t % 2])
            for t in range(n_z)
        ] + [pltpu.make_async_copy(down_s, ag_block(0, z, core, True), load_sems.at[3])]
        for c in own[:2]:
            c.start()

        before = jnp.where(
            lax.broadcasted_iota(jnp.int32, (local_len, local_len), 1) < lax.broadcasted_iota(jnp.int32, (local_len, local_len), 0), 1.0, 0.0
        ).astype(bf)
        for m in range(seqs):
            named = jnp.where(lane == eid_ref[m], 1.0, 0.0)
            earlier = jnp.sum(mm(before, named.astype(bf)) * named, axis=1, keepdims=True)
            slot_s[m] = jnp.broadcast_to(eid_ref[m].astype(f32) * cap + earlier, (local_len, 128))

        each(n_dev, lambda i: small_copy(i).wait_recv())
        smalls[...] = jnp.zeros(smalls.shape, f32)
        tally[...] = jnp.zeros(tally.shape, f32)
        for s in range(n_dev):
            block = small_all[s].astype(f32)
            tally[...] += block[8:16, :]
            lo = s * oc // 128 * 128
            spread = pltpu.roll(jnp.concatenate([block, jnp.zeros_like(block)], axis=1), s * oc - lo, 1)
            hi = min(lo + 256, dim)
            smalls[:, lo:hi] += spread[:, 0 : hi - lo]
        gain_one, shift_one = smalls[0:1, :], smalls[2:3, :]
        gain_two, shift_two = smalls[1:2, :], smalls[3:4, :]
        for c in w_line:
            c.wait_recv()
        w_pair = wires.copy(i_pair, wt_b.at[core], wt_b.at[core], at.partner())
        w_pair.start()
        for c in wo_line:
            c.wait_recv()
        for step in range(min(2, n_z)):
            ag_start(order(step))
        wo_plane = [wires.copy(i_wo2 + d, wo_b.at[core, ex], wo_b.at[core, ex], at.on_ex(at.ex_peer(d))) for d in peers]
        for c in wo_plane:
            c.start()
        w_pair.wait_recv()
        for sec in range(3):
            for zz in range(n_z):
                for cc in range(2):
                    row = (zz * 2 + cc) * piece
                    wide[row : row + piece, :] = wt_b[cc, zz, sec].astype(f32)
            w_v[sec] = wide[0:width, :].astype(bf)

        def project(m):
            def one(d, carry):
                src = (ex - d + n_ex) % n_ex
                pl.when(d > 0)(lambda: token_copy(m, d).wait_recv())
                rows = pl.ds(pl.multiple_of(src * local_len, local_len), local_len)
                hat, _ = normalised(inbox[m, src].reshape(local_len, dim).astype(f32))
                low = (hat * gain_one + shift_one).astype(bf)
                xn_v[rows, :] = low
                q_v[m, rows, :] = mm(low, w_v[0], NT).astype(bf)
                k_v[m, rows, :] = mm(low, w_v[1], NT).astype(bf)
                v_v[m, rows, :] = mm(low, w_v[2], NT).astype(bf)
                return carry

            lax.fori_loop(0, n_ex, one, 0)

        def attend(m):
            for i in range(n_ex):
                end = (i + 1) * local_len
                here = slice(i * local_len, end)

                def one_head(h, carry):
                    mine = lane_head == h
                    qb = q_v[m, here, :]
                    s = mm(jnp.where(mine, qb, jnp.zeros_like(qb)), k_v[m, 0:end, :], NT) * scale
                    top = jnp.max(s, axis=-1, keepdims=True)
                    e = jnp.exp(s - top)
                    total = jnp.sum(e, axis=-1, keepdims=True)
                    p = (e / total).astype(bf)
                    att_acc[...] = jnp.where(mine, mm(p, v_v[m, 0:end, :]), att_acc[...])
                    lse_acc[...] = jnp.where(lane == h, top + jnp.log(total), lse_acc[...])
                    return carry

                lax.fori_loop(0, heads, one_head, 0)
                rowbox[m, i] = att_acc[...].astype(bf)
                lse[m, :, here] = lse_acc[...].T[0:8, :]
            for d in peers:
                back_copy(m, d).start()
            attr[m, ex] = rowbox[m, ex]

        def route(m):
            for d in peers:
                back_copy(m, d).wait_recv()
            mid = x_ref[m].reshape(local_len, dim).astype(f32)
            for b in range(n_ex):
                mid += mm(attr[m, b], wo_v[b], NT)
            mid_v[m] = mid
            hat, _ = normalised(mid)
            mixed = (hat * gain_two + shift_two).astype(bf)
            mix_v[m] = mixed
            logits = mm(mixed, smalls[...].astype(bf), NT)
            mine = lax.broadcasted_iota(jnp.int32, logits.shape, 1) == eid_ref[m] + 4
            gate = jax.nn.sigmoid(jnp.sum(jnp.where(mine, logits, 0.0), axis=1, keepdims=True))
            gate_s[m] = jnp.broadcast_to(gate, (local_len, 128))
            scaled = (gate * cot_ref[m].astype(f32)).astype(bf)
            place = jnp.where(
                slot_s[m].T[0:1, :] == lax.broadcasted_iota(jnp.int32, (slots, local_len), 0).astype(f32), 1.0, 0.0
            ).astype(bf)
            outbox[m, :, 0] = mm(place, mixed).astype(bf).reshape(n_ex, cap, dim)
            outbox[m, :, 1] = mm(place, scaled).astype(bf).reshape(n_ex, cap, dim)
            for d in peers:
                out_copy(m, d).start()
            work[m, ex] = outbox[m, ex]

        att_acc[...] = jnp.zeros(att_acc.shape, f32)
        lse_acc[...] = jnp.zeros(lse_acc.shape, f32)

        def xn_out(m):
            return pltpu.make_async_copy(xn_v, xn_hbm.at[m], load_sems.at[2])

        project(0)
        xn_out(0).start()
        attend(0)
        for i, c in enumerate(own):
            if i >= 2:
                if i < n_z:
                    own[i - 2].wait()
                c.start()
        for c in own[n_z - 2 :]:
            c.wait()
        for m in range(1, seqs):
            xn_out(m - 1).wait()
            project(m)
            xn_out(m).start()
            attend(m)
        for c in wo_plane:
            c.wait_recv()
        wo_pair = wires.copy(i_pair + 1, wo_b.at[core], wo_b.at[core], at.partner())
        wo_pair.start()
        ag_pass(order(0))
        for step in range(2, n_z - 1):
            ag_start(order(step))
        wo_pair.wait_recv()
        for b in range(n_ex):
            for s in range(n_dev):
                wide[s * oc : (s + 1) * oc, 0:width] = wo_b[s // n_ex % 2, s % n_ex, s // n_ex // 2, b].astype(f32)
            wo_v[b] = wide[0:dim, 0:width].astype(bf)
        for m in range(seqs):
            route(m)
        ag_pass(order(1))
        if n_z > 2:
            ag_start(order(n_z - 1))
        xn_out(seqs - 1).wait()
        keep = [
            pltpu.make_async_copy(src, dst, load_sems.at[i])
            for i, (src, dst) in enumerate(((q_v, q_hbm), (k_v, k_hbm), (v_v, v_hbm), (mid_v, mid_hbm), (mix_v, mix_hbm), (w_v, w_hbm), (wo_v, wo_hbm)))
        ]
        for c in keep:
            c.start()
        for m in range(seqs):
            for d in peers:
                back_copy(m, d).wait_send()
                token_copy(m, d).wait_send()
        for copy, away, _ in pieces:
            pl.when(away)(copy.wait_send)
        each(n_dev, lambda i: small_copy(i).wait_send())
        for c in [*w_line, w_pair, *wo_line, *wo_plane, wo_pair]:
            c.wait_send()
        for c in keep:
            c.wait()

    pl.run_scoped(
        forward,
        pltpu.VMEM((seqs, total_len, width), bf), pltpu.VMEM((seqs, total_len, width), bf), pltpu.VMEM((seqs, total_len, width), bf),
        pltpu.VMEM((total_len, dim), bf), pltpu.VMEM((dim, dim), f32),
        pltpu.VMEM((local_len, width), f32), pltpu.VMEM((local_len, 128), f32),
        pltpu.VMEM((seqs, local_len, dim), f32), pltpu.VMEM((seqs, local_len, dim), bf),
        pltpu.VMEM((3, width, dim), bf), pltpu.VMEM((n_ex, dim, width), bf),
        pltpu.VMEM((shard, ff), bf), pltpu.VMEM((half, dim), bf),
    )

    def experts(up_t, down_t, res_acc, gar_acc, hid, gpre, x_t, g_t):
        sub = 256 if tile % 256 == 0 else tile
        pair = n_z - 2

        def loads(step, slot):
            return (
                pltpu.make_async_copy(up_full.at[order(step)], up_t.at[slot], load_sems.at[2 * slot]),
                pltpu.make_async_copy(down_full.at[ag_columns(order(step)), :], down_t.at[slot], load_sems.at[2 * slot + 1]),
            )

        def fetch(step, slot):
            ag_far(order(step))
            ag_ready(order(step))
            for c in loads(step, slot):
                c.start()

        fetch(0, 0)

        def one_round(k, carry):
            per = jnp.where(k == pair, 2, 1)

            def one(q, q_carry):
                m, step = q // per, k + q % per
                j = step % 2
                mine = pl.ds(pl.multiple_of(m * slots, slots), slots)

                @pl.when(m == 0)
                def _():
                    for c in loads(step, j):
                        c.wait()

                @pl.when(step == 0)
                def _():
                    for d in peers:
                        out_copy(m, d).wait()
                    res_acc[m] = jnp.zeros((slots, dim), f32)
                    gar_acc[m] = jnp.zeros((slots, dim), f32)

                def one_sub(u, c_):
                    cols = pl.ds(pl.multiple_of(u * sub, sub), sub)
                    rows = work[m, :, 0].reshape(slots, dim)
                    grads = work[m, :, 1].reshape(slots, dim)
                    pre = mm(rows, up_t[j, :, cols])
                    cdf = 0.5 * (1.0 + lax.erf(pre * (2.0 ** -0.5)))
                    hidden = (pre * cdf).astype(bf)
                    slope = cdf + pre * jnp.exp(-0.5 * pre * pre) * ((2.0 * math.pi) ** -0.5)
                    hid[j, mine, cols] = hidden
                    res_acc[m] += mm(hidden, down_t[j, cols, :])
                    low = (mm(grads, down_t[j, cols, :], NT) * slope).astype(bf)
                    gpre[j, mine, cols] = low
                    gar_acc[m] += mm(low, up_t[j, :, cols], NT)
                    return c_

                lax.fori_loop(0, tile // sub, one_sub, 0)

                @pl.when(step == n_z - 1)
                def _():
                    outbox[m, :, 0] = res_acc[m].astype(bf).reshape(n_ex, cap, dim)
                    outbox[m, :, 1] = gar_acc[m].astype(bf).reshape(n_ex, cap, dim)
                    for d in peers:
                        return_copy(m, d).start()
                    inbox[m, ex] = outbox[m, ex]

                for ahead in range(2, n_z):
                    @pl.when((k == ahead - 2) & (q == 0))
                    def _():
                        ag_pass(order(ahead))

                pl.when((k == pair) & (q == 0))(lambda: fetch(n_z - 1, (n_z - 1) % 2))
                for late in range(n_z - 2):
                    pl.when((k == late + 1) & (q == 0))(lambda: fold(order(late)))
                if n_z > 3:
                    pl.when((k == pair) & (q == seqs))(lambda: add_far(order(0)))
                return q_carry

            lax.fori_loop(0, seqs * per, one, 0)

            @pl.when(k == 0)
            def _():
                for s in range(seqs):
                    lanes = slice(s * slots, (s + 1) * slots)
                    x_t[:, lanes] = work[s, :, 0].reshape(slots, dim).T
                    g_t[:, lanes] = work[s, :, 1].reshape(slots, dim).T

            def weight_grads(jj, jj_carry):
                step = k + jj
                j, t = step % 2, order(step)
                pl.when(k < pair)(lambda: fetch(step + 1, 1 - j))

                def some(u, c_):
                    at_rows = pl.ds(pl.multiple_of(u * mid_dim, mid_dim), mid_dim)
                    up_grad = mm(x_t[at_rows, :], gpre[j]).astype(bf)
                    for s in range(n_z):
                        gup[s % 2, t, u * (n_z // 2) + s // 2] = up_grad[s * shard : (s + 1) * shard, :]
                    down_grad = mm(g_t[at_rows, :], hid[j]).astype(bf)
                    for c in range(2):
                        gdt[c, t, at_rows, :] = down_grad[:, c * half : (c + 1) * half]
                    return c_

                lax.fori_loop(0, 2, some, 0)
                for c in pair_copies(t):
                    c.start()
                pl.when(step == n_z - 1)(lambda: fold(order(n_z - 2)))
                return jj_carry

            lax.fori_loop(0, per, weight_grads, 0)
            return carry

        lax.fori_loop(0, pair + 1, one_round, 0)

    every = seqs * slots
    pl.run_scoped(
        experts,
        pltpu.VMEM((2, dim, tile), bf), pltpu.VMEM((2, tile, dim), bf),
        pltpu.VMEM((seqs, slots, dim), f32), pltpu.VMEM((seqs, slots, dim), f32),
        pltpu.VMEM((2, every, tile), bf), pltpu.VMEM((2, every, tile), bf),
        pltpu.VMEM((dim, every), bf), pltpu.VMEM((dim, every), bf),
    )
    fold(order(n_z - 1))
    ag_finish()

    gain_one, gain_two = smalls[0:1, :], smalls[1:2, :]
    counts = jnp.where(lane < n_ex, 16.0 * tally[0:1, :] + tally[1:2, :], 0.0)
    mean_load = jnp.sum(counts, axis=1, keepdims=True) / n_ex
    load_ratio = (counts - mean_load) / mean_load
    small_out[...] = jnp.zeros(small_out.shape, f32)
    i_gob, i_gw = wires.take(1 + n_ex + n_z), wires.take(1 + n_z + 3)
    gob_pair_copy = wires.copy(i_gob, gob.at[1 - core], gob_pair, at.partner())

    def gob_plane_copy(d):
        peer = at.ex_peer(d)
        return wires.copy(i_gob + 1 + d, gob.at[core, peer], gob_plane.at[d - 1], at.on_ex(peer))

    def gob_line_copy(d):
        peer = at.z_peer(d)
        return wires.copy(i_gob + 1 + n_ex + d, gob_mine.at[peer], gob_line.at[d - 1], at.on_z(peer))

    gws_pair_copy = wires.copy(i_gw, gws.at[1 - core], gws_pair, at.partner())

    def gws_line_copy(d):
        peer = at.z_peer(d)
        return wires.copy(i_gw + 1 + d, gws.at[core, peer], gws_line.at[d - 1], at.on_z(peer))

    me_j = ex * n_dp + at.dp
    finals = []
    for sec in range(3):
        c = sec * n_dev + me_j
        owner, r = c // 3, c % 3
        copy = wires.copy(i_gw + 1 + n_z + r, gws_sum.at[sec], gq_ref.at[r], at.numbered(owner))
        finals.append((copy, owner != at.flat, sec, r))

    def backward(gb_t, q_v, k_v, v_v, xn_v, mix_v, mid_v, w_v, wo_v, dq, dk, dv, gw, gtok, out_v):
        pairs = ((wo_hbm, wo_v), (mix_hbm, mix_v), (mid_hbm, mid_v), (w_hbm, w_v), (q_hbm, q_v), (k_hbm, k_v), (v_hbm, v_v))
        brought = [pltpu.make_async_copy(src, dst, load_sems.at[i]) for i, (src, dst) in enumerate(pairs)]
        for c in brought:
            c.start()
        for c in brought:
            c.wait()

        def head(m):
            for d in peers:
                return_copy(m, d).wait()
            def some_rows(u, carry):
                at_rows = pl.ds(pl.multiple_of(u * 128, 128), 128)
                place = jnp.where(
                    slot_s[m, at_rows, 0:1] == lax.broadcasted_iota(jnp.int32, (128, slots), 1).astype(f32), 1.0, 0.0
                ).astype(bf)
                expert_out = mm(place, inbox[m, :, 0].reshape(slots, dim))
                gate, named = gate_s[m, at_rows, 0:1], eid_ref[m, at_rows, :]
                cot = cot_ref[m, at_rows, :].astype(f32)
                out_v[m, at_rows, :] = (mid_v[m, at_rows, :] + gate * expert_out).astype(bf)
                grad_gate = jnp.sum(cot * expert_out, axis=1, keepdims=True) + balance_coef * jnp.sum(
                    jnp.where(lane == named, load_ratio, 0.0), axis=1, keepdims=True
                )
                grad_logit = grad_gate * gate * (1.0 - gate)
                grad_mixed = mm(place, inbox[m, :, 1].reshape(slots, dim))
                mixed = mix_v[m, at_rows, :].astype(f32)
                for e in range(n_ex):
                    routed = jnp.where(named == e, grad_logit, 0.0)
                    grad_mixed += routed * smalls[4 + e : 5 + e, :]
                    small_out[4 + e : 5 + e, 0:dim] += jnp.sum(routed * mixed, axis=0, keepdims=True)
                hat, inv = normalised(mid_v[m, at_rows, :])
                small_out[1:2, 0:dim] += jnp.sum(grad_mixed * hat, axis=0, keepdims=True)
                small_out[3:4, 0:dim] += jnp.sum(grad_mixed, axis=0, keepdims=True)
                grad_middle = norm_back(grad_mixed * gain_two, hat, inv) + cot
                gtok[m, at_rows, :] = grad_middle
                branch = grad_middle.astype(bf)
                for e in range(n_ex):
                    rowbox[m, e, at_rows, :] = mm(branch, wo_v[e]).astype(bf)
                gb_t[m, :, at_rows] = branch.T
                return carry

            lax.fori_loop(0, local_len // 128, some_rows, 0)
            for d in peers:
                ga_copy(m, d).start()
            gar[m, ex] = rowbox[m, ex]

        head(0)
        if n_z > 2:
            add_far(order(n_z - 3))
        for m in range(1, seqs):
            head(m)
        wrote = pltpu.make_async_copy(out_v, out_hbm, load_sems.at[0])
        wrote.start()

        for b in range(n_ex):
            total = mm(gb_t[0], attr[0, b])
            for m in range(1, seqs):
                total += mm(gb_t[m], attr[m, b])
            for s in range(n_dev):
                gob[s // n_ex % 2, s % n_ex, s // n_ex // 2, b] = total[s * oc : (s + 1) * oc].astype(bf)
        gob_pair_copy.start()
        gw[...] = jnp.zeros(gw.shape, f32)

        def gob_up():
            gob_pair_copy.wait()
            for e in range(n_ex):
                for zz in range(n_z):
                    gob[core, e, zz] = (gob[core, e, zz].astype(f32) + gob_pair[e, zz].astype(f32)).astype(bf)
            for d in peers:
                gob_plane_copy(d).start()

        def attention_back(m, first=lambda: None):
            xn_copy = pltpu.make_async_copy(xn_hbm.at[m], xn_v, load_sems.at[7])
            xn_copy.start()
            for d in peers:
                ga_copy(m, d).wait()
            first()
            dk[...] = jnp.zeros(dk.shape, f32)
            dv[...] = jnp.zeros(dv.shape, f32)
            dq[...] = jnp.zeros(dq.shape, f32)
            for i in reversed(range(n_ex)):
                end = (i + 1) * local_len
                here = slice(i * local_len, end)

                def one_head(h, carry):
                    mine = lane_head == h
                    qb, ga = q_v[m, here, :], gar[m, i]
                    q_h = jnp.where(mine, qb, jnp.zeros_like(qb))
                    ga_h = jnp.where(mine, ga, jnp.zeros_like(ga))
                    kk = k_v[m, 0:end, :]
                    p = jnp.exp(mm(kk, q_h, NT) * scale - lse[m, pl.ds(h, 1), here])
                    dp = mm(v_v[m, 0:end, :], ga_h, NT)
                    delta = jnp.sum(p * dp, axis=0, keepdims=True)
                    ds = (p * (dp - delta) * scale).astype(bf)
                    dv[0:end, :] += mm(p.astype(bf), ga_h)
                    dk[0:end, :] += mm(ds, q_h)
                    dq[here, :] += jnp.where(mine, mm(ds, kk, TN), 0.0)
                    return carry

                lax.fori_loop(0, heads, one_head, 0)
                part = mm(dq[here, :].astype(bf), w_v[0]) + mm(dk[here, :].astype(bf), w_v[1]) + mm(dv[here, :].astype(bf), w_v[2])
                outbox[m, i] = part.astype(bf).reshape(2, cap, dim)
                for d in peers:
                    pl.when(at.ex_peer(d) == i)(part_copy(m, d).start)
            inbox[m, ex] = outbox[m, ex]
            xn_copy.wait()
            for sec, g in enumerate((dq, dk, dv)):
                gw[sec] += mm(g[...].astype(bf), xn_v[...], TN)

        attention_back(0, gob_up)
        if n_z > 2:
            add_far(order(n_z - 2))
        for d in peers:
            gob_plane_copy(d).wait()
        for zz in range(n_z):
            total = gob[core, ex, zz].astype(f32)
            for d in peers:
                total += gob_plane[d - 1, zz].astype(f32)
            gob_mine[zz] = total.astype(bf)
        for d in lines:
            gob_line_copy(d).start()
        for m in range(1, seqs):
            attention_back(m)
        add_far(order(n_z - 1))
        for sec in range(3):
            for j in range(n_dp):
                gws[j % 2, j // 2, sec] = gw[sec, j * piece : (j + 1) * piece, :].astype(bf)
        gws_pair_copy.start()
        gws_pair_copy.wait()
        gws[core] = (gws[core].astype(f32) + gws_pair[...].astype(f32)).astype(bf)
        for d in lines:
            gws_line_copy(d).start()

        def tail(m):
            for d in peers:
                part_copy(m, d).wait()
            grad_normed = jnp.zeros((local_len, dim), f32)
            for e in range(n_ex):
                grad_normed += inbox[m, e].reshape(local_len, dim).astype(f32)
            hat, inv = normalised(x_ref[m].reshape(local_len, dim).astype(f32))
            small_out[0:1, 0:dim] += jnp.sum(grad_normed * hat, axis=0, keepdims=True)
            small_out[2:3, 0:dim] += jnp.sum(grad_normed, axis=0, keepdims=True)
            gtok[m] += norm_back(grad_normed * gain_one, hat, inv)

        for m in range(seqs - 1):
            tail(m)
        for d in lines:
            gws_line_copy(d).wait()
        total = gws[core, z].astype(f32)
        for d in lines:
            total += gws_line[d - 1].astype(f32)
        gws_sum[...] = total.astype(bf)
        for copy, away, sec, r in finals:
            pl.when(away)(copy.start)
        tail(seqs - 1)
        wrote.wait()
        wrote_tok = pltpu.make_async_copy(gtok, gtok_hbm, load_sems.at[0])
        wrote_tok.start()
        wrote_tok.wait()

    pl.run_scoped(
        backward,
        pltpu.VMEM((seqs, dim, local_len), bf),
        pltpu.VMEM((seqs, total_len, width), bf), pltpu.VMEM((seqs, total_len, width), bf), pltpu.VMEM((seqs, total_len, width), bf),
        pltpu.VMEM((total_len, dim), bf), pltpu.VMEM((seqs, local_len, dim), bf), pltpu.VMEM((seqs, local_len, dim), f32),
        pltpu.VMEM((3, width, dim), bf), pltpu.VMEM((n_ex, dim, width), bf),
        pltpu.VMEM((total_len, width), f32), pltpu.VMEM((total_len, width), f32), pltpu.VMEM((total_len, width), f32),
        pltpu.VMEM((3, width, dim), f32),
        pltpu.VMEM((seqs, local_len, dim), f32), pltpu.VMEM((seqs, local_len, dim), bf),
    )

    i_last = wires.take(n_dev)

    def window(t):
        return pl.ds(pl.multiple_of(t * oc // 128 * 128, 128), 256)

    def last_copy(i):
        t = (at.flat + i) % n_dev
        return wires.copy(i_last + i, small_out.at[:, window(t)], small_in.at[at.flat], at.numbered(t))

    each(n_dev, lambda i: last_copy(i).start())
    small_in[at.flat] = small_out[:, window(at.flat)]
    for d in lines:
        gob_line_copy(d).wait()
    total = gob_mine[z].astype(f32)
    for d in lines:
        total += gob_line[d - 1].astype(f32)
    gout_ref[...] = total

    def settle(up_v, down_v):
        def done(t, carry):
            for c in pair_copies(t):
                c.wait_send()
            for src, dest in pairs_far_first:
                pl.when(z == src)(lambda: line_each(t, src, dest, lambda down: line_copy(t, src, dest, down).wait_send()))
                if abs(dest - src) < 3:
                    pl.when(z == dest)(lambda: line_each(t, src, dest, lambda down: line_copy(t, src, dest, down).wait_recv()))
            return carry

        lax.fori_loop(0, n_z, done, 0)
        for dest in range(n_z):
            came = [s for s in range(n_z) if s != dest and abs(s - dest) < 3]
            places = [2 if abs(s - dest) == 2 else 0 if dest > s else 1 for s in came]

            @pl.when(z == dest)
            def _():
                def some_up(t, carry):
                    total = gup[core, t, dest].astype(f32)
                    for s in places:
                        total += zin_up[s, t].astype(f32)
                    up_v[:, ag_columns(t)] = total
                    return carry

                def some_down(u, carry):
                    at_rows = pl.ds(pl.multiple_of(u * 128, 128), 128)
                    total = gdt[core, dest, at_rows, :].astype(f32)
                    for s in places:
                        total += zin_dn[s, at_rows, :].astype(f32)
                    down_v[:, at_rows] = total.T
                    return carry

                lax.fori_loop(0, n_z, some_up, 0)
                lax.fori_loop(0, dim // 128, some_down, 0)

        wrote = (pltpu.make_async_copy(up_v, gup_hbm, load_sems.at[0]), pltpu.make_async_copy(down_v, gdown_hbm, load_sems.at[1]))
        for c in wrote:
            c.start()
        for c in wrote:
            c.wait()

    pl.run_scoped(settle, pltpu.VMEM((shard, ff), f32), pltpu.VMEM((half, dim), f32))
    for copy, away, sec, r in finals:
        @pl.when(away)
        def _():
            copy.wait()

        @pl.when(jnp.logical_not(away))
        def _():
            gq_ref[r] = gws_sum[sec]

    each(n_dev, lambda i: last_copy(i).wait())
    total = jnp.zeros((8, 256), f32)
    for s in range(n_dev):
        total += small_in[s]
    gsmall_ref[...] = total


def whole_layer(n_dp, n_ex, x, cot, eid, wq, wo, small, w_up, w_down):
    bf, f32, i32 = jnp.bfloat16, jnp.float32, jnp.int32
    seqs, local_len, dim = cot.shape
    width, total_len, n_z, n_dev = dim // n_ex, local_len * n_ex, n_dp // 2, n_dp * n_ex
    cap = x.shape[2]
    shard, ff = w_up.shape
    half = w_down.shape[0]
    piece, oc, tile = wq.shape[1], wo.shape[1], ff // n_z
    vmem_outs = [((3, piece, dim), bf), ((n_ex, oc, width), f32), ((8, 256), f32)]
    hbm_outs = [
        ((seqs, local_len, dim), bf), ((seqs, local_len, dim), f32), ((shard, ff), f32), ((half, dim), f32),
        ((n_z, dim, ff // n_z), bf), ((ff, dim), bf),
        ((seqs, total_len, width), bf), ((seqs, total_len, width), bf), ((seqs, total_len, width), bf), ((seqs, total_len, dim), bf),
        ((seqs, local_len, dim), bf), ((seqs, local_len, dim), f32), ((3, width, dim), bf), ((n_ex, dim, width), bf),
    ]
    box = pltpu.VMEM((seqs, n_ex, 2, cap, dim), bf)
    rows = pltpu.VMEM((seqs, n_ex, local_len, width), bf)
    n_sems = 2 * n_dev + 6 * seqs * n_ex + 25 * (n_z + 1) + 2 * n_z + 3 + 2 + 2 * n_z + n_ex + 1 + n_ex + n_z + 1 + n_z + 3
    sems = pltpu.SemaphoreType.DMA((n_sems,))
    return pl.pallas_call(
        functools.partial(layer_kernel, n_dp, n_ex),
        out_shape=[jax.ShapeDtypeStruct(s, d) for s, d in vmem_outs + hbm_outs],
        in_specs=[VMEM] * 6 + [HBM] * 2,
        out_specs=[VMEM] * len(vmem_outs) + [HBM] * len(hbm_outs),
        scratch_shapes=[
            box, box, box,
            pltpu.VMEM((2, n_z, dim, half), bf), pltpu.VMEM((2, n_z, n_z, shard, tile), bf),
            pltpu.VMEM((n_z, dim, half), bf), pltpu.VMEM((n_z, n_z, shard, tile), bf),
            pltpu.VMEM((3, dim, half), bf), pltpu.VMEM((3, n_z, shard, tile), bf),
            pltpu.VMEM((dim, half), bf), pltpu.VMEM((n_z, shard, tile), bf),
            rows, rows, rows,
            pltpu.VMEM((2, n_ex, n_z, n_ex, oc, width), bf), pltpu.VMEM((n_ex, n_z, n_ex, oc, width), bf),
            pltpu.VMEM((n_z - 1, n_ex, oc, width), bf), pltpu.VMEM((n_z, n_ex, oc, width), bf), pltpu.VMEM((n_ex - 1, n_z, n_ex, oc, width), bf),
            pltpu.VMEM((3, piece, dim), bf), pltpu.VMEM((2, n_z, 3, piece, dim), bf), pltpu.VMEM((n_z, 3, piece, dim), bf),
            pltpu.VMEM((n_z - 1, 3, piece, dim), bf), pltpu.VMEM((3, piece, dim), bf),
            pltpu.VMEM((n_dev, 16, 128), bf), pltpu.VMEM((n_dev, 8, 256), f32), pltpu.VMEM((8, dim + 256), f32),
            pltpu.VMEM((16, dim), f32), pltpu.VMEM((8, 128), f32),
            pltpu.VMEM((seqs, local_len, 128), f32), pltpu.VMEM((seqs, local_len, 128), f32), pltpu.VMEM((seqs, 8, total_len), f32),
            sems, sems, pltpu.SemaphoreType.DMA((8,)),
        ],
        compiler_params=pltpu.CompilerParams(collective_id=0, has_side_effects=True, vmem_limit_bytes=67043328),
        name="whole_layer",
    )(x, cot, eid, wq, wo, small, w_up, w_down)


def fast_body(tokens, cotangent, expert_ids, w_qkv, w_out, ln_gains, ln_biases, router, w_up, w_down):
    bf, f32 = jnp.bfloat16, jnp.float32
    n_expert, n_dp = lax.axis_size("expert"), lax.axis_size("dp")
    seqs, local_len, dim = tokens.shape[0] * tokens.shape[1], tokens.shape[2], tokens.shape[3]
    experts, width = n_expert, dim // n_expert
    qc, oc = w_qkv.shape[1], w_out.shape[1]
    flat = lax.axis_index("dp") * n_expert + lax.axis_index("expert")
    ids = expert_ids.reshape(seqs, local_len)
    counts = jnp.sum((ids[..., None] == lax.iota(jnp.int32, experts)).astype(f32), axis=(0, 1))
    high = jnp.floor(counts / 16)
    tally = jnp.stack([high, counts - 16 * high]).astype(bf)
    n_small = 4 + experts
    small = jnp.concatenate([ln_gains, ln_biases, router.T], axis=0)
    small = jnp.pad(small, ((0, 0), (0, 128 - oc)))
    tally = jnp.pad(tally, ((0, 16 - n_small - 2), (0, 128 - experts)))
    wq = w_qkv.T.reshape(3, qc // 3, dim)
    wo = w_out.reshape(n_expert, width, oc).transpose(0, 2, 1)
    got = whole_layer(
        n_dp, n_expert, tokens.reshape(seqs, 2, local_len // 2, dim), cotangent.reshape(seqs, local_len, dim), ids[..., None], wq, wo,
        jnp.concatenate([small, tally], axis=0), w_up[0], w_down[0],
    )
    gq, gout, gs, output, grad_tokens, gu, gd = got[:7]
    grad_qkv = gq.reshape(qc, dim).T.astype(f32)
    grad_out = gout.transpose(0, 2, 1).reshape(dim, oc)
    gs = lax.dynamic_slice(gs, (0, lax.rem(flat * oc, 128)), (n_small, oc))
    shape = tokens.shape
    return (output.reshape(shape), grad_tokens.reshape(shape), grad_qkv, grad_out, gs[0:2], gs[2:4], gs[4:].T, gu[None], gd[None])


def solution(mesh):
    in_specs = (
        P(None, "dp", "expert", None),
        P(None, "dp", "expert", None),
        P(None, "dp", "expert", None),
        P(None, ("dp", "expert")),
        P(None, ("dp", "expert")),
        P(None, ("dp", "expert")),
        P(None, ("dp", "expert")),
        P(("dp", "expert"), None),
        P("expert", "dp", None),
        P("expert", "dp", None),
    )
    out_specs = (
        P(None, "dp", "expert", None),
        P(None, "dp", "expert", None),
        P(None, ("dp", "expert")),
        P(None, ("dp", "expert")),
        P(None, ("dp", "expert")),
        P(None, ("dp", "expert")),
        P(("dp", "expert"), None),
        P("expert", "dp", None),
        P("expert", "dp", None),
    )
    n_expert, n_dp = mesh.shape["expert"], mesh.shape["dp"]
    chosen = fast_body if n_expert == 4 and n_dp % 4 == 0 and n_dp <= 8 else body
    return jax.shard_map(chosen, mesh=mesh, in_specs=in_specs, out_specs=out_specs, check_vma=False)
```

```python
import functools
import math

import jax
import jax.numpy as jnp
from jax import lax
from jax.experimental import pallas as pl
from jax.experimental.pallas import tpu as pltpu
from jax.sharding import PartitionSpec as P

HEADS = 12
FF = 3072
BLK = 256
MICRO = 2


epsilon = 1e-05
balance_coef = 8.0
neg_big = -1e30


def layer_norm(features, gain_vec, shift_vec):
    centre = features - jnp.mean(features, axis=-1, keepdims=True)
    spread = jnp.mean(centre * centre, axis=-1, keepdims=True)
    return centre * lax.rsqrt(spread + epsilon) * gain_vec + shift_vec


def gelu_exact(preact):
    return jax.nn.gelu(preact, approximate=False)


def fetch_all(w_qkv, w_out, ln_gains, ln_biases, router, w_up, w_down):
    dense_set = (
        lax.all_gather(w_qkv, ("dp", "expert"), axis=1, tiled=True),
        lax.all_gather(w_out, ("dp", "expert"), axis=1, tiled=True),
        lax.all_gather(ln_gains, ("dp", "expert"), axis=1, tiled=True),
        lax.all_gather(ln_biases, ("dp", "expert"), axis=1, tiled=True),
        lax.all_gather(router, ("dp", "expert"), axis=0, tiled=True),
    )
    expert_set = (
        lax.all_gather(w_up, "dp", axis=1, tiled=True),
        lax.all_gather(w_down, "dp", axis=1, tiled=True),
    )
    return tuple(dense_set) + tuple(expert_set)


def route_slots(expert_of, experts, capacity):
    seq_here, local_len = expert_of.shape
    matches = (expert_of[..., None] == lax.iota(jnp.int32, experts)).astype(jnp.int32)
    order_in = jnp.sum((jnp.cumsum(matches, axis=1) - matches) * matches, axis=-1)
    seq_index = lax.broadcasted_iota(jnp.int32, (seq_here, local_len), 0)
    target = (expert_of * (seq_here * capacity) + seq_index * capacity + order_in).reshape(-1)
    slot_table = jnp.full((experts * seq_here * capacity,), seq_here * local_len, jnp.int32)
    slot_table = slot_table.at[target].set(lax.iota(jnp.int32, seq_here * local_len))
    return (target, slot_table)


def to_slots(features, slot_table):
    flat_rows = features.reshape(-1, features.shape[-1])
    padded = jnp.concatenate(
        [flat_rows, jnp.zeros((1, flat_rows.shape[1]), flat_rows.dtype)], axis=0
    )
    return padded[slot_table]


def score_terms(
    queries, grad_rows, key_block, value_block, log_total, row_delta, allowed, score_scale
):
    scores = (
        jnp.einsum("sqhd,skhd->shqk", queries, key_block, preferred_element_type=jnp.float32)
        * score_scale
    )
    weights = jnp.where(allowed, jnp.exp(scores - log_total[..., None]), 0.0)
    grad_weights = jnp.einsum(
        "sqhd,skhd->shqk", grad_rows, value_block, preferred_element_type=jnp.float32
    )
    grad_scores = (weights * (grad_weights - row_delta[..., None]) * score_scale).astype(
        jnp.bfloat16
    )
    return (weights.astype(jnp.bfloat16), grad_scores)


def attention_forward(queries, key_rows, value_rows, query_pos, score_scale):
    seq_here, local_len, head_count, head_dim = queries.shape
    last_block = query_pos[local_len - 1] // BLK
    start_state = (
        jnp.full((seq_here, head_count, local_len), neg_big, jnp.float32),
        jnp.zeros((seq_here, head_count, local_len), jnp.float32),
        jnp.zeros((seq_here, local_len, head_count, head_dim), jnp.float32),
    )
    key_part = lax.all_gather(key_rows, "expert", axis=1, tiled=True)
    value_part = lax.all_gather(value_rows, "expert", axis=1, tiled=True)
    piece_len = key_part.shape[1]
    block_len = math.gcd(piece_len, 512)

    def attention_one_block(block_index, carried):
        within = block_index * block_len
        key_block = lax.dynamic_slice_in_dim(key_part, within, block_len, 1).reshape(
            seq_here, block_len, head_count, head_dim
        )
        value_block = lax.dynamic_slice_in_dim(value_part, within, block_len, 1).reshape(
            seq_here, block_len, head_count, head_dim
        )
        key_pos = within + lax.iota(jnp.int32, block_len)
        allowed = key_pos[None, :] // BLK <= query_pos[:, None] // BLK

        def attention_compute(current):
            run_max, run_sum, weighted = current
            scores = (
                jnp.einsum(
                    "sqhd,skhd->shqk", queries, key_block, preferred_element_type=jnp.float32
                )
                * score_scale
            )
            new_max = jnp.maximum(run_max, jnp.max(jnp.where(allowed, scores, neg_big), axis=-1))
            weights = jnp.where(allowed, jnp.exp(scores - new_max[..., None]), 0.0)
            factor = jnp.exp(run_max - new_max)
            run_sum = run_sum * factor + jnp.sum(weights, axis=-1)
            addition = jnp.einsum(
                "shqk,skhd->sqhd",
                weights.astype(jnp.bfloat16),
                value_block,
                preferred_element_type=jnp.float32,
            )
            weighted = weighted * jnp.swapaxes(factor, 1, 2)[..., None] + addition
            return (new_max, run_sum, weighted)

        return lax.cond(
            within // BLK <= last_block, attention_compute, lambda current: current, carried
        )

    run_max, run_sum, weighted = lax.fori_loop(
        0, piece_len // block_len, attention_one_block, start_state
    )
    log_total = run_max + jnp.log(run_sum)
    attended = weighted / jnp.swapaxes(run_sum, 1, 2)[..., None]
    return (log_total, attended)


def query_grads(
    queries, grad_rows, key_rows, value_rows, log_total, row_delta, query_pos, score_scale, seq_len
):
    seq_here, local_len, head_count, head_dim = queries.shape
    model_dim = head_count * head_dim
    last_block = query_pos[local_len - 1] // BLK
    start_query = jnp.zeros((seq_here, local_len, head_count, head_dim), jnp.float32)
    start_state = (start_query, jnp.zeros((seq_here, seq_len, 2 * model_dim), jnp.float32))
    key_part = lax.all_gather(key_rows, "expert", axis=1, tiled=True)
    value_part = lax.all_gather(value_rows, "expert", axis=1, tiled=True)
    piece_len = key_part.shape[1]
    block_len = math.gcd(piece_len, 512)

    def query_one_block(block_index, carried):
        within = block_index * block_len
        key_block = lax.dynamic_slice_in_dim(key_part, within, block_len, 1).reshape(
            seq_here, block_len, head_count, head_dim
        )
        value_block = lax.dynamic_slice_in_dim(value_part, within, block_len, 1).reshape(
            seq_here, block_len, head_count, head_dim
        )
        key_pos = within + lax.iota(jnp.int32, block_len)
        allowed = key_pos[None, :] // BLK <= query_pos[:, None] // BLK

        def query_compute(current):
            weights, grad_scores = score_terms(
                queries,
                grad_rows,
                key_block,
                value_block,
                log_total,
                row_delta,
                allowed,
                score_scale,
            )
            grad_query = current[0] + jnp.einsum(
                "shqk,skhd->sqhd", grad_scores, key_block, preferred_element_type=jnp.float32
            )
            grad_key = jnp.einsum(
                "shqk,sqhd->skhd", grad_scores, queries, preferred_element_type=jnp.float32
            ).reshape(seq_here, block_len, model_dim)
            grad_value = jnp.einsum(
                "shqk,sqhd->skhd", weights, grad_rows, preferred_element_type=jnp.float32
            ).reshape(seq_here, block_len, model_dim)
            old_rows = lax.dynamic_slice_in_dim(current[1], within, block_len, 1)
            summed = old_rows + jnp.concatenate([grad_key, grad_value], axis=-1)
            return (grad_query, lax.dynamic_update_slice_in_dim(current[1], summed, within, 1))

        return lax.cond(
            within // BLK <= last_block, query_compute, lambda current: current, carried
        )

    return lax.fori_loop(0, piece_len // block_len, query_one_block, start_state)


def body(tokens, cotangent, expert_ids, w_qkv, w_out, ln_gains, ln_biases, router, w_up, w_down):
    n_expert = lax.axis_size("expert")
    seq_part = lax.axis_index("expert")
    seq_here, local_len, model_dim = (tokens.shape[1], tokens.shape[2], tokens.shape[3])
    head_count = HEADS
    head_dim = model_dim // head_count
    score_scale = head_dim ** (-0.5)
    exp_dev = w_up.shape[0]
    experts = exp_dev * n_expert
    capacity = 2 * local_len // experts
    seq_len = local_len * n_expert
    query_pos = seq_part * local_len + lax.iota(jnp.int32, local_len)
    expert_range = lax.iota(jnp.int32, experts)
    all_ids = expert_ids[..., 0]
    local_counts = jnp.sum((all_ids[..., None] == expert_range).astype(jnp.float32), axis=(0, 1, 2))
    counts = lax.psum(local_counts, ("dp", "expert"))
    mean_load = jnp.sum(counts) / experts
    load_ratio = (counts - mean_load) / mean_load
    grad_qkv_w = jnp.zeros((model_dim, 3 * model_dim), jnp.float32)
    grad_out_w = jnp.zeros((model_dim, model_dim), jnp.float32)
    grad_gains = jnp.zeros((2, model_dim), jnp.float32)
    grad_shifts = jnp.zeros((2, model_dim), jnp.float32)
    grad_router = jnp.zeros((model_dim, experts), jnp.float32)
    grad_up = jnp.zeros((exp_dev, model_dim, FF), jnp.float32)
    grad_down = jnp.zeros((exp_dev, FF, model_dim), jnp.float32)
    outputs = []
    input_grads = []
    for micro_index in range(MICRO):
        fetched = fetch_all(w_qkv, w_out, ln_gains, ln_biases, router, w_up, w_down)
        qkv_full, out_full, gains_full, shifts_full, router_full, up_full, down_full = fetched
        gain_rows = gains_full.astype(jnp.float32)
        shift_rows = shifts_full.astype(jnp.float32)
        inputs = tokens[micro_index].astype(jnp.float32)
        expert_of = all_ids[micro_index]
        normed = layer_norm(inputs, gain_rows[0], shift_rows[0])
        normed_low = normed.astype(jnp.bfloat16)
        projected = jnp.einsum(
            "scd,de->sce", normed_low, qkv_full, preferred_element_type=jnp.float32
        ).astype(jnp.bfloat16)
        query_rows = projected[..., :model_dim]
        queries = query_rows.reshape(seq_here, local_len, head_count, head_dim)
        key_rows = projected[..., model_dim : 2 * model_dim]
        value_rows = projected[..., 2 * model_dim :]
        log_total, attended = attention_forward(
            queries, key_rows, value_rows, query_pos, score_scale
        )
        attended_low = attended.reshape(seq_here, local_len, model_dim).astype(jnp.bfloat16)
        middle = inputs + jnp.einsum(
            "scd,de->sce", attended_low, out_full, preferred_element_type=jnp.float32
        )
        mixed_low = layer_norm(middle, gain_rows[1], shift_rows[1]).astype(jnp.bfloat16)
        onehot = (expert_of[..., None] == expert_range).astype(jnp.float32)
        logits = jnp.einsum(
            "scd,de->sce", mixed_low, router_full, preferred_element_type=jnp.float32
        )
        gates = jax.nn.sigmoid(jnp.sum(logits * onehot, axis=-1))
        target, slot_table = route_slots(expert_of, experts, capacity)
        outgoing = to_slots(mixed_low, slot_table).reshape(
            n_expert, exp_dev, seq_here * capacity, model_dim
        )
        arrived = lax.all_to_all(outgoing, "expert", split_axis=0, concat_axis=0, tiled=True)
        preact = jnp.einsum("pesd,edf->pesf", arrived, up_full, preferred_element_type=jnp.float32)
        hidden = gelu_exact(preact).astype(jnp.bfloat16)
        result = jnp.einsum(
            "pesf,efd->pesd", hidden, down_full, preferred_element_type=jnp.float32
        ).astype(jnp.bfloat16)
        returned = lax.all_to_all(result, "expert", split_axis=0, concat_axis=0, tiled=True)
        expert_out = (
            returned.reshape(-1, model_dim)[target]
            .reshape(seq_here, local_len, model_dim)
            .astype(jnp.float32)
        )
        final = middle + gates[..., None] * expert_out
        outputs.append(final.astype(jnp.bfloat16))
        fetched = fetch_all(w_qkv, w_out, ln_gains, ln_biases, router, w_up, w_down)
        qkv_full, out_full, gains_full, shifts_full, router_full, up_full, down_full = fetched
        gain_rows = gains_full.astype(jnp.float32)
        shift_rows = shifts_full.astype(jnp.float32)
        grad_final = cotangent[micro_index].astype(jnp.float32)
        grad_gate = jnp.sum(grad_final * expert_out, axis=-1) + balance_coef * jnp.sum(
            onehot * load_ratio, axis=-1
        )
        grad_logit = grad_gate * gates * (1.0 - gates)
        grad_expert = (gates[..., None] * grad_final).astype(jnp.bfloat16)
        sent_grads = to_slots(grad_expert, slot_table).reshape(
            n_expert, exp_dev, seq_here * capacity, model_dim
        )
        grads_here = lax.all_to_all(sent_grads, "expert", split_axis=0, concat_axis=0, tiled=True)
        hidden_low = gelu_exact(preact).astype(jnp.bfloat16)
        grad_down = grad_down + jnp.einsum(
            "pesf,pesd->efd", hidden_low, grads_here, preferred_element_type=jnp.float32
        )
        grad_hidden = jnp.einsum(
            "pesd,efd->pesf", grads_here, down_full, preferred_element_type=jnp.float32
        )
        grad_pre = jax.vjp(gelu_exact, preact)[1](grad_hidden)[0].astype(jnp.bfloat16)
        grad_up = grad_up + jnp.einsum(
            "pesd,pesf->edf", arrived, grad_pre, preferred_element_type=jnp.float32
        )
        grad_arrived = jnp.einsum(
            "pesf,edf->pesd", grad_pre, up_full, preferred_element_type=jnp.float32
        ).astype(jnp.bfloat16)
        grads_back = lax.all_to_all(grad_arrived, "expert", split_axis=0, concat_axis=0, tiled=True)
        grad_mixed = (
            grads_back.reshape(-1, model_dim)[target]
            .reshape(seq_here, local_len, model_dim)
            .astype(jnp.float32)
        )
        router_cols = jnp.einsum("sce,de->scd", onehot, router_full.astype(jnp.float32))
        grad_mixed = grad_mixed + grad_logit[..., None] * router_cols
        grad_router = grad_router + jnp.einsum(
            "scd,sce->de", mixed_low.astype(jnp.float32), grad_logit[..., None] * onehot
        )
        second_back = jax.vjp(layer_norm, middle, gain_rows[1], shift_rows[1])[1]
        grad_middle, grad_gain_two, grad_shift_two = second_back(grad_mixed)
        grad_middle = grad_middle + grad_final
        grad_branch = grad_middle.astype(jnp.bfloat16)
        grad_out_w = grad_out_w + jnp.einsum(
            "scd,sce->de", attended_low, grad_branch, preferred_element_type=jnp.float32
        )
        grad_attended = jnp.einsum(
            "sce,de->scd", grad_branch, out_full, preferred_element_type=jnp.float32
        ).astype(jnp.bfloat16)
        grad_heads = grad_attended.reshape(seq_here, local_len, head_count, head_dim)
        row_delta = jnp.swapaxes(jnp.sum(grad_heads.astype(jnp.float32) * attended, axis=-1), 1, 2)
        folded = query_grads(
            queries,
            grad_heads,
            key_rows,
            value_rows,
            log_total,
            row_delta,
            query_pos,
            score_scale,
            seq_len,
        )
        grad_query = folded[0].reshape(seq_here, local_len, model_dim)
        key_value = lax.psum_scatter(
            folded[1].astype(jnp.bfloat16), "expert", scatter_dimension=1, tiled=True
        ).astype(jnp.float32)
        grad_key = key_value[..., :model_dim]
        grad_value = key_value[..., model_dim:]
        grad_projected = jnp.concatenate([grad_query, grad_key, grad_value], axis=-1).astype(
            jnp.bfloat16
        )
        grad_qkv_w = grad_qkv_w + jnp.einsum(
            "scd,sce->de", normed_low, grad_projected, preferred_element_type=jnp.float32
        )
        grad_normed = jnp.einsum(
            "sce,de->scd", grad_projected, qkv_full, preferred_element_type=jnp.float32
        )
        first_back = jax.vjp(layer_norm, inputs, gain_rows[0], shift_rows[0])[1]
        grad_inputs, grad_gain_one, grad_shift_one = first_back(grad_normed)
        grad_gains = grad_gains + jnp.stack([grad_gain_one, grad_gain_two])
        grad_shifts = grad_shifts + jnp.stack([grad_shift_one, grad_shift_two])
        input_grads.append(grad_middle + grad_inputs)
    dense_grads = (
        lax.psum_scatter(grad_qkv_w, ("dp", "expert"), scatter_dimension=1, tiled=True),
        lax.psum_scatter(grad_out_w, ("dp", "expert"), scatter_dimension=1, tiled=True),
        lax.psum_scatter(grad_gains, ("dp", "expert"), scatter_dimension=1, tiled=True),
        lax.psum_scatter(grad_shifts, ("dp", "expert"), scatter_dimension=1, tiled=True),
        lax.psum_scatter(grad_router, ("dp", "expert"), scatter_dimension=0, tiled=True),
    )
    expert_grads = (
        lax.psum_scatter(
            grad_up.astype(jnp.bfloat16), "dp", scatter_dimension=1, tiled=True
        ).astype(jnp.float32),
        lax.psum_scatter(
            grad_down.astype(jnp.bfloat16), "dp", scatter_dimension=1, tiled=True
        ).astype(jnp.float32),
    )
    return (jnp.stack(outputs), jnp.stack(input_grads)) + tuple(dense_grads) + tuple(expert_grads)


MESH_ID = pl.DeviceIdType.MESH
NT = (((1,), (1,)), ((), ()))
NN = (((1,), (0,)), ((), ()))
TN = (((0,), (0,)), ((), ()))
VMEM = pl.BlockSpec(memory_space=pltpu.VMEM)
HBM = pl.BlockSpec(memory_space=pl.ANY)


def mm(a, b, dims=NN):
    return lax.dot_general(a, b, dims, preferred_element_type=jnp.float32)


def normalised(v):
    centre = v - jnp.mean(v, axis=-1, keepdims=True)
    spread = jnp.mean(centre * centre, axis=-1, keepdims=True)
    inv = lax.rsqrt(spread + epsilon)
    return centre * inv, inv


def norm_back(grad_hat, hat, inv):
    return inv * (grad_hat - jnp.mean(grad_hat, axis=1, keepdims=True) - hat * jnp.mean(grad_hat * hat, axis=1, keepdims=True))


def add_into(target, other, step):
    def some(u, carry):
        rows = pl.ds(pl.multiple_of(u * step, step), step)
        target[rows, :] = (target[rows, :].astype(jnp.float32) + other[rows, :].astype(jnp.float32)).astype(target.dtype)
        return carry

    lax.fori_loop(0, target.shape[0] // step, some, 0)


class Place:
    def __init__(self, n_dp, n_ex):
        self.n_dp, self.n_ex, self.n_dev, self.n_z = n_dp, n_ex, n_dp * n_ex, n_dp // 2
        self.dp, self.ex = lax.axis_index("dp"), lax.axis_index("expert")
        self.z, self.core = self.dp // 2, self.dp % 2
        self.flat = self.dp * n_ex + self.ex

    def z_peer(self, d):
        return (self.z + d) % self.n_z

    def ex_peer(self, d):
        return (self.ex + d) % self.n_ex

    def on_z(self, z):
        return (z * 2 + self.core, self.ex)

    def on_ex(self, e):
        return (self.dp, e)

    def partner(self):
        return (self.z * 2 + 1 - self.core, self.ex)

    def numbered(self, t):
        return (t // self.n_ex, t % self.n_ex)


def entry_barrier(at):
    sem = pltpu.get_barrier_semaphore()

    def tell(i, carry):
        pl.semaphore_signal(sem, inc=1, device_id=at.numbered((at.flat + i) % at.n_dev), device_id_type=MESH_ID)
        return carry

    lax.fori_loop(1, at.n_dev, tell, 0)
    pl.semaphore_wait(sem, at.n_dev - 1)


class Wires:
    def __init__(self, send_sems, recv_sems):
        self.send_sems, self.recv_sems, self.used = send_sems, recv_sems, 0

    def take(self, n):
        base = self.used
        self.used = base + n
        return base

    def copy(self, i, src, dst, device):
        return pltpu.make_async_remote_copy(
            src_ref=src, dst_ref=dst, send_sem=self.send_sems.at[i], recv_sem=self.recv_sems.at[i],
            device_id=device, device_id_type=MESH_ID,
        )

    def all_came(self, i, blocks):
        pltpu.make_async_copy(blocks, blocks, self.recv_sems.at[i]).wait()

    def all_left(self, i, blocks):
        pltpu.make_async_copy(blocks, blocks, self.send_sems.at[i]).wait()


def layer_kernel(
    n_dp, n_ex, x_ref, cot_ref, ids_ref, wq_ref, wo_ref, gain_ref, bias_ref, router_ref, up_hbm, down_hbm,
    gq_ref, gout_ref, gsmall_ref, out_hbm, gtok_hbm, gup_hbm, gdown_hbm, up_full, down_full, q_hbm, k_hbm, v_hbm, xn_hbm, mix_hbm, mid_hbm, w_hbm, wo_hbm,
    outbox, inbox, work, gdt, gup, pin_dn, pin_up, zin_dn, zin_up, via_dn, via_up, rowbox, attr, gar,
    gob, gob_pair, gob_line, gob_mine, gob_plane, wt_a, gws, gws_pair, gws_line, gws_sum,
    small_b, wo_s, gq_in, small_all, small_in, small_out, smalls, tally, gate_s, slot_s, eid_s, lse, send_sems, recv_sems, load_sems,
):
    bf, f32 = jnp.bfloat16, jnp.float32
    at = Place(n_dp, n_ex)
    wires = Wires(send_sems, recv_sems)
    n_dev, n_z, ex, z, core = at.n_dev, at.n_z, at.ex, at.z, at.core
    seqs, dim = x_ref.shape[0], x_ref.shape[3]
    cap = x_ref.shape[2]
    local_len = 2 * cap
    total_len, width, slots = local_len * n_ex, dim // n_ex, n_ex * cap
    head_dim = dim // HEADS
    heads = width // head_dim
    piece, oc = wq_ref.shape[1], wo_ref.shape[0]
    shard, ff = up_hbm.shape
    half = down_hbm.shape[0]
    tile, mid_dim = ff // n_z, dim // 2
    scale = head_dim ** -0.5
    wt_b, wo_b = gws, gob
    lane = lax.broadcasted_iota(jnp.int32, (1, 128), 1).astype(f32)
    lane_head = lax.broadcasted_iota(jnp.int32, (1, width), 1) // head_dim
    peers = range(1, n_ex)

    small_out[...] = jnp.zeros(small_out.shape, f32)
    small_out[0:2, 0:oc] = gain_ref[...].astype(f32)
    small_out[2:4, 0:oc] = bias_ref[...].astype(f32)
    unit = jnp.where(lax.broadcasted_iota(jnp.int32, (oc, oc), 0) == lax.broadcasted_iota(jnp.int32, (oc, oc), 1), 1.0, 0.0).astype(bf)
    small_out[4 : 4 + n_ex, 0:oc] = mm(router_ref[...], unit, TN)
    held_rows = jnp.zeros((1, 128), f32)
    for m in range(seqs):
        eid_s[m] = jnp.broadcast_to(ids_ref[m : m + 1, :].astype(f32), (128, local_len)).T
        held_rows += jnp.sum(jnp.where(lane == eid_s[m], 1.0, 0.0), axis=0, keepdims=True)
    high = jnp.floor(held_rows * (1.0 / 16.0))
    small_b[0:8, :] = small_out[0:8, 0:128].astype(bf)
    row = lax.broadcasted_iota(jnp.int32, (8, 128), 0)
    small_b[8:16, :] = jnp.where(row == 0, high, jnp.where(row == 1, held_rows - 16.0 * high, 0.0)).astype(bf)
    for b in range(n_ex):
        wo_s[b] = wo_ref[:, b * width : (b + 1) * width]
    lines = range(1, n_z)
    entry_barrier(at)

    i_tok, i_back, i_out, i_ret, i_ga, i_part = (wires.take(seqs) for _ in range(6))

    def token_copy(m, d):
        return wires.copy(i_tok + m, x_ref.at[m], inbox.at[m, ex], at.on_ex(at.ex_peer(d)))

    def back_copy(m, d):
        peer = at.ex_peer(d)
        return wires.copy(i_back + m, rowbox.at[m, peer], attr.at[m, ex], at.on_ex(peer))

    def out_copy(m, d):
        peer = at.ex_peer(d)
        return wires.copy(i_out + m, outbox.at[m, peer], work.at[m, ex], at.on_ex(peer))

    def return_copy(m, d):
        peer = at.ex_peer(d)
        return wires.copy(i_ret + m, outbox.at[m, peer], inbox.at[m, ex], at.on_ex(peer))

    def ga_copy(m, d):
        peer = at.ex_peer(d)
        return wires.copy(i_ga + m, rowbox.at[m, peer], gar.at[m, ex], at.on_ex(peer))

    def part_copy(m, d):
        peer = at.ex_peer(d)
        return wires.copy(i_part + m, outbox.at[m, peer], inbox.at[m, ex], at.on_ex(peer))

    reach = [d for d in (2, 1) if d < n_z]

    def order(step):
        return (n_z - 1) * step % n_z

    relay = n_z > 3
    kinds = n_z + 1
    i_ag, i_agp = wires.take(5 * kinds), wires.take(5 * kinds)

    def ag_columns(t):
        return pl.ds(pl.multiple_of(t * tile, tile), tile)

    def ag_block(t, zz, cc, down):
        if down:
            return down_full.at[pl.ds(pl.multiple_of((zz * 2 + cc) * half, half), half), :]
        return up_full.at[t, pl.ds(pl.multiple_of((zz * 2 + cc) * shard, shard), shard), :]

    def ag_own(t, down):
        return down_hbm if down else up_hbm.at[:, ag_columns(t)]

    def ag_code(right, d, t, down):
        return (d if d != 1 or right else 4) * kinds + (n_z if down else t)

    def ag_copy(right, d, t, down):
        return wires.copy(i_ag + ag_code(right, d, t, down), ag_own(t, down), ag_block(t, z, core, down), at.on_z(z + d if right else z - d))

    def ag_relay(right, t, down):
        block = ag_block(t, z - 2 if right else z + 2, core, down)
        return wires.copy(i_ag + ag_code(right, 3, t, down), block, block, at.on_z(z + 1 if right else z - 1))

    def ag_pair(right, d, t, down):
        block = ag_block(t, z - d if right else z + d, core, down)
        return wires.copy(i_agp + ag_code(right, d, t, down), ag_own(t, down) if d == 0 else block, block, at.partner())

    def ag_sends(right, d):
        return z + d < n_z if right else z - d >= 0

    def ag_comes(right, d):
        return z - d >= 0 if right else z + d < n_z

    def ag_relays(right):
        return z == n_z - 2 if right else z == 1

    def ag_from(right, d, t, act):
        @pl.when(ag_comes(right, d))
        def _():
            act(False)
            pl.when((z - d if right else z + d) == t)(lambda: act(True))

    def ag_start(t):
        for d in reach:
            for right in (True, False):
                @pl.when(ag_sends(right, d))
                def _():
                    ag_copy(right, d, t, False).start()
                    pl.when(z == t)(ag_copy(right, d, t, True).start)
        ag_from(True, 0, t, lambda down: ag_pair(True, 0, t, down).start())

    def ag_pass(t):
        for d in reach:
            for right in (True, False):
                def act(down, right=right, d=d):
                    ag_copy(right, d, t, down).wait_recv()
                    if d == 2 and relay:
                        pl.when(ag_relays(right))(ag_relay(right, t, down).start)
                    ag_pair(right, d, t, down).start()

                ag_from(right, d, t, act)

    def ag_far(t):
        if relay:
            for right in (True, False):
                def act(down, right=right):
                    ag_copy(right, 3, t, down).wait_recv()
                    ag_pair(right, 3, t, down).start()

                ag_from(right, 3, t, act)

    far = [0] + sorted(reach) + ([3] if relay else [])

    def ag_ready(t):
        for d in far:
            for right in (True, False) if d else (True,):
                ag_from(right, d, t, lambda down, right=right, d=d: ag_pair(right, d, t, down).wait_recv())

    def ag_finish():
        def one(t, carry):
            for d in far:
                for right in (True, False) if d else (True,):
                    ag_from(right, d, t, lambda down, right=right, d=d: ag_pair(right, d, t, down).wait_send())
            for d in reach:
                for right in (True, False):
                    @pl.when(ag_sends(right, d))
                    def _():
                        ag_copy(right, d, t, False).wait_send()
                        pl.when(z == t)(ag_copy(right, d, t, True).wait_send)
            if relay:
                for right in (True, False):
                    @pl.when(ag_relays(right))
                    def _():
                        ag_relay(right, t, False).wait_send()
                        pl.when((z - 2 if right else z + 2) == t)(ag_relay(right, t, True).wait_send)
            return carry

        lax.fori_loop(0, n_z, one, 0)

    i_gp, i_gl, i_gv = wires.take(2 * n_z), wires.take(3 * kinds), wires.take(kinds)

    def pair_copies(t):
        return (
            wires.copy(i_gp + 2 * t, gdt.at[1 - core, t], pin_dn.at[t], at.partner()),
            wires.copy(i_gp + 2 * t + 1, gup.at[1 - core, t], pin_up.at[t], at.partner()),
        )

    def line_copy(t, src, dest, down):
        right, d = dest > src, abs(dest - src)
        block = gdt.at[core, t] if down else gup.at[core, t, dest]
        kind = n_z if down else t
        if d == 3:
            return wires.copy(i_gv + kind, block, via_dn if down else via_up.at[t], at.on_z(src + 1 if right else src - 1))
        slot = 2 if d == 2 else 0 if right else 1
        return wires.copy(
            i_gl + slot * kinds + kind, block, zin_dn.at[slot] if down else zin_up.at[slot, t], at.on_z(dest)
        )

    pairs_far_first = sorted(((s_, d_) for s_ in range(n_z) for d_ in range(n_z) if s_ != d_), key=lambda u: -abs(u[0] - u[1]))

    def held(src, dest):
        return relay and abs(dest - src) == 2 and src in (1, n_z - 2) and dest in (0, n_z - 1)

    def line_each(t, src, dest, act):
        act(False)
        pl.when(t == dest)(lambda: act(True))

    def fold(t):
        for c in pair_copies(t):
            c.wait_recv()
        add_into(gdt.at[core, t], pin_dn.at[t], 96)
        for zz in range(n_z):
            add_into(gup.at[core, t, zz], pin_up.at[t, zz], 48)
        for src, dest in pairs_far_first:
            if not held(src, dest):
                @pl.when(z == src)
                def _():
                    line_each(t, src, dest, lambda down: line_copy(t, src, dest, down).start())

    def add_far(t):
        for src, dest in pairs_far_first:
            if held(src, dest):
                @pl.when(z == src)
                def _():
                    def act(down):
                        line_copy(t, dest - 3 if dest > src else dest + 3, dest, down).wait_recv()
                        if down:
                            add_into(gdt.at[core, t], via_dn, 96)
                        else:
                            add_into(gup.at[core, t, dest], via_up.at[t], 48)
                        line_copy(t, src, dest, down).start()

                    line_each(t, src, dest, act)

    i_small = wires.take(1)

    def small_copy(i):
        return wires.copy(i_small, small_b, small_all.at[at.flat], at.numbered((at.flat + i) % n_dev))

    def each(n, act):
        def step(i, carry):
            act(i)
            return carry

        lax.fori_loop(1, n, step, 0)

    i_piece, i_line, i_pair, i_wo, i_wo2 = wires.take(3), wires.take(1), wires.take(2), wires.take(1), wires.take(1)

    def forward(q_v, k_v, v_v, xn_v, wide, att_acc, lse_acc, mid_v, mix_v, w_v, wo_v, up_s, down_s):
        stage = (
            pltpu.make_async_copy(up_hbm, up_s, load_sems.at[0]),
            pltpu.make_async_copy(down_hbm, down_s, load_sems.at[1]),
        )
        for c in stage:
            c.start()
        me_j = ex * n_dp + at.dp
        pieces = []
        for r in range(3):
            c = 3 * at.flat + r
            sec, j = c // n_dev, c % n_dev
            copy = wires.copy(i_piece + r, wq_ref.at[r], wt_a.at[sec], (j % n_dp, j // n_dp))
            away = j != me_j
            pl.when(away)(copy.start)
            pieces.append((copy, away, sec))
        each(n_dev, lambda i: small_copy(i).start())
        for m in range(seqs):
            for d in peers:
                token_copy(m, d).start()
        small_all[at.flat] = small_b[...]
        wo_b[core, ex, z] = wo_s[...]
        for m in range(seqs):
            inbox[m, ex] = x_ref[m]
        for r, (copy, away, sec) in enumerate(pieces):
            pl.when(away)(copy.wait_recv)

            @pl.when(jnp.logical_not(away))
            def _():
                wt_a[sec] = wq_ref[r]

        w_line = [wires.copy(i_line, wt_a, wt_b.at[core, z], at.on_z(at.z_peer(d))) for d in lines]
        for c in w_line:
            c.start()
        wo_line = [wires.copy(i_wo, wo_s, wo_b.at[core, ex, z], at.on_z(at.z_peer(d))) for d in lines]
        for c in wo_line:
            c.start()
        wt_b[core, z] = wt_a[...]
        for c in stage:
            c.wait()
        own = [
            pltpu.make_async_copy(up_s.at[:, t * tile : (t + 1) * tile], ag_block(t, z, core, False), load_sems.at[t % 2])
            for t in range(n_z)
        ] + [pltpu.make_async_copy(down_s, ag_block(0, z, core, True), load_sems.at[3])]
        for c in own[:2]:
            c.start()

        before = jnp.where(
            lax.broadcasted_iota(jnp.int32, (local_len, local_len), 1) < lax.broadcasted_iota(jnp.int32, (local_len, local_len), 0), 1.0, 0.0
        ).astype(bf)
        for m in range(seqs):
            named = jnp.where(lane == eid_s[m], 1.0, 0.0)
            earlier = jnp.sum(mm(before, named.astype(bf)) * named, axis=1, keepdims=True)
            slot_s[m] = eid_s[m] * cap + earlier

        wires.all_came(i_small, small_all.at[pl.ds(0, n_dev - 1)])
        smalls[...] = jnp.zeros(smalls.shape, f32)
        tally[...] = jnp.zeros(tally.shape, f32)
        for s in range(n_dev):
            block = small_all[s].astype(f32)
            tally[...] += block[8:16, :]
            lo = s * oc // 128 * 128
            spread = pltpu.roll(jnp.concatenate([block, jnp.zeros_like(block)], axis=1), s * oc - lo, 1)
            hi = min(lo + 256, dim)
            smalls[:, lo:hi] += spread[:, 0 : hi - lo]
        gain_one, shift_one = smalls[0:1, :], smalls[2:3, :]
        gain_two, shift_two = smalls[1:2, :], smalls[3:4, :]
        wires.all_came(i_line, wt_b.at[0, pl.ds(0, n_z - 1)])
        w_pair = wires.copy(i_pair, wt_b.at[core], wt_b.at[core], at.partner())
        w_pair.start()
        wires.all_came(i_wo, wo_b.at[0, 0, pl.ds(0, n_z - 1)])
        for step in range(min(2, n_z)):
            ag_start(order(step))
        wo_plane = [wires.copy(i_wo2, wo_b.at[core, ex], wo_b.at[core, ex], at.on_ex(at.ex_peer(d))) for d in peers]
        for c in wo_plane:
            c.start()
        w_pair.wait_recv()
        for sec in range(3):
            for zz in range(n_z):
                for cc in range(2):
                    row = (zz * 2 + cc) * piece
                    wide[row : row + piece, :] = wt_b[cc, zz, sec].astype(f32)
            w_v[sec] = wide[0:width, :].astype(bf)

        def project(m):
            def one(d, carry):
                src = (ex - d + n_ex) % n_ex

                @pl.when(d == 1)
                def _():
                    wires.all_came(i_tok + m, inbox.at[m, pl.ds(0, n_ex - 1)])

                rows = pl.ds(pl.multiple_of(src * local_len, local_len), local_len)
                hat, _ = normalised(inbox[m, src].reshape(local_len, dim).astype(f32))
                low = (hat * gain_one + shift_one).astype(bf)
                xn_v[rows, :] = low
                q_v[m, rows, :] = mm(low, w_v[0], NT).astype(bf)
                k_v[m, rows, :] = mm(low, w_v[1], NT).astype(bf)
                v_v[m, rows, :] = mm(low, w_v[2], NT).astype(bf)
                return carry

            lax.fori_loop(0, n_ex, one, 0)

        def attend(m):
            for i in range(n_ex):
                end = (i + 1) * local_len
                here = slice(i * local_len, end)

                def one_head(h, carry):
                    mine = lane_head == h
                    qb = q_v[m, here, :]
                    s = mm(jnp.where(mine, qb * scale, jnp.zeros_like(qb)), k_v[m, 0:end, :], NT)
                    top = jnp.max(s, axis=-1, keepdims=True)
                    e = jnp.exp(s - top)
                    total = jnp.sum(e, axis=-1, keepdims=True)
                    p = (e * (1.0 / total)).astype(bf)
                    att_acc[...] = jnp.where(mine, mm(p, v_v[m, 0:end, :]), att_acc[...])
                    lse_acc[...] = jnp.where(lane == h.astype(f32), top + jnp.log(total), lse_acc[...])
                    return carry

                lax.fori_loop(0, heads, one_head, 0)
                rowbox[m, i] = att_acc[...].astype(bf)
                lse[m, :, here] = lse_acc[...].T[0:8, :]
            for d in peers:
                back_copy(m, d).start()
            attr[m, ex] = rowbox[m, ex]

        def route(m):
            wires.all_came(i_back + m, attr.at[m, pl.ds(0, n_ex - 1)])
            mid = x_ref[m].reshape(local_len, dim).astype(f32)
            for b in range(n_ex):
                mid += mm(attr[m, b], wo_v[b], NT)
            mid_v[m] = mid
            hat, _ = normalised(mid)
            mixed = (hat * gain_two + shift_two).astype(bf)
            mix_v[m] = mixed
            logits = mm(mixed, smalls[...].astype(bf), NT)
            mine = lax.broadcasted_iota(jnp.int32, logits.shape, 1).astype(f32) == eid_s[m][:, 0:1] + 4.0
            gate = jax.nn.sigmoid(jnp.sum(jnp.where(mine, logits, 0.0), axis=1, keepdims=True))
            gate_s[m] = jnp.broadcast_to(gate, (local_len, 128))
            scaled = (gate * cot_ref[m].astype(f32)).astype(bf)
            place = jnp.where(
                slot_s[m].T[0:1, :] == lax.broadcasted_iota(jnp.int32, (slots, local_len), 0).astype(f32), 1.0, 0.0
            ).astype(bf)
            outbox[m, :, 0] = mm(place, mixed).astype(bf).reshape(n_ex, cap, dim)
            outbox[m, :, 1] = mm(place, scaled).astype(bf).reshape(n_ex, cap, dim)
            for d in peers:
                out_copy(m, d).start()
            work[m, ex] = outbox[m, ex]

        att_acc[...] = jnp.zeros(att_acc.shape, f32)
        lse_acc[...] = jnp.zeros(lse_acc.shape, f32)

        def xn_out(m):
            return pltpu.make_async_copy(xn_v, xn_hbm.at[m], load_sems.at[2])

        project(0)
        xn_out(0).start()
        attend(0)
        for i, c in enumerate(own):
            if i >= 2:
                if i < n_z:
                    own[i - 2].wait()
                c.start()
        for c in own[n_z - 2 :]:
            c.wait()
        for m in range(1, seqs):
            xn_out(m - 1).wait()
            project(m)
            xn_out(m).start()
            attend(m)
        wires.all_came(i_wo2, wo_b.at[0, pl.ds(0, n_ex - 1)])
        wo_pair = wires.copy(i_pair + 1, wo_b.at[core], wo_b.at[core], at.partner())
        wo_pair.start()
        ag_pass(order(0))
        for step in range(2, n_z - 1):
            ag_start(order(step))
        wo_pair.wait_recv()
        for b in range(n_ex):
            for s in range(n_dev):
                wide[s * oc : (s + 1) * oc, 0:width] = wo_b[s // n_ex % 2, s % n_ex, s // n_ex // 2, b].astype(f32)
            wo_v[b] = wide[0:dim, 0:width].astype(bf)
        for m in range(seqs):
            route(m)
        ag_pass(order(1))
        if n_z > 2:
            ag_start(order(n_z - 1))
        xn_out(seqs - 1).wait()
        keep = [
            pltpu.make_async_copy(src, dst, load_sems.at[i])
            for i, (src, dst) in enumerate(((q_v, q_hbm), (k_v, k_hbm), (v_v, v_hbm), (mid_v, mid_hbm), (mix_v, mix_hbm), (w_v, w_hbm), (wo_v, wo_hbm)))
        ]
        for c in keep:
            c.start()
        for m in range(seqs):
            wires.all_left(i_back + m, attr.at[m, pl.ds(0, n_ex - 1)])
            wires.all_left(i_tok + m, inbox.at[m, pl.ds(0, n_ex - 1)])
        for copy, away, _ in pieces:
            pl.when(away)(copy.wait_send)
        wires.all_left(i_small, small_all.at[pl.ds(0, n_dev - 1)])
        wires.all_left(i_line, wt_b.at[0, pl.ds(0, n_z - 1)])
        wires.all_left(i_wo, wo_b.at[0, 0, pl.ds(0, n_z - 1)])
        wires.all_left(i_wo2, wo_b.at[0, pl.ds(0, n_ex - 1)])
        for c in (w_pair, wo_pair):
            c.wait_send()
        for c in keep:
            c.wait()

    pl.run_scoped(
        forward,
        pltpu.VMEM((seqs, total_len, width), bf), pltpu.VMEM((seqs, total_len, width), bf), pltpu.VMEM((seqs, total_len, width), bf),
        pltpu.VMEM((total_len, dim), bf), pltpu.VMEM((dim, dim), f32),
        pltpu.VMEM((local_len, width), f32), pltpu.VMEM((local_len, 128), f32),
        pltpu.VMEM((seqs, local_len, dim), f32), pltpu.VMEM((seqs, local_len, dim), bf),
        pltpu.VMEM((3, width, dim), bf), pltpu.VMEM((n_ex, dim, width), bf),
        pltpu.VMEM((shard, ff), bf), pltpu.VMEM((half, dim), bf),
    )

    def experts(up_t, down_t, res_acc, gar_acc, hid, gpre, x_t, g_t):
        sub = 256 if tile % 256 == 0 else tile
        pair = n_z - 2

        def loads(step, slot):
            return (
                pltpu.make_async_copy(up_full.at[order(step)], up_t.at[slot], load_sems.at[2 * slot]),
                pltpu.make_async_copy(down_full.at[ag_columns(order(step)), :], down_t.at[slot], load_sems.at[2 * slot + 1]),
            )

        def fetch(step, slot):
            ag_far(order(step))
            ag_ready(order(step))
            for c in loads(step, slot):
                c.start()

        fetch(0, 0)

        def one_round(k, carry):
            per = jnp.where(k == pair, 2, 1)

            def one(q, q_carry):
                m, step = q // per, k + q % per
                j = step % 2
                mine = pl.ds(pl.multiple_of(m * slots, slots), slots)

                @pl.when(m == 0)
                def _():
                    for c in loads(step, j):
                        c.wait()

                @pl.when(step == 0)
                def _():
                    wires.all_came(i_out + m, work.at[m, pl.ds(0, n_ex - 1)])
                    wires.all_left(i_out + m, work.at[m, pl.ds(0, n_ex - 1)])
                    res_acc[m] = jnp.zeros((slots, dim), f32)
                    gar_acc[m] = jnp.zeros((slots, dim), f32)

                def one_sub(u, c_):
                    cols = pl.ds(pl.multiple_of(u * sub, sub), sub)
                    rows = work[m, :, 0].reshape(slots, dim)
                    grads = work[m, :, 1].reshape(slots, dim)
                    pre = mm(rows, up_t[j, :, cols])
                    cdf = 0.5 * (1.0 + lax.erf(pre * (2.0 ** -0.5)))
                    hidden = (pre * cdf).astype(bf)
                    slope = cdf + pre * jnp.exp(-0.5 * pre * pre) * ((2.0 * math.pi) ** -0.5)
                    hid[j, mine, cols] = hidden
                    res_acc[m] += mm(hidden, down_t[j, cols, :])
                    low = (mm(grads, down_t[j, cols, :], NT) * slope).astype(bf)
                    gpre[j, mine, cols] = low
                    gar_acc[m] += mm(low, up_t[j, :, cols], NT)
                    return c_

                lax.fori_loop(0, tile // sub, one_sub, 0)

                @pl.when(step == n_z - 1)
                def _():
                    outbox[m, :, 0] = res_acc[m].astype(bf).reshape(n_ex, cap, dim)
                    outbox[m, :, 1] = gar_acc[m].astype(bf).reshape(n_ex, cap, dim)
                    for d in peers:
                        return_copy(m, d).start()
                    inbox[m, ex] = outbox[m, ex]

                for ahead in range(2, n_z):
                    @pl.when((k == ahead - 2) & (q == 0))
                    def _():
                        ag_pass(order(ahead))

                pl.when((k == pair) & (q == 0))(lambda: fetch(n_z - 1, (n_z - 1) % 2))
                for late in range(n_z - 2):
                    pl.when((k == late + 1) & (q == 0))(lambda: fold(order(late)))
                if n_z > 3:
                    pl.when((k == pair) & (q == seqs))(lambda: add_far(order(0)))
                return q_carry

            lax.fori_loop(0, seqs * per, one, 0)

            @pl.when(k == 0)
            def _():
                for s in range(seqs):
                    lanes = slice(s * slots, (s + 1) * slots)
                    x_t[:, lanes] = work[s, :, 0].reshape(slots, dim).T
                    g_t[:, lanes] = work[s, :, 1].reshape(slots, dim).T

            def weight_grads(jj, jj_carry):
                step = k + jj
                j, t = step % 2, order(step)
                pl.when(k < pair)(lambda: fetch(step + 1, 1 - j))

                def some(u, c_):
                    at_rows = pl.ds(pl.multiple_of(u * mid_dim, mid_dim), mid_dim)
                    up_grad = mm(x_t[at_rows, :], gpre[j]).astype(bf)
                    for s in range(n_z):
                        gup[s % 2, t, u * (n_z // 2) + s // 2] = up_grad[s * shard : (s + 1) * shard, :]
                    down_grad = mm(g_t[at_rows, :], hid[j]).astype(bf)
                    for c in range(2):
                        gdt[c, t, at_rows, :] = down_grad[:, c * half : (c + 1) * half]
                    return c_

                lax.fori_loop(0, 2, some, 0)
                for c in pair_copies(t):
                    c.start()
                pl.when(step == n_z - 1)(lambda: fold(order(n_z - 2)))
                return jj_carry

            lax.fori_loop(0, per, weight_grads, 0)
            return carry

        lax.fori_loop(0, pair + 1, one_round, 0)

    every = seqs * slots
    pl.run_scoped(
        experts,
        pltpu.VMEM((2, dim, tile), bf), pltpu.VMEM((2, tile, dim), bf),
        pltpu.VMEM((seqs, slots, dim), f32), pltpu.VMEM((seqs, slots, dim), f32),
        pltpu.VMEM((2, every, tile), bf), pltpu.VMEM((2, every, tile), bf),
        pltpu.VMEM((dim, every), bf), pltpu.VMEM((dim, every), bf),
    )
    fold(order(n_z - 1))
    ag_finish()

    gain_one, gain_two = smalls[0:1, :], smalls[1:2, :]
    counts = jnp.where(lane < n_ex, 16.0 * tally[0:1, :] + tally[1:2, :], 0.0)
    mean_load = jnp.sum(counts, axis=1, keepdims=True) / n_ex
    load_ratio = (counts - mean_load) / mean_load
    small_out[...] = jnp.zeros(small_out.shape, f32)
    i_gob, i_gw = wires.take(3), wires.take(5)
    gob_pair_copy = wires.copy(i_gob, gob.at[1 - core], gob_pair, at.partner())

    def gob_plane_copy(d):
        peer = at.ex_peer(d)
        return wires.copy(i_gob + 1, gob.at[core, peer], gob_plane.at[d - 1], at.on_ex(peer))

    def gob_line_copy(d):
        peer = at.z_peer(d)
        return wires.copy(i_gob + 2, gob_mine.at[peer], gob_line.at[d - 1], at.on_z(peer))

    gws_pair_copy = wires.copy(i_gw, gws.at[1 - core], gws_pair, at.partner())

    def gws_line_copy(d):
        peer = at.z_peer(d)
        return wires.copy(i_gw + 1, gws.at[core, peer], gws_line.at[d - 1], at.on_z(peer))

    me_j = ex * n_dp + at.dp
    finals = []
    for sec in range(3):
        c = sec * n_dev + me_j
        owner, r = c // 3, c % 3
        copy = wires.copy(i_gw + 2 + r, gws_sum.at[sec], gq_in.at[r], at.numbered(owner))
        finals.append((copy, owner != at.flat, sec, r))

    def backward(gb_t, q_v, k_v, v_v, xn_v, mix_v, mid_v, w_v, wo_v, dq, dk, dv, gw, gtok, out_v):
        pairs = ((wo_hbm, wo_v), (mix_hbm, mix_v), (mid_hbm, mid_v), (w_hbm, w_v), (q_hbm, q_v), (k_hbm, k_v), (v_hbm, v_v))
        brought = [pltpu.make_async_copy(src, dst, load_sems.at[i]) for i, (src, dst) in enumerate(pairs)]
        for c in brought:
            c.start()
        for c in brought:
            c.wait()

        def head(m):
            wires.all_came(i_ret + m, inbox.at[m, pl.ds(0, n_ex - 1)])
            wires.all_left(i_ret + m, inbox.at[m, pl.ds(0, n_ex - 1)])
            def some_rows(u, carry):
                at_rows = pl.ds(pl.multiple_of(u * 128, 128), 128)
                place = jnp.where(
                    slot_s[m, at_rows, 0:1] == lax.broadcasted_iota(jnp.int32, (128, slots), 1).astype(f32), 1.0, 0.0
                ).astype(bf)
                expert_out = mm(place, inbox[m, :, 0].reshape(slots, dim))
                gate, named = gate_s[m, at_rows, 0:1], eid_s[m, at_rows, :]
                cot = cot_ref[m, at_rows, :].astype(f32)
                out_v[m, at_rows, :] = mid_v[m, at_rows, :] + gate * expert_out
                grad_gate = jnp.sum(cot * expert_out, axis=1, keepdims=True) + balance_coef * jnp.sum(
                    jnp.where(lane == named, load_ratio, 0.0), axis=1, keepdims=True
                )
                grad_logit = grad_gate * gate * (1.0 - gate)
                grad_mixed = mm(place, inbox[m, :, 1].reshape(slots, dim))
                mixed = mix_v[m, at_rows, :].astype(f32)
                for e in range(n_ex):
                    routed = jnp.where(named[:, 0:1] == float(e), grad_logit, 0.0)
                    grad_mixed += routed * smalls[4 + e : 5 + e, :]
                    small_out[4 + e : 5 + e, 0:dim] += jnp.sum(routed * mixed, axis=0, keepdims=True)
                hat, inv = normalised(mid_v[m, at_rows, :])
                small_out[1:2, 0:dim] += jnp.sum(grad_mixed * hat, axis=0, keepdims=True)
                small_out[3:4, 0:dim] += jnp.sum(grad_mixed, axis=0, keepdims=True)
                grad_middle = norm_back(grad_mixed * gain_two, hat, inv) + cot
                gtok[m, at_rows, :] = grad_middle
                branch = grad_middle.astype(bf)
                for e in range(n_ex):
                    rowbox[m, e, at_rows, :] = mm(branch, wo_v[e]).astype(bf)
                gb_t[m, :, at_rows] = branch.T
                return carry

            lax.fori_loop(0, local_len // 128, some_rows, 0)
            for d in peers:
                ga_copy(m, d).start()
            gar[m, ex] = rowbox[m, ex]

        head(0)
        if n_z > 2:
            add_far(order(n_z - 3))
        for m in range(1, seqs):
            head(m)
        wrote = pltpu.make_async_copy(out_v, out_hbm, load_sems.at[0])
        wrote.start()

        for b in range(n_ex):
            total = mm(gb_t[0], attr[0, b])
            for m in range(1, seqs):
                total += mm(gb_t[m], attr[m, b])
            for s in range(n_dev):
                gob[s // n_ex % 2, s % n_ex, s // n_ex // 2, b] = total[s * oc : (s + 1) * oc].astype(bf)
        gob_pair_copy.start()
        gw[...] = jnp.zeros(gw.shape, f32)

        def gob_up():
            gob_pair_copy.wait()
            for e in range(n_ex):
                for zz in range(n_z):
                    gob[core, e, zz] = (gob[core, e, zz].astype(f32) + gob_pair[e, zz].astype(f32)).astype(bf)
            for d in peers:
                gob_plane_copy(d).start()

        def attention_back(m, first=lambda: None):
            xn_copy = pltpu.make_async_copy(xn_hbm.at[m], xn_v, load_sems.at[7])
            xn_copy.start()
            wires.all_came(i_ga + m, gar.at[m, pl.ds(0, n_ex - 1)])
            wires.all_left(i_ga + m, gar.at[m, pl.ds(0, n_ex - 1)])
            first()
            dk[...] = jnp.zeros(dk.shape, f32)
            dv[...] = jnp.zeros(dv.shape, f32)
            dq[...] = jnp.zeros(dq.shape, f32)
            for i in reversed(range(n_ex)):
                end = (i + 1) * local_len
                here = slice(i * local_len, end)

                def one_head(h, carry):
                    mine = lane_head == h
                    qb, ga = q_v[m, here, :], gar[m, i]
                    q_h = jnp.where(mine, qb * scale, jnp.zeros_like(qb))
                    ga_h = jnp.where(mine, ga, jnp.zeros_like(ga))
                    kk = k_v[m, 0:end, :]
                    p = jnp.exp(mm(kk, q_h, NT) - lse[m, pl.ds(h, 1), here])
                    dp = mm(v_v[m, 0:end, :], ga_h, NT)
                    delta = jnp.sum(p * dp, axis=0, keepdims=True)
                    ds = (p * (dp - delta)).astype(bf)
                    dv[0:end, :] += mm(p.astype(bf), ga_h)
                    dk[0:end, :] += mm(ds, q_h)
                    dq[here, :] += jnp.where(mine, mm(ds, kk, TN) * scale, 0.0)
                    return carry

                lax.fori_loop(0, heads, one_head, 0)
                part = mm(dq[here, :].astype(bf), w_v[0]) + mm(dk[here, :].astype(bf), w_v[1]) + mm(dv[here, :].astype(bf), w_v[2])
                outbox[m, i] = part.astype(bf).reshape(2, cap, dim)
                for d in peers:
                    pl.when(at.ex_peer(d) == i)(part_copy(m, d).start)
            inbox[m, ex] = outbox[m, ex]
            xn_copy.wait()
            for sec, g in enumerate((dq, dk, dv)):
                gw[sec] += mm(g[...].astype(bf), xn_v[...], TN)

        attention_back(0, gob_up)
        if n_z > 2:
            add_far(order(n_z - 2))
        wires.all_came(i_gob + 1, gob_plane)
        wires.all_left(i_gob + 1, gob_plane)
        for zz in range(n_z):
            total = gob[core, ex, zz].astype(f32)
            for d in peers:
                total += gob_plane[d - 1, zz].astype(f32)
            gob_mine[zz] = total.astype(bf)
        for d in lines:
            gob_line_copy(d).start()
        for m in range(1, seqs):
            attention_back(m)
        add_far(order(n_z - 1))
        for sec in range(3):
            for j in range(n_dp):
                gws[j % 2, j // 2, sec] = gw[sec, j * piece : (j + 1) * piece, :].astype(bf)
        gws_pair_copy.start()
        gws_pair_copy.wait()
        gws[core] = (gws[core].astype(f32) + gws_pair[...].astype(f32)).astype(bf)
        for d in lines:
            gws_line_copy(d).start()

        def tail(m):
            wires.all_came(i_part + m, inbox.at[m, pl.ds(0, n_ex - 1)])
            wires.all_left(i_part + m, inbox.at[m, pl.ds(0, n_ex - 1)])
            grad_normed = jnp.zeros((local_len, dim), f32)
            for e in range(n_ex):
                grad_normed += inbox[m, e].reshape(local_len, dim).astype(f32)
            hat, inv = normalised(x_ref[m].reshape(local_len, dim).astype(f32))
            small_out[0:1, 0:dim] += jnp.sum(grad_normed * hat, axis=0, keepdims=True)
            small_out[2:3, 0:dim] += jnp.sum(grad_normed, axis=0, keepdims=True)
            gtok[m] += norm_back(grad_normed * gain_one, hat, inv)

        for m in range(seqs - 1):
            tail(m)
        wires.all_came(i_gw + 1, gws_line)
        wires.all_left(i_gw + 1, gws_line)
        total = gws[core, z].astype(f32)
        for d in lines:
            total += gws_line[d - 1].astype(f32)
        gws_sum[...] = total.astype(bf)
        for copy, away, sec, r in finals:
            pl.when(away)(copy.start)
        tail(seqs - 1)
        wrote.wait()
        wrote_tok = pltpu.make_async_copy(gtok, gtok_hbm, load_sems.at[0])
        wrote_tok.start()
        wrote_tok.wait()

    pl.run_scoped(
        backward,
        pltpu.VMEM((seqs, dim, local_len), bf),
        pltpu.VMEM((seqs, total_len, width), bf), pltpu.VMEM((seqs, total_len, width), bf), pltpu.VMEM((seqs, total_len, width), bf),
        pltpu.VMEM((total_len, dim), bf), pltpu.VMEM((seqs, local_len, dim), bf), pltpu.VMEM((seqs, local_len, dim), f32),
        pltpu.VMEM((3, width, dim), bf), pltpu.VMEM((n_ex, dim, width), bf),
        pltpu.VMEM((total_len, width), f32), pltpu.VMEM((total_len, width), f32), pltpu.VMEM((total_len, width), f32),
        pltpu.VMEM((3, width, dim), f32),
        pltpu.VMEM((seqs, local_len, dim), f32), pltpu.VMEM((seqs, local_len, dim), f32),
    )

    i_last = wires.take(1)

    def window(t):
        return pl.ds(pl.multiple_of(t * oc // 128 * 128, 128), 256)

    def last_copy(i):
        t = (at.flat + i) % n_dev
        return wires.copy(i_last, small_out.at[:, window(t)], small_in.at[at.flat], at.numbered(t))

    each(n_dev, lambda i: last_copy(i).start())
    small_in[at.flat] = small_out[:, window(at.flat)]
    wires.all_came(i_gob + 2, gob_line)
    wires.all_left(i_gob + 2, gob_line)
    total = gob_mine[z].astype(f32)
    for d in lines:
        total += gob_line[d - 1].astype(f32)
    gout_ref[...] = jnp.concatenate([total[b] for b in range(n_ex)], axis=1)

    def settle(up_v, down_v):
        def done(t, carry):
            for c in pair_copies(t):
                c.wait_send()
            for src, dest in pairs_far_first:
                pl.when(z == src)(lambda: line_each(t, src, dest, lambda down: line_copy(t, src, dest, down).wait_send()))
                if abs(dest - src) < 3:
                    pl.when(z == dest)(lambda: line_each(t, src, dest, lambda down: line_copy(t, src, dest, down).wait_recv()))
            return carry

        lax.fori_loop(0, n_z, done, 0)
        for dest in range(n_z):
            came = [s for s in range(n_z) if s != dest and abs(s - dest) < 3]
            places = [2 if abs(s - dest) == 2 else 0 if dest > s else 1 for s in came]

            @pl.when(z == dest)
            def _():
                def some_up(t, carry):
                    total = gup[core, t, dest].astype(f32)
                    for s in places:
                        total += zin_up[s, t].astype(f32)
                    up_v[:, ag_columns(t)] = total
                    return carry

                def some_down(u, carry):
                    at_rows = pl.ds(pl.multiple_of(u * 128, 128), 128)
                    total = gdt[core, dest, at_rows, :].astype(f32)
                    for s in places:
                        total += zin_dn[s, at_rows, :].astype(f32)
                    down_v[:, at_rows] = total.T
                    return carry

                lax.fori_loop(0, n_z, some_up, 0)
                lax.fori_loop(0, dim // 128, some_down, 0)

        wrote = (pltpu.make_async_copy(up_v, gup_hbm, load_sems.at[0]), pltpu.make_async_copy(down_v, gdown_hbm, load_sems.at[1]))
        for c in wrote:
            c.start()
        for c in wrote:
            c.wait()

    pl.run_scoped(settle, pltpu.VMEM((shard, ff), f32), pltpu.VMEM((half, dim), f32))
    for copy, away, sec, r in finals:
        @pl.when(away)
        def _():
            copy.wait()

        @pl.when(jnp.logical_not(away))
        def _():
            gq_in[r] = gws_sum[sec]

    for r in range(3):
        gq_ref[r * piece : (r + 1) * piece, :] = gq_in[r].astype(f32)
    wires.all_came(i_last, small_in.at[pl.ds(0, n_dev - 1)])
    wires.all_left(i_last, small_in.at[pl.ds(0, n_dev - 1)])
    total = jnp.zeros((8, 256), f32)
    for s in range(n_dev):
        total += small_in[s]
    gsmall_ref[...] = total


def whole_layer(n_dp, n_ex, x, cot, ids, wq, wo, gains, biases, router, w_up, w_down):
    bf, f32 = jnp.bfloat16, jnp.float32
    seqs, local_len, dim = cot.shape
    width, total_len, n_z, n_dev = dim // n_ex, local_len * n_ex, n_dp // 2, n_dp * n_ex
    cap = x.shape[2]
    shard, ff = w_up.shape
    half = w_down.shape[0]
    piece, oc, tile = wq.shape[1], wo.shape[0], ff // n_z
    vmem_outs = [((3 * piece, dim), f32), ((oc, dim), f32), ((8, 256), f32)]
    hbm_outs = [
        ((seqs, local_len, dim), f32), ((seqs, local_len, dim), f32), ((shard, ff), f32), ((half, dim), f32),
        ((n_z, dim, ff // n_z), bf), ((ff, dim), bf),
        ((seqs, total_len, width), bf), ((seqs, total_len, width), bf), ((seqs, total_len, width), bf), ((seqs, total_len, dim), bf),
        ((seqs, local_len, dim), bf), ((seqs, local_len, dim), f32), ((3, width, dim), bf), ((n_ex, dim, width), bf),
    ]
    box = pltpu.VMEM((seqs, n_ex, 2, cap, dim), bf)
    rows = pltpu.VMEM((seqs, n_ex, local_len, width), bf)
    n_sems = 2 + 6 * seqs + 14 * (n_z + 1) + 2 * n_z + 8 + 8
    sems = pltpu.SemaphoreType.DMA((n_sems,))
    return pl.pallas_call(
        functools.partial(layer_kernel, n_dp, n_ex),
        out_shape=[jax.ShapeDtypeStruct(s, d) for s, d in vmem_outs + hbm_outs],
        in_specs=[VMEM] * 8 + [HBM] * 2,
        out_specs=[VMEM] * len(vmem_outs) + [HBM] * len(hbm_outs),
        scratch_shapes=[
            box, box, box,
            pltpu.VMEM((2, n_z, dim, half), bf), pltpu.VMEM((2, n_z, n_z, shard, tile), bf),
            pltpu.VMEM((n_z, dim, half), bf), pltpu.VMEM((n_z, n_z, shard, tile), bf),
            pltpu.VMEM((3, dim, half), bf), pltpu.VMEM((3, n_z, shard, tile), bf),
            pltpu.VMEM((dim, half), bf), pltpu.VMEM((n_z, shard, tile), bf),
            rows, rows, rows,
            pltpu.VMEM((2, n_ex, n_z, n_ex, oc, width), bf), pltpu.VMEM((n_ex, n_z, n_ex, oc, width), bf),
            pltpu.VMEM((n_z - 1, n_ex, oc, width), bf), pltpu.VMEM((n_z, n_ex, oc, width), bf), pltpu.VMEM((n_ex - 1, n_z, n_ex, oc, width), bf),
            pltpu.VMEM((3, piece, dim), bf), pltpu.VMEM((2, n_z, 3, piece, dim), bf), pltpu.VMEM((n_z, 3, piece, dim), bf),
            pltpu.VMEM((n_z - 1, 3, piece, dim), bf), pltpu.VMEM((3, piece, dim), bf),
            pltpu.VMEM((16, 128), bf), pltpu.VMEM((n_ex, oc, width), bf), pltpu.VMEM((3, piece, dim), bf),
            pltpu.VMEM((n_dev, 16, 128), bf), pltpu.VMEM((n_dev, 8, 256), f32), pltpu.VMEM((8, dim + 256), f32),
            pltpu.VMEM((16, dim), f32), pltpu.VMEM((8, 128), f32),
            pltpu.VMEM((seqs, local_len, 128), f32), pltpu.VMEM((seqs, local_len, 128), f32), pltpu.VMEM((seqs, local_len, 128), f32),
            pltpu.VMEM((seqs, 8, total_len), f32),
            sems, sems, pltpu.SemaphoreType.DMA((8,)),
        ],
        compiler_params=pltpu.CompilerParams(collective_id=0, has_side_effects=True, vmem_limit_bytes=67043328),
        name="whole_layer",
    )(x, cot, ids, wq, wo, gains, biases, router, w_up, w_down)


def fast_body(tokens, cotangent, expert_ids, w_qkv, w_out, ln_gains, ln_biases, router, w_up, w_down):
    bf = jnp.bfloat16
    n_expert, n_dp = lax.axis_size("expert"), lax.axis_size("dp")
    seqs, local_len, dim = tokens.shape[0] * tokens.shape[1], tokens.shape[2], tokens.shape[3]
    qc, oc = w_qkv.shape[1], w_out.shape[1]
    n_small = 4 + n_expert
    flat = lax.axis_index("dp") * n_expert + lax.axis_index("expert")
    got = whole_layer(
        n_dp, n_expert, tokens.reshape(seqs, 2, local_len // 2, dim), cotangent.reshape(seqs, local_len, dim), expert_ids.reshape(seqs, local_len),
        w_qkv.T.reshape(3, qc // 3, dim), w_out.T, ln_gains, ln_biases, router, w_up[0], w_down[0],
    )
    gq, gout, gs, output, grad_tokens, gu, gd = got[:7]
    grad_qkv, grad_out = gq.T, gout.T
    gs = lax.dynamic_slice(gs, (0, lax.rem(flat * oc, 128)), (n_small, oc))
    shape = tokens.shape
    return (output.astype(bf).reshape(shape), grad_tokens.reshape(shape), grad_qkv, grad_out, gs[0:2], gs[2:4], gs[4:].T, gu[None], gd[None])


def solution(mesh):
    in_specs = (
        P(None, "dp", "expert", None),
        P(None, "dp", "expert", None),
        P(None, "dp", "expert", None),
        P(None, ("dp", "expert")),
        P(None, ("dp", "expert")),
        P(None, ("dp", "expert")),
        P(None, ("dp", "expert")),
        P(("dp", "expert"), None),
        P("expert", "dp", None),
        P("expert", "dp", None),
    )
    out_specs = (
        P(None, "dp", "expert", None),
        P(None, "dp", "expert", None),
        P(None, ("dp", "expert")),
        P(None, ("dp", "expert")),
        P(None, ("dp", "expert")),
        P(None, ("dp", "expert")),
        P(("dp", "expert"), None),
        P("expert", "dp", None),
        P("expert", "dp", None),
    )
    n_expert, n_dp = mesh.shape["expert"], mesh.shape["dp"]
    chosen = fast_body if n_expert == 4 and n_dp % 4 == 0 and n_dp <= 8 else body
    return jax.shard_map(chosen, mesh=mesh, in_specs=in_specs, out_specs=out_specs, check_vma=False)
```

```python
import functools
import math

import jax
import jax.numpy as jnp
from jax import lax
from jax.experimental import pallas as pl
from jax.experimental.pallas import tpu as pltpu
from jax.sharding import PartitionSpec as P

HEADS = 12
FF = 3072
BLK = 256
MICRO = 2


epsilon = 1e-05
balance_coef = 8.0
neg_big = -1e30


def layer_norm(features, gain_vec, shift_vec):
    centre = features - jnp.mean(features, axis=-1, keepdims=True)
    spread = jnp.mean(centre * centre, axis=-1, keepdims=True)
    return centre * lax.rsqrt(spread + epsilon) * gain_vec + shift_vec


def gelu_exact(preact):
    return jax.nn.gelu(preact, approximate=False)


def fetch_all(w_qkv, w_out, ln_gains, ln_biases, router, w_up, w_down):
    dense_set = (
        lax.all_gather(w_qkv, ("dp", "expert"), axis=1, tiled=True),
        lax.all_gather(w_out, ("dp", "expert"), axis=1, tiled=True),
        lax.all_gather(ln_gains, ("dp", "expert"), axis=1, tiled=True),
        lax.all_gather(ln_biases, ("dp", "expert"), axis=1, tiled=True),
        lax.all_gather(router, ("dp", "expert"), axis=0, tiled=True),
    )
    expert_set = (
        lax.all_gather(w_up, "dp", axis=1, tiled=True),
        lax.all_gather(w_down, "dp", axis=1, tiled=True),
    )
    return tuple(dense_set) + tuple(expert_set)


def route_slots(expert_of, experts, capacity):
    seq_here, local_len = expert_of.shape
    matches = (expert_of[..., None] == lax.iota(jnp.int32, experts)).astype(jnp.int32)
    order_in = jnp.sum((jnp.cumsum(matches, axis=1) - matches) * matches, axis=-1)
    seq_index = lax.broadcasted_iota(jnp.int32, (seq_here, local_len), 0)
    target = (expert_of * (seq_here * capacity) + seq_index * capacity + order_in).reshape(-1)
    slot_table = jnp.full((experts * seq_here * capacity,), seq_here * local_len, jnp.int32)
    slot_table = slot_table.at[target].set(lax.iota(jnp.int32, seq_here * local_len))
    return (target, slot_table)


def to_slots(features, slot_table):
    flat_rows = features.reshape(-1, features.shape[-1])
    padded = jnp.concatenate(
        [flat_rows, jnp.zeros((1, flat_rows.shape[1]), flat_rows.dtype)], axis=0
    )
    return padded[slot_table]


def score_terms(
    queries, grad_rows, key_block, value_block, log_total, row_delta, allowed, score_scale
):
    scores = (
        jnp.einsum("sqhd,skhd->shqk", queries, key_block, preferred_element_type=jnp.float32)
        * score_scale
    )
    weights = jnp.where(allowed, jnp.exp(scores - log_total[..., None]), 0.0)
    grad_weights = jnp.einsum(
        "sqhd,skhd->shqk", grad_rows, value_block, preferred_element_type=jnp.float32
    )
    grad_scores = (weights * (grad_weights - row_delta[..., None]) * score_scale).astype(
        jnp.bfloat16
    )
    return (weights.astype(jnp.bfloat16), grad_scores)


def attention_forward(queries, key_rows, value_rows, query_pos, score_scale):
    seq_here, local_len, head_count, head_dim = queries.shape
    last_block = query_pos[local_len - 1] // BLK
    start_state = (
        jnp.full((seq_here, head_count, local_len), neg_big, jnp.float32),
        jnp.zeros((seq_here, head_count, local_len), jnp.float32),
        jnp.zeros((seq_here, local_len, head_count, head_dim), jnp.float32),
    )
    key_part = lax.all_gather(key_rows, "expert", axis=1, tiled=True)
    value_part = lax.all_gather(value_rows, "expert", axis=1, tiled=True)
    piece_len = key_part.shape[1]
    block_len = math.gcd(piece_len, 512)

    def attention_one_block(block_index, carried):
        within = block_index * block_len
        key_block = lax.dynamic_slice_in_dim(key_part, within, block_len, 1).reshape(
            seq_here, block_len, head_count, head_dim
        )
        value_block = lax.dynamic_slice_in_dim(value_part, within, block_len, 1).reshape(
            seq_here, block_len, head_count, head_dim
        )
        key_pos = within + lax.iota(jnp.int32, block_len)
        allowed = key_pos[None, :] // BLK <= query_pos[:, None] // BLK

        def attention_compute(current):
            run_max, run_sum, weighted = current
            scores = (
                jnp.einsum(
                    "sqhd,skhd->shqk", queries, key_block, preferred_element_type=jnp.float32
                )
                * score_scale
            )
            new_max = jnp.maximum(run_max, jnp.max(jnp.where(allowed, scores, neg_big), axis=-1))
            weights = jnp.where(allowed, jnp.exp(scores - new_max[..., None]), 0.0)
            factor = jnp.exp(run_max - new_max)
            run_sum = run_sum * factor + jnp.sum(weights, axis=-1)
            addition = jnp.einsum(
                "shqk,skhd->sqhd",
                weights.astype(jnp.bfloat16),
                value_block,
                preferred_element_type=jnp.float32,
            )
            weighted = weighted * jnp.swapaxes(factor, 1, 2)[..., None] + addition
            return (new_max, run_sum, weighted)

        return lax.cond(
            within // BLK <= last_block, attention_compute, lambda current: current, carried
        )

    run_max, run_sum, weighted = lax.fori_loop(
        0, piece_len // block_len, attention_one_block, start_state
    )
    log_total = run_max + jnp.log(run_sum)
    attended = weighted / jnp.swapaxes(run_sum, 1, 2)[..., None]
    return (log_total, attended)


def query_grads(
    queries, grad_rows, key_rows, value_rows, log_total, row_delta, query_pos, score_scale, seq_len
):
    seq_here, local_len, head_count, head_dim = queries.shape
    model_dim = head_count * head_dim
    last_block = query_pos[local_len - 1] // BLK
    start_query = jnp.zeros((seq_here, local_len, head_count, head_dim), jnp.float32)
    start_state = (start_query, jnp.zeros((seq_here, seq_len, 2 * model_dim), jnp.float32))
    key_part = lax.all_gather(key_rows, "expert", axis=1, tiled=True)
    value_part = lax.all_gather(value_rows, "expert", axis=1, tiled=True)
    piece_len = key_part.shape[1]
    block_len = math.gcd(piece_len, 512)

    def query_one_block(block_index, carried):
        within = block_index * block_len
        key_block = lax.dynamic_slice_in_dim(key_part, within, block_len, 1).reshape(
            seq_here, block_len, head_count, head_dim
        )
        value_block = lax.dynamic_slice_in_dim(value_part, within, block_len, 1).reshape(
            seq_here, block_len, head_count, head_dim
        )
        key_pos = within + lax.iota(jnp.int32, block_len)
        allowed = key_pos[None, :] // BLK <= query_pos[:, None] // BLK

        def query_compute(current):
            weights, grad_scores = score_terms(
                queries,
                grad_rows,
                key_block,
                value_block,
                log_total,
                row_delta,
                allowed,
                score_scale,
            )
            grad_query = current[0] + jnp.einsum(
                "shqk,skhd->sqhd", grad_scores, key_block, preferred_element_type=jnp.float32
            )
            grad_key = jnp.einsum(
                "shqk,sqhd->skhd", grad_scores, queries, preferred_element_type=jnp.float32
            ).reshape(seq_here, block_len, model_dim)
            grad_value = jnp.einsum(
                "shqk,sqhd->skhd", weights, grad_rows, preferred_element_type=jnp.float32
            ).reshape(seq_here, block_len, model_dim)
            old_rows = lax.dynamic_slice_in_dim(current[1], within, block_len, 1)
            summed = old_rows + jnp.concatenate([grad_key, grad_value], axis=-1)
            return (grad_query, lax.dynamic_update_slice_in_dim(current[1], summed, within, 1))

        return lax.cond(
            within // BLK <= last_block, query_compute, lambda current: current, carried
        )

    return lax.fori_loop(0, piece_len // block_len, query_one_block, start_state)


def body(tokens, cotangent, expert_ids, w_qkv, w_out, ln_gains, ln_biases, router, w_up, w_down):
    n_expert = lax.axis_size("expert")
    seq_part = lax.axis_index("expert")
    seq_here, local_len, model_dim = (tokens.shape[1], tokens.shape[2], tokens.shape[3])
    head_count = HEADS
    head_dim = model_dim // head_count
    score_scale = head_dim ** (-0.5)
    exp_dev = w_up.shape[0]
    experts = exp_dev * n_expert
    capacity = 2 * local_len // experts
    seq_len = local_len * n_expert
    query_pos = seq_part * local_len + lax.iota(jnp.int32, local_len)
    expert_range = lax.iota(jnp.int32, experts)
    all_ids = expert_ids[..., 0]
    local_counts = jnp.sum((all_ids[..., None] == expert_range).astype(jnp.float32), axis=(0, 1, 2))
    counts = lax.psum(local_counts, ("dp", "expert"))
    mean_load = jnp.sum(counts) / experts
    load_ratio = (counts - mean_load) / mean_load
    grad_qkv_w = jnp.zeros((model_dim, 3 * model_dim), jnp.float32)
    grad_out_w = jnp.zeros((model_dim, model_dim), jnp.float32)
    grad_gains = jnp.zeros((2, model_dim), jnp.float32)
    grad_shifts = jnp.zeros((2, model_dim), jnp.float32)
    grad_router = jnp.zeros((model_dim, experts), jnp.float32)
    grad_up = jnp.zeros((exp_dev, model_dim, FF), jnp.float32)
    grad_down = jnp.zeros((exp_dev, FF, model_dim), jnp.float32)
    outputs = []
    input_grads = []
    for micro_index in range(MICRO):
        fetched = fetch_all(w_qkv, w_out, ln_gains, ln_biases, router, w_up, w_down)
        qkv_full, out_full, gains_full, shifts_full, router_full, up_full, down_full = fetched
        gain_rows = gains_full.astype(jnp.float32)
        shift_rows = shifts_full.astype(jnp.float32)
        inputs = tokens[micro_index].astype(jnp.float32)
        expert_of = all_ids[micro_index]
        normed = layer_norm(inputs, gain_rows[0], shift_rows[0])
        normed_low = normed.astype(jnp.bfloat16)
        projected = jnp.einsum(
            "scd,de->sce", normed_low, qkv_full, preferred_element_type=jnp.float32
        ).astype(jnp.bfloat16)
        query_rows = projected[..., :model_dim]
        queries = query_rows.reshape(seq_here, local_len, head_count, head_dim)
        key_rows = projected[..., model_dim : 2 * model_dim]
        value_rows = projected[..., 2 * model_dim :]
        log_total, attended = attention_forward(
            queries, key_rows, value_rows, query_pos, score_scale
        )
        attended_low = attended.reshape(seq_here, local_len, model_dim).astype(jnp.bfloat16)
        middle = inputs + jnp.einsum(
            "scd,de->sce", attended_low, out_full, preferred_element_type=jnp.float32
        )
        mixed_low = layer_norm(middle, gain_rows[1], shift_rows[1]).astype(jnp.bfloat16)
        onehot = (expert_of[..., None] == expert_range).astype(jnp.float32)
        logits = jnp.einsum(
            "scd,de->sce", mixed_low, router_full, preferred_element_type=jnp.float32
        )
        gates = jax.nn.sigmoid(jnp.sum(logits * onehot, axis=-1))
        target, slot_table = route_slots(expert_of, experts, capacity)
        outgoing = to_slots(mixed_low, slot_table).reshape(
            n_expert, exp_dev, seq_here * capacity, model_dim
        )
        arrived = lax.all_to_all(outgoing, "expert", split_axis=0, concat_axis=0, tiled=True)
        preact = jnp.einsum("pesd,edf->pesf", arrived, up_full, preferred_element_type=jnp.float32)
        hidden = gelu_exact(preact).astype(jnp.bfloat16)
        result = jnp.einsum(
            "pesf,efd->pesd", hidden, down_full, preferred_element_type=jnp.float32
        ).astype(jnp.bfloat16)
        returned = lax.all_to_all(result, "expert", split_axis=0, concat_axis=0, tiled=True)
        expert_out = (
            returned.reshape(-1, model_dim)[target]
            .reshape(seq_here, local_len, model_dim)
            .astype(jnp.float32)
        )
        final = middle + gates[..., None] * expert_out
        outputs.append(final.astype(jnp.bfloat16))
        fetched = fetch_all(w_qkv, w_out, ln_gains, ln_biases, router, w_up, w_down)
        qkv_full, out_full, gains_full, shifts_full, router_full, up_full, down_full = fetched
        gain_rows = gains_full.astype(jnp.float32)
        shift_rows = shifts_full.astype(jnp.float32)
        grad_final = cotangent[micro_index].astype(jnp.float32)
        grad_gate = jnp.sum(grad_final * expert_out, axis=-1) + balance_coef * jnp.sum(
            onehot * load_ratio, axis=-1
        )
        grad_logit = grad_gate * gates * (1.0 - gates)
        grad_expert = (gates[..., None] * grad_final).astype(jnp.bfloat16)
        sent_grads = to_slots(grad_expert, slot_table).reshape(
            n_expert, exp_dev, seq_here * capacity, model_dim
        )
        grads_here = lax.all_to_all(sent_grads, "expert", split_axis=0, concat_axis=0, tiled=True)
        hidden_low = gelu_exact(preact).astype(jnp.bfloat16)
        grad_down = grad_down + jnp.einsum(
            "pesf,pesd->efd", hidden_low, grads_here, preferred_element_type=jnp.float32
        )
        grad_hidden = jnp.einsum(
            "pesd,efd->pesf", grads_here, down_full, preferred_element_type=jnp.float32
        )
        grad_pre = jax.vjp(gelu_exact, preact)[1](grad_hidden)[0].astype(jnp.bfloat16)
        grad_up = grad_up + jnp.einsum(
            "pesd,pesf->edf", arrived, grad_pre, preferred_element_type=jnp.float32
        )
        grad_arrived = jnp.einsum(
            "pesf,edf->pesd", grad_pre, up_full, preferred_element_type=jnp.float32
        ).astype(jnp.bfloat16)
        grads_back = lax.all_to_all(grad_arrived, "expert", split_axis=0, concat_axis=0, tiled=True)
        grad_mixed = (
            grads_back.reshape(-1, model_dim)[target]
            .reshape(seq_here, local_len, model_dim)
            .astype(jnp.float32)
        )
        router_cols = jnp.einsum("sce,de->scd", onehot, router_full.astype(jnp.float32))
        grad_mixed = grad_mixed + grad_logit[..., None] * router_cols
        grad_router = grad_router + jnp.einsum(
            "scd,sce->de", mixed_low.astype(jnp.float32), grad_logit[..., None] * onehot
        )
        second_back = jax.vjp(layer_norm, middle, gain_rows[1], shift_rows[1])[1]
        grad_middle, grad_gain_two, grad_shift_two = second_back(grad_mixed)
        grad_middle = grad_middle + grad_final
        grad_branch = grad_middle.astype(jnp.bfloat16)
        grad_out_w = grad_out_w + jnp.einsum(
            "scd,sce->de", attended_low, grad_branch, preferred_element_type=jnp.float32
        )
        grad_attended = jnp.einsum(
            "sce,de->scd", grad_branch, out_full, preferred_element_type=jnp.float32
        ).astype(jnp.bfloat16)
        grad_heads = grad_attended.reshape(seq_here, local_len, head_count, head_dim)
        row_delta = jnp.swapaxes(jnp.sum(grad_heads.astype(jnp.float32) * attended, axis=-1), 1, 2)
        folded = query_grads(
            queries,
            grad_heads,
            key_rows,
            value_rows,
            log_total,
            row_delta,
            query_pos,
            score_scale,
            seq_len,
        )
        grad_query = folded[0].reshape(seq_here, local_len, model_dim)
        key_value = lax.psum_scatter(
            folded[1].astype(jnp.bfloat16), "expert", scatter_dimension=1, tiled=True
        ).astype(jnp.float32)
        grad_key = key_value[..., :model_dim]
        grad_value = key_value[..., model_dim:]
        grad_projected = jnp.concatenate([grad_query, grad_key, grad_value], axis=-1).astype(
            jnp.bfloat16
        )
        grad_qkv_w = grad_qkv_w + jnp.einsum(
            "scd,sce->de", normed_low, grad_projected, preferred_element_type=jnp.float32
        )
        grad_normed = jnp.einsum(
            "sce,de->scd", grad_projected, qkv_full, preferred_element_type=jnp.float32
        )
        first_back = jax.vjp(layer_norm, inputs, gain_rows[0], shift_rows[0])[1]
        grad_inputs, grad_gain_one, grad_shift_one = first_back(grad_normed)
        grad_gains = grad_gains + jnp.stack([grad_gain_one, grad_gain_two])
        grad_shifts = grad_shifts + jnp.stack([grad_shift_one, grad_shift_two])
        input_grads.append(grad_middle + grad_inputs)
    dense_grads = (
        lax.psum_scatter(grad_qkv_w, ("dp", "expert"), scatter_dimension=1, tiled=True),
        lax.psum_scatter(grad_out_w, ("dp", "expert"), scatter_dimension=1, tiled=True),
        lax.psum_scatter(grad_gains, ("dp", "expert"), scatter_dimension=1, tiled=True),
        lax.psum_scatter(grad_shifts, ("dp", "expert"), scatter_dimension=1, tiled=True),
        lax.psum_scatter(grad_router, ("dp", "expert"), scatter_dimension=0, tiled=True),
    )
    expert_grads = (
        lax.psum_scatter(
            grad_up.astype(jnp.bfloat16), "dp", scatter_dimension=1, tiled=True
        ).astype(jnp.float32),
        lax.psum_scatter(
            grad_down.astype(jnp.bfloat16), "dp", scatter_dimension=1, tiled=True
        ).astype(jnp.float32),
    )
    return (jnp.stack(outputs), jnp.stack(input_grads)) + tuple(dense_grads) + tuple(expert_grads)


MESH_ID = pl.DeviceIdType.MESH
NT = (((1,), (1,)), ((), ()))
NN = (((1,), (0,)), ((), ()))
TN = (((0,), (0,)), ((), ()))
VMEM = pl.BlockSpec(memory_space=pltpu.VMEM)
HBM = pl.BlockSpec(memory_space=pl.ANY)


def mm(a, b, dims=NN):
    return lax.dot_general(a, b, dims, preferred_element_type=jnp.float32)


def normalised(v):
    centre = v - jnp.mean(v, axis=-1, keepdims=True)
    spread = jnp.mean(centre * centre, axis=-1, keepdims=True)
    inv = lax.rsqrt(spread + epsilon)
    return centre * inv, inv


def norm_back(grad_hat, hat, inv):
    return inv * (grad_hat - jnp.mean(grad_hat, axis=1, keepdims=True) - hat * jnp.mean(grad_hat * hat, axis=1, keepdims=True))


def add_into(target, other, step):
    def some(u, carry):
        rows = pl.ds(pl.multiple_of(u * step, step), step)
        target[rows, :] = (target[rows, :].astype(jnp.float32) + other[rows, :].astype(jnp.float32)).astype(target.dtype)
        return carry

    lax.fori_loop(0, target.shape[0] // step, some, 0)


class Place:
    def __init__(self, n_dp, n_ex):
        self.n_dp, self.n_ex, self.n_dev, self.n_z = n_dp, n_ex, n_dp * n_ex, n_dp // 2
        self.dp, self.ex = lax.axis_index("dp"), lax.axis_index("expert")
        self.z, self.core = self.dp // 2, self.dp % 2
        self.flat = self.dp * n_ex + self.ex

    def z_peer(self, d):
        return (self.z + d) % self.n_z

    def ex_peer(self, d):
        return (self.ex + d) % self.n_ex

    def on_z(self, z):
        return (z * 2 + self.core, self.ex)

    def on_ex(self, e):
        return (self.dp, e)

    def partner(self):
        return (self.z * 2 + 1 - self.core, self.ex)

    def numbered(self, t):
        return (t // self.n_ex, t % self.n_ex)


def entry_barrier(at):
    sem = pltpu.get_barrier_semaphore()

    def tell(i, carry):
        pl.semaphore_signal(sem, inc=1, device_id=at.numbered((at.flat + i) % at.n_dev), device_id_type=MESH_ID)
        return carry

    lax.fori_loop(1, at.n_dev, tell, 0)
    pl.semaphore_wait(sem, at.n_dev - 1)


class Wires:
    def __init__(self, send_sems, recv_sems):
        self.send_sems, self.recv_sems, self.used = send_sems, recv_sems, 0

    def take(self, n):
        base = self.used
        self.used = base + n
        return base

    def copy(self, i, src, dst, device):
        return pltpu.make_async_remote_copy(
            src_ref=src, dst_ref=dst, send_sem=self.send_sems.at[i], recv_sem=self.recv_sems.at[i],
            device_id=device, device_id_type=MESH_ID,
        )

    def all_came(self, i, blocks):
        pltpu.make_async_copy(blocks, blocks, self.recv_sems.at[i]).wait()

    def all_left(self, i, blocks):
        pltpu.make_async_copy(blocks, blocks, self.send_sems.at[i]).wait()


def layer_kernel(
    n_dp, n_ex, x_ref, cot_ref, ids_ref, wq_ref, wo_ref, gain_ref, bias_ref, router_ref, up_hbm, down_hbm,
    gq_ref, gout_ref, gsmall_ref, out_hbm, gtok_hbm, gup_hbm, gdown_hbm, up_full, down_full, q_hbm, k_hbm, v_hbm, xn_hbm, mix_hbm, mid_hbm, w_hbm, wo_hbm,
    outbox, inbox, work, gdt, gup, pin_dn, pin_up, zin_dn, zin_up, via_dn, via_up, rowbox, attr, gar,
    gob, gob_pair, gob_line, gob_mine, gob_plane, wt_a, gws, gws_pair, gws_line, gws_sum,
    small_b, wo_s, gq_in, small_all, small_in, small_out, smalls, tally, gate_s, slot_s, eid_s, lse, send_sems, recv_sems, load_sems,
):
    bf, f32 = jnp.bfloat16, jnp.float32
    at = Place(n_dp, n_ex)
    wires = Wires(send_sems, recv_sems)
    n_dev, n_z, ex, z, core = at.n_dev, at.n_z, at.ex, at.z, at.core
    seqs, dim = x_ref.shape[0], x_ref.shape[3]
    cap = x_ref.shape[2]
    local_len = 2 * cap
    total_len, width, slots = local_len * n_ex, dim // n_ex, n_ex * cap
    head_dim = dim // HEADS
    heads = width // head_dim
    piece, oc = wq_ref.shape[1], wo_ref.shape[0]
    shard, ff = up_hbm.shape
    half = down_hbm.shape[0]
    tile, mid_dim = ff // n_z, dim // 2
    scale = head_dim ** -0.5
    wt_b, wo_b = gws, gob
    lane = lax.broadcasted_iota(jnp.int32, (1, 128), 1).astype(f32)
    lane_head = lax.broadcasted_iota(jnp.int32, (1, width), 1) // head_dim
    peers = range(1, n_ex)

    small_out[...] = jnp.zeros(small_out.shape, f32)
    small_out[0:2, 0:oc] = gain_ref[...].astype(f32)
    small_out[2:4, 0:oc] = bias_ref[...].astype(f32)
    unit = jnp.where(lax.broadcasted_iota(jnp.int32, (oc, oc), 0) == lax.broadcasted_iota(jnp.int32, (oc, oc), 1), 1.0, 0.0).astype(bf)
    small_out[4 : 4 + n_ex, 0:oc] = mm(router_ref[...], unit, TN)
    held_rows = jnp.zeros((1, 128), f32)
    for m in range(seqs):
        eid_s[m] = jnp.broadcast_to(ids_ref[m : m + 1, :].astype(f32), (128, local_len)).T
        held_rows += jnp.sum(jnp.where(lane == eid_s[m], 1.0, 0.0), axis=0, keepdims=True)
    high = jnp.floor(held_rows * (1.0 / 16.0))
    small_b[0:8, :] = small_out[0:8, 0:128].astype(bf)
    row = lax.broadcasted_iota(jnp.int32, (8, 128), 0)
    small_b[8:16, :] = jnp.where(row == 0, high, jnp.where(row == 1, held_rows - 16.0 * high, 0.0)).astype(bf)
    for b in range(n_ex):
        wo_s[b] = wo_ref[:, b * width : (b + 1) * width]
    lines = range(1, n_z)
    entry_barrier(at)

    i_tok, i_back, i_out, i_ret, i_ga, i_part = (wires.take(seqs) for _ in range(6))

    def token_copy(m, d):
        return wires.copy(i_tok + m, x_ref.at[m], inbox.at[m, ex], at.on_ex(at.ex_peer(d)))

    def back_copy(m, d):
        peer = at.ex_peer(d)
        return wires.copy(i_back + m, rowbox.at[m, peer], attr.at[m, ex], at.on_ex(peer))

    def out_copy(m, d):
        peer = at.ex_peer(d)
        return wires.copy(i_out + m, outbox.at[m, peer], work.at[m, ex], at.on_ex(peer))

    def return_copy(m, d):
        peer = at.ex_peer(d)
        return wires.copy(i_ret + m, outbox.at[m, peer], inbox.at[m, ex], at.on_ex(peer))

    def ga_copy(m, d):
        peer = at.ex_peer(d)
        return wires.copy(i_ga + m, rowbox.at[m, peer], gar.at[m, ex], at.on_ex(peer))

    def part_copy(m, d):
        peer = at.ex_peer(d)
        return wires.copy(i_part + m, outbox.at[m, peer], inbox.at[m, ex], at.on_ex(peer))

    reach = [d for d in (2, 1) if d < n_z]

    def order(step):
        return (n_z - 1) * step % n_z

    relay = n_z > 3
    kinds = n_z + 1
    i_ag, i_agp = wires.take(5 * kinds), wires.take(5 * kinds)

    def ag_columns(t):
        return pl.ds(pl.multiple_of(t * tile, tile), tile)

    def ag_block(t, zz, cc, down):
        if down:
            return down_full.at[pl.ds(pl.multiple_of((zz * 2 + cc) * half, half), half), :]
        return up_full.at[t, pl.ds(pl.multiple_of((zz * 2 + cc) * shard, shard), shard), :]

    def ag_own(t, down):
        return down_hbm if down else up_hbm.at[:, ag_columns(t)]

    def ag_code(right, d, t, down):
        return (d if d != 1 or right else 4) * kinds + (n_z if down else t)

    def ag_copy(right, d, t, down):
        return wires.copy(i_ag + ag_code(right, d, t, down), ag_own(t, down), ag_block(t, z, core, down), at.on_z(z + d if right else z - d))

    def ag_relay(right, t, down):
        block = ag_block(t, z - 2 if right else z + 2, core, down)
        return wires.copy(i_ag + ag_code(right, 3, t, down), block, block, at.on_z(z + 1 if right else z - 1))

    def ag_pair(right, d, t, down):
        block = ag_block(t, z - d if right else z + d, core, down)
        return wires.copy(i_agp + ag_code(right, d, t, down), ag_own(t, down) if d == 0 else block, block, at.partner())

    def ag_sends(right, d):
        return z + d < n_z if right else z - d >= 0

    def ag_comes(right, d):
        return z - d >= 0 if right else z + d < n_z

    def ag_relays(right):
        return z == n_z - 2 if right else z == 1

    def ag_from(right, d, t, act):
        @pl.when(ag_comes(right, d))
        def _():
            act(False)
            pl.when((z - d if right else z + d) == t)(lambda: act(True))

    def ag_start(t):
        for d in reach:
            for right in (True, False):
                @pl.when(ag_sends(right, d))
                def _():
                    ag_copy(right, d, t, False).start()
                    pl.when(z == t)(ag_copy(right, d, t, True).start)
        ag_from(True, 0, t, lambda down: ag_pair(True, 0, t, down).start())

    def ag_pass(t):
        for d in reach:
            for right in (True, False):
                def act(down, right=right, d=d):
                    ag_copy(right, d, t, down).wait_recv()
                    if d == 2 and relay:
                        pl.when(ag_relays(right))(ag_relay(right, t, down).start)
                    ag_pair(right, d, t, down).start()

                ag_from(right, d, t, act)

    def ag_far(t):
        if relay:
            for right in (True, False):
                def act(down, right=right):
                    ag_copy(right, 3, t, down).wait_recv()
                    ag_pair(right, 3, t, down).start()

                ag_from(right, 3, t, act)

    far = [0] + sorted(reach) + ([3] if relay else [])

    def ag_ready(t):
        for d in far:
            for right in (True, False) if d else (True,):
                ag_from(right, d, t, lambda down, right=right, d=d: ag_pair(right, d, t, down).wait_recv())

    def ag_finish():
        def one(t, carry):
            for d in far:
                for right in (True, False) if d else (True,):
                    ag_from(right, d, t, lambda down, right=right, d=d: ag_pair(right, d, t, down).wait_send())
            for d in reach:
                for right in (True, False):
                    @pl.when(ag_sends(right, d))
                    def _():
                        ag_copy(right, d, t, False).wait_send()
                        pl.when(z == t)(ag_copy(right, d, t, True).wait_send)
            if relay:
                for right in (True, False):
                    @pl.when(ag_relays(right))
                    def _():
                        ag_relay(right, t, False).wait_send()
                        pl.when((z - 2 if right else z + 2) == t)(ag_relay(right, t, True).wait_send)
            return carry

        lax.fori_loop(0, n_z, one, 0)

    i_gp, i_gl, i_gv = wires.take(2 * n_z), wires.take(3 * kinds), wires.take(kinds)

    def pair_copies(t):
        return (
            wires.copy(i_gp + 2 * t, gdt.at[1 - core, t], pin_dn.at[t], at.partner()),
            wires.copy(i_gp + 2 * t + 1, gup.at[1 - core, t], pin_up.at[t], at.partner()),
        )

    def line_copy(t, src, dest, down):
        right, d = dest > src, abs(dest - src)
        block = gdt.at[core, t] if down else gup.at[core, t, dest]
        kind = n_z if down else t
        if d == 3:
            return wires.copy(i_gv + kind, block, via_dn if down else via_up.at[t], at.on_z(src + 1 if right else src - 1))
        slot = 2 if d == 2 else 0 if right else 1
        return wires.copy(
            i_gl + slot * kinds + kind, block, zin_dn.at[slot] if down else zin_up.at[slot, t], at.on_z(dest)
        )

    pairs_far_first = sorted(((s_, d_) for s_ in range(n_z) for d_ in range(n_z) if s_ != d_), key=lambda u: -abs(u[0] - u[1]))

    def held(src, dest):
        return relay and abs(dest - src) == 2 and src in (1, n_z - 2) and dest in (0, n_z - 1)

    def line_each(t, src, dest, act):
        act(False)
        pl.when(t == dest)(lambda: act(True))

    def fold(t):
        for c in pair_copies(t):
            c.wait_recv()
        add_into(gdt.at[core, t], pin_dn.at[t], 96)
        for zz in range(n_z):
            add_into(gup.at[core, t, zz], pin_up.at[t, zz], 48)
        for src, dest in pairs_far_first:
            if not held(src, dest):
                @pl.when(z == src)
                def _():
                    line_each(t, src, dest, lambda down: line_copy(t, src, dest, down).start())

    def add_far(t):
        for src, dest in pairs_far_first:
            if held(src, dest):
                @pl.when(z == src)
                def _():
                    def act(down):
                        line_copy(t, dest - 3 if dest > src else dest + 3, dest, down).wait_recv()
                        if down:
                            add_into(gdt.at[core, t], via_dn, 96)
                        else:
                            add_into(gup.at[core, t, dest], via_up.at[t], 48)
                        line_copy(t, src, dest, down).start()

                    line_each(t, src, dest, act)

    i_small = wires.take(1)

    def small_copy(i):
        return wires.copy(i_small, small_b, small_all.at[at.flat], at.numbered((at.flat + i) % n_dev))

    def each(n, act):
        def step(i, carry):
            act(i)
            return carry

        lax.fori_loop(1, n, step, 0)

    i_piece, i_line, i_pair, i_wo, i_wo2 = wires.take(3), wires.take(1), wires.take(2), wires.take(1), wires.take(1)

    def forward(q_v, k_v, v_v, xn_v, wide, att_acc, lse_acc, mid_v, mix_v, w_v, wo_v, up_s, down_s):
        stage = (
            pltpu.make_async_copy(up_hbm, up_s, load_sems.at[0]),
            pltpu.make_async_copy(down_hbm, down_s, load_sems.at[1]),
        )
        for c in stage:
            c.start()
        me_j = ex * n_dp + at.dp
        pieces = []
        for r in range(3):
            c = 3 * at.flat + r
            sec, j = c // n_dev, c % n_dev
            copy = wires.copy(i_piece + r, wq_ref.at[r], wt_a.at[sec], (j % n_dp, j // n_dp))
            away = j != me_j
            pl.when(away)(copy.start)
            pieces.append((copy, away, sec))
        each(n_dev, lambda i: small_copy(i).start())
        for m in range(seqs):
            for d in peers:
                token_copy(m, d).start()
        small_all[at.flat] = small_b[...]
        wo_b[core, ex, z] = wo_s[...]
        for m in range(seqs):
            inbox[m, ex] = x_ref[m]
        for r, (copy, away, sec) in enumerate(pieces):
            pl.when(away)(copy.wait_recv)

            @pl.when(jnp.logical_not(away))
            def _():
                wt_a[sec] = wq_ref[r]

        w_line = [wires.copy(i_line, wt_a, wt_b.at[core, z], at.on_z(at.z_peer(d))) for d in lines]
        for c in w_line:
            c.start()
        wo_line = [wires.copy(i_wo, wo_s, wo_b.at[core, ex, z], at.on_z(at.z_peer(d))) for d in lines]
        for c in wo_line:
            c.start()
        wt_b[core, z] = wt_a[...]
        for c in stage:
            c.wait()
        own = [
            pltpu.make_async_copy(up_s.at[:, t * tile : (t + 1) * tile], ag_block(t, z, core, False), load_sems.at[t % 2])
            for t in range(n_z)
        ] + [pltpu.make_async_copy(down_s, ag_block(0, z, core, True), load_sems.at[3])]
        for c in own[:2]:
            c.start()

        before = jnp.where(
            lax.broadcasted_iota(jnp.int32, (local_len, local_len), 1) < lax.broadcasted_iota(jnp.int32, (local_len, local_len), 0), 1.0, 0.0
        ).astype(bf)
        for m in range(seqs):
            named = jnp.where(lane == eid_s[m], 1.0, 0.0)
            earlier = jnp.sum(mm(before, named.astype(bf)) * named, axis=1, keepdims=True)
            slot_s[m] = eid_s[m] * cap + earlier

        wires.all_came(i_small, small_all.at[pl.ds(0, n_dev - 1)])
        smalls[...] = jnp.zeros(smalls.shape, f32)
        tally[...] = jnp.zeros(tally.shape, f32)
        for s in range(n_dev):
            block = small_all[s].astype(f32)
            tally[...] += block[8:16, :]
            lo = s * oc // 128 * 128
            spread = pltpu.roll(jnp.concatenate([block, jnp.zeros_like(block)], axis=1), s * oc - lo, 1)
            hi = min(lo + 256, dim)
            smalls[:, lo:hi] += spread[:, 0 : hi - lo]
        gain_one, shift_one = smalls[0:1, :], smalls[2:3, :]
        gain_two, shift_two = smalls[1:2, :], smalls[3:4, :]
        wires.all_came(i_line, wt_b.at[0, pl.ds(0, n_z - 1)])
        w_pair = wires.copy(i_pair, wt_b.at[core], wt_b.at[core], at.partner())
        w_pair.start()
        wires.all_came(i_wo, wo_b.at[0, 0, pl.ds(0, n_z - 1)])
        for step in range(min(2, n_z)):
            ag_start(order(step))
        wo_plane = [wires.copy(i_wo2, wo_b.at[core, ex], wo_b.at[core, ex], at.on_ex(at.ex_peer(d))) for d in peers]
        for c in wo_plane:
            c.start()
        w_pair.wait_recv()
        for sec in range(3):
            for zz in range(n_z):
                for cc in range(2):
                    row = (zz * 2 + cc) * piece
                    wide[row : row + piece, :] = wt_b[cc, zz, sec].astype(f32)
            w_v[sec] = wide[0:width, :].astype(bf)

        def project(m):
            def one(d, carry):
                src = (ex - d + n_ex) % n_ex

                @pl.when(d == 1)
                def _():
                    wires.all_came(i_tok + m, inbox.at[m, pl.ds(0, n_ex - 1)])

                rows = pl.ds(pl.multiple_of(src * local_len, local_len), local_len)
                hat, _ = normalised(inbox[m, src].reshape(local_len, dim).astype(f32))
                low = (hat * gain_one + shift_one).astype(bf)
                xn_v[rows, :] = low
                q_v[m, rows, :] = mm(low, w_v[0], NT).astype(bf)
                k_v[m, rows, :] = mm(low, w_v[1], NT).astype(bf)
                v_v[m, rows, :] = mm(low, w_v[2], NT).astype(bf)
                return carry

            lax.fori_loop(0, n_ex, one, 0)

        def attend(m):
            for i in range(n_ex):
                end = (i + 1) * local_len
                here = slice(i * local_len, end)

                def one_head(h, carry):
                    mine = lane_head == h
                    qb = q_v[m, here, :]
                    s = mm(jnp.where(mine, qb * scale, jnp.zeros_like(qb)), k_v[m, 0:end, :], NT)
                    top = jnp.max(s, axis=-1, keepdims=True)
                    e = jnp.exp(s - top)
                    total = jnp.sum(e, axis=-1, keepdims=True)
                    p = (e * (1.0 / total)).astype(bf)
                    att_acc[...] = jnp.where(mine, mm(p, v_v[m, 0:end, :]), att_acc[...])
                    lse_acc[...] = jnp.where(lane == h.astype(f32), top + jnp.log(total), lse_acc[...])
                    return carry

                lax.fori_loop(0, heads, one_head, 0)
                rowbox[m, i] = att_acc[...].astype(bf)
                lse[m, :, here] = lse_acc[...].T[0:8, :]
            for d in peers:
                back_copy(m, d).start()
            attr[m, ex] = rowbox[m, ex]

        def route(m):
            wires.all_came(i_back + m, attr.at[m, pl.ds(0, n_ex - 1)])
            mid = x_ref[m].reshape(local_len, dim).astype(f32)
            for b in range(n_ex):
                mid += mm(attr[m, b], wo_v[b], NT)
            mid_v[m] = mid
            hat, _ = normalised(mid)
            mixed = (hat * gain_two + shift_two).astype(bf)
            mix_v[m] = mixed
            logits = mm(mixed, smalls[...].astype(bf), NT)
            mine = lax.broadcasted_iota(jnp.int32, logits.shape, 1).astype(f32) == eid_s[m][:, 0:1] + 4.0
            gate = jax.nn.sigmoid(jnp.sum(jnp.where(mine, logits, 0.0), axis=1, keepdims=True))
            gate_s[m] = jnp.broadcast_to(gate, (local_len, 128))
            scaled = (gate * cot_ref[m].astype(f32)).astype(bf)
            place = jnp.where(
                slot_s[m].T[0:1, :] == lax.broadcasted_iota(jnp.int32, (slots, local_len), 0).astype(f32), 1.0, 0.0
            ).astype(bf)
            outbox[m, :, 0] = mm(place, mixed).astype(bf).reshape(n_ex, cap, dim)
            outbox[m, :, 1] = mm(place, scaled).astype(bf).reshape(n_ex, cap, dim)
            for d in peers:
                out_copy(m, d).start()
            work[m, ex] = outbox[m, ex]

        att_acc[...] = jnp.zeros(att_acc.shape, f32)
        lse_acc[...] = jnp.zeros(lse_acc.shape, f32)

        def xn_out(m):
            return pltpu.make_async_copy(xn_v, xn_hbm.at[m], load_sems.at[2])

        project(0)
        xn_out(0).start()
        attend(0)
        for i, c in enumerate(own):
            if i >= 2:
                if i < n_z:
                    own[i - 2].wait()
                c.start()
        for c in own[n_z - 2 :]:
            c.wait()
        for m in range(1, seqs):
            xn_out(m - 1).wait()
            project(m)
            xn_out(m).start()
            if m == 1:
                ag_pass(order(0))
                for step in range(2, n_z - 1):
                    ag_start(order(step))
            attend(m)
        ag_pass(order(1))
        if n_z > 2:
            ag_start(order(n_z - 1))
        wires.all_came(i_wo2, wo_b.at[0, pl.ds(0, n_ex - 1)])
        wo_pair = wires.copy(i_pair + 1, wo_b.at[core], wo_b.at[core], at.partner())
        wo_pair.start()
        wo_pair.wait_recv()
        for b in range(n_ex):
            for s in range(n_dev):
                wide[s * oc : (s + 1) * oc, 0:width] = wo_b[s // n_ex % 2, s % n_ex, s // n_ex // 2, b].astype(f32)
            wo_v[b] = wide[0:dim, 0:width].astype(bf)
        for m in range(seqs):
            route(m)
        xn_out(seqs - 1).wait()
        keep = [
            pltpu.make_async_copy(src, dst, load_sems.at[i])
            for i, (src, dst) in enumerate(((q_v, q_hbm), (k_v, k_hbm), (v_v, v_hbm), (mid_v, mid_hbm), (mix_v, mix_hbm), (w_v, w_hbm), (wo_v, wo_hbm)))
        ]
        for c in keep:
            c.start()
        for m in range(seqs):
            wires.all_left(i_back + m, attr.at[m, pl.ds(0, n_ex - 1)])
            wires.all_left(i_tok + m, inbox.at[m, pl.ds(0, n_ex - 1)])
        for copy, away, _ in pieces:
            pl.when(away)(copy.wait_send)
        wires.all_left(i_small, small_all.at[pl.ds(0, n_dev - 1)])
        wires.all_left(i_line, wt_b.at[0, pl.ds(0, n_z - 1)])
        wires.all_left(i_wo, wo_b.at[0, 0, pl.ds(0, n_z - 1)])
        wires.all_left(i_wo2, wo_b.at[0, pl.ds(0, n_ex - 1)])
        for c in (w_pair, wo_pair):
            c.wait_send()
        for c in keep:
            c.wait()

    pl.run_scoped(
        forward,
        pltpu.VMEM((seqs, total_len, width), bf), pltpu.VMEM((seqs, total_len, width), bf), pltpu.VMEM((seqs, total_len, width), bf),
        pltpu.VMEM((total_len, dim), bf), pltpu.VMEM((dim, dim), f32),
        pltpu.VMEM((local_len, width), f32), pltpu.VMEM((local_len, 128), f32),
        pltpu.VMEM((seqs, local_len, dim), f32), pltpu.VMEM((seqs, local_len, dim), bf),
        pltpu.VMEM((3, width, dim), bf), pltpu.VMEM((n_ex, dim, width), bf),
        pltpu.VMEM((shard, ff), bf), pltpu.VMEM((half, dim), bf),
    )

    def experts(up_t, down_t, res_acc, gar_acc, hid, gpre, x_t, g_t):
        sub = 256 if tile % 256 == 0 else tile
        pair = n_z - 2

        def loads(step, slot):
            return (
                pltpu.make_async_copy(up_full.at[order(step)], up_t.at[slot], load_sems.at[2 * slot]),
                pltpu.make_async_copy(down_full.at[ag_columns(order(step)), :], down_t.at[slot], load_sems.at[2 * slot + 1]),
            )

        def fetch(step, slot):
            ag_far(order(step))
            ag_ready(order(step))
            for c in loads(step, slot):
                c.start()

        fetch(0, 0)

        def one_round(k, carry):
            per = jnp.where(k == pair, 2, 1)

            def one(q, q_carry):
                m, step = q // per, k + q % per
                j = step % 2
                mine = pl.ds(pl.multiple_of(m * slots, slots), slots)

                @pl.when(m == 0)
                def _():
                    for c in loads(step, j):
                        c.wait()

                @pl.when(step == 0)
                def _():
                    wires.all_came(i_out + m, work.at[m, pl.ds(0, n_ex - 1)])
                    wires.all_left(i_out + m, work.at[m, pl.ds(0, n_ex - 1)])
                    res_acc[m] = jnp.zeros((slots, dim), f32)
                    gar_acc[m] = jnp.zeros((slots, dim), f32)

                def one_sub(u, c_):
                    cols = pl.ds(pl.multiple_of(u * sub, sub), sub)
                    rows = work[m, :, 0].reshape(slots, dim)
                    grads = work[m, :, 1].reshape(slots, dim)
                    pre = mm(rows, up_t[j, :, cols])
                    cdf = 0.5 * (1.0 + lax.erf(pre * (2.0 ** -0.5)))
                    hidden = (pre * cdf).astype(bf)
                    slope = cdf + pre * jnp.exp(-0.5 * pre * pre) * ((2.0 * math.pi) ** -0.5)
                    hid[j, mine, cols] = hidden
                    res_acc[m] += mm(hidden, down_t[j, cols, :])
                    low = (mm(grads, down_t[j, cols, :], NT) * slope).astype(bf)
                    gpre[j, mine, cols] = low
                    gar_acc[m] += mm(low, up_t[j, :, cols], NT)
                    return c_

                lax.fori_loop(0, tile // sub, one_sub, 0)

                @pl.when(step == n_z - 1)
                def _():
                    outbox[m, :, 0] = res_acc[m].astype(bf).reshape(n_ex, cap, dim)
                    outbox[m, :, 1] = gar_acc[m].astype(bf).reshape(n_ex, cap, dim)
                    for d in peers:
                        return_copy(m, d).start()
                    inbox[m, ex] = outbox[m, ex]

                for ahead in range(2, n_z):
                    @pl.when((k == ahead - 2) & (q == 0))
                    def _():
                        ag_pass(order(ahead))

                pl.when((k == pair) & (q == 0))(lambda: fetch(n_z - 1, (n_z - 1) % 2))
                for late in range(n_z - 2):
                    pl.when((k == late + 1) & (q == 0))(lambda: fold(order(late)))
                if n_z > 3:
                    pl.when((k == pair) & (q == seqs))(lambda: add_far(order(0)))
                return q_carry

            lax.fori_loop(0, seqs * per, one, 0)

            @pl.when(k == 0)
            def _():
                for s in range(seqs):
                    lanes = slice(s * slots, (s + 1) * slots)
                    x_t[:, lanes] = work[s, :, 0].reshape(slots, dim).T
                    g_t[:, lanes] = work[s, :, 1].reshape(slots, dim).T

            def weight_grads(jj, jj_carry):
                step = k + jj
                j, t = step % 2, order(step)
                pl.when(k < pair)(lambda: fetch(step + 1, 1 - j))

                def some(u, c_):
                    at_rows = pl.ds(pl.multiple_of(u * mid_dim, mid_dim), mid_dim)
                    up_grad = mm(x_t[at_rows, :], gpre[j]).astype(bf)
                    for s in range(n_z):
                        gup[s % 2, t, u * (n_z // 2) + s // 2] = up_grad[s * shard : (s + 1) * shard, :]
                    down_grad = mm(g_t[at_rows, :], hid[j]).astype(bf)
                    for c in range(2):
                        gdt[c, t, at_rows, :] = down_grad[:, c * half : (c + 1) * half]
                    return c_

                lax.fori_loop(0, 2, some, 0)
                for c in pair_copies(t):
                    c.start()
                pl.when(step == n_z - 1)(lambda: fold(order(n_z - 2)))
                return jj_carry

            lax.fori_loop(0, per, weight_grads, 0)
            return carry

        lax.fori_loop(0, pair + 1, one_round, 0)

    every = seqs * slots
    pl.run_scoped(
        experts,
        pltpu.VMEM((2, dim, tile), bf), pltpu.VMEM((2, tile, dim), bf),
        pltpu.VMEM((seqs, slots, dim), f32), pltpu.VMEM((seqs, slots, dim), f32),
        pltpu.VMEM((2, every, tile), bf), pltpu.VMEM((2, every, tile), bf),
        pltpu.VMEM((dim, every), bf), pltpu.VMEM((dim, every), bf),
    )
    fold(order(n_z - 1))
    ag_finish()

    gain_one, gain_two = smalls[0:1, :], smalls[1:2, :]
    counts = jnp.where(lane < n_ex, 16.0 * tally[0:1, :] + tally[1:2, :], 0.0)
    mean_load = jnp.sum(counts, axis=1, keepdims=True) / n_ex
    load_ratio = (counts - mean_load) / mean_load
    small_out[...] = jnp.zeros(small_out.shape, f32)
    i_gob, i_gw = wires.take(3), wires.take(5)
    gob_pair_copy = wires.copy(i_gob, gob.at[1 - core], gob_pair, at.partner())

    def gob_plane_copy(d):
        peer = at.ex_peer(d)
        return wires.copy(i_gob + 1, gob.at[core, peer], gob_plane.at[d - 1], at.on_ex(peer))

    def gob_line_copy(d):
        peer = at.z_peer(d)
        return wires.copy(i_gob + 2, gob_mine.at[peer], gob_line.at[d - 1], at.on_z(peer))

    gws_pair_copy = wires.copy(i_gw, gws.at[1 - core], gws_pair, at.partner())

    def gws_line_copy(d):
        peer = at.z_peer(d)
        return wires.copy(i_gw + 1, gws.at[core, peer], gws_line.at[d - 1], at.on_z(peer))

    me_j = ex * n_dp + at.dp
    finals = []
    for sec in range(3):
        c = sec * n_dev + me_j
        owner, r = c // 3, c % 3
        copy = wires.copy(i_gw + 2 + r, gws_sum.at[sec], gq_in.at[r], at.numbered(owner))
        finals.append((copy, owner != at.flat, sec, r))

    def backward(gb_t, q_v, k_v, v_v, xn_v, mix_v, mid_v, w_v, wo_v, dq, dk, dv, gw, gtok, out_v):
        pairs = ((wo_hbm, wo_v), (mix_hbm, mix_v), (mid_hbm, mid_v), (w_hbm, w_v), (q_hbm, q_v), (k_hbm, k_v), (v_hbm, v_v))
        brought = [pltpu.make_async_copy(src, dst, load_sems.at[i]) for i, (src, dst) in enumerate(pairs)]
        for c in brought:
            c.start()
        for c in brought:
            c.wait()

        def head(m):
            wires.all_came(i_ret + m, inbox.at[m, pl.ds(0, n_ex - 1)])
            wires.all_left(i_ret + m, inbox.at[m, pl.ds(0, n_ex - 1)])
            def some_rows(u, carry):
                at_rows = pl.ds(pl.multiple_of(u * 128, 128), 128)
                place = jnp.where(
                    slot_s[m, at_rows, 0:1] == lax.broadcasted_iota(jnp.int32, (128, slots), 1).astype(f32), 1.0, 0.0
                ).astype(bf)
                expert_out = mm(place, inbox[m, :, 0].reshape(slots, dim))
                gate, named = gate_s[m, at_rows, 0:1], eid_s[m, at_rows, :]
                cot = cot_ref[m, at_rows, :].astype(f32)
                out_v[m, at_rows, :] = (mid_v[m, at_rows, :] + gate * expert_out).astype(bf)
                grad_gate = jnp.sum(cot * expert_out, axis=1, keepdims=True) + balance_coef * jnp.sum(
                    jnp.where(lane == named, load_ratio, 0.0), axis=1, keepdims=True
                )
                grad_logit = grad_gate * gate * (1.0 - gate)
                grad_mixed = mm(place, inbox[m, :, 1].reshape(slots, dim))
                mixed = mix_v[m, at_rows, :].astype(f32)
                for e in range(n_ex):
                    routed = jnp.where(named[:, 0:1] == float(e), grad_logit, 0.0)
                    grad_mixed += routed * smalls[4 + e : 5 + e, :]
                    small_out[4 + e : 5 + e, 0:dim] += jnp.sum(routed * mixed, axis=0, keepdims=True)
                hat, inv = normalised(mid_v[m, at_rows, :])
                small_out[1:2, 0:dim] += jnp.sum(grad_mixed * hat, axis=0, keepdims=True)
                small_out[3:4, 0:dim] += jnp.sum(grad_mixed, axis=0, keepdims=True)
                grad_middle = norm_back(grad_mixed * gain_two, hat, inv) + cot
                gtok[m, at_rows, :] = grad_middle
                branch = grad_middle.astype(bf)
                for e in range(n_ex):
                    rowbox[m, e, at_rows, :] = mm(branch, wo_v[e]).astype(bf)
                gb_t[m, :, at_rows] = branch.T
                return carry

            lax.fori_loop(0, local_len // 128, some_rows, 0)
            for d in peers:
                ga_copy(m, d).start()
            gar[m, ex] = rowbox[m, ex]

        head(0)
        if n_z > 2:
            add_far(order(n_z - 3))
        for m in range(1, seqs):
            head(m)
        wrote = pltpu.make_async_copy(out_v, out_hbm, load_sems.at[0])
        wrote.start()

        for b in range(n_ex):
            total = mm(gb_t[0], attr[0, b])
            for m in range(1, seqs):
                total += mm(gb_t[m], attr[m, b])
            for s in range(n_dev):
                gob[s // n_ex % 2, s % n_ex, s // n_ex // 2, b] = total[s * oc : (s + 1) * oc].astype(bf)
        gob_pair_copy.start()
        gw[...] = jnp.zeros(gw.shape, f32)

        def gob_up():
            gob_pair_copy.wait()
            for e in range(n_ex):
                for zz in range(n_z):
                    gob[core, e, zz] = (gob[core, e, zz].astype(f32) + gob_pair[e, zz].astype(f32)).astype(bf)
            for d in peers:
                gob_plane_copy(d).start()

        def attention_back(m, first=lambda: None):
            xn_copy = pltpu.make_async_copy(xn_hbm.at[m], xn_v, load_sems.at[7])
            xn_copy.start()
            wires.all_came(i_ga + m, gar.at[m, pl.ds(0, n_ex - 1)])
            wires.all_left(i_ga + m, gar.at[m, pl.ds(0, n_ex - 1)])
            first()
            dk[...] = jnp.zeros(dk.shape, f32)
            dv[...] = jnp.zeros(dv.shape, f32)
            dq[...] = jnp.zeros(dq.shape, f32)
            for i in reversed(range(n_ex)):
                end = (i + 1) * local_len
                here = slice(i * local_len, end)

                def one_head(h, carry):
                    mine = lane_head == h
                    qb, ga = q_v[m, here, :], gar[m, i]
                    q_h = jnp.where(mine, qb * scale, jnp.zeros_like(qb))
                    ga_h = jnp.where(mine, ga, jnp.zeros_like(ga))
                    kk = k_v[m, 0:end, :]
                    p = jnp.exp(mm(kk, q_h, NT) - lse[m, pl.ds(h, 1), here])
                    dp = mm(v_v[m, 0:end, :], ga_h, NT)
                    delta = jnp.sum(p * dp, axis=0, keepdims=True)
                    ds = (p * (dp - delta)).astype(bf)
                    dv[0:end, :] += mm(p.astype(bf), ga_h)
                    dk[0:end, :] += mm(ds, q_h)
                    dq[here, :] += jnp.where(mine, mm(ds, kk, TN) * scale, 0.0)
                    return carry

                lax.fori_loop(0, heads, one_head, 0)
                part = mm(dq[here, :].astype(bf), w_v[0]) + mm(dk[here, :].astype(bf), w_v[1]) + mm(dv[here, :].astype(bf), w_v[2])
                outbox[m, i] = part.astype(bf).reshape(2, cap, dim)
                for d in peers:
                    pl.when(at.ex_peer(d) == i)(part_copy(m, d).start)
            inbox[m, ex] = outbox[m, ex]
            xn_copy.wait()
            for sec, g in enumerate((dq, dk, dv)):
                gw[sec] += mm(g[...].astype(bf), xn_v[...], TN)

        attention_back(0, gob_up)
        if n_z > 2:
            add_far(order(n_z - 2))
        wires.all_came(i_gob + 1, gob_plane)
        wires.all_left(i_gob + 1, gob_plane)
        for zz in range(n_z):
            total = gob[core, ex, zz].astype(f32)
            for d in peers:
                total += gob_plane[d - 1, zz].astype(f32)
            gob_mine[zz] = total.astype(bf)
        for d in lines:
            gob_line_copy(d).start()
        for m in range(1, seqs):
            attention_back(m)
        add_far(order(n_z - 1))
        for sec in range(3):
            for j in range(n_dp):
                gws[j % 2, j // 2, sec] = gw[sec, j * piece : (j + 1) * piece, :].astype(bf)
        gws_pair_copy.start()
        gws_pair_copy.wait()
        gws[core] = (gws[core].astype(f32) + gws_pair[...].astype(f32)).astype(bf)
        for d in lines:
            gws_line_copy(d).start()

        def tail(m):
            wires.all_came(i_part + m, inbox.at[m, pl.ds(0, n_ex - 1)])
            wires.all_left(i_part + m, inbox.at[m, pl.ds(0, n_ex - 1)])
            grad_normed = jnp.zeros((local_len, dim), f32)
            for e in range(n_ex):
                grad_normed += inbox[m, e].reshape(local_len, dim).astype(f32)
            hat, inv = normalised(x_ref[m].reshape(local_len, dim).astype(f32))
            small_out[0:1, 0:dim] += jnp.sum(grad_normed * hat, axis=0, keepdims=True)
            small_out[2:3, 0:dim] += jnp.sum(grad_normed, axis=0, keepdims=True)
            gtok[m] += norm_back(grad_normed * gain_one, hat, inv)

        for m in range(seqs - 1):
            tail(m)
        wires.all_came(i_gw + 1, gws_line)
        wires.all_left(i_gw + 1, gws_line)
        total = gws[core, z].astype(f32)
        for d in lines:
            total += gws_line[d - 1].astype(f32)
        gws_sum[...] = total.astype(bf)
        for copy, away, sec, r in finals:
            pl.when(away)(copy.start)
        tail(seqs - 1)
        wrote.wait()
        wrote_tok = pltpu.make_async_copy(gtok, gtok_hbm, load_sems.at[0])
        wrote_tok.start()
        wrote_tok.wait()

    pl.run_scoped(
        backward,
        pltpu.VMEM((seqs, dim, local_len), bf),
        pltpu.VMEM((seqs, total_len, width), bf), pltpu.VMEM((seqs, total_len, width), bf), pltpu.VMEM((seqs, total_len, width), bf),
        pltpu.VMEM((total_len, dim), bf), pltpu.VMEM((seqs, local_len, dim), bf), pltpu.VMEM((seqs, local_len, dim), f32),
        pltpu.VMEM((3, width, dim), bf), pltpu.VMEM((n_ex, dim, width), bf),
        pltpu.VMEM((total_len, width), f32), pltpu.VMEM((total_len, width), f32), pltpu.VMEM((total_len, width), f32),
        pltpu.VMEM((3, width, dim), f32),
        pltpu.VMEM((seqs, local_len, dim), f32), pltpu.VMEM((seqs, local_len, dim), bf),
    )

    i_last = wires.take(1)

    def window(t):
        return pl.ds(pl.multiple_of(t * oc // 128 * 128, 128), 256)

    def last_copy(i):
        t = (at.flat + i) % n_dev
        return wires.copy(i_last, small_out.at[:, window(t)], small_in.at[at.flat], at.numbered(t))

    each(n_dev, lambda i: last_copy(i).start())
    small_in[at.flat] = small_out[:, window(at.flat)]
    wires.all_came(i_gob + 2, gob_line)
    wires.all_left(i_gob + 2, gob_line)
    total = gob_mine[z].astype(f32)
    for d in lines:
        total += gob_line[d - 1].astype(f32)
    gout_ref[...] = jnp.concatenate([total[b] for b in range(n_ex)], axis=1)

    def settle(up_v, down_v):
        def done(t, carry):
            for c in pair_copies(t):
                c.wait_send()
            for src, dest in pairs_far_first:
                pl.when(z == src)(lambda: line_each(t, src, dest, lambda down: line_copy(t, src, dest, down).wait_send()))
                if abs(dest - src) < 3:
                    pl.when(z == dest)(lambda: line_each(t, src, dest, lambda down: line_copy(t, src, dest, down).wait_recv()))
            return carry

        lax.fori_loop(0, n_z, done, 0)
        for dest in range(n_z):
            came = [s for s in range(n_z) if s != dest and abs(s - dest) < 3]
            places = [2 if abs(s - dest) == 2 else 0 if dest > s else 1 for s in came]

            @pl.when(z == dest)
            def _():
                def some_up(t, carry):
                    total = gup[core, t, dest].astype(f32)
                    for s in places:
                        total += zin_up[s, t].astype(f32)
                    up_v[:, ag_columns(t)] = total
                    return carry

                def some_down(u, carry):
                    at_rows = pl.ds(pl.multiple_of(u * 128, 128), 128)
                    total = gdt[core, dest, at_rows, :].astype(f32)
                    for s in places:
                        total += zin_dn[s, at_rows, :].astype(f32)
                    down_v[:, at_rows] = total.T
                    return carry

                lax.fori_loop(0, n_z, some_up, 0)
                lax.fori_loop(0, dim // 128, some_down, 0)

        wrote = (pltpu.make_async_copy(up_v, gup_hbm, load_sems.at[0]), pltpu.make_async_copy(down_v, gdown_hbm, load_sems.at[1]))
        for c in wrote:
            c.start()
        for c in wrote:
            c.wait()

    pl.run_scoped(settle, pltpu.VMEM((shard, ff), f32), pltpu.VMEM((half, dim), f32))
    for copy, away, sec, r in finals:
        @pl.when(away)
        def _():
            copy.wait()

        @pl.when(jnp.logical_not(away))
        def _():
            gq_in[r] = gws_sum[sec]

    for r in range(3):
        gq_ref[r * piece : (r + 1) * piece, :] = gq_in[r].astype(f32)
    wires.all_came(i_last, small_in.at[pl.ds(0, n_dev - 1)])
    wires.all_left(i_last, small_in.at[pl.ds(0, n_dev - 1)])
    total = jnp.zeros((8, 256), f32)
    for s in range(n_dev):
        total += small_in[s]
    gsmall_ref[...] = total


def whole_layer(n_dp, n_ex, x, cot, ids, wq, wo, gains, biases, router, w_up, w_down):
    bf, f32 = jnp.bfloat16, jnp.float32
    seqs, local_len, dim = cot.shape
    width, total_len, n_z, n_dev = dim // n_ex, local_len * n_ex, n_dp // 2, n_dp * n_ex
    cap = x.shape[2]
    shard, ff = w_up.shape
    half = w_down.shape[0]
    piece, oc, tile = wq.shape[1], wo.shape[0], ff // n_z
    vmem_outs = [((3 * piece, dim), f32), ((oc, dim), f32), ((8, 256), f32)]
    hbm_outs = [
        ((seqs, local_len, dim), bf), ((seqs, local_len, dim), f32), ((shard, ff), f32), ((half, dim), f32),
        ((n_z, dim, ff // n_z), bf), ((ff, dim), bf),
        ((seqs, total_len, width), bf), ((seqs, total_len, width), bf), ((seqs, total_len, width), bf), ((seqs, total_len, dim), bf),
        ((seqs, local_len, dim), bf), ((seqs, local_len, dim), f32), ((3, width, dim), bf), ((n_ex, dim, width), bf),
    ]
    box = pltpu.VMEM((seqs, n_ex, 2, cap, dim), bf)
    rows = pltpu.VMEM((seqs, n_ex, local_len, width), bf)
    n_sems = 2 + 6 * seqs + 14 * (n_z + 1) + 2 * n_z + 8 + 8
    sems = pltpu.SemaphoreType.DMA((n_sems,))
    return pl.pallas_call(
        functools.partial(layer_kernel, n_dp, n_ex),
        out_shape=[jax.ShapeDtypeStruct(s, d) for s, d in vmem_outs + hbm_outs],
        in_specs=[VMEM] * 8 + [HBM] * 2,
        out_specs=[VMEM] * len(vmem_outs) + [HBM] * len(hbm_outs),
        scratch_shapes=[
            box, box, box,
            pltpu.VMEM((2, n_z, dim, half), bf), pltpu.VMEM((2, n_z, n_z, shard, tile), bf),
            pltpu.VMEM((n_z, dim, half), bf), pltpu.VMEM((n_z, n_z, shard, tile), bf),
            pltpu.VMEM((3, dim, half), bf), pltpu.VMEM((3, n_z, shard, tile), bf),
            pltpu.VMEM((dim, half), bf), pltpu.VMEM((n_z, shard, tile), bf),
            rows, rows, rows,
            pltpu.VMEM((2, n_ex, n_z, n_ex, oc, width), bf), pltpu.VMEM((n_ex, n_z, n_ex, oc, width), bf),
            pltpu.VMEM((n_z - 1, n_ex, oc, width), bf), pltpu.VMEM((n_z, n_ex, oc, width), bf), pltpu.VMEM((n_ex - 1, n_z, n_ex, oc, width), bf),
            pltpu.VMEM((3, piece, dim), bf), pltpu.VMEM((2, n_z, 3, piece, dim), bf), pltpu.VMEM((n_z, 3, piece, dim), bf),
            pltpu.VMEM((n_z - 1, 3, piece, dim), bf), pltpu.VMEM((3, piece, dim), bf),
            pltpu.VMEM((16, 128), bf), pltpu.VMEM((n_ex, oc, width), bf), pltpu.VMEM((3, piece, dim), bf),
            pltpu.VMEM((n_dev, 16, 128), bf), pltpu.VMEM((n_dev, 8, 256), f32), pltpu.VMEM((8, dim + 256), f32),
            pltpu.VMEM((16, dim), f32), pltpu.VMEM((8, 128), f32),
            pltpu.VMEM((seqs, local_len, 128), f32), pltpu.VMEM((seqs, local_len, 128), f32), pltpu.VMEM((seqs, local_len, 128), f32),
            pltpu.VMEM((seqs, 8, total_len), f32),
            sems, sems, pltpu.SemaphoreType.DMA((8,)),
        ],
        compiler_params=pltpu.CompilerParams(collective_id=0, has_side_effects=True, vmem_limit_bytes=67043328),
        name="whole_layer",
    )(x, cot, ids, wq, wo, gains, biases, router, w_up, w_down)


def fast_body(tokens, cotangent, expert_ids, w_qkv, w_out, ln_gains, ln_biases, router, w_up, w_down):
    n_expert, n_dp = lax.axis_size("expert"), lax.axis_size("dp")
    seqs, local_len, dim = tokens.shape[0] * tokens.shape[1], tokens.shape[2], tokens.shape[3]
    qc, oc = w_qkv.shape[1], w_out.shape[1]
    n_small = 4 + n_expert
    flat = lax.axis_index("dp") * n_expert + lax.axis_index("expert")
    got = whole_layer(
        n_dp, n_expert, tokens.reshape(seqs, 2, local_len // 2, dim), cotangent.reshape(seqs, local_len, dim), expert_ids.reshape(seqs, local_len),
        w_qkv.T.reshape(3, qc // 3, dim), w_out.T, ln_gains, ln_biases, router, w_up[0], w_down[0],
    )
    gq, gout, gs, output, grad_tokens, gu, gd = got[:7]
    grad_qkv, grad_out = gq.T, gout.T
    gs = lax.dynamic_slice(gs, (0, lax.rem(flat * oc, 128)), (n_small, oc))
    shape = tokens.shape
    return (output.reshape(shape), grad_tokens.reshape(shape), grad_qkv, grad_out, gs[0:2], gs[2:4], gs[4:].T, gu[None], gd[None])


def solution(mesh):
    in_specs = (
        P(None, "dp", "expert", None),
        P(None, "dp", "expert", None),
        P(None, "dp", "expert", None),
        P(None, ("dp", "expert")),
        P(None, ("dp", "expert")),
        P(None, ("dp", "expert")),
        P(None, ("dp", "expert")),
        P(("dp", "expert"), None),
        P("expert", "dp", None),
        P("expert", "dp", None),
    )
    out_specs = (
        P(None, "dp", "expert", None),
        P(None, "dp", "expert", None),
        P(None, ("dp", "expert")),
        P(None, ("dp", "expert")),
        P(None, ("dp", "expert")),
        P(None, ("dp", "expert")),
        P(("dp", "expert"), None),
        P("expert", "dp", None),
        P("expert", "dp", None),
    )
    n_expert, n_dp = mesh.shape["expert"], mesh.shape["dp"]
    chosen = fast_body if n_expert == 4 and n_dp % 4 == 0 and n_dp <= 8 else body
    return jax.shard_map(chosen, mesh=mesh, in_specs=in_specs, out_specs=out_specs, check_vma=False)
```

```python
import functools
import math

import jax
import jax.numpy as jnp
from jax import lax
from jax.experimental import pallas as pl
from jax.experimental.pallas import tpu as pltpu
from jax.sharding import PartitionSpec as P

HEADS = 12
FF = 3072
BLK = 256
MICRO = 2


epsilon = 1e-05
balance_coef = 8.0
neg_big = -1e30


def layer_norm(features, gain_vec, shift_vec):
    centre = features - jnp.mean(features, axis=-1, keepdims=True)
    spread = jnp.mean(centre * centre, axis=-1, keepdims=True)
    return centre * lax.rsqrt(spread + epsilon) * gain_vec + shift_vec


def gelu_exact(preact):
    return jax.nn.gelu(preact, approximate=False)


def fetch_all(w_qkv, w_out, ln_gains, ln_biases, router, w_up, w_down):
    dense_set = (
        lax.all_gather(w_qkv, ("dp", "expert"), axis=1, tiled=True),
        lax.all_gather(w_out, ("dp", "expert"), axis=1, tiled=True),
        lax.all_gather(ln_gains, ("dp", "expert"), axis=1, tiled=True),
        lax.all_gather(ln_biases, ("dp", "expert"), axis=1, tiled=True),
        lax.all_gather(router, ("dp", "expert"), axis=0, tiled=True),
    )
    expert_set = (
        lax.all_gather(w_up, "dp", axis=1, tiled=True),
        lax.all_gather(w_down, "dp", axis=1, tiled=True),
    )
    return tuple(dense_set) + tuple(expert_set)


def route_slots(expert_of, experts, capacity):
    seq_here, local_len = expert_of.shape
    matches = (expert_of[..., None] == lax.iota(jnp.int32, experts)).astype(jnp.int32)
    order_in = jnp.sum((jnp.cumsum(matches, axis=1) - matches) * matches, axis=-1)
    seq_index = lax.broadcasted_iota(jnp.int32, (seq_here, local_len), 0)
    target = (expert_of * (seq_here * capacity) + seq_index * capacity + order_in).reshape(-1)
    slot_table = jnp.full((experts * seq_here * capacity,), seq_here * local_len, jnp.int32)
    slot_table = slot_table.at[target].set(lax.iota(jnp.int32, seq_here * local_len))
    return (target, slot_table)


def to_slots(features, slot_table):
    flat_rows = features.reshape(-1, features.shape[-1])
    padded = jnp.concatenate(
        [flat_rows, jnp.zeros((1, flat_rows.shape[1]), flat_rows.dtype)], axis=0
    )
    return padded[slot_table]


def score_terms(
    queries, grad_rows, key_block, value_block, log_total, row_delta, allowed, score_scale
):
    scores = (
        jnp.einsum("sqhd,skhd->shqk", queries, key_block, preferred_element_type=jnp.float32)
        * score_scale
    )
    weights = jnp.where(allowed, jnp.exp(scores - log_total[..., None]), 0.0)
    grad_weights = jnp.einsum(
        "sqhd,skhd->shqk", grad_rows, value_block, preferred_element_type=jnp.float32
    )
    grad_scores = (weights * (grad_weights - row_delta[..., None]) * score_scale).astype(
        jnp.bfloat16
    )
    return (weights.astype(jnp.bfloat16), grad_scores)


def attention_forward(queries, key_rows, value_rows, query_pos, score_scale):
    seq_here, local_len, head_count, head_dim = queries.shape
    last_block = query_pos[local_len - 1] // BLK
    start_state = (
        jnp.full((seq_here, head_count, local_len), neg_big, jnp.float32),
        jnp.zeros((seq_here, head_count, local_len), jnp.float32),
        jnp.zeros((seq_here, local_len, head_count, head_dim), jnp.float32),
    )
    key_part = lax.all_gather(key_rows, "expert", axis=1, tiled=True)
    value_part = lax.all_gather(value_rows, "expert", axis=1, tiled=True)
    piece_len = key_part.shape[1]
    block_len = math.gcd(piece_len, 512)

    def attention_one_block(block_index, carried):
        within = block_index * block_len
        key_block = lax.dynamic_slice_in_dim(key_part, within, block_len, 1).reshape(
            seq_here, block_len, head_count, head_dim
        )
        value_block = lax.dynamic_slice_in_dim(value_part, within, block_len, 1).reshape(
            seq_here, block_len, head_count, head_dim
        )
        key_pos = within + lax.iota(jnp.int32, block_len)
        allowed = key_pos[None, :] // BLK <= query_pos[:, None] // BLK

        def attention_compute(current):
            run_max, run_sum, weighted = current
            scores = (
                jnp.einsum(
                    "sqhd,skhd->shqk", queries, key_block, preferred_element_type=jnp.float32
                )
                * score_scale
            )
            new_max = jnp.maximum(run_max, jnp.max(jnp.where(allowed, scores, neg_big), axis=-1))
            weights = jnp.where(allowed, jnp.exp(scores - new_max[..., None]), 0.0)
            factor = jnp.exp(run_max - new_max)
            run_sum = run_sum * factor + jnp.sum(weights, axis=-1)
            addition = jnp.einsum(
                "shqk,skhd->sqhd",
                weights.astype(jnp.bfloat16),
                value_block,
                preferred_element_type=jnp.float32,
            )
            weighted = weighted * jnp.swapaxes(factor, 1, 2)[..., None] + addition
            return (new_max, run_sum, weighted)

        return lax.cond(
            within // BLK <= last_block, attention_compute, lambda current: current, carried
        )

    run_max, run_sum, weighted = lax.fori_loop(
        0, piece_len // block_len, attention_one_block, start_state
    )
    log_total = run_max + jnp.log(run_sum)
    attended = weighted / jnp.swapaxes(run_sum, 1, 2)[..., None]
    return (log_total, attended)


def query_grads(
    queries, grad_rows, key_rows, value_rows, log_total, row_delta, query_pos, score_scale, seq_len
):
    seq_here, local_len, head_count, head_dim = queries.shape
    model_dim = head_count * head_dim
    last_block = query_pos[local_len - 1] // BLK
    start_query = jnp.zeros((seq_here, local_len, head_count, head_dim), jnp.float32)
    start_state = (start_query, jnp.zeros((seq_here, seq_len, 2 * model_dim), jnp.float32))
    key_part = lax.all_gather(key_rows, "expert", axis=1, tiled=True)
    value_part = lax.all_gather(value_rows, "expert", axis=1, tiled=True)
    piece_len = key_part.shape[1]
    block_len = math.gcd(piece_len, 512)

    def query_one_block(block_index, carried):
        within = block_index * block_len
        key_block = lax.dynamic_slice_in_dim(key_part, within, block_len, 1).reshape(
            seq_here, block_len, head_count, head_dim
        )
        value_block = lax.dynamic_slice_in_dim(value_part, within, block_len, 1).reshape(
            seq_here, block_len, head_count, head_dim
        )
        key_pos = within + lax.iota(jnp.int32, block_len)
        allowed = key_pos[None, :] // BLK <= query_pos[:, None] // BLK

        def query_compute(current):
            weights, grad_scores = score_terms(
                queries,
                grad_rows,
                key_block,
                value_block,
                log_total,
                row_delta,
                allowed,
                score_scale,
            )
            grad_query = current[0] + jnp.einsum(
                "shqk,skhd->sqhd", grad_scores, key_block, preferred_element_type=jnp.float32
            )
            grad_key = jnp.einsum(
                "shqk,sqhd->skhd", grad_scores, queries, preferred_element_type=jnp.float32
            ).reshape(seq_here, block_len, model_dim)
            grad_value = jnp.einsum(
                "shqk,sqhd->skhd", weights, grad_rows, preferred_element_type=jnp.float32
            ).reshape(seq_here, block_len, model_dim)
            old_rows = lax.dynamic_slice_in_dim(current[1], within, block_len, 1)
            summed = old_rows + jnp.concatenate([grad_key, grad_value], axis=-1)
            return (grad_query, lax.dynamic_update_slice_in_dim(current[1], summed, within, 1))

        return lax.cond(
            within // BLK <= last_block, query_compute, lambda current: current, carried
        )

    return lax.fori_loop(0, piece_len // block_len, query_one_block, start_state)


def body(tokens, cotangent, expert_ids, w_qkv, w_out, ln_gains, ln_biases, router, w_up, w_down):
    n_expert = lax.axis_size("expert")
    seq_part = lax.axis_index("expert")
    seq_here, local_len, model_dim = (tokens.shape[1], tokens.shape[2], tokens.shape[3])
    head_count = HEADS
    head_dim = model_dim // head_count
    score_scale = head_dim ** (-0.5)
    exp_dev = w_up.shape[0]
    experts = exp_dev * n_expert
    capacity = 2 * local_len // experts
    seq_len = local_len * n_expert
    query_pos = seq_part * local_len + lax.iota(jnp.int32, local_len)
    expert_range = lax.iota(jnp.int32, experts)
    all_ids = expert_ids[..., 0]
    local_counts = jnp.sum((all_ids[..., None] == expert_range).astype(jnp.float32), axis=(0, 1, 2))
    counts = lax.psum(local_counts, ("dp", "expert"))
    mean_load = jnp.sum(counts) / experts
    load_ratio = (counts - mean_load) / mean_load
    grad_qkv_w = jnp.zeros((model_dim, 3 * model_dim), jnp.float32)
    grad_out_w = jnp.zeros((model_dim, model_dim), jnp.float32)
    grad_gains = jnp.zeros((2, model_dim), jnp.float32)
    grad_shifts = jnp.zeros((2, model_dim), jnp.float32)
    grad_router = jnp.zeros((model_dim, experts), jnp.float32)
    grad_up = jnp.zeros((exp_dev, model_dim, FF), jnp.float32)
    grad_down = jnp.zeros((exp_dev, FF, model_dim), jnp.float32)
    outputs = []
    input_grads = []
    for micro_index in range(MICRO):
        fetched = fetch_all(w_qkv, w_out, ln_gains, ln_biases, router, w_up, w_down)
        qkv_full, out_full, gains_full, shifts_full, router_full, up_full, down_full = fetched
        gain_rows = gains_full.astype(jnp.float32)
        shift_rows = shifts_full.astype(jnp.float32)
        inputs = tokens[micro_index].astype(jnp.float32)
        expert_of = all_ids[micro_index]
        normed = layer_norm(inputs, gain_rows[0], shift_rows[0])
        normed_low = normed.astype(jnp.bfloat16)
        projected = jnp.einsum(
            "scd,de->sce", normed_low, qkv_full, preferred_element_type=jnp.float32
        ).astype(jnp.bfloat16)
        query_rows = projected[..., :model_dim]
        queries = query_rows.reshape(seq_here, local_len, head_count, head_dim)
        key_rows = projected[..., model_dim : 2 * model_dim]
        value_rows = projected[..., 2 * model_dim :]
        log_total, attended = attention_forward(
            queries, key_rows, value_rows, query_pos, score_scale
        )
        attended_low = attended.reshape(seq_here, local_len, model_dim).astype(jnp.bfloat16)
        middle = inputs + jnp.einsum(
            "scd,de->sce", attended_low, out_full, preferred_element_type=jnp.float32
        )
        mixed_low = layer_norm(middle, gain_rows[1], shift_rows[1]).astype(jnp.bfloat16)
        onehot = (expert_of[..., None] == expert_range).astype(jnp.float32)
        logits = jnp.einsum(
            "scd,de->sce", mixed_low, router_full, preferred_element_type=jnp.float32
        )
        gates = jax.nn.sigmoid(jnp.sum(logits * onehot, axis=-1))
        target, slot_table = route_slots(expert_of, experts, capacity)
        outgoing = to_slots(mixed_low, slot_table).reshape(
            n_expert, exp_dev, seq_here * capacity, model_dim
        )
        arrived = lax.all_to_all(outgoing, "expert", split_axis=0, concat_axis=0, tiled=True)
        preact = jnp.einsum("pesd,edf->pesf", arrived, up_full, preferred_element_type=jnp.float32)
        hidden = gelu_exact(preact).astype(jnp.bfloat16)
        result = jnp.einsum(
            "pesf,efd->pesd", hidden, down_full, preferred_element_type=jnp.float32
        ).astype(jnp.bfloat16)
        returned = lax.all_to_all(result, "expert", split_axis=0, concat_axis=0, tiled=True)
        expert_out = (
            returned.reshape(-1, model_dim)[target]
            .reshape(seq_here, local_len, model_dim)
            .astype(jnp.float32)
        )
        final = middle + gates[..., None] * expert_out
        outputs.append(final.astype(jnp.bfloat16))
        fetched = fetch_all(w_qkv, w_out, ln_gains, ln_biases, router, w_up, w_down)
        qkv_full, out_full, gains_full, shifts_full, router_full, up_full, down_full = fetched
        gain_rows = gains_full.astype(jnp.float32)
        shift_rows = shifts_full.astype(jnp.float32)
        grad_final = cotangent[micro_index].astype(jnp.float32)
        grad_gate = jnp.sum(grad_final * expert_out, axis=-1) + balance_coef * jnp.sum(
            onehot * load_ratio, axis=-1
        )
        grad_logit = grad_gate * gates * (1.0 - gates)
        grad_expert = (gates[..., None] * grad_final).astype(jnp.bfloat16)
        sent_grads = to_slots(grad_expert, slot_table).reshape(
            n_expert, exp_dev, seq_here * capacity, model_dim
        )
        grads_here = lax.all_to_all(sent_grads, "expert", split_axis=0, concat_axis=0, tiled=True)
        hidden_low = gelu_exact(preact).astype(jnp.bfloat16)
        grad_down = grad_down + jnp.einsum(
            "pesf,pesd->efd", hidden_low, grads_here, preferred_element_type=jnp.float32
        )
        grad_hidden = jnp.einsum(
            "pesd,efd->pesf", grads_here, down_full, preferred_element_type=jnp.float32
        )
        grad_pre = jax.vjp(gelu_exact, preact)[1](grad_hidden)[0].astype(jnp.bfloat16)
        grad_up = grad_up + jnp.einsum(
            "pesd,pesf->edf", arrived, grad_pre, preferred_element_type=jnp.float32
        )
        grad_arrived = jnp.einsum(
            "pesf,edf->pesd", grad_pre, up_full, preferred_element_type=jnp.float32
        ).astype(jnp.bfloat16)
        grads_back = lax.all_to_all(grad_arrived, "expert", split_axis=0, concat_axis=0, tiled=True)
        grad_mixed = (
            grads_back.reshape(-1, model_dim)[target]
            .reshape(seq_here, local_len, model_dim)
            .astype(jnp.float32)
        )
        router_cols = jnp.einsum("sce,de->scd", onehot, router_full.astype(jnp.float32))
        grad_mixed = grad_mixed + grad_logit[..., None] * router_cols
        grad_router = grad_router + jnp.einsum(
            "scd,sce->de", mixed_low.astype(jnp.float32), grad_logit[..., None] * onehot
        )
        second_back = jax.vjp(layer_norm, middle, gain_rows[1], shift_rows[1])[1]
        grad_middle, grad_gain_two, grad_shift_two = second_back(grad_mixed)
        grad_middle = grad_middle + grad_final
        grad_branch = grad_middle.astype(jnp.bfloat16)
        grad_out_w = grad_out_w + jnp.einsum(
            "scd,sce->de", attended_low, grad_branch, preferred_element_type=jnp.float32
        )
        grad_attended = jnp.einsum(
            "sce,de->scd", grad_branch, out_full, preferred_element_type=jnp.float32
        ).astype(jnp.bfloat16)
        grad_heads = grad_attended.reshape(seq_here, local_len, head_count, head_dim)
        row_delta = jnp.swapaxes(jnp.sum(grad_heads.astype(jnp.float32) * attended, axis=-1), 1, 2)
        folded = query_grads(
            queries,
            grad_heads,
            key_rows,
            value_rows,
            log_total,
            row_delta,
            query_pos,
            score_scale,
            seq_len,
        )
        grad_query = folded[0].reshape(seq_here, local_len, model_dim)
        key_value = lax.psum_scatter(
            folded[1].astype(jnp.bfloat16), "expert", scatter_dimension=1, tiled=True
        ).astype(jnp.float32)
        grad_key = key_value[..., :model_dim]
        grad_value = key_value[..., model_dim:]
        grad_projected = jnp.concatenate([grad_query, grad_key, grad_value], axis=-1).astype(
            jnp.bfloat16
        )
        grad_qkv_w = grad_qkv_w + jnp.einsum(
            "scd,sce->de", normed_low, grad_projected, preferred_element_type=jnp.float32
        )
        grad_normed = jnp.einsum(
            "sce,de->scd", grad_projected, qkv_full, preferred_element_type=jnp.float32
        )
        first_back = jax.vjp(layer_norm, inputs, gain_rows[0], shift_rows[0])[1]
        grad_inputs, grad_gain_one, grad_shift_one = first_back(grad_normed)
        grad_gains = grad_gains + jnp.stack([grad_gain_one, grad_gain_two])
        grad_shifts = grad_shifts + jnp.stack([grad_shift_one, grad_shift_two])
        input_grads.append(grad_middle + grad_inputs)
    dense_grads = (
        lax.psum_scatter(grad_qkv_w, ("dp", "expert"), scatter_dimension=1, tiled=True),
        lax.psum_scatter(grad_out_w, ("dp", "expert"), scatter_dimension=1, tiled=True),
        lax.psum_scatter(grad_gains, ("dp", "expert"), scatter_dimension=1, tiled=True),
        lax.psum_scatter(grad_shifts, ("dp", "expert"), scatter_dimension=1, tiled=True),
        lax.psum_scatter(grad_router, ("dp", "expert"), scatter_dimension=0, tiled=True),
    )
    expert_grads = (
        lax.psum_scatter(
            grad_up.astype(jnp.bfloat16), "dp", scatter_dimension=1, tiled=True
        ).astype(jnp.float32),
        lax.psum_scatter(
            grad_down.astype(jnp.bfloat16), "dp", scatter_dimension=1, tiled=True
        ).astype(jnp.float32),
    )
    return (jnp.stack(outputs), jnp.stack(input_grads)) + tuple(dense_grads) + tuple(expert_grads)


MESH_ID = pl.DeviceIdType.MESH
NT = (((1,), (1,)), ((), ()))
NN = (((1,), (0,)), ((), ()))
TN = (((0,), (0,)), ((), ()))
VMEM = pl.BlockSpec(memory_space=pltpu.VMEM)
HBM = pl.BlockSpec(memory_space=pl.ANY)


def mm(a, b, dims=NN):
    return lax.dot_general(a, b, dims, preferred_element_type=jnp.float32)


def normalised(v):
    centre = v - jnp.mean(v, axis=-1, keepdims=True)
    spread = jnp.mean(centre * centre, axis=-1, keepdims=True)
    inv = lax.rsqrt(spread + epsilon)
    return centre * inv, inv


def norm_back(grad_hat, hat, inv):
    return inv * (grad_hat - jnp.mean(grad_hat, axis=1, keepdims=True) - hat * jnp.mean(grad_hat * hat, axis=1, keepdims=True))


def add_into(target, other, step):
    def some(u, carry):
        rows = pl.ds(pl.multiple_of(u * step, step), step)
        target[rows, :] = (target[rows, :].astype(jnp.float32) + other[rows, :].astype(jnp.float32)).astype(target.dtype)
        return carry

    lax.fori_loop(0, target.shape[0] // step, some, 0)


class Place:
    def __init__(self, n_dp, n_ex):
        self.n_dp, self.n_ex, self.n_dev, self.n_z = n_dp, n_ex, n_dp * n_ex, n_dp // 2
        self.dp, self.ex = lax.axis_index("dp"), lax.axis_index("expert")
        self.z, self.core = self.dp // 2, self.dp % 2
        self.flat = self.dp * n_ex + self.ex

    def z_peer(self, d):
        return (self.z + d) % self.n_z

    def ex_peer(self, d):
        return (self.ex + d) % self.n_ex

    def on_z(self, z):
        return (z * 2 + self.core, self.ex)

    def on_ex(self, e):
        return (self.dp, e)

    def partner(self):
        return (self.z * 2 + 1 - self.core, self.ex)

    def numbered(self, t):
        return (t // self.n_ex, t % self.n_ex)


def entry_barrier(at):
    sem = pltpu.get_barrier_semaphore()

    def tell(i, carry):
        pl.semaphore_signal(sem, inc=1, device_id=at.numbered((at.flat + i) % at.n_dev), device_id_type=MESH_ID)
        return carry

    lax.fori_loop(1, at.n_dev, tell, 0)
    pl.semaphore_wait(sem, at.n_dev - 1)


class Wires:
    def __init__(self, send_sems, recv_sems):
        self.send_sems, self.recv_sems, self.used = send_sems, recv_sems, 0

    def take(self, n):
        base = self.used
        self.used = base + n
        return base

    def copy(self, i, src, dst, device):
        return pltpu.make_async_remote_copy(
            src_ref=src, dst_ref=dst, send_sem=self.send_sems.at[i], recv_sem=self.recv_sems.at[i],
            device_id=device, device_id_type=MESH_ID,
        )

    def all_came(self, i, blocks):
        pltpu.make_async_copy(blocks, blocks, self.recv_sems.at[i]).wait()

    def all_left(self, i, blocks):
        pltpu.make_async_copy(blocks, blocks, self.send_sems.at[i]).wait()


def layer_kernel(
    n_dp, n_ex, x_ref, cot_ref, ids_ref, wq_ref, wo_ref, gain_ref, bias_ref, router_ref, up_hbm, down_hbm,
    gq_ref, gout_ref, gsmall_ref, out_hbm, gtok_hbm, gup_hbm, gdown_hbm, up_full, down_full, q_hbm, k_hbm, v_hbm, xn_hbm, mix_hbm, mid_hbm, w_hbm, wo_hbm,
    outbox, inbox, work, gdt, gup, pin_dn, pin_up, zin_dn, zin_up, via_dn, via_up, rowbox, attr, gar,
    gob, gob_pair, gob_line, gob_mine, gob_plane, wt_a, gws, gws_pair, gws_line, gws_sum,
    small_b, wo_s, gq_in, small_all, small_in, small_out, smalls, tally, gate_s, slot_s, eid_s, lse, send_sems, recv_sems, load_sems,
):
    bf, f32 = jnp.bfloat16, jnp.float32
    at = Place(n_dp, n_ex)
    wires = Wires(send_sems, recv_sems)
    n_dev, n_z, ex, z, core = at.n_dev, at.n_z, at.ex, at.z, at.core
    seqs, dim = x_ref.shape[0], x_ref.shape[3]
    cap = x_ref.shape[2]
    local_len = 2 * cap
    total_len, width, slots = local_len * n_ex, dim // n_ex, n_ex * cap
    head_dim = dim // HEADS
    heads = width // head_dim
    piece, oc = wq_ref.shape[1], wo_ref.shape[0]
    shard, ff = up_hbm.shape
    half = down_hbm.shape[0]
    tile, mid_dim = ff // n_z, dim // 2
    scale = head_dim ** -0.5
    wt_b, wo_b = gws, gob
    lane = lax.broadcasted_iota(jnp.int32, (1, 128), 1).astype(f32)
    lane_head = lax.broadcasted_iota(jnp.int32, (1, width), 1) // head_dim
    peers = range(1, n_ex)

    small_out[...] = jnp.zeros(small_out.shape, f32)
    small_out[0:2, 0:oc] = gain_ref[...].astype(f32)
    small_out[2:4, 0:oc] = bias_ref[...].astype(f32)
    unit = jnp.where(lax.broadcasted_iota(jnp.int32, (oc, oc), 0) == lax.broadcasted_iota(jnp.int32, (oc, oc), 1), 1.0, 0.0).astype(bf)
    small_out[4 : 4 + n_ex, 0:oc] = mm(router_ref[...], unit, TN)
    held_rows = jnp.zeros((1, 128), f32)
    for m in range(seqs):
        eid_s[m] = jnp.broadcast_to(ids_ref[m : m + 1, :].astype(f32), (128, local_len)).T
        held_rows += jnp.sum(jnp.where(lane == eid_s[m], 1.0, 0.0), axis=0, keepdims=True)
    high = jnp.floor(held_rows * (1.0 / 16.0))
    small_b[0:8, :] = small_out[0:8, 0:128].astype(bf)
    row = lax.broadcasted_iota(jnp.int32, (8, 128), 0)
    small_b[8:16, :] = jnp.where(row == 0, high, jnp.where(row == 1, held_rows - 16.0 * high, 0.0)).astype(bf)
    for b in range(n_ex):
        wo_s[b] = wo_ref[:, b * width : (b + 1) * width]
    lines = range(1, n_z)
    entry_barrier(at)

    i_tok, i_back, i_out, i_ret, i_ga, i_part = (wires.take(seqs) for _ in range(6))

    def token_copy(m, d):
        return wires.copy(i_tok + m, x_ref.at[m], inbox.at[m, ex], at.on_ex(at.ex_peer(d)))

    def back_copy(m, d):
        peer = at.ex_peer(d)
        return wires.copy(i_back + m, rowbox.at[m, peer], attr.at[m, ex], at.on_ex(peer))

    def out_copy(m, d):
        peer = at.ex_peer(d)
        return wires.copy(i_out + m, outbox.at[m, peer], work.at[m, ex], at.on_ex(peer))

    def return_copy(m, d):
        peer = at.ex_peer(d)
        return wires.copy(i_ret + m, outbox.at[m, peer], inbox.at[m, ex], at.on_ex(peer))

    def ga_copy(m, d):
        peer = at.ex_peer(d)
        return wires.copy(i_ga + m, rowbox.at[m, peer], gar.at[m, ex], at.on_ex(peer))

    def part_copy(m, d):
        peer = at.ex_peer(d)
        return wires.copy(i_part + m, outbox.at[m, peer], inbox.at[m, ex], at.on_ex(peer))

    reach = [d for d in (2, 1) if d < n_z]

    def order(step):
        return (n_z - 1) * step % n_z

    relay = n_z > 3
    kinds = n_z + 1
    i_ag, i_agp = wires.take(5 * kinds), wires.take(5 * kinds)

    def ag_columns(t):
        return pl.ds(pl.multiple_of(t * tile, tile), tile)

    def ag_block(t, zz, cc, down):
        if down:
            return down_full.at[pl.ds(pl.multiple_of((zz * 2 + cc) * half, half), half), :]
        return up_full.at[t, pl.ds(pl.multiple_of((zz * 2 + cc) * shard, shard), shard), :]

    def ag_own(t, down):
        return down_hbm if down else up_hbm.at[:, ag_columns(t)]

    def ag_code(right, d, t, down):
        return (d if d != 1 or right else 4) * kinds + (n_z if down else t)

    def ag_copy(right, d, t, down):
        return wires.copy(i_ag + ag_code(right, d, t, down), ag_own(t, down), ag_block(t, z, core, down), at.on_z(z + d if right else z - d))

    def ag_relay(right, t, down):
        block = ag_block(t, z - 2 if right else z + 2, core, down)
        return wires.copy(i_ag + ag_code(right, 3, t, down), block, block, at.on_z(z + 1 if right else z - 1))

    def ag_pair(right, d, t, down):
        block = ag_block(t, z - d if right else z + d, core, down)
        return wires.copy(i_agp + ag_code(right, d, t, down), ag_own(t, down) if d == 0 else block, block, at.partner())

    def ag_sends(right, d):
        return z + d < n_z if right else z - d >= 0

    def ag_comes(right, d):
        return z - d >= 0 if right else z + d < n_z

    def ag_relays(right):
        return z == n_z - 2 if right else z == 1

    def ag_from(right, d, t, act):
        @pl.when(ag_comes(right, d))
        def _():
            act(False)
            pl.when((z - d if right else z + d) == t)(lambda: act(True))

    def ag_start(t):
        for d in reach:
            for right in (True, False):
                @pl.when(ag_sends(right, d))
                def _():
                    ag_copy(right, d, t, False).start()
                    pl.when(z == t)(ag_copy(right, d, t, True).start)
        ag_from(True, 0, t, lambda down: ag_pair(True, 0, t, down).start())

    def ag_pass(t):
        for d in reach:
            for right in (True, False):
                def act(down, right=right, d=d):
                    ag_copy(right, d, t, down).wait_recv()
                    if d == 2 and relay:
                        pl.when(ag_relays(right))(ag_relay(right, t, down).start)
                    ag_pair(right, d, t, down).start()

                ag_from(right, d, t, act)

    def ag_far(t):
        if relay:
            for right in (True, False):
                def act(down, right=right):
                    ag_copy(right, 3, t, down).wait_recv()
                    ag_pair(right, 3, t, down).start()

                ag_from(right, 3, t, act)

    far = [0] + sorted(reach) + ([3] if relay else [])

    def ag_ready(t):
        for d in far:
            for right in (True, False) if d else (True,):
                ag_from(right, d, t, lambda down, right=right, d=d: ag_pair(right, d, t, down).wait_recv())

    def ag_finish():
        def one(t, carry):
            for d in far:
                for right in (True, False) if d else (True,):
                    ag_from(right, d, t, lambda down, right=right, d=d: ag_pair(right, d, t, down).wait_send())
            for d in reach:
                for right in (True, False):
                    @pl.when(ag_sends(right, d))
                    def _():
                        ag_copy(right, d, t, False).wait_send()
                        pl.when(z == t)(ag_copy(right, d, t, True).wait_send)
            if relay:
                for right in (True, False):
                    @pl.when(ag_relays(right))
                    def _():
                        ag_relay(right, t, False).wait_send()
                        pl.when((z - 2 if right else z + 2) == t)(ag_relay(right, t, True).wait_send)
            return carry

        lax.fori_loop(0, n_z, one, 0)

    i_gp, i_gl, i_gv = wires.take(2 * n_z), wires.take(3 * kinds), wires.take(kinds)

    def pair_copies(t):
        return (
            wires.copy(i_gp + 2 * t, gdt.at[1 - core, t], pin_dn.at[t], at.partner()),
            wires.copy(i_gp + 2 * t + 1, gup.at[1 - core, t], pin_up.at[t], at.partner()),
        )

    def line_copy(t, src, dest, down):
        right, d = dest > src, abs(dest - src)
        block = gdt.at[core, t] if down else gup.at[core, t, dest]
        kind = n_z if down else t
        if d == 3:
            return wires.copy(i_gv + kind, block, via_dn if down else via_up.at[t], at.on_z(src + 1 if right else src - 1))
        slot = 2 if d == 2 else 0 if right else 1
        return wires.copy(
            i_gl + slot * kinds + kind, block, zin_dn.at[slot] if down else zin_up.at[slot, t], at.on_z(dest)
        )

    pairs_far_first = sorted(((s_, d_) for s_ in range(n_z) for d_ in range(n_z) if s_ != d_), key=lambda u: -abs(u[0] - u[1]))

    def held(src, dest):
        return relay and abs(dest - src) == 2 and src in (1, n_z - 2) and dest in (0, n_z - 1)

    def line_each(t, src, dest, act):
        act(False)
        pl.when(t == dest)(lambda: act(True))

    def fold(t):
        for c in pair_copies(t):
            c.wait_recv()
        add_into(gdt.at[core, t], pin_dn.at[t], 96)
        for zz in range(n_z):
            add_into(gup.at[core, t, zz], pin_up.at[t, zz], 48)
        for src, dest in pairs_far_first:
            if not held(src, dest):
                @pl.when(z == src)
                def _():
                    line_each(t, src, dest, lambda down: line_copy(t, src, dest, down).start())

    def add_far(t):
        for src, dest in pairs_far_first:
            if held(src, dest):
                @pl.when(z == src)
                def _():
                    def act(down):
                        line_copy(t, dest - 3 if dest > src else dest + 3, dest, down).wait_recv()
                        if down:
                            add_into(gdt.at[core, t], via_dn, 96)
                        else:
                            add_into(gup.at[core, t, dest], via_up.at[t], 48)
                        line_copy(t, src, dest, down).start()

                    line_each(t, src, dest, act)

    i_small = wires.take(1)

    def small_copy(i):
        return wires.copy(i_small, small_b, small_all.at[at.flat], at.numbered((at.flat + i) % n_dev))

    def each(n, act):
        def step(i, carry):
            act(i)
            return carry

        lax.fori_loop(1, n, step, 0)

    i_piece, i_line, i_pair, i_wo, i_wo2 = wires.take(3), wires.take(1), wires.take(2), wires.take(1), wires.take(1)

    def forward(q_v, k_v, v_v, xn_v, wide, att_acc, lse_acc, mid_v, mix_v, w_v, wo_v, up_s, down_s):
        stage = (
            pltpu.make_async_copy(up_hbm, up_s, load_sems.at[0]),
            pltpu.make_async_copy(down_hbm, down_s, load_sems.at[1]),
        )
        for c in stage:
            c.start()
        me_j = ex * n_dp + at.dp
        pieces = []
        for r in range(3):
            c = 3 * at.flat + r
            sec, j = c // n_dev, c % n_dev
            copy = wires.copy(i_piece + r, wq_ref.at[r], wt_a.at[sec], (j % n_dp, j // n_dp))
            away = j != me_j
            pl.when(away)(copy.start)
            pieces.append((copy, away, sec))
        each(n_dev, lambda i: small_copy(i).start())
        for m in range(seqs):
            for d in peers:
                token_copy(m, d).start()
        small_all[at.flat] = small_b[...]
        wo_b[core, ex, z] = wo_s[...]
        for m in range(seqs):
            inbox[m, ex] = x_ref[m]
        for r, (copy, away, sec) in enumerate(pieces):
            pl.when(away)(copy.wait_recv)

            @pl.when(jnp.logical_not(away))
            def _():
                wt_a[sec] = wq_ref[r]

        w_line = [wires.copy(i_line, wt_a, wt_b.at[core, z], at.on_z(at.z_peer(d))) for d in lines]
        for c in w_line:
            c.start()
        wo_line = [wires.copy(i_wo, wo_s, wo_b.at[core, ex, z], at.on_z(at.z_peer(d))) for d in lines]
        for c in wo_line:
            c.start()
        wt_b[core, z] = wt_a[...]
        for c in stage:
            c.wait()
        own = [
            pltpu.make_async_copy(up_s.at[:, t * tile : (t + 1) * tile], ag_block(t, z, core, False), load_sems.at[t % 2])
            for t in range(n_z)
        ] + [pltpu.make_async_copy(down_s, ag_block(0, z, core, True), load_sems.at[3])]
        for c in own[:2]:
            c.start()

        before = jnp.where(
            lax.broadcasted_iota(jnp.int32, (local_len, local_len), 1) < lax.broadcasted_iota(jnp.int32, (local_len, local_len), 0), 1.0, 0.0
        ).astype(bf)
        for m in range(seqs):
            named = jnp.where(lane == eid_s[m], 1.0, 0.0)
            earlier = jnp.sum(mm(before, named.astype(bf)) * named, axis=1, keepdims=True)
            slot_s[m] = eid_s[m] * cap + earlier

        wires.all_came(i_small, small_all.at[pl.ds(0, n_dev - 1)])
        smalls[...] = jnp.zeros(smalls.shape, f32)
        tally[...] = jnp.zeros(tally.shape, f32)
        for s in range(n_dev):
            block = small_all[s].astype(f32)
            tally[...] += block[8:16, :]
            lo = s * oc // 128 * 128
            spread = pltpu.roll(jnp.concatenate([block, jnp.zeros_like(block)], axis=1), s * oc - lo, 1)
            hi = min(lo + 256, dim)
            smalls[:, lo:hi] += spread[:, 0 : hi - lo]
        gain_one, shift_one = smalls[0:1, :], smalls[2:3, :]
        gain_two, shift_two = smalls[1:2, :], smalls[3:4, :]
        wires.all_came(i_line, wt_b.at[0, pl.ds(0, n_z - 1)])
        w_pair = wires.copy(i_pair, wt_b.at[core], wt_b.at[core], at.partner())
        w_pair.start()
        wires.all_came(i_wo, wo_b.at[0, 0, pl.ds(0, n_z - 1)])
        for step in range(min(2, n_z)):
            ag_start(order(step))
        wo_plane = [wires.copy(i_wo2, wo_b.at[core, ex], wo_b.at[core, ex], at.on_ex(at.ex_peer(d))) for d in peers]
        for c in wo_plane:
            c.start()
        w_pair.wait_recv()
        for sec in range(3):
            for zz in range(n_z):
                for cc in range(2):
                    row = (zz * 2 + cc) * piece
                    wide[row : row + piece, :] = wt_b[cc, zz, sec].astype(f32)
            w_v[sec] = wide[0:width, :].astype(bf)

        def project(m):
            def one(d, carry):
                src = (ex - d + n_ex) % n_ex

                @pl.when(d == 1)
                def _():
                    wires.all_came(i_tok + m, inbox.at[m, pl.ds(0, n_ex - 1)])

                rows = pl.ds(pl.multiple_of(src * local_len, local_len), local_len)
                hat, _ = normalised(inbox[m, src].reshape(local_len, dim).astype(f32))
                low = (hat * gain_one + shift_one).astype(bf)
                xn_v[rows, :] = low
                q_v[m, rows, :] = mm(low, w_v[0], NT).astype(bf)
                k_v[m, rows, :] = mm(low, w_v[1], NT).astype(bf)
                v_v[m, rows, :] = mm(low, w_v[2], NT).astype(bf)
                return carry

            lax.fori_loop(0, n_ex, one, 0)

        def attend(m):
            for i in range(n_ex):
                end = (i + 1) * local_len
                here = slice(i * local_len, end)

                def one_head(h, carry):
                    mine = lane_head == h
                    qb = q_v[m, here, :]
                    s = mm(jnp.where(mine, qb * scale, jnp.zeros_like(qb)), k_v[m, 0:end, :], NT)
                    top = jnp.max(s, axis=-1, keepdims=True)
                    e = jnp.exp(s - top)
                    total = jnp.sum(e, axis=-1, keepdims=True)
                    p = (e * (1.0 / total)).astype(bf)
                    att_acc[...] = jnp.where(mine, mm(p, v_v[m, 0:end, :]), att_acc[...])
                    lse_acc[...] = jnp.where(lane == h.astype(f32), top + jnp.log(total), lse_acc[...])
                    return carry

                lax.fori_loop(0, heads, one_head, 0)
                rowbox[m, i] = att_acc[...].astype(bf)
                lse[m, :, here] = lse_acc[...].T[0:8, :]
            for d in peers:
                back_copy(m, d).start()
            attr[m, ex] = rowbox[m, ex]

        def route(m):
            wires.all_came(i_back + m, attr.at[m, pl.ds(0, n_ex - 1)])
            mid = x_ref[m].reshape(local_len, dim).astype(f32)
            for b in range(n_ex):
                mid += mm(attr[m, b], wo_v[b], NT)
            mid_v[m] = mid
            hat, _ = normalised(mid)
            mixed = (hat * gain_two + shift_two).astype(bf)
            mix_v[m] = mixed
            logits = mm(mixed, smalls[...].astype(bf), NT)
            mine = lax.broadcasted_iota(jnp.int32, logits.shape, 1).astype(f32) == eid_s[m][:, 0:1] + 4.0
            gate = jax.nn.sigmoid(jnp.sum(jnp.where(mine, logits, 0.0), axis=1, keepdims=True))
            gate_s[m] = jnp.broadcast_to(gate, (local_len, 128))
            scaled = (gate * cot_ref[m].astype(f32)).astype(bf)
            place = jnp.where(
                slot_s[m].T[0:1, :] == lax.broadcasted_iota(jnp.int32, (slots, local_len), 0).astype(f32), 1.0, 0.0
            ).astype(bf)
            outbox[m, :, 0] = mm(place, mixed).astype(bf).reshape(n_ex, cap, dim)
            outbox[m, :, 1] = mm(place, scaled).astype(bf).reshape(n_ex, cap, dim)
            for d in peers:
                out_copy(m, d).start()
            work[m, ex] = outbox[m, ex]

        att_acc[...] = jnp.zeros(att_acc.shape, f32)
        lse_acc[...] = jnp.zeros(lse_acc.shape, f32)

        def xn_out(m):
            return pltpu.make_async_copy(xn_v, xn_hbm.at[m], load_sems.at[2])

        project(0)
        xn_out(0).start()
        attend(0)
        for i, c in enumerate(own):
            if i >= 2:
                if i < n_z:
                    own[i - 2].wait()
                c.start()
        for c in own[n_z - 2 :]:
            c.wait()
        for m in range(1, seqs):
            xn_out(m - 1).wait()
            project(m)
            xn_out(m).start()
            if m == 1:
                ag_pass(order(0))
                for step in range(2, n_z - 1):
                    ag_start(order(step))
            attend(m)
        ag_pass(order(1))
        if n_z > 2:
            ag_start(order(n_z - 1))
        wires.all_came(i_wo2, wo_b.at[0, pl.ds(0, n_ex - 1)])
        wo_pair = wires.copy(i_pair + 1, wo_b.at[core], wo_b.at[core], at.partner())
        wo_pair.start()
        wo_pair.wait_recv()
        for b in range(n_ex):
            for s in range(n_dev):
                wide[s * oc : (s + 1) * oc, 0:width] = wo_b[s // n_ex % 2, s % n_ex, s // n_ex // 2, b].astype(f32)
            wo_v[b] = wide[0:dim, 0:width].astype(bf)
        for m in range(seqs):
            route(m)
        xn_out(seqs - 1).wait()
        keep = [
            pltpu.make_async_copy(src, dst, load_sems.at[i])
            for i, (src, dst) in enumerate(((q_v, q_hbm), (k_v, k_hbm), (v_v, v_hbm), (mid_v, mid_hbm), (mix_v, mix_hbm), (w_v, w_hbm), (wo_v, wo_hbm)))
        ]
        for c in keep:
            c.start()
        for m in range(seqs):
            wires.all_left(i_back + m, attr.at[m, pl.ds(0, n_ex - 1)])
            wires.all_left(i_tok + m, inbox.at[m, pl.ds(0, n_ex - 1)])
        for copy, away, _ in pieces:
            pl.when(away)(copy.wait_send)
        wires.all_left(i_small, small_all.at[pl.ds(0, n_dev - 1)])
        wires.all_left(i_line, wt_b.at[0, pl.ds(0, n_z - 1)])
        wires.all_left(i_wo, wo_b.at[0, 0, pl.ds(0, n_z - 1)])
        wires.all_left(i_wo2, wo_b.at[0, pl.ds(0, n_ex - 1)])
        for c in (w_pair, wo_pair):
            c.wait_send()
        for c in keep:
            c.wait()

    pl.run_scoped(
        forward,
        pltpu.VMEM((seqs, total_len, width), bf), pltpu.VMEM((seqs, total_len, width), bf), pltpu.VMEM((seqs, total_len, width), bf),
        pltpu.VMEM((total_len, dim), bf), pltpu.VMEM((dim, dim), f32),
        pltpu.VMEM((local_len, width), f32), pltpu.VMEM((local_len, 128), f32),
        pltpu.VMEM((seqs, local_len, dim), f32), pltpu.VMEM((seqs, local_len, dim), bf),
        pltpu.VMEM((3, width, dim), bf), pltpu.VMEM((n_ex, dim, width), bf),
        pltpu.VMEM((shard, ff), bf), pltpu.VMEM((half, dim), bf),
    )

    def experts(up_t, down_t, res_acc, gar_acc, hid, gpre, x_t, g_t):
        sub = 256 if tile % 256 == 0 else tile
        pair = n_z - 2

        def loads(step, slot):
            return (
                pltpu.make_async_copy(up_full.at[order(step)], up_t.at[slot], load_sems.at[2 * slot]),
                pltpu.make_async_copy(down_full.at[ag_columns(order(step)), :], down_t.at[slot], load_sems.at[2 * slot + 1]),
            )

        def fetch(step, slot):
            ag_far(order(step))
            ag_ready(order(step))
            for c in loads(step, slot):
                c.start()

        fetch(0, 0)

        def one_round(k, carry):
            per = jnp.where(k == pair, 2, 1)

            def one(q, q_carry):
                m, step = q // per, k + q % per
                j = step % 2
                mine = pl.ds(pl.multiple_of(m * slots, slots), slots)

                @pl.when(m == 0)
                def _():
                    for c in loads(step, j):
                        c.wait()

                @pl.when(step == 0)
                def _():
                    wires.all_came(i_out + m, work.at[m, pl.ds(0, n_ex - 1)])
                    wires.all_left(i_out + m, work.at[m, pl.ds(0, n_ex - 1)])
                    res_acc[m] = jnp.zeros((slots, dim), f32)
                    gar_acc[m] = jnp.zeros((slots, dim), f32)

                def one_sub(u, c_):
                    cols = pl.ds(pl.multiple_of(u * sub, sub), sub)
                    rows = work[m, :, 0].reshape(slots, dim)
                    grads = work[m, :, 1].reshape(slots, dim)
                    pre = mm(rows, up_t[j, :, cols])
                    cdf = 0.5 * (1.0 + lax.erf(pre * (2.0 ** -0.5)))
                    hidden = (pre * cdf).astype(bf)
                    slope = cdf + pre * jnp.exp(-0.5 * pre * pre) * ((2.0 * math.pi) ** -0.5)
                    hid[j, mine, cols] = hidden
                    res_acc[m] += mm(hidden, down_t[j, cols, :])
                    low = (mm(grads, down_t[j, cols, :], NT) * slope).astype(bf)
                    gpre[j, mine, cols] = low
                    gar_acc[m] += mm(low, up_t[j, :, cols], NT)
                    return c_

                lax.fori_loop(0, tile // sub, one_sub, 0)

                @pl.when(step == n_z - 1)
                def _():
                    outbox[m, :, 0] = res_acc[m].astype(bf).reshape(n_ex, cap, dim)
                    outbox[m, :, 1] = gar_acc[m].astype(bf).reshape(n_ex, cap, dim)
                    for d in peers:
                        return_copy(m, d).start()
                    inbox[m, ex] = outbox[m, ex]

                for ahead in range(2, n_z):
                    @pl.when((k == ahead - 2) & (q == 0))
                    def _():
                        ag_pass(order(ahead))

                pl.when((k == pair) & (q == 0))(lambda: fetch(n_z - 1, (n_z - 1) % 2))
                for late in range(n_z - 2):
                    pl.when((k == late + 1) & (q == 0))(lambda: fold(order(late)))
                if n_z > 3:
                    pl.when((k == pair) & (q == seqs))(lambda: add_far(order(0)))
                return q_carry

            lax.fori_loop(0, seqs * per, one, 0)

            @pl.when(k == 0)
            def _():
                for s in range(seqs):
                    lanes = slice(s * slots, (s + 1) * slots)
                    x_t[:, lanes] = work[s, :, 0].reshape(slots, dim).T
                    g_t[:, lanes] = work[s, :, 1].reshape(slots, dim).T

            def weight_grads(jj, jj_carry):
                step = k + jj
                j, t = step % 2, order(step)
                pl.when(k < pair)(lambda: fetch(step + 1, 1 - j))

                def some(u, c_):
                    at_rows = pl.ds(pl.multiple_of(u * mid_dim, mid_dim), mid_dim)
                    up_grad = mm(x_t[at_rows, :], gpre[j]).astype(bf)
                    for s in range(n_z):
                        gup[s % 2, t, u * (n_z // 2) + s // 2] = up_grad[s * shard : (s + 1) * shard, :]
                    down_grad = mm(g_t[at_rows, :], hid[j]).astype(bf)
                    for c in range(2):
                        gdt[c, t, at_rows, :] = down_grad[:, c * half : (c + 1) * half]
                    return c_

                lax.fori_loop(0, 2, some, 0)
                for c in pair_copies(t):
                    c.start()
                pl.when(step == n_z - 1)(lambda: fold(order(n_z - 2)))
                return jj_carry

            lax.fori_loop(0, per, weight_grads, 0)
            return carry

        lax.fori_loop(0, pair + 1, one_round, 0)

    every = seqs * slots
    pl.run_scoped(
        experts,
        pltpu.VMEM((2, dim, tile), bf), pltpu.VMEM((2, tile, dim), bf),
        pltpu.VMEM((seqs, slots, dim), f32), pltpu.VMEM((seqs, slots, dim), f32),
        pltpu.VMEM((2, every, tile), bf), pltpu.VMEM((2, every, tile), bf),
        pltpu.VMEM((dim, every), bf), pltpu.VMEM((dim, every), bf),
    )
    fold(order(n_z - 1))
    ag_finish()

    gain_one, gain_two = smalls[0:1, :], smalls[1:2, :]
    counts = jnp.where(lane < n_ex, 16.0 * tally[0:1, :] + tally[1:2, :], 0.0)
    mean_load = jnp.sum(counts, axis=1, keepdims=True) / n_ex
    load_ratio = (counts - mean_load) / mean_load
    small_out[...] = jnp.zeros(small_out.shape, f32)
    i_gob, i_gw = wires.take(3), wires.take(5)
    gob_pair_copy = wires.copy(i_gob, gob.at[1 - core], gob_pair, at.partner())

    def gob_plane_copy(d):
        peer = at.ex_peer(d)
        return wires.copy(i_gob + 1, gob.at[core, peer], gob_plane.at[d - 1], at.on_ex(peer))

    def gob_line_copy(d):
        peer = at.z_peer(d)
        return wires.copy(i_gob + 2, gob_mine.at[peer], gob_line.at[d - 1], at.on_z(peer))

    gws_pair_copy = wires.copy(i_gw, gws.at[1 - core], gws_pair, at.partner())

    def gws_line_copy(d):
        peer = at.z_peer(d)
        return wires.copy(i_gw + 1, gws.at[core, peer], gws_line.at[d - 1], at.on_z(peer))

    me_j = ex * n_dp + at.dp
    finals = []
    for sec in range(3):
        c = sec * n_dev + me_j
        owner, r = c // 3, c % 3
        copy = wires.copy(i_gw + 2 + r, gws_sum.at[sec], gq_in.at[r], at.numbered(owner))
        finals.append((copy, owner != at.flat, sec, r))

    i_last = wires.take(1)

    def window(t):
        return pl.ds(pl.multiple_of(t * oc // 128 * 128, 128), 256)

    def last_copy(i):
        t = (at.flat + i) % n_dev
        return wires.copy(i_last, small_out.at[:, window(t)], small_in.at[at.flat], at.numbered(t))

    def backward(gb_t, q_v, k_v, v_v, xn_v, mix_v, mid_v, w_v, wo_v, dq, dk, dv, gw, gtok, out_v):
        pairs = ((wo_hbm, wo_v), (mix_hbm, mix_v), (mid_hbm, mid_v), (w_hbm, w_v), (q_hbm, q_v), (k_hbm, k_v), (v_hbm, v_v))
        brought = [pltpu.make_async_copy(src, dst, load_sems.at[i]) for i, (src, dst) in enumerate(pairs)]
        for c in brought:
            c.start()
        for c in brought:
            c.wait()

        def head(m):
            wires.all_came(i_ret + m, inbox.at[m, pl.ds(0, n_ex - 1)])
            wires.all_left(i_ret + m, inbox.at[m, pl.ds(0, n_ex - 1)])
            def some_rows(u, carry):
                at_rows = pl.ds(pl.multiple_of(u * 128, 128), 128)
                place = jnp.where(
                    slot_s[m, at_rows, 0:1] == lax.broadcasted_iota(jnp.int32, (128, slots), 1).astype(f32), 1.0, 0.0
                ).astype(bf)
                expert_out = mm(place, inbox[m, :, 0].reshape(slots, dim))
                gate, named = gate_s[m, at_rows, 0:1], eid_s[m, at_rows, :]
                cot = cot_ref[m, at_rows, :].astype(f32)
                out_v[m, at_rows, :] = (mid_v[m, at_rows, :] + gate * expert_out).astype(bf)
                grad_gate = jnp.sum(cot * expert_out, axis=1, keepdims=True) + balance_coef * jnp.sum(
                    jnp.where(lane == named, load_ratio, 0.0), axis=1, keepdims=True
                )
                grad_logit = grad_gate * gate * (1.0 - gate)
                grad_mixed = mm(place, inbox[m, :, 1].reshape(slots, dim))
                mixed = mix_v[m, at_rows, :].astype(f32)
                for e in range(n_ex):
                    routed = jnp.where(named[:, 0:1] == float(e), grad_logit, 0.0)
                    grad_mixed += routed * smalls[4 + e : 5 + e, :]
                    small_out[4 + e : 5 + e, 0:dim] += jnp.sum(routed * mixed, axis=0, keepdims=True)
                hat, inv = normalised(mid_v[m, at_rows, :])
                small_out[1:2, 0:dim] += jnp.sum(grad_mixed * hat, axis=0, keepdims=True)
                small_out[3:4, 0:dim] += jnp.sum(grad_mixed, axis=0, keepdims=True)
                grad_middle = norm_back(grad_mixed * gain_two, hat, inv) + cot
                gtok[m, at_rows, :] = grad_middle
                branch = grad_middle.astype(bf)
                for e in range(n_ex):
                    rowbox[m, e, at_rows, :] = mm(branch, wo_v[e]).astype(bf)
                gb_t[m, :, at_rows] = branch.T
                return carry

            lax.fori_loop(0, local_len // 128, some_rows, 0)
            for d in peers:
                ga_copy(m, d).start()
            gar[m, ex] = rowbox[m, ex]

        head(0)
        if n_z > 2:
            add_far(order(n_z - 3))
        for m in range(1, seqs):
            head(m)
        wrote = pltpu.make_async_copy(out_v, out_hbm, load_sems.at[0])
        wrote.start()

        for b in range(n_ex):
            total = mm(gb_t[0], attr[0, b])
            for m in range(1, seqs):
                total += mm(gb_t[m], attr[m, b])
            for s in range(n_dev):
                gob[s // n_ex % 2, s % n_ex, s // n_ex // 2, b] = total[s * oc : (s + 1) * oc].astype(bf)
        gob_pair_copy.start()
        gw[...] = jnp.zeros(gw.shape, f32)

        def gob_up():
            gob_pair_copy.wait()
            for e in range(n_ex):
                for zz in range(n_z):
                    gob[core, e, zz] = (gob[core, e, zz].astype(f32) + gob_pair[e, zz].astype(f32)).astype(bf)
            for d in peers:
                gob_plane_copy(d).start()

        def attention_back(m, first=lambda: None):
            xn_copy = pltpu.make_async_copy(xn_hbm.at[m], xn_v, load_sems.at[7])
            xn_copy.start()
            wires.all_came(i_ga + m, gar.at[m, pl.ds(0, n_ex - 1)])
            wires.all_left(i_ga + m, gar.at[m, pl.ds(0, n_ex - 1)])
            first()
            dk[...] = jnp.zeros(dk.shape, f32)
            dv[...] = jnp.zeros(dv.shape, f32)
            dq[...] = jnp.zeros(dq.shape, f32)
            for i in reversed(range(n_ex)):
                end = (i + 1) * local_len
                here = slice(i * local_len, end)

                def one_head(h, carry):
                    mine = lane_head == h
                    qb, ga = q_v[m, here, :], gar[m, i]
                    q_h = jnp.where(mine, qb * scale, jnp.zeros_like(qb))
                    ga_h = jnp.where(mine, ga, jnp.zeros_like(ga))
                    kk = k_v[m, 0:end, :]
                    p = jnp.exp(mm(kk, q_h, NT) - lse[m, pl.ds(h, 1), here])
                    dp = mm(v_v[m, 0:end, :], ga_h, NT)
                    delta = jnp.sum(p * dp, axis=0, keepdims=True)
                    ds = (p * (dp - delta)).astype(bf)
                    dv[0:end, :] += mm(p.astype(bf), ga_h)
                    dk[0:end, :] += mm(ds, q_h)
                    dq[here, :] += jnp.where(mine, mm(ds, kk, TN) * scale, 0.0)
                    return carry

                lax.fori_loop(0, heads, one_head, 0)
                part = mm(dq[here, :].astype(bf), w_v[0]) + mm(dk[here, :].astype(bf), w_v[1]) + mm(dv[here, :].astype(bf), w_v[2])
                outbox[m, i] = part.astype(bf).reshape(2, cap, dim)
                for d in peers:
                    pl.when(at.ex_peer(d) == i)(part_copy(m, d).start)
            inbox[m, ex] = outbox[m, ex]
            xn_copy.wait()
            for sec, g in enumerate((dq, dk, dv)):
                gw[sec] += mm(g[...].astype(bf), xn_v[...], TN)

        attention_back(0, gob_up)
        if n_z > 2:
            add_far(order(n_z - 2))
        wires.all_came(i_gob + 1, gob_plane)
        wires.all_left(i_gob + 1, gob_plane)
        for zz in range(n_z):
            total = gob[core, ex, zz].astype(f32)
            for d in peers:
                total += gob_plane[d - 1, zz].astype(f32)
            gob_mine[zz] = total.astype(bf)
        for d in lines:
            gob_line_copy(d).start()
        for m in range(1, seqs):
            attention_back(m)
        add_far(order(n_z - 1))
        for sec in range(3):
            for j in range(n_dp):
                gws[j % 2, j // 2, sec] = gw[sec, j * piece : (j + 1) * piece, :].astype(bf)
        gws_pair_copy.start()
        gws_pair_copy.wait()
        gws[core] = (gws[core].astype(f32) + gws_pair[...].astype(f32)).astype(bf)
        for d in lines:
            gws_line_copy(d).start()

        def tail(m):
            wires.all_came(i_part + m, inbox.at[m, pl.ds(0, n_ex - 1)])
            wires.all_left(i_part + m, inbox.at[m, pl.ds(0, n_ex - 1)])
            grad_normed = jnp.zeros((local_len, dim), f32)
            for e in range(n_ex):
                grad_normed += inbox[m, e].reshape(local_len, dim).astype(f32)
            hat, inv = normalised(x_ref[m].reshape(local_len, dim).astype(f32))
            small_out[0:1, 0:dim] += jnp.sum(grad_normed * hat, axis=0, keepdims=True)
            small_out[2:3, 0:dim] += jnp.sum(grad_normed, axis=0, keepdims=True)
            gtok[m] += norm_back(grad_normed * gain_one, hat, inv)

        for m in range(seqs):
            tail(m)
        each(n_dev, lambda i: last_copy(i).start())
        small_in[at.flat] = small_out[:, window(at.flat)]
        wrote.wait()
        wrote_tok = pltpu.make_async_copy(gtok, gtok_hbm, load_sems.at[0])
        wrote_tok.start()
        wires.all_came(i_gw + 1, gws_line)
        wires.all_left(i_gw + 1, gws_line)
        total = gws[core, z].astype(f32)
        for d in lines:
            total += gws_line[d - 1].astype(f32)
        gws_sum[...] = total.astype(bf)
        for copy, away, sec, r in finals:
            pl.when(away)(copy.start)
        wrote_tok.wait()

    pl.run_scoped(
        backward,
        pltpu.VMEM((seqs, dim, local_len), bf),
        pltpu.VMEM((seqs, total_len, width), bf), pltpu.VMEM((seqs, total_len, width), bf), pltpu.VMEM((seqs, total_len, width), bf),
        pltpu.VMEM((total_len, dim), bf), pltpu.VMEM((seqs, local_len, dim), bf), pltpu.VMEM((seqs, local_len, dim), f32),
        pltpu.VMEM((3, width, dim), bf), pltpu.VMEM((n_ex, dim, width), bf),
        pltpu.VMEM((total_len, width), f32), pltpu.VMEM((total_len, width), f32), pltpu.VMEM((total_len, width), f32),
        pltpu.VMEM((3, width, dim), f32),
        pltpu.VMEM((seqs, local_len, dim), f32), pltpu.VMEM((seqs, local_len, dim), bf),
    )

    wires.all_came(i_gob + 2, gob_line)
    wires.all_left(i_gob + 2, gob_line)
    total = gob_mine[z].astype(f32)
    for d in lines:
        total += gob_line[d - 1].astype(f32)
    gout_ref[...] = jnp.concatenate([total[b] for b in range(n_ex)], axis=1)

    def settle(up_v, down_v):
        def done(t, carry):
            for c in pair_copies(t):
                c.wait_send()
            for src, dest in pairs_far_first:
                pl.when(z == src)(lambda: line_each(t, src, dest, lambda down: line_copy(t, src, dest, down).wait_send()))
                if abs(dest - src) < 3:
                    pl.when(z == dest)(lambda: line_each(t, src, dest, lambda down: line_copy(t, src, dest, down).wait_recv()))
            return carry

        lax.fori_loop(0, n_z, done, 0)
        for dest in range(n_z):
            came = [s for s in range(n_z) if s != dest and abs(s - dest) < 3]
            places = [2 if abs(s - dest) == 2 else 0 if dest > s else 1 for s in came]

            @pl.when(z == dest)
            def _():
                def some_up(t, carry):
                    total = gup[core, t, dest].astype(f32)
                    for s in places:
                        total += zin_up[s, t].astype(f32)
                    up_v[:, ag_columns(t)] = total
                    return carry

                def some_down(u, carry):
                    at_rows = pl.ds(pl.multiple_of(u * 128, 128), 128)
                    total = gdt[core, dest, at_rows, :].astype(f32)
                    for s in places:
                        total += zin_dn[s, at_rows, :].astype(f32)
                    down_v[:, at_rows] = total.T
                    return carry

                lax.fori_loop(0, n_z, some_up, 0)
                lax.fori_loop(0, dim // 128, some_down, 0)

        wrote = (pltpu.make_async_copy(up_v, gup_hbm, load_sems.at[0]), pltpu.make_async_copy(down_v, gdown_hbm, load_sems.at[1]))
        for c in wrote:
            c.start()
        for c in wrote:
            c.wait()

    pl.run_scoped(settle, pltpu.VMEM((shard, ff), f32), pltpu.VMEM((half, dim), f32))
    for copy, away, sec, r in finals:
        @pl.when(away)
        def _():
            copy.wait()

        @pl.when(jnp.logical_not(away))
        def _():
            gq_in[r] = gws_sum[sec]

    for r in range(3):
        gq_ref[r * piece : (r + 1) * piece, :] = gq_in[r].astype(f32)
    wires.all_came(i_last, small_in.at[pl.ds(0, n_dev - 1)])
    wires.all_left(i_last, small_in.at[pl.ds(0, n_dev - 1)])
    total = jnp.zeros((8, 256), f32)
    for s in range(n_dev):
        total += small_in[s]
    gsmall_ref[...] = total


def whole_layer(n_dp, n_ex, x, cot, ids, wq, wo, gains, biases, router, w_up, w_down):
    bf, f32 = jnp.bfloat16, jnp.float32
    seqs, local_len, dim = cot.shape
    width, total_len, n_z, n_dev = dim // n_ex, local_len * n_ex, n_dp // 2, n_dp * n_ex
    cap = x.shape[2]
    shard, ff = w_up.shape
    half = w_down.shape[0]
    piece, oc, tile = wq.shape[1], wo.shape[0], ff // n_z
    vmem_outs = [((3 * piece, dim), f32), ((oc, dim), f32), ((8, 256), f32)]
    hbm_outs = [
        ((seqs, local_len, dim), bf), ((seqs, local_len, dim), f32), ((shard, ff), f32), ((half, dim), f32),
        ((n_z, dim, ff // n_z), bf), ((ff, dim), bf),
        ((seqs, total_len, width), bf), ((seqs, total_len, width), bf), ((seqs, total_len, width), bf), ((seqs, total_len, dim), bf),
        ((seqs, local_len, dim), bf), ((seqs, local_len, dim), f32), ((3, width, dim), bf), ((n_ex, dim, width), bf),
    ]
    box = pltpu.VMEM((seqs, n_ex, 2, cap, dim), bf)
    rows = pltpu.VMEM((seqs, n_ex, local_len, width), bf)
    n_sems = 2 + 6 * seqs + 14 * (n_z + 1) + 2 * n_z + 8 + 8
    sems = pltpu.SemaphoreType.DMA((n_sems,))
    return pl.pallas_call(
        functools.partial(layer_kernel, n_dp, n_ex),
        out_shape=[jax.ShapeDtypeStruct(s, d) for s, d in vmem_outs + hbm_outs],
        in_specs=[VMEM] * 8 + [HBM] * 2,
        out_specs=[VMEM] * len(vmem_outs) + [HBM] * len(hbm_outs),
        scratch_shapes=[
            box, box, box,
            pltpu.VMEM((2, n_z, dim, half), bf), pltpu.VMEM((2, n_z, n_z, shard, tile), bf),
            pltpu.VMEM((n_z, dim, half), bf), pltpu.VMEM((n_z, n_z, shard, tile), bf),
            pltpu.VMEM((3, dim, half), bf), pltpu.VMEM((3, n_z, shard, tile), bf),
            pltpu.VMEM((dim, half), bf), pltpu.VMEM((n_z, shard, tile), bf),
            rows, rows, rows,
            pltpu.VMEM((2, n_ex, n_z, n_ex, oc, width), bf), pltpu.VMEM((n_ex, n_z, n_ex, oc, width), bf),
            pltpu.VMEM((n_z - 1, n_ex, oc, width), bf), pltpu.VMEM((n_z, n_ex, oc, width), bf), pltpu.VMEM((n_ex - 1, n_z, n_ex, oc, width), bf),
            pltpu.VMEM((3, piece, dim), bf), pltpu.VMEM((2, n_z, 3, piece, dim), bf), pltpu.VMEM((n_z, 3, piece, dim), bf),
            pltpu.VMEM((n_z - 1, 3, piece, dim), bf), pltpu.VMEM((3, piece, dim), bf),
            pltpu.VMEM((16, 128), bf), pltpu.VMEM((n_ex, oc, width), bf), pltpu.VMEM((3, piece, dim), bf),
            pltpu.VMEM((n_dev, 16, 128), bf), pltpu.VMEM((n_dev, 8, 256), f32), pltpu.VMEM((8, dim + 256), f32),
            pltpu.VMEM((16, dim), f32), pltpu.VMEM((8, 128), f32),
            pltpu.VMEM((seqs, local_len, 128), f32), pltpu.VMEM((seqs, local_len, 128), f32), pltpu.VMEM((seqs, local_len, 128), f32),
            pltpu.VMEM((seqs, 8, total_len), f32),
            sems, sems, pltpu.SemaphoreType.DMA((8,)),
        ],
        compiler_params=pltpu.CompilerParams(collective_id=0, has_side_effects=True, vmem_limit_bytes=67043328),
        name="whole_layer",
    )(x, cot, ids, wq, wo, gains, biases, router, w_up, w_down)


def fast_body(tokens, cotangent, expert_ids, w_qkv, w_out, ln_gains, ln_biases, router, w_up, w_down):
    n_expert, n_dp = lax.axis_size("expert"), lax.axis_size("dp")
    seqs, local_len, dim = tokens.shape[0] * tokens.shape[1], tokens.shape[2], tokens.shape[3]
    qc, oc = w_qkv.shape[1], w_out.shape[1]
    n_small = 4 + n_expert
    flat = lax.axis_index("dp") * n_expert + lax.axis_index("expert")
    got = whole_layer(
        n_dp, n_expert, tokens.reshape(seqs, 2, local_len // 2, dim), cotangent.reshape(seqs, local_len, dim), expert_ids.reshape(seqs, local_len),
        w_qkv.T.reshape(3, qc // 3, dim), w_out.T, ln_gains, ln_biases, router, w_up[0], w_down[0],
    )
    gq, gout, gs, output, grad_tokens, gu, gd = got[:7]
    grad_qkv, grad_out = gq.T, gout.T
    gs = lax.dynamic_slice(gs, (0, lax.rem(flat * oc, 128)), (n_small, oc))
    shape = tokens.shape
    return (output.reshape(shape), grad_tokens.reshape(shape), grad_qkv, grad_out, gs[0:2], gs[2:4], gs[4:].T, gu[None], gd[None])


def solution(mesh):
    in_specs = (
        P(None, "dp", "expert", None),
        P(None, "dp", "expert", None),
        P(None, "dp", "expert", None),
        P(None, ("dp", "expert")),
        P(None, ("dp", "expert")),
        P(None, ("dp", "expert")),
        P(None, ("dp", "expert")),
        P(("dp", "expert"), None),
        P("expert", "dp", None),
        P("expert", "dp", None),
    )
    out_specs = (
        P(None, "dp", "expert", None),
        P(None, "dp", "expert", None),
        P(None, ("dp", "expert")),
        P(None, ("dp", "expert")),
        P(None, ("dp", "expert")),
        P(None, ("dp", "expert")),
        P(("dp", "expert"), None),
        P("expert", "dp", None),
        P("expert", "dp", None),
    )
    n_expert, n_dp = mesh.shape["expert"], mesh.shape["dp"]
    chosen = fast_body if n_expert == 4 and n_dp % 4 == 0 and n_dp <= 8 else body
    return jax.shard_map(chosen, mesh=mesh, in_specs=in_specs, out_specs=out_specs, check_vma=False)
```

```python
import functools
import math

import jax
import jax.numpy as jnp
from jax import lax
from jax.experimental import pallas as pl
from jax.experimental.pallas import tpu as pltpu
from jax.sharding import PartitionSpec as P

HEADS = 12
FF = 3072
BLK = 256
MICRO = 2


epsilon = 1e-05
balance_coef = 8.0
neg_big = -1e30


def layer_norm(features, gain_vec, shift_vec):
    centre = features - jnp.mean(features, axis=-1, keepdims=True)
    spread = jnp.mean(centre * centre, axis=-1, keepdims=True)
    return centre * lax.rsqrt(spread + epsilon) * gain_vec + shift_vec


def gelu_exact(preact):
    return jax.nn.gelu(preact, approximate=False)


def fetch_all(w_qkv, w_out, ln_gains, ln_biases, router, w_up, w_down):
    dense_set = (
        lax.all_gather(w_qkv, ("dp", "expert"), axis=1, tiled=True),
        lax.all_gather(w_out, ("dp", "expert"), axis=1, tiled=True),
        lax.all_gather(ln_gains, ("dp", "expert"), axis=1, tiled=True),
        lax.all_gather(ln_biases, ("dp", "expert"), axis=1, tiled=True),
        lax.all_gather(router, ("dp", "expert"), axis=0, tiled=True),
    )
    expert_set = (
        lax.all_gather(w_up, "dp", axis=1, tiled=True),
        lax.all_gather(w_down, "dp", axis=1, tiled=True),
    )
    return tuple(dense_set) + tuple(expert_set)


def route_slots(expert_of, experts, capacity):
    seq_here, local_len = expert_of.shape
    matches = (expert_of[..., None] == lax.iota(jnp.int32, experts)).astype(jnp.int32)
    order_in = jnp.sum((jnp.cumsum(matches, axis=1) - matches) * matches, axis=-1)
    seq_index = lax.broadcasted_iota(jnp.int32, (seq_here, local_len), 0)
    target = (expert_of * (seq_here * capacity) + seq_index * capacity + order_in).reshape(-1)
    slot_table = jnp.full((experts * seq_here * capacity,), seq_here * local_len, jnp.int32)
    slot_table = slot_table.at[target].set(lax.iota(jnp.int32, seq_here * local_len))
    return (target, slot_table)


def to_slots(features, slot_table):
    flat_rows = features.reshape(-1, features.shape[-1])
    padded = jnp.concatenate(
        [flat_rows, jnp.zeros((1, flat_rows.shape[1]), flat_rows.dtype)], axis=0
    )
    return padded[slot_table]


def score_terms(
    queries, grad_rows, key_block, value_block, log_total, row_delta, allowed, score_scale
):
    scores = (
        jnp.einsum("sqhd,skhd->shqk", queries, key_block, preferred_element_type=jnp.float32)
        * score_scale
    )
    weights = jnp.where(allowed, jnp.exp(scores - log_total[..., None]), 0.0)
    grad_weights = jnp.einsum(
        "sqhd,skhd->shqk", grad_rows, value_block, preferred_element_type=jnp.float32
    )
    grad_scores = (weights * (grad_weights - row_delta[..., None]) * score_scale).astype(
        jnp.bfloat16
    )
    return (weights.astype(jnp.bfloat16), grad_scores)


def attention_forward(queries, key_rows, value_rows, query_pos, score_scale):
    seq_here, local_len, head_count, head_dim = queries.shape
    last_block = query_pos[local_len - 1] // BLK
    start_state = (
        jnp.full((seq_here, head_count, local_len), neg_big, jnp.float32),
        jnp.zeros((seq_here, head_count, local_len), jnp.float32),
        jnp.zeros((seq_here, local_len, head_count, head_dim), jnp.float32),
    )
    key_part = lax.all_gather(key_rows, "expert", axis=1, tiled=True)
    value_part = lax.all_gather(value_rows, "expert", axis=1, tiled=True)
    piece_len = key_part.shape[1]
    block_len = math.gcd(piece_len, 512)

    def attention_one_block(block_index, carried):
        within = block_index * block_len
        key_block = lax.dynamic_slice_in_dim(key_part, within, block_len, 1).reshape(
            seq_here, block_len, head_count, head_dim
        )
        value_block = lax.dynamic_slice_in_dim(value_part, within, block_len, 1).reshape(
            seq_here, block_len, head_count, head_dim
        )
        key_pos = within + lax.iota(jnp.int32, block_len)
        allowed = key_pos[None, :] // BLK <= query_pos[:, None] // BLK

        def attention_compute(current):
            run_max, run_sum, weighted = current
            scores = (
                jnp.einsum(
                    "sqhd,skhd->shqk", queries, key_block, preferred_element_type=jnp.float32
                )
                * score_scale
            )
            new_max = jnp.maximum(run_max, jnp.max(jnp.where(allowed, scores, neg_big), axis=-1))
            weights = jnp.where(allowed, jnp.exp(scores - new_max[..., None]), 0.0)
            factor = jnp.exp(run_max - new_max)
            run_sum = run_sum * factor + jnp.sum(weights, axis=-1)
            addition = jnp.einsum(
                "shqk,skhd->sqhd",
                weights.astype(jnp.bfloat16),
                value_block,
                preferred_element_type=jnp.float32,
            )
            weighted = weighted * jnp.swapaxes(factor, 1, 2)[..., None] + addition
            return (new_max, run_sum, weighted)

        return lax.cond(
            within // BLK <= last_block, attention_compute, lambda current: current, carried
        )

    run_max, run_sum, weighted = lax.fori_loop(
        0, piece_len // block_len, attention_one_block, start_state
    )
    log_total = run_max + jnp.log(run_sum)
    attended = weighted / jnp.swapaxes(run_sum, 1, 2)[..., None]
    return (log_total, attended)


def query_grads(
    queries, grad_rows, key_rows, value_rows, log_total, row_delta, query_pos, score_scale, seq_len
):
    seq_here, local_len, head_count, head_dim = queries.shape
    model_dim = head_count * head_dim
    last_block = query_pos[local_len - 1] // BLK
    start_query = jnp.zeros((seq_here, local_len, head_count, head_dim), jnp.float32)
    start_state = (start_query, jnp.zeros((seq_here, seq_len, 2 * model_dim), jnp.float32))
    key_part = lax.all_gather(key_rows, "expert", axis=1, tiled=True)
    value_part = lax.all_gather(value_rows, "expert", axis=1, tiled=True)
    piece_len = key_part.shape[1]
    block_len = math.gcd(piece_len, 512)

    def query_one_block(block_index, carried):
        within = block_index * block_len
        key_block = lax.dynamic_slice_in_dim(key_part, within, block_len, 1).reshape(
            seq_here, block_len, head_count, head_dim
        )
        value_block = lax.dynamic_slice_in_dim(value_part, within, block_len, 1).reshape(
            seq_here, block_len, head_count, head_dim
        )
        key_pos = within + lax.iota(jnp.int32, block_len)
        allowed = key_pos[None, :] // BLK <= query_pos[:, None] // BLK

        def query_compute(current):
            weights, grad_scores = score_terms(
                queries,
                grad_rows,
                key_block,
                value_block,
                log_total,
                row_delta,
                allowed,
                score_scale,
            )
            grad_query = current[0] + jnp.einsum(
                "shqk,skhd->sqhd", grad_scores, key_block, preferred_element_type=jnp.float32
            )
            grad_key = jnp.einsum(
                "shqk,sqhd->skhd", grad_scores, queries, preferred_element_type=jnp.float32
            ).reshape(seq_here, block_len, model_dim)
            grad_value = jnp.einsum(
                "shqk,sqhd->skhd", weights, grad_rows, preferred_element_type=jnp.float32
            ).reshape(seq_here, block_len, model_dim)
            old_rows = lax.dynamic_slice_in_dim(current[1], within, block_len, 1)
            summed = old_rows + jnp.concatenate([grad_key, grad_value], axis=-1)
            return (grad_query, lax.dynamic_update_slice_in_dim(current[1], summed, within, 1))

        return lax.cond(
            within // BLK <= last_block, query_compute, lambda current: current, carried
        )

    return lax.fori_loop(0, piece_len // block_len, query_one_block, start_state)


def body(tokens, cotangent, expert_ids, w_qkv, w_out, ln_gains, ln_biases, router, w_up, w_down):
    n_expert = lax.axis_size("expert")
    seq_part = lax.axis_index("expert")
    seq_here, local_len, model_dim = (tokens.shape[1], tokens.shape[2], tokens.shape[3])
    head_count = HEADS
    head_dim = model_dim // head_count
    score_scale = head_dim ** (-0.5)
    exp_dev = w_up.shape[0]
    experts = exp_dev * n_expert
    capacity = 2 * local_len // experts
    seq_len = local_len * n_expert
    query_pos = seq_part * local_len + lax.iota(jnp.int32, local_len)
    expert_range = lax.iota(jnp.int32, experts)
    all_ids = expert_ids[..., 0]
    local_counts = jnp.sum((all_ids[..., None] == expert_range).astype(jnp.float32), axis=(0, 1, 2))
    counts = lax.psum(local_counts, ("dp", "expert"))
    mean_load = jnp.sum(counts) / experts
    load_ratio = (counts - mean_load) / mean_load
    grad_qkv_w = jnp.zeros((model_dim, 3 * model_dim), jnp.float32)
    grad_out_w = jnp.zeros((model_dim, model_dim), jnp.float32)
    grad_gains = jnp.zeros((2, model_dim), jnp.float32)
    grad_shifts = jnp.zeros((2, model_dim), jnp.float32)
    grad_router = jnp.zeros((model_dim, experts), jnp.float32)
    grad_up = jnp.zeros((exp_dev, model_dim, FF), jnp.float32)
    grad_down = jnp.zeros((exp_dev, FF, model_dim), jnp.float32)
    outputs = []
    input_grads = []
    for micro_index in range(MICRO):
        fetched = fetch_all(w_qkv, w_out, ln_gains, ln_biases, router, w_up, w_down)
        qkv_full, out_full, gains_full, shifts_full, router_full, up_full, down_full = fetched
        gain_rows = gains_full.astype(jnp.float32)
        shift_rows = shifts_full.astype(jnp.float32)
        inputs = tokens[micro_index].astype(jnp.float32)
        expert_of = all_ids[micro_index]
        normed = layer_norm(inputs, gain_rows[0], shift_rows[0])
        normed_low = normed.astype(jnp.bfloat16)
        projected = jnp.einsum(
            "scd,de->sce", normed_low, qkv_full, preferred_element_type=jnp.float32
        ).astype(jnp.bfloat16)
        query_rows = projected[..., :model_dim]
        queries = query_rows.reshape(seq_here, local_len, head_count, head_dim)
        key_rows = projected[..., model_dim : 2 * model_dim]
        value_rows = projected[..., 2 * model_dim :]
        log_total, attended = attention_forward(
            queries, key_rows, value_rows, query_pos, score_scale
        )
        attended_low = attended.reshape(seq_here, local_len, model_dim).astype(jnp.bfloat16)
        middle = inputs + jnp.einsum(
            "scd,de->sce", attended_low, out_full, preferred_element_type=jnp.float32
        )
        mixed_low = layer_norm(middle, gain_rows[1], shift_rows[1]).astype(jnp.bfloat16)
        onehot = (expert_of[..., None] == expert_range).astype(jnp.float32)
        logits = jnp.einsum(
            "scd,de->sce", mixed_low, router_full, preferred_element_type=jnp.float32
        )
        gates = jax.nn.sigmoid(jnp.sum(logits * onehot, axis=-1))
        target, slot_table = route_slots(expert_of, experts, capacity)
        outgoing = to_slots(mixed_low, slot_table).reshape(
            n_expert, exp_dev, seq_here * capacity, model_dim
        )
        arrived = lax.all_to_all(outgoing, "expert", split_axis=0, concat_axis=0, tiled=True)
        preact = jnp.einsum("pesd,edf->pesf", arrived, up_full, preferred_element_type=jnp.float32)
        hidden = gelu_exact(preact).astype(jnp.bfloat16)
        result = jnp.einsum(
            "pesf,efd->pesd", hidden, down_full, preferred_element_type=jnp.float32
        ).astype(jnp.bfloat16)
        returned = lax.all_to_all(result, "expert", split_axis=0, concat_axis=0, tiled=True)
        expert_out = (
            returned.reshape(-1, model_dim)[target]
            .reshape(seq_here, local_len, model_dim)
            .astype(jnp.float32)
        )
        final = middle + gates[..., None] * expert_out
        outputs.append(final.astype(jnp.bfloat16))
        fetched = fetch_all(w_qkv, w_out, ln_gains, ln_biases, router, w_up, w_down)
        qkv_full, out_full, gains_full, shifts_full, router_full, up_full, down_full = fetched
        gain_rows = gains_full.astype(jnp.float32)
        shift_rows = shifts_full.astype(jnp.float32)
        grad_final = cotangent[micro_index].astype(jnp.float32)
        grad_gate = jnp.sum(grad_final * expert_out, axis=-1) + balance_coef * jnp.sum(
            onehot * load_ratio, axis=-1
        )
        grad_logit = grad_gate * gates * (1.0 - gates)
        grad_expert = (gates[..., None] * grad_final).astype(jnp.bfloat16)
        sent_grads = to_slots(grad_expert, slot_table).reshape(
            n_expert, exp_dev, seq_here * capacity, model_dim
        )
        grads_here = lax.all_to_all(sent_grads, "expert", split_axis=0, concat_axis=0, tiled=True)
        hidden_low = gelu_exact(preact).astype(jnp.bfloat16)
        grad_down = grad_down + jnp.einsum(
            "pesf,pesd->efd", hidden_low, grads_here, preferred_element_type=jnp.float32
        )
        grad_hidden = jnp.einsum(
            "pesd,efd->pesf", grads_here, down_full, preferred_element_type=jnp.float32
        )
        grad_pre = jax.vjp(gelu_exact, preact)[1](grad_hidden)[0].astype(jnp.bfloat16)
        grad_up = grad_up + jnp.einsum(
            "pesd,pesf->edf", arrived, grad_pre, preferred_element_type=jnp.float32
        )
        grad_arrived = jnp.einsum(
            "pesf,edf->pesd", grad_pre, up_full, preferred_element_type=jnp.float32
        ).astype(jnp.bfloat16)
        grads_back = lax.all_to_all(grad_arrived, "expert", split_axis=0, concat_axis=0, tiled=True)
        grad_mixed = (
            grads_back.reshape(-1, model_dim)[target]
            .reshape(seq_here, local_len, model_dim)
            .astype(jnp.float32)
        )
        router_cols = jnp.einsum("sce,de->scd", onehot, router_full.astype(jnp.float32))
        grad_mixed = grad_mixed + grad_logit[..., None] * router_cols
        grad_router = grad_router + jnp.einsum(
            "scd,sce->de", mixed_low.astype(jnp.float32), grad_logit[..., None] * onehot
        )
        second_back = jax.vjp(layer_norm, middle, gain_rows[1], shift_rows[1])[1]
        grad_middle, grad_gain_two, grad_shift_two = second_back(grad_mixed)
        grad_middle = grad_middle + grad_final
        grad_branch = grad_middle.astype(jnp.bfloat16)
        grad_out_w = grad_out_w + jnp.einsum(
            "scd,sce->de", attended_low, grad_branch, preferred_element_type=jnp.float32
        )
        grad_attended = jnp.einsum(
            "sce,de->scd", grad_branch, out_full, preferred_element_type=jnp.float32
        ).astype(jnp.bfloat16)
        grad_heads = grad_attended.reshape(seq_here, local_len, head_count, head_dim)
        row_delta = jnp.swapaxes(jnp.sum(grad_heads.astype(jnp.float32) * attended, axis=-1), 1, 2)
        folded = query_grads(
            queries,
            grad_heads,
            key_rows,
            value_rows,
            log_total,
            row_delta,
            query_pos,
            score_scale,
            seq_len,
        )
        grad_query = folded[0].reshape(seq_here, local_len, model_dim)
        key_value = lax.psum_scatter(
            folded[1].astype(jnp.bfloat16), "expert", scatter_dimension=1, tiled=True
        ).astype(jnp.float32)
        grad_key = key_value[..., :model_dim]
        grad_value = key_value[..., model_dim:]
        grad_projected = jnp.concatenate([grad_query, grad_key, grad_value], axis=-1).astype(
            jnp.bfloat16
        )
        grad_qkv_w = grad_qkv_w + jnp.einsum(
            "scd,sce->de", normed_low, grad_projected, preferred_element_type=jnp.float32
        )
        grad_normed = jnp.einsum(
            "sce,de->scd", grad_projected, qkv_full, preferred_element_type=jnp.float32
        )
        first_back = jax.vjp(layer_norm, inputs, gain_rows[0], shift_rows[0])[1]
        grad_inputs, grad_gain_one, grad_shift_one = first_back(grad_normed)
        grad_gains = grad_gains + jnp.stack([grad_gain_one, grad_gain_two])
        grad_shifts = grad_shifts + jnp.stack([grad_shift_one, grad_shift_two])
        input_grads.append(grad_middle + grad_inputs)
    dense_grads = (
        lax.psum_scatter(grad_qkv_w, ("dp", "expert"), scatter_dimension=1, tiled=True),
        lax.psum_scatter(grad_out_w, ("dp", "expert"), scatter_dimension=1, tiled=True),
        lax.psum_scatter(grad_gains, ("dp", "expert"), scatter_dimension=1, tiled=True),
        lax.psum_scatter(grad_shifts, ("dp", "expert"), scatter_dimension=1, tiled=True),
        lax.psum_scatter(grad_router, ("dp", "expert"), scatter_dimension=0, tiled=True),
    )
    expert_grads = (
        lax.psum_scatter(
            grad_up.astype(jnp.bfloat16), "dp", scatter_dimension=1, tiled=True
        ).astype(jnp.float32),
        lax.psum_scatter(
            grad_down.astype(jnp.bfloat16), "dp", scatter_dimension=1, tiled=True
        ).astype(jnp.float32),
    )
    return (jnp.stack(outputs), jnp.stack(input_grads)) + tuple(dense_grads) + tuple(expert_grads)


MESH_ID = pl.DeviceIdType.MESH
NT = (((1,), (1,)), ((), ()))
NN = (((1,), (0,)), ((), ()))
TN = (((0,), (0,)), ((), ()))
VMEM = pl.BlockSpec(memory_space=pltpu.VMEM)
HBM = pl.BlockSpec(memory_space=pl.ANY)


def mm(a, b, dims=NN):
    return lax.dot_general(a, b, dims, preferred_element_type=jnp.float32)


def normalised(v):
    centre = v - jnp.mean(v, axis=-1, keepdims=True)
    spread = jnp.mean(centre * centre, axis=-1, keepdims=True)
    inv = lax.rsqrt(spread + epsilon)
    return centre * inv, inv


def side_by_side(v):
    half = v.shape[0] // 2
    return jnp.concatenate([v[:half], v[half:]], axis=1)


def stacked(v):
    half = v.shape[1] // 2
    return jnp.concatenate([v[:, :half], v[:, half:]], axis=0)


def norm_back(grad_hat, hat, inv):
    return inv * (grad_hat - jnp.mean(grad_hat, axis=1, keepdims=True) - hat * jnp.mean(grad_hat * hat, axis=1, keepdims=True))


def add_into(target, other, step):
    def some(u, carry):
        rows = pl.ds(pl.multiple_of(u * step, step), step)
        target[rows, :] = (target[rows, :].astype(jnp.float32) + other[rows, :].astype(jnp.float32)).astype(target.dtype)
        return carry

    lax.fori_loop(0, target.shape[0] // step, some, 0)


class Place:
    def __init__(self, n_dp, n_ex):
        self.n_dp, self.n_ex, self.n_dev, self.n_z = n_dp, n_ex, n_dp * n_ex, n_dp // 2
        self.dp, self.ex = lax.axis_index("dp"), lax.axis_index("expert")
        self.z, self.core = self.dp // 2, self.dp % 2
        self.flat = self.dp * n_ex + self.ex

    def z_peer(self, d):
        return (self.z + d) % self.n_z

    def ex_peer(self, d):
        return (self.ex + d) % self.n_ex

    def on_z(self, z):
        return (z * 2 + self.core, self.ex)

    def on_ex(self, e):
        return (self.dp, e)

    def partner(self):
        return (self.z * 2 + 1 - self.core, self.ex)

    def numbered(self, t):
        return (t // self.n_ex, t % self.n_ex)


def entry_barrier(at):
    sem = pltpu.get_barrier_semaphore()

    def tell(i, carry):
        pl.semaphore_signal(sem, inc=1, device_id=at.numbered((at.flat + i) % at.n_dev), device_id_type=MESH_ID)
        return carry

    lax.fori_loop(1, at.n_dev, tell, 0)
    pl.semaphore_wait(sem, at.n_dev - 1)


class Wires:
    def __init__(self, send_sems, recv_sems):
        self.send_sems, self.recv_sems, self.used = send_sems, recv_sems, 0

    def take(self, n):
        base = self.used
        self.used = base + n
        return base

    def copy(self, i, src, dst, device):
        return pltpu.make_async_remote_copy(
            src_ref=src, dst_ref=dst, send_sem=self.send_sems.at[i], recv_sem=self.recv_sems.at[i],
            device_id=device, device_id_type=MESH_ID,
        )

    def all_came(self, i, blocks):
        pltpu.make_async_copy(blocks, blocks, self.recv_sems.at[i]).wait()

    def all_left(self, i, blocks):
        pltpu.make_async_copy(blocks, blocks, self.send_sems.at[i]).wait()


def layer_kernel(
    n_dp, n_ex, x_ref, cot_ref, ids_ref, wq_ref, wo_ref, gain_ref, bias_ref, router_ref, up_hbm, down_hbm,
    gq_ref, gout_ref, gsmall_ref, out_hbm, gtok_hbm, gup_hbm, gdown_hbm, up_full, down_full, q_hbm, k_hbm, v_hbm, xn_hbm, mix_hbm, mid_hbm, w_hbm, wo_hbm,
    outbox, inbox, work, gdt, gup, pin_dn, pin_up, zin_dn, zin_up, via_dn, via_up, rowbox, attr, gar,
    gob, gob_pair, gob_line, gob_mine, gob_plane, wt_a, gws, gws_pair, gws_line, gws_sum,
    small_b, wo_s, gq_in, small_all, small_in, small_out, smalls, tally, gate_s, slot_s, eid_s, lse, send_sems, recv_sems, load_sems,
):
    bf, f32 = jnp.bfloat16, jnp.float32
    at = Place(n_dp, n_ex)
    wires = Wires(send_sems, recv_sems)
    n_dev, n_z, ex, z, core = at.n_dev, at.n_z, at.ex, at.z, at.core
    seqs, dim = x_ref.shape[0], x_ref.shape[3]
    cap = x_ref.shape[2]
    local_len = 2 * cap
    total_len, width, slots = local_len * n_ex, dim // n_ex, n_ex * cap
    head_dim = dim // HEADS
    heads = width // head_dim
    piece, oc = wq_ref.shape[1], wo_ref.shape[0]
    shard, ff = up_hbm.shape
    half = down_hbm.shape[0]
    tile, mid_dim = ff // n_z, dim // 2
    scale = head_dim ** -0.5
    wt_b, wo_b = gws, gob
    lane = lax.broadcasted_iota(jnp.int32, (1, 128), 1).astype(f32)
    lane_head = lax.broadcasted_iota(jnp.int32, (1, width), 1) // head_dim
    peers = range(1, n_ex)

    small_out[...] = jnp.zeros(small_out.shape, f32)
    small_out[0:2, 0:oc] = gain_ref[...].astype(f32)
    small_out[2:4, 0:oc] = bias_ref[...].astype(f32)
    unit = jnp.where(lax.broadcasted_iota(jnp.int32, (oc, oc), 0) == lax.broadcasted_iota(jnp.int32, (oc, oc), 1), 1.0, 0.0).astype(bf)
    small_out[4 : 4 + n_ex, 0:oc] = mm(router_ref[...], unit, TN)
    held_rows = jnp.zeros((1, 128), f32)
    for m in range(seqs):
        eid_s[m] = jnp.broadcast_to(ids_ref[m : m + 1, :].astype(f32), (128, local_len)).T
        held_rows += jnp.sum(jnp.where(lane == eid_s[m], 1.0, 0.0), axis=0, keepdims=True)
    high = jnp.floor(held_rows * (1.0 / 16.0))
    small_b[0:8, :] = small_out[0:8, 0:128].astype(bf)
    row = lax.broadcasted_iota(jnp.int32, (8, 128), 0)
    small_b[8:16, :] = jnp.where(row == 0, high, jnp.where(row == 1, held_rows - 16.0 * high, 0.0)).astype(bf)
    for b in range(n_ex):
        wo_s[b] = wo_ref[:, b * width : (b + 1) * width]
    lines = range(1, n_z)
    entry_barrier(at)

    i_tok, i_back, i_out, i_ret, i_ga, i_part = (wires.take(seqs) for _ in range(6))

    def token_copy(m, d):
        return wires.copy(i_tok + m, x_ref.at[m], inbox.at[m, ex], at.on_ex(at.ex_peer(d)))

    def back_copy(m, d):
        peer = at.ex_peer(d)
        return wires.copy(i_back + m, rowbox.at[m, peer], attr.at[m, ex], at.on_ex(peer))

    def out_copy(m, d):
        peer = at.ex_peer(d)
        return wires.copy(i_out + m, outbox.at[m, peer], work.at[m, ex], at.on_ex(peer))

    def return_copy(m, d):
        peer = at.ex_peer(d)
        return wires.copy(i_ret + m, outbox.at[m, peer], inbox.at[m, ex], at.on_ex(peer))

    def ga_copy(m, d):
        peer = at.ex_peer(d)
        return wires.copy(i_ga + m, rowbox.at[m, peer], gar.at[m, ex], at.on_ex(peer))

    def part_copy(m, d):
        peer = at.ex_peer(d)
        return wires.copy(i_part + m, outbox.at[m, peer], inbox.at[m, ex], at.on_ex(peer))

    reach = [d for d in (2, 1) if d < n_z]

    def order(step):
        return (n_z - 1) * step % n_z

    relay = n_z > 3
    kinds = n_z + 1
    i_ag, i_agp = wires.take(5 * kinds), wires.take(5 * kinds)

    def ag_columns(t):
        return pl.ds(pl.multiple_of(t * tile, tile), tile)

    def ag_block(t, zz, cc, down):
        if down:
            return down_full.at[pl.ds(pl.multiple_of((zz * 2 + cc) * half, half), half), :]
        return up_full.at[t, pl.ds(pl.multiple_of((zz * 2 + cc) * shard, shard), shard), :]

    def ag_own(t, down):
        return down_hbm if down else up_hbm.at[:, ag_columns(t)]

    def ag_code(right, d, t, down):
        return (d if d != 1 or right else 4) * kinds + (n_z if down else t)

    def ag_copy(right, d, t, down):
        return wires.copy(i_ag + ag_code(right, d, t, down), ag_own(t, down), ag_block(t, z, core, down), at.on_z(z + d if right else z - d))

    def ag_relay(right, t, down):
        block = ag_block(t, z - 2 if right else z + 2, core, down)
        return wires.copy(i_ag + ag_code(right, 3, t, down), block, block, at.on_z(z + 1 if right else z - 1))

    def ag_pair(right, d, t, down):
        block = ag_block(t, z - d if right else z + d, core, down)
        return wires.copy(i_agp + ag_code(right, d, t, down), ag_own(t, down) if d == 0 else block, block, at.partner())

    def ag_sends(right, d):
        return z + d < n_z if right else z - d >= 0

    def ag_comes(right, d):
        return z - d >= 0 if right else z + d < n_z

    def ag_relays(right):
        return z == n_z - 2 if right else z == 1

    def ag_from(right, d, t, act):
        @pl.when(ag_comes(right, d))
        def _():
            act(False)
            pl.when((z - d if right else z + d) == t)(lambda: act(True))

    def ag_start(t):
        for d in reach:
            for right in (True, False):
                @pl.when(ag_sends(right, d))
                def _():
                    ag_copy(right, d, t, False).start()
                    pl.when(z == t)(ag_copy(right, d, t, True).start)
        ag_from(True, 0, t, lambda down: ag_pair(True, 0, t, down).start())

    def ag_pass(t):
        for d in reach:
            for right in (True, False):
                def act(down, right=right, d=d):
                    ag_copy(right, d, t, down).wait_recv()
                    if d == 2 and relay:
                        pl.when(ag_relays(right))(ag_relay(right, t, down).start)
                    ag_pair(right, d, t, down).start()

                ag_from(right, d, t, act)

    def ag_far(t):
        if relay:
            for right in (True, False):
                def act(down, right=right):
                    ag_copy(right, 3, t, down).wait_recv()
                    ag_pair(right, 3, t, down).start()

                ag_from(right, 3, t, act)

    far = [0] + sorted(reach) + ([3] if relay else [])

    def ag_ready(t):
        for d in far:
            for right in (True, False) if d else (True,):
                ag_from(right, d, t, lambda down, right=right, d=d: ag_pair(right, d, t, down).wait_recv())

    def ag_finish():
        def one(t, carry):
            for d in far:
                for right in (True, False) if d else (True,):
                    ag_from(right, d, t, lambda down, right=right, d=d: ag_pair(right, d, t, down).wait_send())
            for d in reach:
                for right in (True, False):
                    @pl.when(ag_sends(right, d))
                    def _():
                        ag_copy(right, d, t, False).wait_send()
                        pl.when(z == t)(ag_copy(right, d, t, True).wait_send)
            if relay:
                for right in (True, False):
                    @pl.when(ag_relays(right))
                    def _():
                        ag_relay(right, t, False).wait_send()
                        pl.when((z - 2 if right else z + 2) == t)(ag_relay(right, t, True).wait_send)
            return carry

        lax.fori_loop(0, n_z, one, 0)

    i_gp, i_gl, i_gv = wires.take(2 * n_z), wires.take(3 * kinds), wires.take(kinds)

    def pair_copies(t):
        return (
            wires.copy(i_gp + 2 * t, gdt.at[1 - core, t], pin_dn.at[t], at.partner()),
            wires.copy(i_gp + 2 * t + 1, gup.at[1 - core, t], pin_up.at[t], at.partner()),
        )

    def line_copy(t, src, dest, down):
        right, d = dest > src, abs(dest - src)
        block = gdt.at[core, t] if down else gup.at[core, t, dest]
        kind = n_z if down else t
        if d == 3:
            return wires.copy(i_gv + kind, block, via_dn if down else via_up.at[t], at.on_z(src + 1 if right else src - 1))
        slot = 2 if d == 2 else 0 if right else 1
        return wires.copy(
            i_gl + slot * kinds + kind, block, zin_dn.at[slot] if down else zin_up.at[slot, t], at.on_z(dest)
        )

    pairs_far_first = sorted(((s_, d_) for s_ in range(n_z) for d_ in range(n_z) if s_ != d_), key=lambda u: -abs(u[0] - u[1]))

    def held(src, dest):
        return relay and abs(dest - src) == 2 and src in (1, n_z - 2) and dest in (0, n_z - 1)

    def line_each(t, src, dest, act):
        act(False)
        pl.when(t == dest)(lambda: act(True))

    def fold(t):
        for c in pair_copies(t):
            c.wait_recv()
        add_into(gdt.at[core, t], pin_dn.at[t], 96)
        for zz in range(n_z):
            add_into(gup.at[core, t, zz], pin_up.at[t, zz], 48)
        for src, dest in pairs_far_first:
            if not held(src, dest):
                @pl.when(z == src)
                def _():
                    line_each(t, src, dest, lambda down: line_copy(t, src, dest, down).start())

    def add_far(t):
        for src, dest in pairs_far_first:
            if held(src, dest):
                @pl.when(z == src)
                def _():
                    def act(down):
                        line_copy(t, dest - 3 if dest > src else dest + 3, dest, down).wait_recv()
                        if down:
                            add_into(gdt.at[core, t], via_dn, 96)
                        else:
                            add_into(gup.at[core, t, dest], via_up.at[t], 48)
                        line_copy(t, src, dest, down).start()

                    line_each(t, src, dest, act)

    i_small = wires.take(1)

    def small_copy(i):
        return wires.copy(i_small, small_b, small_all.at[at.flat], at.numbered((at.flat + i) % n_dev))

    def each(n, act):
        def step(i, carry):
            act(i)
            return carry

        lax.fori_loop(1, n, step, 0)

    i_piece, i_line, i_pair, i_wo, i_wo2 = wires.take(3), wires.take(1), wires.take(2), wires.take(1), wires.take(1)

    def forward(q_v, k_v, v_v, xn_v, wide, att_acc, lse_acc, mid_v, mix_v, w_v, wo_v, up_s, down_s):
        stage = (
            pltpu.make_async_copy(up_hbm, up_s, load_sems.at[0]),
            pltpu.make_async_copy(down_hbm, down_s, load_sems.at[1]),
        )
        for c in stage:
            c.start()
        me_j = ex * n_dp + at.dp
        pieces = []
        for r in range(3):
            c = 3 * at.flat + r
            sec, j = c // n_dev, c % n_dev
            copy = wires.copy(i_piece + r, wq_ref.at[r], wt_a.at[sec], (j % n_dp, j // n_dp))
            away = j != me_j
            pl.when(away)(copy.start)
            pieces.append((copy, away, sec))
        each(n_dev, lambda i: small_copy(i).start())
        for m in range(seqs):
            for d in peers:
                token_copy(m, d).start()
        small_all[at.flat] = small_b[...]
        wo_b[core, ex, z] = wo_s[...]
        for m in range(seqs):
            inbox[m, ex] = x_ref[m]
        for r, (copy, away, sec) in enumerate(pieces):
            pl.when(away)(copy.wait_recv)

            @pl.when(jnp.logical_not(away))
            def _():
                wt_a[sec] = wq_ref[r]

        w_line = [wires.copy(i_line, wt_a, wt_b.at[core, z], at.on_z(at.z_peer(d))) for d in lines]
        for c in w_line:
            c.start()
        wo_line = [wires.copy(i_wo, wo_s, wo_b.at[core, ex, z], at.on_z(at.z_peer(d))) for d in lines]
        for c in wo_line:
            c.start()
        wt_b[core, z] = wt_a[...]
        for c in stage:
            c.wait()
        own = [
            pltpu.make_async_copy(up_s.at[:, t * tile : (t + 1) * tile], ag_block(t, z, core, False), load_sems.at[t % 2])
            for t in range(n_z)
        ] + [pltpu.make_async_copy(down_s, ag_block(0, z, core, True), load_sems.at[3])]
        for c in own[:2]:
            c.start()

        before = jnp.where(
            lax.broadcasted_iota(jnp.int32, (local_len, local_len), 1) < lax.broadcasted_iota(jnp.int32, (local_len, local_len), 0), 1.0, 0.0
        ).astype(bf)
        for m in range(seqs):
            named = jnp.where(lane == eid_s[m], 1.0, 0.0)
            earlier = jnp.sum(mm(before, named.astype(bf)) * named, axis=1, keepdims=True)
            slot_s[m] = eid_s[m] * cap + earlier

        wires.all_came(i_small, small_all.at[pl.ds(0, n_dev - 1)])
        smalls[...] = jnp.zeros(smalls.shape, f32)
        tally[...] = jnp.zeros(tally.shape, f32)
        for s in range(n_dev):
            block = small_all[s].astype(f32)
            tally[...] += block[8:16, :]
            lo = s * oc // 128 * 128
            spread = pltpu.roll(jnp.concatenate([block, jnp.zeros_like(block)], axis=1), s * oc - lo, 1)
            hi = min(lo + 256, dim)
            smalls[:, lo:hi] += spread[:, 0 : hi - lo]
        gain_one, shift_one = smalls[0:1, :], smalls[2:3, :]
        gain_two, shift_two = smalls[1:2, :], smalls[3:4, :]
        wires.all_came(i_line, wt_b.at[0, pl.ds(0, n_z - 1)])
        w_pair = wires.copy(i_pair, wt_b.at[core], wt_b.at[core], at.partner())
        w_pair.start()
        wires.all_came(i_wo, wo_b.at[0, 0, pl.ds(0, n_z - 1)])
        for step in range(min(2, n_z)):
            ag_start(order(step))
        wo_plane = [wires.copy(i_wo2, wo_b.at[core, ex], wo_b.at[core, ex], at.on_ex(at.ex_peer(d))) for d in peers]
        for c in wo_plane:
            c.start()
        w_pair.wait_recv()
        for sec in range(3):
            for zz in range(n_z):
                for cc in range(2):
                    row = (zz * 2 + cc) * piece
                    wide[row : row + piece, :] = wt_b[cc, zz, sec].astype(f32)
            w_v[sec] = wide[0:width, :].astype(bf)

        def project(m):
            def one(d, carry):
                src = (ex - d + n_ex) % n_ex

                @pl.when(d == 1)
                def _():
                    wires.all_came(i_tok + m, inbox.at[m, pl.ds(0, n_ex - 1)])

                rows = pl.ds(pl.multiple_of(src * local_len, local_len), local_len)
                hat, _ = normalised(inbox[m, src].reshape(local_len, dim).astype(f32))
                low = (hat * gain_one + shift_one).astype(bf)
                xn_v[rows, :] = low
                q_v[m, rows, :] = mm(low, w_v[0], NT).astype(bf)
                k_v[m, rows, :] = mm(low, w_v[1], NT).astype(bf)
                v_v[m, rows, :] = mm(low, w_v[2], NT).astype(bf)
                return carry

            lax.fori_loop(0, n_ex, one, 0)

        def attend(m):
            for i in range(n_ex):
                end = (i + 1) * local_len
                here = slice(i * local_len, end)

                def one_head(h, carry):
                    mine = lane_head == h
                    qb = q_v[m, here, :]
                    s = mm(jnp.where(mine, qb * scale, jnp.zeros_like(qb)), k_v[m, 0:end, :], NT)
                    top = jnp.max(s, axis=-1, keepdims=True)
                    e = jnp.exp(s - top)
                    total = jnp.sum(e, axis=-1, keepdims=True)
                    p = (e * (1.0 / total)).astype(bf)
                    att_acc[...] = jnp.where(mine, mm(p, v_v[m, 0:end, :]), att_acc[...])
                    lse_acc[...] = jnp.where(lane == h.astype(f32), top + jnp.log(total), lse_acc[...])
                    return carry

                lax.fori_loop(0, heads, one_head, 0)
                rowbox[m, i] = side_by_side(att_acc[...].astype(bf))
                lse[m, :, here] = lse_acc[...].T[0:8, :]
            for d in peers:
                back_copy(m, d).start()
            attr[m, ex] = rowbox[m, ex]

        def route(m):
            wires.all_came(i_back + m, attr.at[m, pl.ds(0, n_ex - 1)])
            mid = x_ref[m].reshape(local_len, dim).astype(f32)
            for b in range(n_ex):
                mid += mm(stacked(attr[m, b]), wo_v[b], NT)
            mid_v[m] = mid
            hat, _ = normalised(mid)
            mixed = (hat * gain_two + shift_two).astype(bf)
            mix_v[m] = mixed
            logits = mm(mixed, smalls[...].astype(bf), NT)
            mine = lax.broadcasted_iota(jnp.int32, logits.shape, 1).astype(f32) == eid_s[m][:, 0:1] + 4.0
            gate = jax.nn.sigmoid(jnp.sum(jnp.where(mine, logits, 0.0), axis=1, keepdims=True))
            gate_s[m] = jnp.broadcast_to(gate, (local_len, 128))
            scaled = (gate * cot_ref[m].astype(f32)).astype(bf)
            place = jnp.where(
                slot_s[m].T[0:1, :] == lax.broadcasted_iota(jnp.int32, (slots, local_len), 0).astype(f32), 1.0, 0.0
            ).astype(bf)
            outbox[m, :, 0] = mm(place, mixed).astype(bf).reshape(n_ex, cap, dim)
            outbox[m, :, 1] = mm(place, scaled).astype(bf).reshape(n_ex, cap, dim)
            for d in peers:
                out_copy(m, d).start()
            work[m, ex] = outbox[m, ex]

        att_acc[...] = jnp.zeros(att_acc.shape, f32)
        lse_acc[...] = jnp.zeros(lse_acc.shape, f32)

        def xn_out(m):
            return pltpu.make_async_copy(xn_v, xn_hbm.at[m], load_sems.at[2])

        project(0)
        xn_out(0).start()
        attend(0)
        for i, c in enumerate(own):
            if i >= 2:
                if i < n_z:
                    own[i - 2].wait()
                c.start()
        for c in own[n_z - 2 :]:
            c.wait()
        for m in range(1, seqs):
            xn_out(m - 1).wait()
            project(m)
            xn_out(m).start()
            if m == 1:
                ag_pass(order(0))
                for step in range(2, n_z - 1):
                    ag_start(order(step))
            attend(m)
        ag_pass(order(1))
        if n_z > 2:
            ag_start(order(n_z - 1))
        wires.all_came(i_wo2, wo_b.at[0, pl.ds(0, n_ex - 1)])
        wo_pair = wires.copy(i_pair + 1, wo_b.at[core], wo_b.at[core], at.partner())
        wo_pair.start()
        wo_pair.wait_recv()
        for b in range(n_ex):
            for s in range(n_dev):
                wide[s * oc : (s + 1) * oc, 0:width] = wo_b[s // n_ex % 2, s % n_ex, s // n_ex // 2, b].astype(f32)
            wo_v[b] = wide[0:dim, 0:width].astype(bf)
        for m in range(seqs):
            route(m)
        xn_out(seqs - 1).wait()
        keep = [
            pltpu.make_async_copy(src, dst, load_sems.at[i])
            for i, (src, dst) in enumerate(((q_v, q_hbm), (k_v, k_hbm), (v_v, v_hbm), (mid_v, mid_hbm), (mix_v, mix_hbm), (w_v, w_hbm), (wo_v, wo_hbm)))
        ]
        for c in keep:
            c.start()
        for m in range(seqs):
            wires.all_left(i_back + m, attr.at[m, pl.ds(0, n_ex - 1)])
            wires.all_left(i_tok + m, inbox.at[m, pl.ds(0, n_ex - 1)])
        for copy, away, _ in pieces:
            pl.when(away)(copy.wait_send)
        wires.all_left(i_small, small_all.at[pl.ds(0, n_dev - 1)])
        wires.all_left(i_line, wt_b.at[0, pl.ds(0, n_z - 1)])
        wires.all_left(i_wo, wo_b.at[0, 0, pl.ds(0, n_z - 1)])
        wires.all_left(i_wo2, wo_b.at[0, pl.ds(0, n_ex - 1)])
        for c in (w_pair, wo_pair):
            c.wait_send()
        for c in keep:
            c.wait()

    pl.run_scoped(
        forward,
        pltpu.VMEM((seqs, total_len, width), bf), pltpu.VMEM((seqs, total_len, width), bf), pltpu.VMEM((seqs, total_len, width), bf),
        pltpu.VMEM((total_len, dim), bf), pltpu.VMEM((dim, dim), f32),
        pltpu.VMEM((local_len, width), f32), pltpu.VMEM((local_len, 128), f32),
        pltpu.VMEM((seqs, local_len, dim), f32), pltpu.VMEM((seqs, local_len, dim), bf),
        pltpu.VMEM((3, width, dim), bf), pltpu.VMEM((n_ex, dim, width), bf),
        pltpu.VMEM((shard, ff), bf), pltpu.VMEM((half, dim), bf),
    )

    def experts(up_t, down_t, res_acc, gar_acc, hid, gpre, x_t, g_t):
        sub = 256 if tile % 256 == 0 else tile
        pair = n_z - 2

        def loads(step, slot):
            return (
                pltpu.make_async_copy(up_full.at[order(step)], up_t.at[slot], load_sems.at[2 * slot]),
                pltpu.make_async_copy(down_full.at[ag_columns(order(step)), :], down_t.at[slot], load_sems.at[2 * slot + 1]),
            )

        def fetch(step, slot):
            ag_far(order(step))
            ag_ready(order(step))
            for c in loads(step, slot):
                c.start()

        fetch(0, 0)

        def one_round(k, carry):
            per = jnp.where(k == pair, 2, 1)

            def one(q, q_carry):
                m, step = q // per, k + q % per
                j = step % 2
                mine = pl.ds(pl.multiple_of(m * slots, slots), slots)

                @pl.when(m == 0)
                def _():
                    for c in loads(step, j):
                        c.wait()

                @pl.when(step == 0)
                def _():
                    wires.all_came(i_out + m, work.at[m, pl.ds(0, n_ex - 1)])
                    wires.all_left(i_out + m, work.at[m, pl.ds(0, n_ex - 1)])
                    res_acc[m] = jnp.zeros((slots, dim), f32)
                    gar_acc[m] = jnp.zeros((slots, dim), f32)

                def one_sub(u, c_):
                    cols = pl.ds(pl.multiple_of(u * sub, sub), sub)
                    rows = work[m, :, 0].reshape(slots, dim)
                    grads = work[m, :, 1].reshape(slots, dim)
                    pre = mm(rows, up_t[j, :, cols])
                    cdf = 0.5 * (1.0 + lax.erf(pre * (2.0 ** -0.5)))
                    hidden = (pre * cdf).astype(bf)
                    slope = cdf + pre * jnp.exp(-0.5 * pre * pre) * ((2.0 * math.pi) ** -0.5)
                    hid[j, mine, cols] = hidden
                    res_acc[m] += mm(hidden, down_t[j, cols, :])
                    low = (mm(grads, down_t[j, cols, :], NT) * slope).astype(bf)
                    gpre[j, mine, cols] = low
                    gar_acc[m] += mm(low, up_t[j, :, cols], NT)
                    return c_

                lax.fori_loop(0, tile // sub, one_sub, 0)

                @pl.when(step == n_z - 1)
                def _():
                    outbox[m, :, 0] = res_acc[m].astype(bf).reshape(n_ex, cap, dim)
                    outbox[m, :, 1] = gar_acc[m].astype(bf).reshape(n_ex, cap, dim)
                    for d in peers:
                        return_copy(m, d).start()
                    inbox[m, ex] = outbox[m, ex]

                for ahead in range(2, n_z):
                    @pl.when((k == ahead - 2) & (q == 0))
                    def _():
                        ag_pass(order(ahead))

                pl.when((k == pair) & (q == 0))(lambda: fetch(n_z - 1, (n_z - 1) % 2))
                for late in range(n_z - 2):
                    pl.when((k == late + 1) & (q == 0))(lambda: fold(order(late)))
                if n_z > 3:
                    pl.when((k == pair) & (q == seqs))(lambda: add_far(order(0)))
                return q_carry

            lax.fori_loop(0, seqs * per, one, 0)

            @pl.when(k == 0)
            def _():
                for s in range(seqs):
                    lanes = slice(s * slots, (s + 1) * slots)
                    x_t[:, lanes] = work[s, :, 0].reshape(slots, dim).T
                    g_t[:, lanes] = work[s, :, 1].reshape(slots, dim).T

            def weight_grads(jj, jj_carry):
                step = k + jj
                j, t = step % 2, order(step)
                pl.when(k < pair)(lambda: fetch(step + 1, 1 - j))

                def some(u, c_):
                    at_rows = pl.ds(pl.multiple_of(u * mid_dim, mid_dim), mid_dim)
                    up_grad = mm(x_t[at_rows, :], gpre[j]).astype(bf)
                    for s in range(n_z):
                        gup[s % 2, t, u * (n_z // 2) + s // 2] = up_grad[s * shard : (s + 1) * shard, :]
                    down_grad = mm(g_t[at_rows, :], hid[j]).astype(bf)
                    for c in range(2):
                        gdt[c, t, at_rows, :] = down_grad[:, c * half : (c + 1) * half]
                    return c_

                lax.fori_loop(0, 2, some, 0)
                for c in pair_copies(t):
                    c.start()
                pl.when(step == n_z - 1)(lambda: fold(order(n_z - 2)))
                return jj_carry

            lax.fori_loop(0, per, weight_grads, 0)
            return carry

        lax.fori_loop(0, pair + 1, one_round, 0)

    every = seqs * slots
    pl.run_scoped(
        experts,
        pltpu.VMEM((2, dim, tile), bf), pltpu.VMEM((2, tile, dim), bf),
        pltpu.VMEM((seqs, slots, dim), f32), pltpu.VMEM((seqs, slots, dim), f32),
        pltpu.VMEM((2, every, tile), bf), pltpu.VMEM((2, every, tile), bf),
        pltpu.VMEM((dim, every), bf), pltpu.VMEM((dim, every), bf),
    )
    fold(order(n_z - 1))
    ag_finish()

    gain_one, gain_two = smalls[0:1, :], smalls[1:2, :]
    counts = jnp.where(lane < n_ex, 16.0 * tally[0:1, :] + tally[1:2, :], 0.0)
    mean_load = jnp.sum(counts, axis=1, keepdims=True) / n_ex
    load_ratio = (counts - mean_load) / mean_load
    small_out[...] = jnp.zeros(small_out.shape, f32)
    i_gob, i_gw = wires.take(3), wires.take(5)
    gob_pair_copy = wires.copy(i_gob, gob.at[1 - core], gob_pair, at.partner())

    def gob_plane_copy(d):
        peer = at.ex_peer(d)
        return wires.copy(i_gob + 1, gob.at[core, peer], gob_plane.at[d - 1], at.on_ex(peer))

    def gob_line_copy(d):
        peer = at.z_peer(d)
        return wires.copy(i_gob + 2, gob_mine.at[peer], gob_line.at[d - 1], at.on_z(peer))

    gws_pair_copy = wires.copy(i_gw, gws.at[1 - core], gws_pair, at.partner())

    def gws_line_copy(d):
        peer = at.z_peer(d)
        return wires.copy(i_gw + 1, gws.at[core, peer], gws_line.at[d - 1], at.on_z(peer))

    me_j = ex * n_dp + at.dp
    finals = []
    for sec in range(3):
        c = sec * n_dev + me_j
        owner, r = c // 3, c % 3
        copy = wires.copy(i_gw + 2 + r, gws_sum.at[sec], gq_in.at[r], at.numbered(owner))
        finals.append((copy, owner != at.flat, sec, r))

    i_last = wires.take(1)

    def window(t):
        return pl.ds(pl.multiple_of(t * oc // 128 * 128, 128), 256)

    def last_copy(i):
        t = (at.flat + i) % n_dev
        return wires.copy(i_last, small_out.at[:, window(t)], small_in.at[at.flat], at.numbered(t))

    def backward(ga_v, gb_t, q_v, k_v, v_v, xn_v, mix_v, mid_v, w_v, wo_v, dq, dk, dv, gw, gtok, out_v):
        pairs = ((wo_hbm, wo_v), (mix_hbm, mix_v), (mid_hbm, mid_v), (w_hbm, w_v), (q_hbm, q_v), (k_hbm, k_v), (v_hbm, v_v))
        brought = [pltpu.make_async_copy(src, dst, load_sems.at[i]) for i, (src, dst) in enumerate(pairs)]
        for c in brought:
            c.start()
        for c in brought:
            c.wait()

        def head(m):
            wires.all_came(i_ret + m, inbox.at[m, pl.ds(0, n_ex - 1)])
            wires.all_left(i_ret + m, inbox.at[m, pl.ds(0, n_ex - 1)])
            def some_rows(u, carry):
                at_rows = pl.ds(pl.multiple_of(u * 128, 128), 128)
                place = jnp.where(
                    slot_s[m, at_rows, 0:1] == lax.broadcasted_iota(jnp.int32, (128, slots), 1).astype(f32), 1.0, 0.0
                ).astype(bf)
                expert_out = mm(place, inbox[m, :, 0].reshape(slots, dim))
                gate, named = gate_s[m, at_rows, 0:1], eid_s[m, at_rows, :]
                cot = cot_ref[m, at_rows, :].astype(f32)
                out_v[m, at_rows, :] = (mid_v[m, at_rows, :] + gate * expert_out).astype(bf)
                grad_gate = jnp.sum(cot * expert_out, axis=1, keepdims=True) + balance_coef * jnp.sum(
                    jnp.where(lane == named, load_ratio, 0.0), axis=1, keepdims=True
                )
                grad_logit = grad_gate * gate * (1.0 - gate)
                grad_mixed = mm(place, inbox[m, :, 1].reshape(slots, dim))
                mixed = mix_v[m, at_rows, :].astype(f32)
                for e in range(n_ex):
                    routed = jnp.where(named[:, 0:1] == float(e), grad_logit, 0.0)
                    grad_mixed += routed * smalls[4 + e : 5 + e, :]
                    small_out[4 + e : 5 + e, 0:dim] += jnp.sum(routed * mixed, axis=0, keepdims=True)
                hat, inv = normalised(mid_v[m, at_rows, :])
                small_out[1:2, 0:dim] += jnp.sum(grad_mixed * hat, axis=0, keepdims=True)
                small_out[3:4, 0:dim] += jnp.sum(grad_mixed, axis=0, keepdims=True)
                grad_middle = norm_back(grad_mixed * gain_two, hat, inv) + cot
                gtok[m, at_rows, :] = grad_middle
                branch = grad_middle.astype(bf)
                for e in range(n_ex):
                    ga_v[e, at_rows, :] = mm(branch, wo_v[e]).astype(bf)
                gb_t[m, :, at_rows] = branch.T
                return carry

            lax.fori_loop(0, local_len // 128, some_rows, 0)
            for e in range(n_ex):
                rowbox[m, e] = side_by_side(ga_v[e])
            for d in peers:
                ga_copy(m, d).start()
            gar[m, ex] = rowbox[m, ex]

        head(0)
        if n_z > 2:
            add_far(order(n_z - 3))
        for m in range(1, seqs):
            head(m)
        wrote = pltpu.make_async_copy(out_v, out_hbm, load_sems.at[0])
        wrote.start()

        for b in range(n_ex):
            total = mm(gb_t[0], stacked(attr[0, b]))
            for m in range(1, seqs):
                total += mm(gb_t[m], stacked(attr[m, b]))
            for s in range(n_dev):
                gob[s // n_ex % 2, s % n_ex, s // n_ex // 2, b] = total[s * oc : (s + 1) * oc].astype(bf)
        gob_pair_copy.start()
        gw[...] = jnp.zeros(gw.shape, f32)

        def gob_up():
            gob_pair_copy.wait()
            for e in range(n_ex):
                for zz in range(n_z):
                    gob[core, e, zz] = (gob[core, e, zz].astype(f32) + gob_pair[e, zz].astype(f32)).astype(bf)
            for d in peers:
                gob_plane_copy(d).start()

        def attention_back(m, first=lambda: None):
            xn_copy = pltpu.make_async_copy(xn_hbm.at[m], xn_v, load_sems.at[7])
            xn_copy.start()
            wires.all_came(i_ga + m, gar.at[m, pl.ds(0, n_ex - 1)])
            wires.all_left(i_ga + m, gar.at[m, pl.ds(0, n_ex - 1)])
            first()
            dk[...] = jnp.zeros(dk.shape, f32)
            dv[...] = jnp.zeros(dv.shape, f32)
            dq[...] = jnp.zeros(dq.shape, f32)
            for i in reversed(range(n_ex)):
                end = (i + 1) * local_len
                here = slice(i * local_len, end)
                ga = stacked(gar[m, i])

                def one_head(h, carry):
                    mine = lane_head == h
                    qb = q_v[m, here, :]
                    q_h = jnp.where(mine, qb * scale, jnp.zeros_like(qb))
                    ga_h = jnp.where(mine, ga, jnp.zeros_like(ga))
                    kk = k_v[m, 0:end, :]
                    p = jnp.exp(mm(kk, q_h, NT) - lse[m, pl.ds(h, 1), here])
                    dp = mm(v_v[m, 0:end, :], ga_h, NT)
                    delta = jnp.sum(p * dp, axis=0, keepdims=True)
                    ds = (p * (dp - delta)).astype(bf)
                    dv[0:end, :] += mm(p.astype(bf), ga_h)
                    dk[0:end, :] += mm(ds, q_h)
                    dq[here, :] += jnp.where(mine, mm(ds, kk, TN) * scale, 0.0)
                    return carry

                lax.fori_loop(0, heads, one_head, 0)
                part = mm(dq[here, :].astype(bf), w_v[0]) + mm(dk[here, :].astype(bf), w_v[1]) + mm(dv[here, :].astype(bf), w_v[2])
                outbox[m, i] = part.astype(bf).reshape(2, cap, dim)
                for d in peers:
                    pl.when(at.ex_peer(d) == i)(part_copy(m, d).start)
            inbox[m, ex] = outbox[m, ex]
            xn_copy.wait()
            for sec, g in enumerate((dq, dk, dv)):
                gw[sec] += mm(g[...].astype(bf), xn_v[...], TN)

        attention_back(0, gob_up)
        if n_z > 2:
            add_far(order(n_z - 2))
        wires.all_came(i_gob + 1, gob_plane)
        wires.all_left(i_gob + 1, gob_plane)
        for zz in range(n_z):
            total = gob[core, ex, zz].astype(f32)
            for d in peers:
                total += gob_plane[d - 1, zz].astype(f32)
            gob_mine[zz] = total.astype(bf)
        for d in lines:
            gob_line_copy(d).start()
        for m in range(1, seqs):
            attention_back(m)
        add_far(order(n_z - 1))
        for sec in range(3):
            for j in range(n_dp):
                gws[j % 2, j // 2, sec] = gw[sec, j * piece : (j + 1) * piece, :].astype(bf)
        gws_pair_copy.start()
        gws_pair_copy.wait()
        gws[core] = (gws[core].astype(f32) + gws_pair[...].astype(f32)).astype(bf)
        for d in lines:
            gws_line_copy(d).start()

        def tail(m):
            wires.all_came(i_part + m, inbox.at[m, pl.ds(0, n_ex - 1)])
            wires.all_left(i_part + m, inbox.at[m, pl.ds(0, n_ex - 1)])
            grad_normed = jnp.zeros((local_len, dim), f32)
            for e in range(n_ex):
                grad_normed += inbox[m, e].reshape(local_len, dim).astype(f32)
            hat, inv = normalised(x_ref[m].reshape(local_len, dim).astype(f32))
            small_out[0:1, 0:dim] += jnp.sum(grad_normed * hat, axis=0, keepdims=True)
            small_out[2:3, 0:dim] += jnp.sum(grad_normed, axis=0, keepdims=True)
            gtok[m] += norm_back(grad_normed * gain_one, hat, inv)

        for m in range(seqs):
            tail(m)
        each(n_dev, lambda i: last_copy(i).start())
        small_in[at.flat] = small_out[:, window(at.flat)]
        wrote.wait()
        wrote_tok = pltpu.make_async_copy(gtok, gtok_hbm, load_sems.at[0])
        wrote_tok.start()
        wires.all_came(i_gw + 1, gws_line)
        wires.all_left(i_gw + 1, gws_line)
        total = gws[core, z].astype(f32)
        for d in lines:
            total += gws_line[d - 1].astype(f32)
        gws_sum[...] = total.astype(bf)
        for copy, away, sec, r in finals:
            pl.when(away)(copy.start)
        wrote_tok.wait()

    pl.run_scoped(
        backward,
        pltpu.VMEM((n_ex, local_len, width), bf), pltpu.VMEM((seqs, dim, local_len), bf),
        pltpu.VMEM((seqs, total_len, width), bf), pltpu.VMEM((seqs, total_len, width), bf), pltpu.VMEM((seqs, total_len, width), bf),
        pltpu.VMEM((total_len, dim), bf), pltpu.VMEM((seqs, local_len, dim), bf), pltpu.VMEM((seqs, local_len, dim), f32),
        pltpu.VMEM((3, width, dim), bf), pltpu.VMEM((n_ex, dim, width), bf),
        pltpu.VMEM((total_len, width), f32), pltpu.VMEM((total_len, width), f32), pltpu.VMEM((total_len, width), f32),
        pltpu.VMEM((3, width, dim), f32),
        pltpu.VMEM((seqs, local_len, dim), f32), pltpu.VMEM((seqs, local_len, dim), bf),
    )

    wires.all_came(i_gob + 2, gob_line)
    wires.all_left(i_gob + 2, gob_line)
    total = gob_mine[z].astype(f32)
    for d in lines:
        total += gob_line[d - 1].astype(f32)
    gout_ref[...] = jnp.concatenate([total[b] for b in range(n_ex)], axis=1)

    def settle(up_v, down_v):
        def done(t, carry):
            for c in pair_copies(t):
                c.wait_send()
            for src, dest in pairs_far_first:
                pl.when(z == src)(lambda: line_each(t, src, dest, lambda down: line_copy(t, src, dest, down).wait_send()))
                if abs(dest - src) < 3:
                    pl.when(z == dest)(lambda: line_each(t, src, dest, lambda down: line_copy(t, src, dest, down).wait_recv()))
            return carry

        lax.fori_loop(0, n_z, done, 0)
        for dest in range(n_z):
            came = [s for s in range(n_z) if s != dest and abs(s - dest) < 3]
            places = [2 if abs(s - dest) == 2 else 0 if dest > s else 1 for s in came]

            @pl.when(z == dest)
            def _():
                def some_up(t, carry):
                    total = gup[core, t, dest].astype(f32)
                    for s in places:
                        total += zin_up[s, t].astype(f32)
                    up_v[:, ag_columns(t)] = total
                    return carry

                def some_down(u, carry):
                    at_rows = pl.ds(pl.multiple_of(u * 128, 128), 128)
                    total = gdt[core, dest, at_rows, :].astype(f32)
                    for s in places:
                        total += zin_dn[s, at_rows, :].astype(f32)
                    down_v[:, at_rows] = total.T
                    return carry

                lax.fori_loop(0, n_z, some_up, 0)
                lax.fori_loop(0, dim // 128, some_down, 0)

        wrote = (pltpu.make_async_copy(up_v, gup_hbm, load_sems.at[0]), pltpu.make_async_copy(down_v, gdown_hbm, load_sems.at[1]))
        for c in wrote:
            c.start()
        for c in wrote:
            c.wait()

    pl.run_scoped(settle, pltpu.VMEM((shard, ff), f32), pltpu.VMEM((half, dim), f32))
    for copy, away, sec, r in finals:
        @pl.when(away)
        def _():
            copy.wait()

        @pl.when(jnp.logical_not(away))
        def _():
            gq_in[r] = gws_sum[sec]

    for r in range(3):
        gq_ref[r * piece : (r + 1) * piece, :] = gq_in[r].astype(f32)
    wires.all_came(i_last, small_in.at[pl.ds(0, n_dev - 1)])
    wires.all_left(i_last, small_in.at[pl.ds(0, n_dev - 1)])
    total = jnp.zeros((8, 256), f32)
    for s in range(n_dev):
        total += small_in[s]
    gsmall_ref[...] = total


def whole_layer(n_dp, n_ex, x, cot, ids, wq, wo, gains, biases, router, w_up, w_down):
    bf, f32 = jnp.bfloat16, jnp.float32
    seqs, local_len, dim = cot.shape
    width, total_len, n_z, n_dev = dim // n_ex, local_len * n_ex, n_dp // 2, n_dp * n_ex
    cap = x.shape[2]
    shard, ff = w_up.shape
    half = w_down.shape[0]
    piece, oc, tile = wq.shape[1], wo.shape[0], ff // n_z
    vmem_outs = [((3 * piece, dim), f32), ((oc, dim), f32), ((8, 256), f32)]
    hbm_outs = [
        ((seqs, local_len, dim), bf), ((seqs, local_len, dim), f32), ((shard, ff), f32), ((half, dim), f32),
        ((n_z, dim, ff // n_z), bf), ((ff, dim), bf),
        ((seqs, total_len, width), bf), ((seqs, total_len, width), bf), ((seqs, total_len, width), bf), ((seqs, total_len, dim), bf),
        ((seqs, local_len, dim), bf), ((seqs, local_len, dim), f32), ((3, width, dim), bf), ((n_ex, dim, width), bf),
    ]
    box = pltpu.VMEM((seqs, n_ex, 2, cap, dim), bf)
    rows = pltpu.VMEM((seqs, n_ex, local_len // 2, 2 * width), bf)
    n_sems = 2 + 6 * seqs + 14 * (n_z + 1) + 2 * n_z + 8 + 8
    sems = pltpu.SemaphoreType.DMA((n_sems,))
    return pl.pallas_call(
        functools.partial(layer_kernel, n_dp, n_ex),
        out_shape=[jax.ShapeDtypeStruct(s, d) for s, d in vmem_outs + hbm_outs],
        in_specs=[VMEM] * 8 + [HBM] * 2,
        out_specs=[VMEM] * len(vmem_outs) + [HBM] * len(hbm_outs),
        scratch_shapes=[
            box, box, box,
            pltpu.VMEM((2, n_z, dim, half), bf), pltpu.VMEM((2, n_z, n_z, shard, tile), bf),
            pltpu.VMEM((n_z, dim, half), bf), pltpu.VMEM((n_z, n_z, shard, tile), bf),
            pltpu.VMEM((3, dim, half), bf), pltpu.VMEM((3, n_z, shard, tile), bf),
            pltpu.VMEM((dim, half), bf), pltpu.VMEM((n_z, shard, tile), bf),
            rows, rows, rows,
            pltpu.VMEM((2, n_ex, n_z, n_ex, oc, width), bf), pltpu.VMEM((n_ex, n_z, n_ex, oc, width), bf),
            pltpu.VMEM((n_z - 1, n_ex, oc, width), bf), pltpu.VMEM((n_z, n_ex, oc, width), bf), pltpu.VMEM((n_ex - 1, n_z, n_ex, oc, width), bf),
            pltpu.VMEM((3, piece, dim), bf), pltpu.VMEM((2, n_z, 3, piece, dim), bf), pltpu.VMEM((n_z, 3, piece, dim), bf),
            pltpu.VMEM((n_z - 1, 3, piece, dim), bf), pltpu.VMEM((3, piece, dim), bf),
            pltpu.VMEM((16, 128), bf), pltpu.VMEM((n_ex, oc, width), bf), pltpu.VMEM((3, piece, dim), bf),
            pltpu.VMEM((n_dev, 16, 128), bf), pltpu.VMEM((n_dev, 8, 256), f32), pltpu.VMEM((8, dim + 256), f32),
            pltpu.VMEM((16, dim), f32), pltpu.VMEM((8, 128), f32),
            pltpu.VMEM((seqs, local_len, 128), f32), pltpu.VMEM((seqs, local_len, 128), f32), pltpu.VMEM((seqs, local_len, 128), f32),
            pltpu.VMEM((seqs, 8, total_len), f32),
            sems, sems, pltpu.SemaphoreType.DMA((8,)),
        ],
        compiler_params=pltpu.CompilerParams(collective_id=0, has_side_effects=True, vmem_limit_bytes=67043328),
        name="whole_layer",
    )(x, cot, ids, wq, wo, gains, biases, router, w_up, w_down)


def fast_body(tokens, cotangent, expert_ids, w_qkv, w_out, ln_gains, ln_biases, router, w_up, w_down):
    n_expert, n_dp = lax.axis_size("expert"), lax.axis_size("dp")
    seqs, local_len, dim = tokens.shape[0] * tokens.shape[1], tokens.shape[2], tokens.shape[3]
    qc, oc = w_qkv.shape[1], w_out.shape[1]
    n_small = 4 + n_expert
    flat = lax.axis_index("dp") * n_expert + lax.axis_index("expert")
    got = whole_layer(
        n_dp, n_expert, tokens.reshape(seqs, 2, local_len // 2, dim), cotangent.reshape(seqs, local_len, dim), expert_ids.reshape(seqs, local_len),
        w_qkv.T.reshape(3, qc // 3, dim), w_out.T, ln_gains, ln_biases, router, w_up[0], w_down[0],
    )
    gq, gout, gs, output, grad_tokens, gu, gd = got[:7]
    grad_qkv, grad_out = gq.T, gout.T
    gs = lax.dynamic_slice(gs, (0, lax.rem(flat * oc, 128)), (n_small, oc))
    shape = tokens.shape
    return (output.reshape(shape), grad_tokens.reshape(shape), grad_qkv, grad_out, gs[0:2], gs[2:4], gs[4:].T, gu[None], gd[None])


def solution(mesh):
    in_specs = (
        P(None, "dp", "expert", None),
        P(None, "dp", "expert", None),
        P(None, "dp", "expert", None),
        P(None, ("dp", "expert")),
        P(None, ("dp", "expert")),
        P(None, ("dp", "expert")),
        P(None, ("dp", "expert")),
        P(("dp", "expert"), None),
        P("expert", "dp", None),
        P("expert", "dp", None),
    )
    out_specs = (
        P(None, "dp", "expert", None),
        P(None, "dp", "expert", None),
        P(None, ("dp", "expert")),
        P(None, ("dp", "expert")),
        P(None, ("dp", "expert")),
        P(None, ("dp", "expert")),
        P(("dp", "expert"), None),
        P("expert", "dp", None),
        P("expert", "dp", None),
    )
    n_expert, n_dp = mesh.shape["expert"], mesh.shape["dp"]
    chosen = fast_body if n_expert == 4 and n_dp % 4 == 0 and n_dp <= 8 else body
    return jax.shard_map(chosen, mesh=mesh, in_specs=in_specs, out_specs=out_specs, check_vma=False)
```
